32 devices in a mesh: var: 4 (over y, x), patch: 8 (over z, core).
Axes of the slice: x: 2, y: 2, z: 4, core: 2. Of those that a mesh axis runs over, the one named last changes fastest.
Arguments:
- field_patches: bfloat16 [48, 4, 8, 2048], P('var', None, 'patch'), may hold values from -6 to 6
- var_ids: int32 [48], replicated, may hold values from 0 to 47, each once
- lead_bucket: int32 [8], P('patch'), may hold values from 0 to 7
- patch_weight: bfloat16 [48, 4, 1024], P('var'), may hold values from -3 to 3
- var_embed: bfloat16 [48, 1024], replicated, may hold values from -6 to 6
- agg_query: bfloat16 [1024], replicated, may hold values from -6 to 6
- agg_key: bfloat16 [1024, 1024], replicated, may hold values from -0.1875 to 0.1875
- agg_value: bfloat16 [1024, 1024], replicated, may hold values from -0.1875 to 0.1875
- agg_out: bfloat16 [1024, 1024], replicated, may hold values from -0.375 to 0.375
- lead_table: bfloat16 [8, 1024], replicated, may hold values from -3 to 3
- ln1_gain: bfloat16 [1024], replicated, may hold values from 0.099609375 to 1.8984375
- attn_qkv: bfloat16 [1024, 3072], replicated, may hold values from -0.25 to 0.25
- attn_out: bfloat16 [1024, 1024], replicated, may hold values from -1.5 to 1.5
- ln2_gain: bfloat16 [1024], replicated, may hold values from 0.099609375 to 1.8984375
- mlp_in: bfloat16 [1024, 4096], replicated, may hold values from -0.1875 to 0.1875
- mlp_in_bias: bfloat16 [4096], replicated, may hold values from -3 to 3
- mlp_out: bfloat16 [4096, 1024], replicated, may hold values from -0.125 to 0.125
- cotangent: bfloat16 [8, 2048, 1024], P('patch', 'var'), may hold values from -6 to 6
Outputs:
- output: bfloat16 [8, 2048, 1024], P('patch', 'var')
- field_grad: float32 [48, 4, 8, 2048], P('var', None, 'patch')
- patch_weight_grad: float32 [48, 4, 1024], P('var')
- var_embed_grad: float32 [48, 1024], P('var')
- agg_query_grad: float32 [1024], P('var')
- agg_key_grad: float32 [1024, 1024], P('var')
- agg_value_grad: float32 [1024, 1024], P('var')
- agg_out_grad: float32 [1024, 1024], P('var')
- lead_table_grad: float32 [8, 1024], P('var')
- ln1_gain_grad: float32 [1024], P('var')
- attn_qkv_grad: float32 [1024, 3072], P('var')
- attn_out_grad: float32 [1024, 1024], P('var')
- ln2_gain_grad: float32 [1024], P('var')
- mlp_in_grad: float32 [1024, 4096], P('var')
- mlp_in_bias_grad: float32 [4096], P('var')
- mlp_out_grad: float32 [4096, 1024], P('var')
The draws below stay inside these ranges and needn't reach their ends.
Inputs may be any that keep to these rules, and one draw needn't show every extreme that they name: var_ids names each of the 48 variables once.
All inputs are finite; a program needn't handle non-finite values.
Results may differ from the reference program's by a relative error of at most 0.02.
Values may be sent and summed in bfloat16 or wider, within the bound.
No kernel may reach another device: no remote copies, remote signals or barrier semaphores. Data moves between devices by JAX's collectives and lax.ppermute only.
A program may use at most 256 MiB of HBM per device.

```python
import jax
import jax.numpy as jnp
from jax import lax

D = 1024
HEADS = 16
FF = 4096
VARS = 48
PIX = 4
LEADS = 8
SEQ = 2048
SAMPLES = 8


def set_ends(array, key, low, largest):
    longest = array.shape.index(max(array.shape))
    spots = []
    for shift in (0, 1):
        where = [jax.random.randint(jax.random.fold_in(key, axis), (), 0, length) for axis, length in enumerate(array.shape)]
        where[longest] = (where[longest] + shift) % array.shape[longest]
        spots.append(tuple(where))
    return array.at[spots[0]].set(low).at[spots[1]].set(largest)


def block_scale(key, extent, cuts, low, top_value):
    level, own = 1.0, jax.random.fold_in(key, 6)
    for axis_at, parts in cuts:
        heights = jnp.exp(jax.random.uniform(jax.random.fold_in(own, axis_at), (parts,), jnp.float32, low / len(cuts), top_value / len(cuts)))
        level = level * jnp.repeat(heights, extent[axis_at] // parts).reshape([-1 if axis == axis_at else 1 for axis in range(len(extent))])
    return level


def bell_draw(key, shape, scale, most, cuts=(), kind=jnp.bfloat16):
    gain = block_scale(key, shape, cuts, -0.22, 0.18) if cuts else 1.0
    entries = jax.random.normal(key, shape, jnp.float32) * scale * gain
    return jnp.minimum(jnp.maximum(entries, -most), most).astype(kind)


def setup_inputs(seed: int = 0) -> dict:
    keys = jax.random.split(jax.random.key(seed), 19)
    field_patches = bell_draw(keys[0], (VARS, PIX, SAMPLES, SEQ), 1.0, 6.0, ((0, 4), (2, 8)))
    var_ids = jax.random.permutation(keys[1], VARS).astype(jnp.int32)
    lead_bucket = set_ends(jax.random.randint(keys[2], (SAMPLES,), 0, LEADS), jax.random.fold_in(keys[2], 1), 0, LEADS - 1).astype(jnp.int32)
    patch_weight = bell_draw(keys[3], (VARS, PIX, D), PIX ** -0.5, 3.0, ((0, 4),))
    var_embed = bell_draw(keys[4], (VARS, D), 1.0, 6.0)
    agg_query = bell_draw(keys[5], (D,), 1.5, 6.0)
    agg_key = bell_draw(keys[6], (D, D), D ** -0.5, 0.1875)
    agg_value = bell_draw(keys[7], (D, D), D ** -0.5, 0.1875)
    agg_out = bell_draw(keys[8], (D, D), (D // 4) ** -0.5, 0.375)
    lead_table = bell_draw(keys[9], (LEADS, D), 0.5, 3.0)
    ln1_gain = jnp.clip(1.0 + 0.18 * jax.random.normal(keys[10], (D,), jnp.float32), 0.099609375, 1.8984375).astype(jnp.bfloat16)
    attn_qkv = bell_draw(keys[11], (D, 3 * D), (D // 2) ** -0.5, 0.25)
    attn_out = bell_draw(keys[12], (D, D), (D // 64) ** -0.5, 1.5)
    ln2_gain = jnp.clip(1.0 + 0.18 * jax.random.normal(keys[13], (D,), jnp.float32), 0.099609375, 1.8984375).astype(jnp.bfloat16)
    mlp_in = bell_draw(keys[14], (D, FF), D ** -0.5, 0.1875)
    mlp_in_bias = bell_draw(keys[15], (FF,), 0.5, 3.0)
    mlp_out = bell_draw(keys[16], (FF, D), (FF // 2) ** -0.5, 0.125)
    cotangent = bell_draw(keys[17], (SAMPLES, SEQ, D), 1.0, 6.0, ((0, 8), (1, 4)))
    return {"field_patches": field_patches, "var_ids": var_ids, "lead_bucket": lead_bucket, "patch_weight": patch_weight, "var_embed": var_embed, "agg_query": agg_query, "agg_key": agg_key, "agg_value": agg_value, "agg_out": agg_out, "lead_table": lead_table, "ln1_gain": ln1_gain, "attn_qkv": attn_qkv, "attn_out": attn_out, "ln2_gain": ln2_gain, "mlp_in": mlp_in, "mlp_in_bias": mlp_in_bias, "mlp_out": mlp_out, "cotangent": cotangent}


@jax.custom_vjp
def low(v):
    return lax.optimization_barrier(v.astype(jnp.bfloat16)).astype(jnp.float32)

@jax.custom_vjp
def low_back(v):
    return v

def low_keep(v):
    return (low(v), None)

def low_pass(kept, grad):
    return (grad,)

def back_keep(v):
    return (v, None)

def back_low(kept, grad):
    return (low(grad),)
low.defvjp(low_keep, low_pass)
low_back.defvjp(back_keep, back_low)
highest = lax.Precision.HIGHEST
epsilon = 1e-05

def norm_rows(inputs, gain_vector):
    centered = inputs - lax.optimization_barrier(jnp.mean(inputs, axis=-1, keepdims=True))
    inverse = lax.rsqrt(lax.optimization_barrier(jnp.mean(centered * centered, axis=-1, keepdims=True)) + epsilon)
    return centered * inverse * gain_vector

def one_sample(params, var_ids, inputs):
    patch_weight, var_embed, agg_query, agg_key, agg_value, agg_out, lead_table, ln1_gain, attn_qkv, attn_out, ln2_gain, mlp_in, mlp_in_bias, mlp_out = params
    pixels, lead_pick = inputs
    width = agg_key.shape[0]
    head_dim = width // HEADS
    embeds = var_embed[var_ids]
    query_keys = jnp.einsum('dhc,hc->dh', agg_key.reshape(width, HEADS, head_dim), agg_query.reshape(HEADS, head_dim), precision=highest) * 0.125
    key_pixels = jnp.einsum('vcd,dh->vch', patch_weight, query_keys, precision=highest)
    key_embeds = jnp.dot(embeds, query_keys, precision=highest)
    scores = jnp.einsum('vcr,vch->vhr', pixels, key_pixels, precision=highest) + key_embeds[:, :, None]
    stacked = jnp.concatenate([patch_weight, embeds[:, None, :]], axis=1)
    projected = jnp.einsum('vkd,de->vke', stacked, agg_value, precision=highest)
    extended = jnp.concatenate([pixels, jnp.ones((VARS, 1, SEQ), jnp.float32)], axis=1)
    row_top = lax.optimization_barrier(jnp.max(scores, axis=0))
    soft = jnp.exp(scores - row_top[None])
    row_total = lax.optimization_barrier(jnp.sum(soft, axis=0))
    weighted = soft[:, None] * extended[:, :, None]
    sums = jnp.einsum('vkhr,vkhe->her', weighted, projected.reshape(VARS, PIX + 1, HEADS, head_dim), precision=highest)
    attended = low_back(low((sums / row_total[:, None, :]).reshape(width, SEQ)))
    agg_rows = low_back(jnp.einsum('dr,de->re', attended, agg_out, precision=highest))
    resid_zero = agg_rows + jnp.dot(lead_pick, lead_table, precision=highest)[None, :]
    hidden_one = low(norm_rows(resid_zero, ln1_gain))
    projections = jnp.dot(hidden_one, attn_qkv, precision=highest)
    queries = low_back(low(projections[:, :width])).reshape(SEQ, HEADS, head_dim)
    key_rows = low_back(low(projections[:, width:2 * width])).reshape(SEQ, HEADS, head_dim)
    value_rows = low_back(low(projections[:, 2 * width:])).reshape(SEQ, HEADS, head_dim)
    attn_scores = low_back(jnp.einsum('qhd,khd->hqk', queries, key_rows, precision=highest) * 0.125)
    weights_low = low(jax.nn.softmax(attn_scores, axis=-1))
    mixed = low_back(low(jnp.einsum('hqk,khd->qhd', weights_low, value_rows, precision=highest).reshape(SEQ, width)))
    resid_one = resid_zero + low_back(jnp.dot(mixed, attn_out, precision=highest))
    hidden_two = low(norm_rows(resid_one, ln2_gain))
    inner = low_back(jnp.dot(hidden_two, mlp_in, precision=highest) + mlp_in_bias)
    activated = low_back(low(jax.nn.gelu(inner, approximate=False)))
    return resid_one + low_back(jnp.dot(activated, mlp_out, precision=highest))

def reference(field_patches, var_ids, lead_bucket, patch_weight, var_embed, agg_query, agg_key, agg_value, agg_out, lead_table, ln1_gain, attn_qkv, attn_out, ln2_gain, mlp_in, mlp_in_bias, mlp_out, cotangent):
    params = tuple((weight.astype(jnp.float32) for weight in (patch_weight, var_embed, agg_query, agg_key, agg_value, agg_out, lead_table, ln1_gain, attn_qkv, attn_out, ln2_gain, mlp_in, mlp_in_bias, mlp_out)))
    pixels = jnp.moveaxis(field_patches.astype(jnp.float32), 2, 0)
    lead_pick = (lead_bucket[:, None] == jnp.arange(LEADS, dtype=jnp.int32)[None, :]).astype(jnp.float32)
    checked = jax.checkpoint(one_sample)

    def forward(weights_all, pixels_all):
        return lax.map(lambda inputs: checked(weights_all, var_ids, inputs), (pixels_all, lead_pick))
    result, pullback = jax.vjp(forward, params, pixels)
    grad_params, grad_pixels = pullback(cotangent.astype(jnp.float32))
    field_grad = jnp.moveaxis(grad_pixels, 0, 2)
    return (result.astype(jnp.bfloat16), field_grad, grad_params[0], grad_params[1], grad_params[2], grad_params[3], grad_params[4], grad_params[5], grad_params[6], grad_params[7], grad_params[8], grad_params[9], grad_params[10], grad_params[11], grad_params[12], grad_params[13])
```

```python
from functools import partial

import jax
import jax.numpy as jnp
from jax import lax
from jax.experimental import pallas as pl
from jax.experimental.pallas import tpu as pltpu
from jax.sharding import PartitionSpec as P

HEADS = 16
PIX = 4
HEAD_DIM = 64

f32, bf16 = jnp.float32, jnp.bfloat16
highest = lax.Precision.HIGHEST
epsilon = 1e-05
NT = (((1,), (1,)), ((), ()))
TN = (((0,), (0,)), ((), ()))


def head_weights(pixels, key_ref, head):
    scores = key_ref[PIX, :, head : head + 1]
    for c in range(PIX):
        scores = scores + pixels[c] * key_ref[c, :, head : head + 1]
    soft = jnp.exp(scores - jnp.max(scores, axis=0, keepdims=True))
    return soft * (1.0 / jnp.sum(soft, axis=0, keepdims=True))


def weighted_pixels(soft, pixels):
    return jnp.concatenate(
        [(soft * pixels[c]).astype(bf16) for c in range(PIX)] + [soft.astype(bf16)], axis=0
    )


def front_kernel(
    member,
    pixel_ref,
    key_ref,
    value_ref,
    out_ref,
    lead_ref,
    gain_ref,
    wq_ref,
    wk_ref,
    wv_ref,
    hidden_ref,
    qkv_ref,
    resid_ref,
    att_ref,
    att_scratch,
):
    pixels = [pixel_ref[c].astype(f32) for c in range(PIX)]
    for head in range(HEADS):
        soft = head_weights(pixels, key_ref, head)
        span = slice(head * HEAD_DIM, (head + 1) * HEAD_DIM)
        att_scratch[span, :] = jnp.dot(
            value_ref[span, :], weighted_pixels(soft, pixels), preferred_element_type=f32
        ).astype(bf16)
    att = att_scratch[...]
    resid = lax.dot_general(att, out_ref[...], TN, preferred_element_type=f32) + lead_ref[...]
    centered = resid - jnp.mean(resid, axis=1, keepdims=True)
    inverse = lax.rsqrt(jnp.mean(centered * centered, axis=1, keepdims=True) + epsilon)
    hidden = (centered * inverse * gain_ref[...]).astype(bf16)
    hidden_ref[...] = hidden
    own = wq_ref.shape[1]
    for t, weight in enumerate((wq_ref, wk_ref, wv_ref)):
        qkv_ref[:, t * own : (t + 1) * own] = jnp.dot(
            hidden, weight[...], preferred_element_type=f32
        ).astype(bf16)

    @pl.when(pl.program_id(0) == 0)
    def _():
        resid_ref[...] = resid
        att_ref[...] = att


def front(member, pixels, key_rows, values_t, agg_out, lead_row, gain, attn_qkv, groups):
    width = agg_out.shape[0]
    own = width // groups
    channels, seq = pixels.shape[1:]
    rows = seq // groups
    spec = pltpu.PrefetchScalarGridSpec(
        num_scalar_prefetch=1,
        grid=(groups,),
        in_specs=[
            pl.BlockSpec((PIX, channels, rows), lambda i, m: (0, 0, m[0] ^ i)),
            pl.BlockSpec(key_rows.shape, lambda i, m: (0, 0, 0)),
            pl.BlockSpec(values_t.shape, lambda i, m: (0, 0)),
            pl.BlockSpec(agg_out.shape, lambda i, m: (0, 0)),
            pl.BlockSpec((1, width), lambda i, m: (0, 0)),
            pl.BlockSpec((1, width), lambda i, m: (0, 0)),
            pl.BlockSpec((width, own), lambda i, m: (0, m[0])),
            pl.BlockSpec((width, own), lambda i, m: (0, groups + m[0])),
            pl.BlockSpec((width, own), lambda i, m: (0, 2 * groups + m[0])),
        ],
        out_specs=[
            pl.BlockSpec((rows, width), lambda i, m: (i, 0)),
            pl.BlockSpec((rows, 3 * own), lambda i, m: (i, 0)),
            pl.BlockSpec((rows, width), lambda i, m: (0, 0)),
            pl.BlockSpec((width, rows), lambda i, m: (0, 0)),
        ],
        scratch_shapes=[pltpu.VMEM((width, rows), bf16)],
    )
    return pl.pallas_call(
        front_kernel,
        grid_spec=spec,
        out_shape=[
            jax.ShapeDtypeStruct((seq, width), bf16),
            jax.ShapeDtypeStruct((seq, 3 * own), bf16),
            jax.ShapeDtypeStruct((rows, width), f32),
            jax.ShapeDtypeStruct((width, rows), bf16),
        ],
        cost_estimate=pl.CostEstimate(
            flops=2 * seq * width * (width + 3 * own), bytes_accessed=16 << 20, transcendentals=seq * channels * HEADS
        ),
        name="front",
    )(member, pixels, key_rows, values_t, agg_out, lead_row, gain, attn_qkv, attn_qkv, attn_qkv)


def attend_kernel(q_ref, k_ref, v_ref, mixed_ref, lse_ref):
    rows = q_ref.shape[0]
    lane = lax.broadcasted_iota(jnp.int32, (1, 2 * HEAD_DIM), 1)
    queries = q_ref[...] * jnp.asarray(0.125, bf16)
    mixed = jnp.zeros((rows, 2 * HEAD_DIM), f32)
    for part in range(2):
        keep = (lane // HEAD_DIM) == part
        query = jnp.where(keep, queries, jnp.zeros_like(queries))
        scores = lax.dot_general(query, k_ref[...], NT, preferred_element_type=f32)
        top = jnp.max(scores, axis=1, keepdims=True)
        soft = jnp.exp(scores - top)
        total = jnp.sum(soft, axis=1, keepdims=True)
        out = jnp.dot(soft.astype(bf16), v_ref[...], preferred_element_type=f32)
        mixed = jnp.where(keep, out * (1.0 / total), mixed)
        lse = jnp.broadcast_to(top + jnp.log(total), (rows, 2 * HEAD_DIM))
        lse_ref[0, part : part + 1, :] = lse.T[0:1, :]
    mixed_ref[...] = mixed.astype(bf16)


def attend(qkv, slot, rows, block):
    seq = qkv.shape[0]
    pair = 2 * HEAD_DIM
    pairs = qkv.shape[1] // (3 * pair)
    steps = rows // block
    return pl.pallas_call(
        attend_kernel,
        grid=(pairs, steps),
        in_specs=[
            pl.BlockSpec((block, pair), lambda p, i: (slot * steps + i, p)),
            pl.BlockSpec((seq, pair), lambda p, i: (0, pairs + p)),
            pl.BlockSpec((seq, pair), lambda p, i: (0, 2 * pairs + p)),
        ],
        out_specs=[
            pl.BlockSpec((block, pair), lambda p, i: (i, p)),
            pl.BlockSpec((1, 2, block), lambda p, i: (p, 0, i)),
        ],
        out_shape=[
            jax.ShapeDtypeStruct((rows, pairs * pair), bf16),
            jax.ShapeDtypeStruct((pairs, 2, rows), f32),
        ],
        cost_estimate=pl.CostEstimate(
            flops=16 * rows * seq * pair * pairs, bytes_accessed=3 << 20, transcendentals=2 * rows * seq * pairs
        ),
        name="attend",
    )(qkv, qkv, qkv)


def attend_back_kernel(q_ref, k_ref, v_ref, g_ref, o_ref, lse_ref, out_ref, dk_acc, dv_acc, kt, *, chunk):
    i = pl.program_id(0)
    block = q_ref.shape[0]
    seq = k_ref.shape[0]
    pair = 2 * HEAD_DIM
    lane = lax.broadcasted_iota(jnp.int32, (1, pair), 1)
    side = lax.broadcasted_iota(jnp.int32, (pair, 1), 0)

    @pl.when(i == 0)
    def _():
        dk_acc[...] = jnp.zeros_like(dk_acc)
        dv_acc[...] = jnp.zeros_like(dv_acc)
        kt[...] = k_ref[...].T

    queries = q_ref[...] * jnp.asarray(0.125, bf16)
    grads = g_ref[...]
    product = (grads.astype(f32) * o_ref[...].astype(f32)).T
    grad_query = jnp.zeros((pair, block), f32)
    for part in range(2):
        keep = (lane // HEAD_DIM) == part
        query = jnp.where(keep, queries, jnp.zeros_like(queries))
        grad = jnp.where(keep, grads, jnp.zeros_like(grads))
        delta = jnp.sum(product[part * HEAD_DIM : (part + 1) * HEAD_DIM], axis=0, keepdims=True)
        lse = lse_ref[0, part : part + 1, :]
        total = jnp.zeros((pair, block), f32)
        for at in range(0, seq, chunk):
            span = pl.ds(at, chunk)
            scores = lax.dot_general(k_ref[span, :], query, NT, preferred_element_type=f32)
            soft = jnp.exp(scores - lse)
            through = lax.dot_general(v_ref[span, :], grad, NT, preferred_element_type=f32)
            grad_scores = (soft * (through - delta)).astype(bf16)
            dv_acc[span, :] += jnp.dot(soft.astype(bf16), grad, preferred_element_type=f32)
            dk_acc[span, :] += jnp.dot(grad_scores, query, preferred_element_type=f32)
            total += jnp.dot(kt[:, span], grad_scores, preferred_element_type=f32)
        grad_query = jnp.where((side // HEAD_DIM) == part, total, grad_query)
    out_ref[pl.ds(pl.multiple_of(i * block, block), block), 0:pair] = (grad_query.T * 0.125).astype(bf16)

    @pl.when(i == pl.num_programs(0) - 1)
    def _():
        out_ref[:, pair : 2 * pair] = dk_acc[...].astype(bf16)
        out_ref[:, 2 * pair : 3 * pair] = dv_acc[...].astype(bf16)


def attend_back(qkv, grads, mixed, lse, which, block, chunk):
    seq = qkv.shape[0]
    pair = 2 * HEAD_DIM
    pairs = qkv.shape[1] // (3 * pair)
    return pl.pallas_call(
        partial(attend_back_kernel, chunk=chunk),
        grid=(seq // block,),
        in_specs=[
            pl.BlockSpec((block, pair), lambda i: (i, which)),
            pl.BlockSpec((seq, pair), lambda i: (0, pairs + which)),
            pl.BlockSpec((seq, pair), lambda i: (0, 2 * pairs + which)),
            pl.BlockSpec((block, pair), lambda i: (i, which)),
            pl.BlockSpec((block, pair), lambda i: (i, which)),
            pl.BlockSpec((1, 2, block), lambda i: (which, 0, i)),
        ],
        out_specs=pl.BlockSpec((seq, 3 * pair), lambda i: (0, 0)),
        out_shape=jax.ShapeDtypeStruct((seq, 3 * pair), bf16),
        scratch_shapes=[pltpu.VMEM((seq, pair), f32), pltpu.VMEM((seq, pair), f32), pltpu.VMEM((pair, seq), bf16)],
        cost_estimate=pl.CostEstimate(
            flops=40 * seq * seq * pair, bytes_accessed=5 << 20, transcendentals=2 * seq * seq
        ),
        name="attend_back",
    )(qkv, qkv, qkv, grads, mixed, lse)


def aggregate_back_kernel(member, pixel_ref, key_ref, value_ref, grad_ref, field_ref, proj_ref, keys_ref):
    count, rows = pixel_ref.shape[1:]
    pair = 2 * HEAD_DIM
    pixels = [pixel_ref[c].astype(f32) for c in range(PIX)]
    lane = lax.broadcasted_iota(jnp.int32, (1, pair), 1)
    side = lax.broadcasted_iota(jnp.int32, (pair, 1), 0)
    field = [jnp.zeros((count, rows), f32) for _ in range(PIX)]
    keys = [jnp.zeros((count, pair), f32) for _ in range(PIX + 1)]
    for which in range(HEADS // 2):
        span = slice(which * pair, (which + 1) * pair)
        values, grads = value_ref[:, span], grad_ref[span, :]
        total = jnp.zeros(((PIX + 1) * count, pair), f32)
        for part in range(2):
            head = which * 2 + part
            grad = jnp.where((side // HEAD_DIM) == part, grads, jnp.zeros_like(grads))
            through = jnp.dot(values, grad, preferred_element_type=f32)
            kinds = [through[c * count : (c + 1) * count] for c in range(PIX + 1)]
            soft = head_weights(pixels, key_ref, head)
            grad_soft = kinds[PIX]
            for c in range(PIX):
                grad_soft = grad_soft + pixels[c] * kinds[c]
            weighed = soft * grad_soft
            grad_scores = weighed - soft * jnp.sum(weighed, axis=0, keepdims=True)
            for c in range(PIX):
                field[c] = field[c] + soft * kinds[c] + grad_scores * key_ref[c, :, head : head + 1]
                keys[c] = jnp.where(lane == head, jnp.sum(grad_scores * pixels[c], axis=1, keepdims=True), keys[c])
            keys[PIX] = jnp.where(lane == head, jnp.sum(grad_scores, axis=1, keepdims=True), keys[PIX])
            total = total + lax.dot_general(weighted_pixels(soft, pixels), grad, NT, preferred_element_type=f32)
        proj_ref[:, span] = total.astype(bf16)
    for c in range(PIX):
        field_ref[c] = field[c].astype(bf16)
    for c in range(PIX + 1):
        keys_ref[c] = keys[c]


def aggregate_back(member, pixels, key_rows, values, grads, groups):
    count, seq = pixels.shape[1:]
    rows = seq // groups
    width = values.shape[1]
    spec = pltpu.PrefetchScalarGridSpec(
        num_scalar_prefetch=1,
        grid=(1,),
        in_specs=[
            pl.BlockSpec((PIX, count, rows), lambda i, m: (0, 0, m[0])),
            pl.BlockSpec(key_rows.shape, lambda i, m: (0, 0, 0)),
            pl.BlockSpec(values.shape, lambda i, m: (0, 0)),
            pl.BlockSpec(grads.shape, lambda i, m: (0, 0)),
        ],
        out_specs=[
            pl.BlockSpec((PIX, count, rows), lambda i, m: (0, 0, 0)),
            pl.BlockSpec(((PIX + 1) * count, width), lambda i, m: (0, 0)),
            pl.BlockSpec((PIX + 1, count, 2 * HEAD_DIM), lambda i, m: (0, 0, 0)),
        ],
    )
    return pl.pallas_call(
        aggregate_back_kernel,
        grid_spec=spec,
        out_shape=[
            jax.ShapeDtypeStruct((PIX, count, rows), bf16),
            jax.ShapeDtypeStruct(((PIX + 1) * count, width), bf16),
            jax.ShapeDtypeStruct((PIX + 1, count, 2 * HEAD_DIM), f32),
        ],
        cost_estimate=pl.CostEstimate(
            flops=16 * (PIX + 1) * count * rows * width, bytes_accessed=3 << 20, transcendentals=rows * count * HEADS
        ),
        name="aggregate_back",
    )(member, pixels, key_rows, values, grads)


def layer_norm(inputs, gain):
    centered = inputs - jnp.mean(inputs, axis=-1, keepdims=True)
    inverse = lax.rsqrt(jnp.mean(centered * centered, axis=-1, keepdims=True) + epsilon)
    normed = centered * inverse
    return normed * gain, normed, inverse


def norm_back(grad_rows, normed, inverse, gain):
    grad_gain = jnp.sum(grad_rows * normed, axis=0)
    grad_normed = grad_rows * gain
    first_mean = jnp.mean(grad_normed, axis=-1, keepdims=True)
    second_mean = jnp.mean(grad_normed * normed, axis=-1, keepdims=True)
    return inverse * (grad_normed - first_mean - normed * second_mean), grad_gain


def swap(value, axis, bits):
    size = lax.axis_size(axis)
    return lax.ppermute(value, axis, [(s, s ^ bits) for s in range(size)])


def to_owners(pieces):
    total = pieces[0].astype(f32)
    for k in range(1, len(pieces)):
        total = total + swap(pieces[k], "var", k).astype(f32)
    return total.astype(bf16)


def from_all(own, groups):
    return [own] + [swap(own, "var", k) for k in range(1, groups)]


def patch_sum(value):
    size = lax.axis_size("patch")
    index = lax.axis_index("patch")
    bits = []
    bit = 2
    while bit < size:
        bits.append(bit)
        bit *= 2
    for bit in bits:
        half = value.shape[0] // 2
        high = (index // bit) % 2
        keep = lax.dynamic_slice_in_dim(value, high * half, half)
        send = lax.dynamic_slice_in_dim(value, (1 - high) * half, half)
        value = (keep.astype(f32) + swap(send, "patch", bit).astype(f32)).astype(bf16)
    for bit in reversed(bits):
        other = swap(value, "patch", bit)
        high = (index // bit) % 2
        value = jnp.where(
            high == 0, jnp.concatenate([value, other], axis=0), jnp.concatenate([other, value], axis=0)
        )
    return value


def join_cores(value, core):
    other = swap(value, "patch", 1)
    return jnp.where(
        core == 0, jnp.concatenate([value, other], axis=-1), jnp.concatenate([other, value], axis=-1)
    )


def all_sum(value):
    for axis in ("patch", "var"):
        bit = 1
        while bit < lax.axis_size(axis):
            value = value + swap(value, axis, bit)
            bit *= 2
    return value


def body(
    field_patches,
    var_ids,
    lead_bucket,
    patch_weight,
    var_embed,
    agg_query,
    agg_key,
    agg_value,
    agg_out,
    lead_table,
    ln1_gain,
    attn_qkv,
    attn_out,
    ln2_gain,
    mlp_in,
    mlp_in_bias,
    mlp_out,
    cotangent,
):
    groups = lax.axis_size("var")
    member = lax.axis_index("var")
    core = lax.axis_index("patch") % 2
    channels, pixel_count, samples, seq = field_patches.shape
    width = agg_key.shape[0]
    inner_width = mlp_in.shape[1]
    leads = lead_table.shape[0]
    vocab = var_embed.shape[0]
    rows = seq // groups
    own = width // groups
    count = channels * groups
    slots = [member ^ k for k in range(groups)]
    member_one = member.reshape(1).astype(jnp.int32)
    gain_one = ln1_gain.astype(f32)
    gain_two = ln2_gain.astype(f32)

    mine = jnp.concatenate(
        [
            field_patches.reshape(channels, pixel_count, seq).transpose(1, 0, 2),
            patch_weight.transpose(1, 0, 2),
        ],
        axis=2,
    )
    gathered = jnp.concatenate(from_all(mine, groups), axis=1)
    pixels = gathered[:, :, :seq]
    ids = jnp.concatenate([lax.dynamic_slice_in_dim(var_ids, slot * channels, channels) for slot in slots])
    table_pick = (ids[:, None] == jnp.arange(vocab, dtype=jnp.int32)[None, :]).astype(bf16)
    embeds = jnp.dot(table_pick, var_embed, preferred_element_type=f32).astype(bf16)
    stacked = jnp.concatenate([gathered[:, :, seq:], embeds[None]], axis=0).reshape(-1, width)
    head_of = jnp.arange(width, dtype=jnp.int32) // HEAD_DIM
    spread = head_of[:, None] == jnp.arange(HEADS, dtype=jnp.int32)[None, :]
    query_block = jnp.where(spread, agg_query[:, None], jnp.zeros((), bf16))
    query_keys = jnp.dot(agg_key, query_block, preferred_element_type=f32) * 0.125
    key_rows = jnp.dot(stacked.astype(f32), query_keys, precision=highest).reshape(PIX + 1, count, HEADS)
    values = jnp.dot(stacked, agg_value, preferred_element_type=f32).astype(bf16)
    values_t = values.T
    lead_row = lax.dynamic_slice_in_dim(lead_table, lead_bucket[0], 1).astype(f32)

    hidden_one, qkv, resid_zero, att_low = front(
        member_one, pixels, key_rows, values_t, agg_out, lead_row, gain_one[None], attn_qkv, groups
    )

    block = min(256, rows)
    mixed_parts, lse_parts, received = [None] * groups, [None] * groups, [None] * groups
    for k in reversed(range(groups)):
        mixed_parts[k], lse_parts[k] = attend(qkv, k, rows, block)
        received[k] = swap(mixed_parts[k], "var", k) if k else mixed_parts[k]
    mixed_heads = jnp.concatenate(mixed_parts, axis=0)
    lse = jnp.concatenate(lse_parts, axis=2)
    mixed = jnp.concatenate(received, axis=1)
    out_rows = jnp.concatenate([lax.dynamic_slice_in_dim(attn_out, slot * own, own) for slot in slots], axis=0)

    resid_one = resid_zero + jnp.dot(mixed, out_rows, preferred_element_type=f32)
    normed_two, plain_two, inverse_two = layer_norm(resid_one, gain_two)
    hidden_two = normed_two.astype(bf16)
    inner = jnp.dot(hidden_two, mlp_in, preferred_element_type=f32) + mlp_in_bias.astype(f32)
    activated = jax.nn.gelu(inner, approximate=False).astype(bf16)
    output = (resid_one + jnp.dot(activated, mlp_out, preferred_element_type=f32)).astype(bf16)
    output = output.reshape(samples, rows, width)

    grad_out = cotangent.reshape(rows, width)
    grad_act = jnp.einsum("rd,fd->rf", grad_out, mlp_out, preferred_element_type=f32)
    unused, gelu_back = jax.vjp(partial(jax.nn.gelu, approximate=False), inner)
    grad_inner = gelu_back(grad_act)[0].astype(bf16)
    grad_bias = jnp.sum(grad_inner.astype(f32), axis=0)
    grad_hidden_two = jnp.einsum("rf,df->rd", grad_inner, mlp_in, preferred_element_type=f32)
    grad_norm_two, grad_gain_two = norm_back(grad_hidden_two, plain_two, inverse_two, gain_two)
    grad_resid_one = grad_out.astype(f32) + grad_norm_two
    grad_branch = grad_resid_one.astype(bf16)
    grad_mixed = jnp.einsum("re,de->rd", grad_branch, out_rows, preferred_element_type=f32).astype(bf16)
    grad_heads = jnp.concatenate(
        [
            swap(grad_mixed[:, k * own : (k + 1) * own], "var", k) if k else grad_mixed[:, :own]
            for k in range(groups)
        ],
        axis=0,
    )

    def halves(grad):
        half = grad.shape[1] // 2
        return (
            lax.dynamic_slice_in_dim(grad, core * half, half, axis=1),
            lax.dynamic_slice_in_dim(grad, (1 - core) * half, half, axis=1),
        )

    def weight_sum(lefts, grad, dims):
        keep, send = halves(grad)
        pieces = []
        for left in lefts:
            theirs = lax.dot_general(left, send, dims, preferred_element_type=f32).astype(bf16)
            ours = lax.dot_general(left, keep, dims, preferred_element_type=f32)
            pieces.append((ours + swap(theirs, "patch", 1).astype(f32)).astype(bf16))
        return join_cores(patch_sum(to_owners(pieces)), core).astype(f32)

    part = inner_width // groups
    sum_mlp_out = weight_sum(
        [lax.dynamic_slice_in_dim(activated, slot * part, part, axis=1) for slot in slots], grad_out, TN
    )
    sum_mlp_in = weight_sum(
        [lax.dynamic_slice_in_dim(hidden_two, slot * own, own, axis=1) for slot in slots], grad_inner, TN
    )
    sum_attn_out = weight_sum(received, grad_branch, TN)

    pair = 2 * HEAD_DIM
    pairs = own // pair
    mine_qkv, weight_qkv = [], []
    arrived = [[None] * pairs for _ in range(groups)]
    for which in range(pairs):
        grads = attend_back(qkv, grad_heads, mixed_heads, lse, which, min(512, rows), 512)
        for k in range(groups):
            piece = grads[k * rows : (k + 1) * rows]
            arrived[k][which] = swap(piece, "var", k) if k else piece
        weight_qkv.append(lax.dot_general(hidden_one, grads, TN, preferred_element_type=f32).astype(bf16))
    grad_proj = jnp.zeros((3, rows, width), bf16)
    for k in range(groups):
        both = jnp.stack(
            [jnp.concatenate([p[:, t * pair : (t + 1) * pair] for p in arrived[k]], axis=1) for t in range(3)]
        )
        grad_proj = lax.dynamic_update_slice(grad_proj, both, (0, 0, slots[k] * own))
    grad_hidden_one = jnp.einsum("re,de->rd", grad_proj[0], attn_qkv[:, :width], preferred_element_type=f32)
    for t in range(1, 3):
        grad_hidden_one = grad_hidden_one + jnp.einsum(
            "re,de->rd", grad_proj[t], attn_qkv[:, t * width : (t + 1) * width], preferred_element_type=f32
        )
    normed_one, plain_one, inverse_one = layer_norm(resid_zero, gain_one)
    grad_norm_one, grad_gain_one = norm_back(grad_hidden_one, plain_one, inverse_one, gain_one)
    grad_resid_zero = grad_resid_one + grad_norm_one
    grad_agg = grad_resid_zero.astype(bf16)
    grad_att = jnp.einsum("re,de->dr", grad_agg, agg_out, preferred_element_type=f32).astype(bf16)

    both_cores = jnp.stack(weight_qkv)
    ours = lax.dynamic_slice_in_dim(both_cores, core, pairs // 2)
    theirs = lax.dynamic_slice_in_dim(both_cores, 1 - core, pairs // 2)
    core_qkv = (ours.astype(f32) + swap(theirs, "patch", 1).astype(f32)).astype(bf16).reshape(groups, own, 3 * pair)
    qkv_chunks = [lax.dynamic_index_in_dim(core_qkv, slot, 0, keepdims=False) for slot in slots]
    qkv_own = jnp.stack([swap(qkv_chunks[k], "var", k) if k else qkv_chunks[0] for k in range(groups)])
    qkv_own = patch_sum(qkv_own.transpose(1, 0, 2))
    qkv_other = swap(qkv_own, "patch", 1)
    ordered = jnp.where(
        core == 0, jnp.stack([qkv_own, qkv_other], axis=2), jnp.stack([qkv_other, qkv_own], axis=2)
    )
    ordered = ordered.reshape(own, groups, pairs, 3, pair).transpose(0, 3, 1, 2, 4).astype(f32)
    sum_qkv = jnp.zeros((own, 3, groups, pairs * pair), f32)
    for k in range(groups):
        sum_qkv = lax.dynamic_update_slice(
            sum_qkv, ordered[:, :, k].reshape(own, 3, 1, pairs * pair), (0, 0, slots[k], 0)
        )
    sum_qkv = sum_qkv.reshape(own, 3 * width)

    sum_agg_out = weight_sum(
        [lax.dynamic_slice_in_dim(att_low, slot * own, own) for slot in slots], grad_agg, (((1,), (0,)), ((), ()))
    )

    sample_sum = jnp.sum(grad_resid_zero, axis=0)
    lead_pick = (lead_bucket[:, None] == jnp.arange(leads, dtype=jnp.int32)[None, :]).astype(f32)
    grad_lead = lead_pick.reshape(leads, 1) * sample_sum[None, :]
    small = jnp.concatenate(
        [grad_bias.reshape(-1, width), grad_gain_two[None], grad_gain_one[None], grad_lead], axis=0
    )
    small = all_sum(small)
    bias_rows = inner_width // width
    sum_bias = lax.dynamic_slice_in_dim(small[:bias_rows].reshape(-1), member * part, part)
    sum_gain_two = lax.dynamic_slice_in_dim(small[bias_rows], member * own, own)
    sum_gain_one = lax.dynamic_slice_in_dim(small[bias_rows + 1], member * own, own)
    sum_lead = lax.dynamic_slice_in_dim(small[bias_rows + 2 :], member * (leads // groups), leads // groups)

    field_own, grad_values, grad_keys = aggregate_back(member_one, pixels, key_rows, values, grad_att, groups)
    field_slots = field_own.reshape(pixel_count, groups, channels, rows)
    field_parts = jnp.stack(
        [swap(field_slots[:, k], "var", k) if k else field_slots[:, 0] for k in range(groups)]
    )
    field_grad = jnp.zeros((channels, pixel_count, seq), f32)
    for k in range(groups):
        field_grad = lax.dynamic_update_slice(
            field_grad, field_parts[k].transpose(1, 0, 2).astype(f32), (0, 0, slots[k] * rows)
        )
    field_grad = field_grad.reshape(channels, pixel_count, samples, seq)

    keep, send = halves(grad_values)
    keys_low = grad_keys.reshape(-1, 2 * HEAD_DIM).astype(bf16)
    keep = jnp.concatenate([keep, keys_low], axis=1)
    send = jnp.concatenate([send, keys_low], axis=1)
    tail = (keep.astype(f32) + swap(send, "patch", 1).astype(f32)).astype(bf16)
    tail = tail.reshape(PIX + 1, groups, channels, -1)
    tail = to_owners([tail[:, k] for k in range(groups)])
    bit = 2
    while bit < lax.axis_size("patch"):
        tail = (tail.astype(f32) + swap(tail, "patch", bit).astype(f32)).astype(bf16)
        bit *= 2
    tail = jnp.stack(from_all(tail, groups), axis=1).reshape((PIX + 1) * count, -1)
    sum_values = join_cores(tail[:, : width // 2], core)
    sum_keys = tail[:, width // 2 : width // 2 + HEADS].astype(f32)

    by_kind = sum_values.reshape(PIX + 1, count, width)
    keys_kind = sum_keys.reshape(PIX + 1, count, HEADS)
    weight_rows = by_kind[:PIX, :channels].reshape(PIX * channels, width)
    weight_keys = keys_kind[:PIX, :channels].reshape(PIX * channels, HEADS)
    own_ids = member * (vocab // groups) + jnp.arange(vocab // groups, dtype=jnp.int32)
    own_pick = own_ids[:, None] == ids[None, :]
    embed_rows = jnp.dot(own_pick.astype(bf16), by_kind[PIX], preferred_element_type=f32).astype(bf16)
    embed_keys = jnp.dot(own_pick.astype(f32), keys_kind[PIX], precision=highest)
    both_rows = jnp.concatenate([weight_rows, embed_rows], axis=0)
    both_keys = jnp.concatenate([weight_keys, embed_keys], axis=0)
    grad_stacked = jnp.einsum("ve,de->vd", both_rows, agg_value, preferred_element_type=f32) + jnp.einsum(
        "vh,dh->vd", both_keys, query_keys, precision=highest
    )
    sum_patch = grad_stacked[: PIX * channels].reshape(pixel_count, channels, width).transpose(1, 0, 2)
    sum_table = grad_stacked[PIX * channels :]
    stacked_own = lax.dynamic_slice_in_dim(stacked, member * own, own, axis=1)
    sum_value = jnp.einsum("vd,ve->de", stacked_own, sum_values, preferred_element_type=f32)
    grad_query_keys = jnp.einsum("vd,vh->dh", stacked.astype(f32), sum_keys, precision=highest)
    own_query_keys = lax.dynamic_slice_in_dim(grad_query_keys, member * own, own)
    sum_key = (
        jnp.dot(own_query_keys, spread.T.astype(f32), precision=highest) * agg_query.astype(f32)[None, :] * 0.125
    )
    agg_key_own = lax.dynamic_slice_in_dim(agg_key, member * own, own, axis=1).astype(f32)
    spread_own = lax.dynamic_slice_in_dim(spread.astype(f32), member * own, own)
    sum_query = (
        jnp.sum(jnp.einsum("dc,dh->ch", agg_key_own, grad_query_keys, precision=highest) * spread_own, axis=1) * 0.125
    )
    return (
        output,
        field_grad,
        sum_patch,
        sum_table,
        sum_query,
        sum_key,
        sum_value,
        sum_agg_out,
        sum_lead,
        sum_gain_one,
        sum_qkv,
        sum_attn_out,
        sum_gain_two,
        sum_mlp_in,
        sum_bias,
        sum_mlp_out,
    )


def solution(mesh):
    placed = (
        P("var", None, "patch", None),
        P(),
        P("patch"),
        P("var", None, None),
        P(),
        P(),
        P(),
        P(),
        P(),
        P(),
        P(),
        P(),
        P(),
        P(),
        P(),
        P(),
        P(),
        P("patch", "var", None),
    )
    return jax.shard_map(
        body,
        mesh=mesh,
        in_specs=placed,
        out_specs=(
            P("patch", "var", None),
            P("var", None, "patch", None),
            P("var", None, None),
            P("var", None),
            P("var"),
            P("var", None),
            P("var", None),
            P("var", None),
            P("var", None),
            P("var"),
            P("var", None),
            P("var", None),
            P("var"),
            P("var", None),
            P("var"),
            P("var", None),
        ),
        check_vma=False,
    )
```

```python
from functools import partial

import jax
import jax.numpy as jnp
from jax import lax
from jax.experimental import pallas as pl
from jax.experimental.pallas import tpu as pltpu
from jax.sharding import PartitionSpec as P

HEADS = 16
PIX = 4
HEAD_DIM = 64
ORDER = (0, 2, 1, 3)
BLOCKS = tuple((k, 0) for k in range(4)) + tuple((k, 1) for k in ORDER)

f32, bf16 = jnp.float32, jnp.bfloat16
highest = lax.Precision.HIGHEST
epsilon = 1e-05
NT = (((1,), (1,)), ((), ()))
TN = (((0,), (0,)), ((), ()))


def head_weights(pixels, key_ref, head):
    scores = key_ref[PIX, :, head : head + 1]
    for c in range(PIX):
        scores = scores + pixels[c] * key_ref[c, :, head : head + 1]
    soft = jnp.exp(scores - jnp.max(scores, axis=0, keepdims=True))
    return soft * (1.0 / jnp.sum(soft, axis=0, keepdims=True))


def slot_spans(member, own):
    return [pl.ds(pl.multiple_of((member[0] ^ k) * own, own), own) for k in ORDER]


def weighted_pixels(soft, pixels):
    return jnp.concatenate(
        [(soft * pixels[c]).astype(bf16) for c in range(PIX)] + [soft.astype(bf16)], axis=0
    )


def front_kernel(
    member,
    pixel_ref,
    key_ref,
    value_ref,
    out_ref,
    lead_ref,
    gain_ref,
    wq_ref,
    wk_ref,
    wv_ref,
    hidden_ref,
    qkv_ref,
    resid_ref,
    att_ref,
    att_scratch,
):
    pixels = [pixel_ref[c].astype(f32) for c in range(PIX)]
    for head in range(HEADS):
        soft = head_weights(pixels, key_ref, head)
        span = slice(head * HEAD_DIM, (head + 1) * HEAD_DIM)
        att_scratch[span, :] = jnp.dot(
            value_ref[span, :], weighted_pixels(soft, pixels), preferred_element_type=f32
        ).astype(bf16)
    att = att_scratch[...]
    resid = lax.dot_general(att, out_ref[...], TN, preferred_element_type=f32) + lead_ref[...]
    centered = resid - jnp.mean(resid, axis=1, keepdims=True)
    inverse = lax.rsqrt(jnp.mean(centered * centered, axis=1, keepdims=True) + epsilon)
    hidden = (centered * inverse * gain_ref[...]).astype(bf16)
    own = wq_ref.shape[1]
    hidden_ref[...] = hidden.T
    for t, weight in enumerate((wq_ref, wk_ref, wv_ref)):
        qkv_ref[:, t * own : (t + 1) * own] = jnp.dot(
            hidden, weight[...], preferred_element_type=f32
        ).astype(bf16)

    @pl.when(pl.program_id(0) == member[0])
    def _():
        resid_ref[...] = resid
        att_ref[...] = att


def front(member, pixels, key_rows, values_t, agg_out, lead_row, gain, attn_qkv, groups):
    width = agg_out.shape[0]
    own = width // groups
    channels, seq = pixels.shape[1:]
    rows = seq // groups
    spec = pltpu.PrefetchScalarGridSpec(
        num_scalar_prefetch=1,
        grid=(groups,),
        in_specs=[
            pl.BlockSpec((PIX, channels, rows), lambda i, m: (0, 0, i)),
            pl.BlockSpec(key_rows.shape, lambda i, m: (0, 0, 0)),
            pl.BlockSpec(values_t.shape, lambda i, m: (0, 0)),
            pl.BlockSpec(agg_out.shape, lambda i, m: (0, 0)),
            pl.BlockSpec((1, width), lambda i, m: (0, 0)),
            pl.BlockSpec((1, width), lambda i, m: (0, 0)),
            pl.BlockSpec((width, own), lambda i, m: (0, m[0])),
            pl.BlockSpec((width, own), lambda i, m: (0, groups + m[0])),
            pl.BlockSpec((width, own), lambda i, m: (0, 2 * groups + m[0])),
        ],
        out_specs=[
            pl.BlockSpec((width, rows), lambda i, m: (0, i)),
            pl.BlockSpec((rows, 3 * own), lambda i, m: (i, 0)),
            pl.BlockSpec((rows, width), lambda i, m: (0, 0)),
            pl.BlockSpec((width, rows), lambda i, m: (0, 0)),
        ],
        scratch_shapes=[pltpu.VMEM((width, rows), bf16)],
    )
    return pl.pallas_call(
        front_kernel,
        grid_spec=spec,
        out_shape=[
            jax.ShapeDtypeStruct((width, seq), bf16),
            jax.ShapeDtypeStruct((seq, 3 * own), bf16),
            jax.ShapeDtypeStruct((rows, width), f32),
            jax.ShapeDtypeStruct((width, rows), bf16),
        ],
        cost_estimate=pl.CostEstimate(
            flops=2 * seq * width * (width + 3 * own), bytes_accessed=16 << 20, transcendentals=seq * channels * HEADS
        ),
        name="front",
    )(member, pixels, key_rows, values_t, agg_out, lead_row, gain, attn_qkv, attn_qkv, attn_qkv)


def attend_kernel(member, q_ref, k_ref, v_ref, mixed_ref, lse_ref):
    rows = q_ref.shape[0]
    lane = lax.broadcasted_iota(jnp.int32, (1, 2 * HEAD_DIM), 1)
    queries = q_ref[...] * jnp.asarray(0.125, bf16)
    mixed = jnp.zeros((rows, 2 * HEAD_DIM), f32)
    for part in range(2):
        keep = (lane // HEAD_DIM) == part
        query = jnp.where(keep, queries, jnp.zeros_like(queries))
        scores = lax.dot_general(query, k_ref[...], NT, preferred_element_type=f32)
        top = jnp.max(scores, axis=1, keepdims=True)
        soft = jnp.exp(scores - top)
        total = jnp.sum(soft, axis=1, keepdims=True)
        out = jnp.dot(soft.astype(bf16), v_ref[...], preferred_element_type=f32)
        mixed = jnp.where(keep, out * (1.0 / total), mixed)
        lse = jnp.broadcast_to(top + jnp.log(total), (rows, 2 * HEAD_DIM))
        lse_ref[0, part : part + 1, :] = lse.T[0:1, :]
    mixed_ref[...] = mixed.astype(bf16)


def attend(member, qkv, slot, rows, block):
    seq = qkv.shape[0]
    pair = 2 * HEAD_DIM
    pairs = qkv.shape[1] // (3 * pair)
    steps = rows // block
    spec = pltpu.PrefetchScalarGridSpec(
        num_scalar_prefetch=1,
        grid=(pairs, steps),
        in_specs=[
            pl.BlockSpec((block, pair), lambda p, i, m: ((m[0] ^ slot) * steps + i, p)),
            pl.BlockSpec((seq, pair), lambda p, i, m: (0, pairs + p)),
            pl.BlockSpec((seq, pair), lambda p, i, m: (0, 2 * pairs + p)),
        ],
        out_specs=[
            pl.BlockSpec((block, pair), lambda p, i, m: (i, p)),
            pl.BlockSpec((1, 2, block), lambda p, i, m: (p, 0, i)),
        ],
    )
    return pl.pallas_call(
        attend_kernel,
        grid_spec=spec,
        out_shape=[
            jax.ShapeDtypeStruct((rows, pairs * pair), bf16),
            jax.ShapeDtypeStruct((pairs, 2, rows), f32),
        ],
        cost_estimate=pl.CostEstimate(
            flops=16 * rows * seq * pair * pairs, bytes_accessed=3 << 20, transcendentals=2 * rows * seq * pairs
        ),
        name="attend",
    )(member, qkv, qkv, qkv)


def attend_back_kernel(member, q_ref, k_ref, v_ref, g_ref, *refs, chunk, groups):
    mixed_refs, lse_refs = refs[:groups], refs[groups : 2 * groups]
    out_ref, dk_acc, dv_acc, kt = refs[2 * groups :]
    i = pl.program_id(0)
    slot = i ^ member[0]
    mixed, lse_rows = mixed_refs[0][...], lse_refs[0][0]
    for k in range(1, groups):
        mixed = jnp.where(slot == k, mixed_refs[k][...], mixed)
        lse_rows = jnp.where(slot == k, lse_refs[k][0], lse_rows)
    block = q_ref.shape[0]
    seq = k_ref.shape[0]
    pair = 2 * HEAD_DIM
    lane = lax.broadcasted_iota(jnp.int32, (1, pair), 1)
    side = lax.broadcasted_iota(jnp.int32, (pair, 1), 0)

    @pl.when(i == 0)
    def _():
        dk_acc[...] = jnp.zeros_like(dk_acc)
        dv_acc[...] = jnp.zeros_like(dv_acc)
        kt[...] = k_ref[...].T

    queries = q_ref[...] * jnp.asarray(0.125, bf16)
    grads = g_ref[...]
    product = (grads.astype(f32) * mixed.astype(f32)).T
    grad_query = jnp.zeros((pair, block), f32)
    for part in range(2):
        keep = (lane // HEAD_DIM) == part
        query = jnp.where(keep, queries, jnp.zeros_like(queries))
        grad = jnp.where(keep, grads, jnp.zeros_like(grads))
        delta = jnp.sum(product[part * HEAD_DIM : (part + 1) * HEAD_DIM], axis=0, keepdims=True)
        lse = lse_rows[part : part + 1, :]
        total = jnp.zeros((pair, block), f32)
        for at in range(0, seq, chunk):
            span = pl.ds(at, chunk)
            scores = lax.dot_general(k_ref[span, :], query, NT, preferred_element_type=f32)
            soft = jnp.exp(scores - lse)
            through = lax.dot_general(v_ref[span, :], grad, NT, preferred_element_type=f32)
            grad_scores = (soft * (through - delta)).astype(bf16)
            dv_acc[span, :] += jnp.dot(soft.astype(bf16), grad, preferred_element_type=f32)
            dk_acc[span, :] += jnp.dot(grad_scores, query, preferred_element_type=f32)
            total += jnp.dot(kt[:, span], grad_scores, preferred_element_type=f32)
        grad_query = jnp.where((side // HEAD_DIM) == part, total, grad_query)
    out_ref[pl.ds(pl.multiple_of(i * block, block), block), 0:pair] = (grad_query.T * 0.125).astype(bf16)

    @pl.when(i == pl.num_programs(0) - 1)
    def _():
        out_ref[:, pair : 2 * pair] = dk_acc[...].astype(bf16)
        out_ref[:, 2 * pair : 3 * pair] = dv_acc[...].astype(bf16)


def attend_back(member, qkv, grads, mixed, lse, which, chunk):
    seq = qkv.shape[0]
    groups = len(mixed)
    rows = seq // groups
    pair = 2 * HEAD_DIM
    pairs = qkv.shape[1] // (3 * pair)
    spec = pltpu.PrefetchScalarGridSpec(
        num_scalar_prefetch=1,
        grid=(groups,),
        in_specs=[
            pl.BlockSpec((rows, pair), lambda i, m: (i, which)),
            pl.BlockSpec((seq, pair), lambda i, m: (0, pairs + which)),
            pl.BlockSpec((seq, pair), lambda i, m: (0, 2 * pairs + which)),
            pl.BlockSpec((rows, pair), lambda i, m: (i, which)),
        ]
        + [pl.BlockSpec((rows, pair), lambda i, m: (0, which))] * groups
        + [pl.BlockSpec((1, 2, rows), lambda i, m: (which, 0, 0))] * groups,
        out_specs=pl.BlockSpec((seq, 3 * pair), lambda i, m: (0, 0)),
        scratch_shapes=[pltpu.VMEM((seq, pair), f32), pltpu.VMEM((seq, pair), f32), pltpu.VMEM((pair, seq), bf16)],
    )
    return pl.pallas_call(
        partial(attend_back_kernel, chunk=min(chunk, seq), groups=groups),
        grid_spec=spec,
        out_shape=jax.ShapeDtypeStruct((seq, 3 * pair), bf16),
        cost_estimate=pl.CostEstimate(
            flops=40 * seq * seq * pair, bytes_accessed=5 << 20, transcendentals=2 * seq * seq
        ),
        name="attend_back",
    )(member, qkv, qkv, qkv, grads, *mixed, *lse)


def put_tail(tail, values, span):
    groups = len(ORDER)
    channels = values.shape[0] // ((PIX + 1) * groups)
    stride = tail.shape[0] // groups
    for at, k in enumerate(ORDER):
        for c in range(PIX + 1):
            row, source = at * stride + c * channels, (c * groups + k) * channels
            tail[row : row + channels, span] = values[source : source + channels]


def aggregate_back_kernel(
    member, core, pixel_ref, key_ref, value_ref, grad_ref, small_ref, field_ref, keep_ref, send_ref, tail
):
    count, rows = pixel_ref.shape[1:]
    pair = 2 * HEAD_DIM
    pixels = [pixel_ref[c].astype(f32) for c in range(PIX)]
    lane = lax.broadcasted_iota(jnp.int32, (1, pair), 1)
    side = lax.broadcasted_iota(jnp.int32, (pair, 1), 0)
    field = [jnp.zeros((count, rows), f32) for _ in range(PIX)]
    keys = [jnp.zeros((count, pair), f32) for _ in range(PIX + 1)]
    for which in range(HEADS // 2):
        span = slice(which * pair, (which + 1) * pair)
        values, grads = value_ref[:, span], grad_ref[span, :]
        total = jnp.zeros(((PIX + 1) * count, pair), f32)
        for part in range(2):
            head = which * 2 + part
            grad = jnp.where((side // HEAD_DIM) == part, grads, jnp.zeros_like(grads))
            through = jnp.dot(values, grad, preferred_element_type=f32)
            kinds = [through[c * count : (c + 1) * count] for c in range(PIX + 1)]
            soft = head_weights(pixels, key_ref, head)
            grad_soft = kinds[PIX]
            for c in range(PIX):
                grad_soft = grad_soft + pixels[c] * kinds[c]
            weighed = soft * grad_soft
            grad_scores = weighed - soft * jnp.sum(weighed, axis=0, keepdims=True)
            for c in range(PIX):
                field[c] = field[c] + soft * kinds[c] + grad_scores * key_ref[c, :, head : head + 1]
                keys[c] = jnp.where(lane == head, jnp.sum(grad_scores * pixels[c], axis=1, keepdims=True), keys[c])
            keys[PIX] = jnp.where(lane == head, jnp.sum(grad_scores, axis=1, keepdims=True), keys[PIX])
            total = total + lax.dot_general(weighted_pixels(soft, pixels), grad, NT, preferred_element_type=f32)
        put_tail(tail, total, span)
    for c in range(PIX):
        field_ref[c] = field[c].astype(bf16)
    width = value_ref.shape[1]
    put_tail(tail, jnp.concatenate(keys, axis=0), slice(width, width + pair))
    stride = tail.shape[0] // len(ORDER)
    free = small_ref.shape[0] // len(ORDER)
    for at in range(len(ORDER)):
        end = (at + 1) * stride
        tail[end - free : end, :width] = small_ref[at * free : (at + 1) * free, :]
        tail[end - free : end, width:] = jnp.zeros((free, pair), f32)
    half = width // 2
    for ref, which in ((keep_ref, core[0]), (send_ref, 1 - core[0])):
        ref[:, :half] = tail[:, pl.ds(pl.multiple_of(which * half, half), half)].astype(bf16)
        ref[:, half:] = tail[:, width:].astype(bf16)


def aggregate_back(member, core, pixels, key_rows, values, grads, small, groups):
    count, seq = pixels.shape[1:]
    rows = seq // groups
    width = values.shape[1]
    free = small.shape[0] // groups
    deep = (PIX + 1) * count + small.shape[0]
    wide = width // 2 + 2 * HEAD_DIM

    def whole(*shape):
        return pl.BlockSpec(shape, lambda i, m, c: (0,) * len(shape))

    spec = pltpu.PrefetchScalarGridSpec(
        num_scalar_prefetch=2,
        grid=(1,),
        in_specs=[
            pl.BlockSpec((PIX, count, rows), lambda i, m, c: (0, 0, m[0])),
            whole(*key_rows.shape),
            whole(*values.shape),
            whole(*grads.shape),
            whole(*small.shape),
        ],
        out_specs=[whole(PIX, count, rows), whole(deep, wide), whole(deep, wide)],
        scratch_shapes=[pltpu.VMEM((deep, width + 2 * HEAD_DIM), f32)],
    )
    return pl.pallas_call(
        aggregate_back_kernel,
        grid_spec=spec,
        out_shape=[
            jax.ShapeDtypeStruct((PIX, count, rows), bf16),
            jax.ShapeDtypeStruct((deep, wide), bf16),
            jax.ShapeDtypeStruct((deep, wide), bf16),
        ],
        cost_estimate=pl.CostEstimate(
            flops=16 * (PIX + 1) * count * rows * width, bytes_accessed=3 << 20, transcendentals=rows * count * HEADS
        ),
        name="aggregate_back",
    )(member, core, pixels, key_rows, values, grads, small)


def middle_kernel(
    member, core, mixed0, mixed1, mixed2, mixed3, wo_ref, resid_ref, gain_ref, w1_ref, b1_ref, w2_ref, ga_ref, g_ref,
    osend_ref, okeep_ref, isend_ref, ikeep_ref, bias_ref, out_ref, gres_ref, gm_ref, ggain_ref,
    normed, hidden, inverse, acc_out, acc_grad, hidden_t, mixed_t,
):
    j = pl.program_id(0)
    steps = pl.num_programs(0) - 1
    parts = (mixed0, mixed1, mixed2, mixed3)
    rows, own = mixed0.shape
    half = g_ref.shape[1] // 2

    def columns(ref, which):
        return ref[:, pl.ds(pl.multiple_of(which * half, half), half)]

    def owner(slot):
        return pl.ds(pl.multiple_of((member[0] ^ slot) * own, own), own)

    @pl.when(j == 0)
    def _():
        resid = resid_ref[...]
        for slot, part in enumerate(parts):
            resid = resid + jnp.dot(part[...], wo_ref[owner(slot), :], preferred_element_type=f32)
        centered = resid - jnp.mean(resid, axis=1, keepdims=True)
        scale = lax.rsqrt(jnp.mean(centered * centered, axis=1, keepdims=True) + epsilon)
        plain = centered * scale
        normed[...] = plain
        inverse[...] = jnp.broadcast_to(scale, inverse.shape)
        hidden[...] = (plain * gain_ref[...]).astype(bf16)
        acc_out[...] = resid
        acc_grad[...] = jnp.zeros_like(acc_grad)
        piece = own // 2
        for at, (slot, side) in enumerate(BLOCKS):
            start = pl.multiple_of((member[0] ^ slot) * own + side * piece, piece)
            hidden_t[at * piece : (at + 1) * piece, :] = hidden[:, pl.ds(start, piece)].T
            mixed_t[at * piece : (at + 1) * piece, :] = parts[slot][:, side * piece : (side + 1) * piece].T

    @pl.when(j < steps)
    def _():
        inner = jnp.dot(hidden[...], w1_ref[...], preferred_element_type=f32) + b1_ref[...]
        below = 0.5 + 0.5 * lax.erf(inner * 0.7071067811865476)
        act = (inner * below).astype(bf16)
        slope = below + inner * (jnp.exp(-0.5 * inner * inner) * 0.3989422804014327)
        gu = (slope * ga_ref[...].astype(f32)).astype(bf16)
        bias_ref[...] = jnp.sum(gu.astype(f32), axis=0, keepdims=True)
        acc_out[...] += jnp.dot(act, w2_ref[...], preferred_element_type=f32)
        acc_grad[...] += lax.dot_general(gu, w1_ref[...], NT, preferred_element_type=f32)
        act_t = act.T
        osend_ref[...] = jnp.dot(act_t, columns(g_ref, 1 - core[0]), preferred_element_type=f32).astype(bf16)
        okeep_ref[...] = jnp.dot(act_t, columns(g_ref, core[0]), preferred_element_type=f32).astype(bf16)
        grad_in = jnp.dot(hidden_t[...], gu, preferred_element_type=f32).astype(bf16)

        @pl.when(j < steps // 2)
        def _():
            isend_ref[...] = grad_in

        @pl.when(j >= steps // 2)
        def _():
            ikeep_ref[...] = grad_in

    @pl.when(j == steps)
    def _():
        out_ref[...] = acc_out[...].astype(bf16)
        grad, plain = acc_grad[...], normed[...]
        ggain_ref[...] = jnp.sum(grad * plain, axis=0, keepdims=True)
        grad = grad * gain_ref[...]
        first = jnp.mean(grad, axis=1, keepdims=True)
        second = jnp.mean(grad * plain, axis=1, keepdims=True)
        gres = g_ref[...].astype(f32) + inverse[:, :1] * (grad - first - plain * second)
        gres_ref[...] = gres
        gb = gres.astype(bf16)
        for p in range(len(parts)):
            gm_ref[p] = lax.dot_general(gb, wo_ref[p * own : (p + 1) * own, :], NT, preferred_element_type=f32).astype(
                bf16
            )
        both = jnp.dot(mixed_t[...], gb, preferred_element_type=f32).astype(bf16)
        for which in range(2):
            mine = both[:, which * half : (which + 1) * half]

            @pl.when(core[0] == which)
            def _():
                ikeep_ref[...] = mine

            @pl.when(core[0] != which)
            def _():
                isend_ref[...] = mine


def middle(member, core, mixed, attn_out, resid, gain, mlp_in, bias, mlp_out, grad_act, grad_out):
    rows, width = resid.shape
    inner = mlp_in.shape[1]
    groups = len(mixed)
    own = width // groups
    block = inner // (2 * groups)
    steps = 2 * groups
    half = width // 2
    assert half == block

    def natural(j, m, c):
        j = jnp.minimum(j, steps - 1)
        return ((j // groups) ^ (1 - c[0])) * groups + j % groups

    def place(j, m, c):
        n = natural(j, m, c)
        slot = (n // 2) ^ m[0]
        return jnp.where(n % 2 == 0, slot, 4 + (slot % 2) * 2 + slot // 2)

    def whole(*shape):
        return pl.BlockSpec(shape, lambda j, m, c: (0,) * len(shape))

    def shape(*dims, kind=bf16):
        return jax.ShapeDtypeStruct(dims, kind)

    spec = pltpu.PrefetchScalarGridSpec(
        num_scalar_prefetch=2,
        grid=(steps + 1,),
        in_specs=[whole(rows, own)] * groups
        + [
            whole(width, width),
            whole(rows, width),
            whole(1, width),
            pl.BlockSpec((width, block), lambda j, m, c: (0, natural(j, m, c))),
            pl.BlockSpec((1, block), lambda j, m, c: (0, natural(j, m, c))),
            pl.BlockSpec((block, width), lambda j, m, c: (natural(j, m, c), 0)),
            pl.BlockSpec((rows, block), lambda j, m, c: (0, natural(j, m, c))),
            whole(rows, width),
        ],
        out_specs=[
            pl.BlockSpec((block, half), lambda j, m, c: (place(j, m, c), 0)),
            pl.BlockSpec((block, half), lambda j, m, c: (place(j, m, c), 0)),
            pl.BlockSpec((width, block), lambda j, m, c: (0, jnp.minimum(j, groups))),
            pl.BlockSpec((width, block), lambda j, m, c: (0, jnp.maximum(j - groups, 0))),
            pl.BlockSpec((1, block), lambda j, m, c: (0, natural(j, m, c))),
            whole(rows, width),
            whole(rows, width),
            whole(groups, rows, own),
            whole(1, width),
        ],
        scratch_shapes=[
            pltpu.VMEM((rows, width), f32),
            pltpu.VMEM((rows, width), bf16),
            pltpu.VMEM((rows, 128), f32),
            pltpu.VMEM((rows, width), f32),
            pltpu.VMEM((rows, width), f32),
            pltpu.VMEM((width, rows), bf16),
            pltpu.VMEM((width, rows), bf16),
        ],
    )
    side = inner // 2 + half
    return pl.pallas_call(
        middle_kernel,
        grid_spec=spec,
        out_shape=[
            shape(inner, half),
            shape(inner, half),
            shape(width, side),
            shape(width, side),
            shape(1, inner, kind=f32),
            shape(rows, width),
            shape(rows, width, kind=f32),
            shape(groups, rows, own),
            shape(1, width, kind=f32),
        ],
        cost_estimate=pl.CostEstimate(
            flops=2 * rows * width * (5 * inner + 3 * width), bytes_accessed=48 << 20, transcendentals=2 * rows * inner
        ),
        name="middle",
    )(member, core, *mixed, attn_out, resid, gain, mlp_in, bias, mlp_out, grad_act, grad_out)


def join_kernel(first_ref, second_ref, wq, wk, wv, resid_ref, gain_ref, gres_ref, out_ref, *refs):
    ga_ref, gatt_ref, ggain_ref, sum_ref, total = refs
    i = pl.program_id(0)
    pair = 2 * HEAD_DIM

    @pl.when(i == 0)
    def _():
        total[...] = jnp.zeros_like(total)

    grad = total[...]
    for t, weight in enumerate((wq, wk, wv)):
        span = slice(t * pair, (t + 1) * pair)
        left = jnp.concatenate([first_ref[:, span], second_ref[:, span]], axis=1)
        grad = grad + lax.dot_general(left, weight[...], NT, preferred_element_type=f32)
    total[...] = grad

    @pl.when(i == pl.num_programs(0) - 1)
    def _():
        resid = resid_ref[...]
        centered = resid - jnp.mean(resid, axis=1, keepdims=True)
        scale = lax.rsqrt(jnp.mean(centered * centered, axis=1, keepdims=True) + epsilon)
        plain = centered * scale
        grad = total[...]
        ggain_ref[...] = jnp.sum(grad * plain, axis=0, keepdims=True)
        grad = grad * gain_ref[...]
        first = jnp.mean(grad, axis=1, keepdims=True)
        second = jnp.mean(grad * plain, axis=1, keepdims=True)
        gres = gres_ref[...] + scale * (grad - first - plain * second)
        sum_ref[...] = jnp.sum(gres, axis=0, keepdims=True)
        ga = gres.astype(bf16)
        ga_ref[...] = ga
        gatt_ref[...] = lax.dot_general(out_ref[...], ga, NT, preferred_element_type=f32).astype(bf16)


def join(first, second, attn_qkv, resid, gain, gres, agg_out):
    rows, width = resid.shape
    groups = first.shape[0] // rows
    own = width // groups
    cols = first.shape[1]

    def whole(*shape):
        return pl.BlockSpec(shape, lambda i: (0,) * len(shape))

    return pl.pallas_call(
        join_kernel,
        grid=(groups,),
        in_specs=[
            pl.BlockSpec((rows, cols), lambda i: (i, 0)),
            pl.BlockSpec((rows, cols), lambda i: (i, 0)),
            pl.BlockSpec((width, own), lambda i: (0, i)),
            pl.BlockSpec((width, own), lambda i: (0, groups + i)),
            pl.BlockSpec((width, own), lambda i: (0, 2 * groups + i)),
            whole(rows, width),
            whole(1, width),
            whole(rows, width),
            whole(width, width),
        ],
        out_specs=[whole(rows, width), whole(width, rows), whole(1, width), whole(1, width)],
        scratch_shapes=[pltpu.VMEM((rows, width), f32)],
        out_shape=[
            jax.ShapeDtypeStruct((rows, width), bf16),
            jax.ShapeDtypeStruct((width, rows), bf16),
            jax.ShapeDtypeStruct((1, width), f32),
            jax.ShapeDtypeStruct((1, width), f32),
        ],
        cost_estimate=pl.CostEstimate(flops=8 * rows * width * width, bytes_accessed=16 << 20, transcendentals=0),
        name="join",
    )(first, second, attn_qkv, attn_qkv, attn_qkv, resid, gain, gres, agg_out)


def add(a, b):
    return (a.astype(f32) + b.astype(f32)).astype(bf16)


def quarter_kernel(keep_ref, came_ref, *outs):
    i = pl.program_id(0)
    total = add(keep_ref[...], came_ref[...])
    for q, out in enumerate(outs):

        @pl.when(i // 2 == q)
        def _():
            out[...] = total


def quarters(keep, came):
    rows, cols = keep.shape
    block = rows // 8

    def at(q):
        return lambda i: (jnp.clip(i - 2 * q, 0, 1), 0)

    return pl.pallas_call(
        quarter_kernel,
        grid=(8,),
        in_specs=[pl.BlockSpec((block, cols), lambda i: (i, 0))] * 2,
        out_specs=[pl.BlockSpec((block, cols), at(q)) for q in range(4)],
        out_shape=[jax.ShapeDtypeStruct((rows // 4, cols), bf16)] * 4,
        cost_estimate=pl.CostEstimate(flops=rows * cols, bytes_accessed=6 * rows * cols, transcendentals=0),
        name="quarters",
    )(keep, came)


def halve_kernel(a_ref, b_ref, c_ref, d_ref, a_low, a_high, c_low, c_high):
    for x, y, low, high in ((a_ref, b_ref, a_low, a_high), (c_ref, d_ref, c_low, c_high)):
        half = low.shape[0]
        low[...] = add(x[:half, :], y[:half, :])
        high[...] = add(x[half:, :], y[half:, :])


def halve_both(a, b, c, d):
    rows, cols = a.shape
    return pl.pallas_call(
        halve_kernel,
        out_shape=[jax.ShapeDtypeStruct((rows // 2, cols), bf16)] * 4,
        cost_estimate=pl.CostEstimate(flops=rows * cols, bytes_accessed=12 * rows * cols, transcendentals=0),
        name="halve_both",
    )(a, b, c, d)


def choose_kernel(high, a_ref, b_ref, c_ref, d_ref, keep, send):
    first, second = add(a_ref[...], b_ref[...]), add(c_ref[...], d_ref[...])
    keep[...] = jnp.where(high[0] == 0, first, second)
    send[...] = jnp.where(high[0] == 0, second, first)


def whole_blocks(shapes):
    return [pl.BlockSpec(shape, lambda i, *_, n=len(shape): (0,) * n) for shape in shapes]


def choose(high, a, b, c, d):
    spec = pltpu.PrefetchScalarGridSpec(
        num_scalar_prefetch=1, grid=(1,), in_specs=whole_blocks([a.shape] * 4), out_specs=whole_blocks([a.shape] * 2)
    )
    return pl.pallas_call(
        choose_kernel,
        grid_spec=spec,
        out_shape=[jax.ShapeDtypeStruct(a.shape, bf16)] * 2,
        cost_estimate=pl.CostEstimate(flops=a.size, bytes_accessed=12 * a.size, transcendentals=0),
        name="choose",
    )(high, a, b, c, d)


def part_kernel(high, a_ref, b_ref, keep, send):
    half = keep.shape[0]
    for out, which in ((keep, high[0]), (send, 1 - high[0])):
        span = pl.ds(pl.multiple_of(which * half, half), half)
        out[...] = add(a_ref[span, :], b_ref[span, :])


def part(high, a, b):
    shape = (a.shape[0] // 2, a.shape[1])
    spec = pltpu.PrefetchScalarGridSpec(
        num_scalar_prefetch=1, grid=(1,), in_specs=whole_blocks([a.shape] * 2), out_specs=whole_blocks([shape] * 2)
    )
    return pl.pallas_call(
        part_kernel,
        grid_spec=spec,
        out_shape=[jax.ShapeDtypeStruct(shape, bf16)] * 2,
        cost_estimate=pl.CostEstimate(flops=a.size, bytes_accessed=6 * a.size, transcendentals=0),
        name="part",
    )(high, a, b)


def gather_sources_kernel(high, came_ref, keep, send, *, cols):
    groups, half = came_ref.shape[0], keep.shape[0]
    for out, which in ((keep, high[0]), (send, 1 - high[0])):
        span = pl.ds(pl.multiple_of(which * half, half), half)
        total = jnp.zeros((half, came_ref.shape[2] - cols), f32)
        for p in range(groups):
            out[:, p * cols : (p + 1) * cols] = came_ref[p, span, :cols]
            total = total + came_ref[p, span, cols:].astype(f32)
        out[:, groups * cols :] = total.astype(bf16)


def gather_sources(high, came, cols):
    groups, rows, wide = came.shape
    shape = (rows // 2, groups * cols + wide - cols)
    spec = pltpu.PrefetchScalarGridSpec(
        num_scalar_prefetch=1, grid=(1,), in_specs=whole_blocks([came.shape]), out_specs=whole_blocks([shape] * 2)
    )
    return pl.pallas_call(
        partial(gather_sources_kernel, cols=cols),
        grid_spec=spec,
        out_shape=[jax.ShapeDtypeStruct(shape, bf16)] * 2,
        cost_estimate=pl.CostEstimate(flops=came.size, bytes_accessed=4 * came.size, transcendentals=0),
        name="gather_sources",
    )(high, came)


def place_kernel(high, core, *refs, spans):
    pieces, outs = refs[:4], refs[4:]
    rows = pieces[0].shape[0]
    for ref, upper, which in (
        (pieces[0], high[0], core[0]),
        (pieces[1], 1 - high[0], core[0]),
        (pieces[2], high[0], 1 - core[0]),
        (pieces[3], 1 - high[0], 1 - core[0]),
    ):
        at = pl.ds(pl.multiple_of(upper * rows, rows), rows)
        for number, source, target, scale, size in spans:
            start = pl.multiple_of(target + which * scale, 128)
            outs[number][at, pl.ds(start, size)] = ref[:, source : source + size].astype(f32)


def place(high, core, pieces, spans, widths):
    rows = 2 * pieces[0].shape[0]
    shapes = [(rows, wide) for wide in widths]
    spec = pltpu.PrefetchScalarGridSpec(
        num_scalar_prefetch=2,
        grid=(1,),
        in_specs=whole_blocks([p.shape for p in pieces]),
        out_specs=whole_blocks(shapes),
    )
    return pl.pallas_call(
        partial(place_kernel, spans=spans),
        grid_spec=spec,
        out_shape=[jax.ShapeDtypeStruct(shape, f32) for shape in shapes],
        cost_estimate=pl.CostEstimate(flops=0, bytes_accessed=6 * rows * sum(widths), transcendentals=0),
        name="place",
    )(high, core, *pieces)


def field_kernel(member, *refs):
    pieces, out = refs[:-1], refs[-1]
    kinds, channels, rows = pieces[0].shape
    for k, piece in enumerate(pieces):
        at = pl.ds(pl.multiple_of((member[0] ^ k) * rows, rows), rows)
        for c in range(kinds):
            out[:, c, at] = piece[c].astype(f32)


def place_field(member, pieces):
    kinds, channels, rows = pieces[0].shape
    shape = (channels, kinds, rows * len(pieces))
    spec = pltpu.PrefetchScalarGridSpec(
        num_scalar_prefetch=1,
        grid=(1,),
        in_specs=whole_blocks([p.shape for p in pieces]),
        out_specs=whole_blocks([shape])[0],
    )
    return pl.pallas_call(
        field_kernel, grid_spec=spec, out_shape=jax.ShapeDtypeStruct(shape, f32), name="place_field"
    )(member, *pieces)


def tail_kernel(member, *refs, groups):
    tails = refs[:groups]
    stacked_ref, pick_ref, value_ref, qk_ref, key_ref, query_ref = refs[groups : groups + 6]
    gvalue_ref, gkey_ref, gquery_ref, rows_ref, gqk = refs[groups + 6 :]
    width = value_ref.shape[0]
    own = gvalue_ref.shape[0]
    at = pl.ds(pl.multiple_of(member[0] * own, own), own)
    tail = jnp.concatenate([t[...] for t in tails], axis=0)
    values, keys = tail[:, :width], tail[:, width:]
    gvalue_ref[...] = lax.dot_general(stacked_ref[:, at], values, TN, preferred_element_type=f32)
    gqk[...] = lax.dot_general(stacked_ref[...], keys, TN, preferred_element_type=f32)
    head = lax.broadcasted_iota(jnp.int32, (keys.shape[1], width), 0)
    column = lax.broadcasted_iota(jnp.int32, (keys.shape[1], width), 1) // HEAD_DIM
    spread = jnp.where(head == column, 1.0, 0.0)
    gkey_ref[...] = (
        jnp.dot(gqk[at, :], spread, precision=highest, preferred_element_type=f32) * (query_ref[...] * 0.125)
    )
    by_head = lax.dot_general(gqk[...], key_ref[...].astype(f32), TN, precision=highest, preferred_element_type=f32)
    head = lax.broadcasted_iota(jnp.int32, by_head.shape, 0)
    column = (lax.broadcasted_iota(jnp.int32, by_head.shape, 1) + member[0] * own) // HEAD_DIM
    gquery_ref[...] = jnp.sum(jnp.where(head == column, by_head, 0.0), axis=0, keepdims=True) * 0.125
    own_rows = tails[0].shape[0]
    table = jnp.dot(pick_ref[...], tail, preferred_element_type=f32).astype(bf16)
    rows = jnp.concatenate([tail[:own_rows], table], axis=0)
    rows_ref[...] = lax.dot_general(rows[:, :width], value_ref[...], NT, preferred_element_type=f32) + lax.dot_general(
        rows[:, width:].astype(f32), qk_ref[...], NT, precision=highest, preferred_element_type=f32
    )


def finish_tail(member, tails, stacked, pick, agg_value, query_keys, agg_key, agg_query):
    groups = len(tails)
    width = agg_value.shape[0]
    own = width // groups
    deep = tails[0].shape[0] + pick.shape[0]
    args = [*tails, stacked, pick, agg_value, query_keys]
    spec = pltpu.PrefetchScalarGridSpec(
        num_scalar_prefetch=1,
        grid=(1,),
        in_specs=whole_blocks([x.shape for x in args])
        + [pl.BlockSpec((width, own), lambda i, m: (0, m[0])), pl.BlockSpec((1, width), lambda i, m: (0, 0))],
        out_specs=whole_blocks([(own, width), (own, width), (1, own), (deep, width)]),
        scratch_shapes=[pltpu.VMEM((width, query_keys.shape[1]), f32)],
    )
    return pl.pallas_call(
        partial(tail_kernel, groups=groups),
        grid_spec=spec,
        out_shape=[
            jax.ShapeDtypeStruct((own, width), f32),
            jax.ShapeDtypeStruct((own, width), f32),
            jax.ShapeDtypeStruct((1, own), f32),
            jax.ShapeDtypeStruct((deep, width), f32),
        ],
        cost_estimate=pl.CostEstimate(flops=1 << 30, bytes_accessed=8 << 20, transcendentals=0),
        name="finish_tail",
    )(member, *args, agg_key, agg_query)


def fence(*values):
    return lax.optimization_barrier(values)


def swap(value, axis, bits):
    size = lax.axis_size(axis)
    return lax.ppermute(value, axis, [(s, s ^ bits) for s in range(size)])


def from_all(own, groups):
    return [own] + [swap(own, "var", k) for k in range(1, groups)]


def exchange(value):
    return lax.all_to_all(value, "var", split_axis=0, concat_axis=0, tiled=True)


def patch_bits():
    bits, bit = [], 2
    while bit < lax.axis_size("patch"):
        bits.append(bit)
        bit *= 2
    return bits


def is_high(bit):
    return ((lax.axis_index("patch") // bit) % 2).reshape(1).astype(jnp.int32)


def sum_over_chips(keep, send):
    bits = patch_bits()
    for bit in bits[1:]:
        keep, send = part(is_high(bit), keep, swap(send, "patch", bit // 2))
    value = add(keep, swap(send, "patch", bits[-1]))
    for bit in reversed(bits[1:]):
        other = swap(value, "patch", bit)
        high = is_high(bit)[0] == 1
        value = jnp.concatenate([jnp.where(high, other, value), jnp.where(high, value, other)], axis=0)
    return value, swap(value, "patch", bits[0])


def with_core(halves):
    return [*halves, *(swap(value, "patch", 1) for value in halves)]


def body(
    field_patches,
    var_ids,
    lead_bucket,
    patch_weight,
    var_embed,
    agg_query,
    agg_key,
    agg_value,
    agg_out,
    lead_table,
    ln1_gain,
    attn_qkv,
    attn_out,
    ln2_gain,
    mlp_in,
    mlp_in_bias,
    mlp_out,
    cotangent,
):
    groups = lax.axis_size("var")
    member = lax.axis_index("var")
    core = lax.axis_index("patch") % 2
    channels, pixel_count, samples, seq = field_patches.shape
    width = agg_key.shape[0]
    inner_width = mlp_in.shape[1]
    leads = lead_table.shape[0]
    vocab = var_embed.shape[0]
    rows = seq // groups
    own = width // groups
    count = channels * groups
    slots = [member ^ k for k in range(groups)]
    member_one = member.reshape(1).astype(jnp.int32)
    core_one = core.reshape(1).astype(jnp.int32)
    high = is_high(2)
    gain_one = ln1_gain.astype(f32)
    gain_two = ln2_gain.astype(f32)

    mine = jnp.concatenate(
        [
            field_patches.reshape(channels, pixel_count, seq).transpose(1, 0, 2),
            patch_weight.transpose(1, 0, 2),
        ],
        axis=2,
    )
    grad_out = cotangent.reshape(rows, width)
    grad_act = lax.dot_general(grad_out, mlp_out, NT, preferred_element_type=f32).astype(bf16)
    ids = jnp.concatenate([lax.dynamic_slice_in_dim(var_ids, slot * channels, channels) for slot in slots])
    table_pick = (ids[:, None] == jnp.arange(vocab, dtype=jnp.int32)[None, :]).astype(bf16)
    embeds = jnp.dot(table_pick, var_embed, preferred_element_type=f32).astype(bf16)
    head_of = jnp.arange(width, dtype=jnp.int32) // HEAD_DIM
    spread = head_of[:, None] == jnp.arange(2 * HEAD_DIM, dtype=jnp.int32)[None, :]
    query_block = jnp.where(spread, agg_query[:, None], jnp.zeros((), bf16))
    query_keys = jnp.dot(agg_key, query_block, preferred_element_type=f32) * 0.125
    lead_row = lax.dynamic_slice_in_dim(lead_table, lead_bucket[0], 1).astype(f32)
    arrived, grad_act, embeds, query_keys, lead_row = fence(
        from_all(mine, groups), grad_act, embeds, query_keys, lead_row
    )
    pixels = jnp.concatenate([value[:, :, :seq] for value in arrived], axis=1)
    stacked = jnp.concatenate([value[:, :, seq:] for value in arrived], axis=1)
    stacked = jnp.concatenate([stacked, embeds[None]], axis=0).reshape(-1, width)
    key_rows = jnp.dot(stacked.astype(f32), query_keys, precision=highest).reshape(PIX + 1, count, 2 * HEAD_DIM)
    values = jnp.dot(stacked, agg_value, preferred_element_type=f32).astype(bf16)
    values_t = values.T

    hidden_t, qkv, resid_zero, att_low = front(
        member_one, pixels, key_rows, values_t, agg_out, lead_row, gain_one[None], attn_qkv, groups
    )

    block = min(256, rows)
    mixed_parts, lse_parts, received = [None] * groups, [None] * groups, [None] * groups
    for k in reversed(range(groups)):
        mixed_parts[k], lse_parts[k] = attend(member_one, qkv, k, rows, block)
        if k + 1 < groups:
            received[k + 1], mixed_parts[k], qkv = fence(received[k + 1], mixed_parts[k], qkv)
        received[k] = swap(mixed_parts[k], "var", k) if k else mixed_parts[k]

    out_send, out_keep, in_send, in_keep, grad_bias, output, grad_resid_one, grad_mixed, grad_gain_two = middle(
        member_one,
        core_one,
        received,
        attn_out,
        resid_zero,
        gain_two[None],
        mlp_in,
        mlp_in_bias.astype(f32)[None],
        mlp_out,
        grad_act,
        grad_out,
    )
    output = output.reshape(samples, rows, width)

    grad_heads = exchange(grad_mixed).reshape(seq, own)
    out_came = swap(out_send, "patch", 1)
    in_came = swap(in_send, "patch", 1)
    out_y, out_y_send, out_x, out_x_send = quarters(out_keep, out_came)
    in_y, in_y_send, in_x, in_x_send = quarters(in_keep, in_came)
    grad_heads, out_y_send, out_x_send, in_y, in_y_send, in_x, in_x_send = fence(
        grad_heads, out_y_send, out_x_send, in_y, in_y_send, in_x, in_x_send
    )

    pair = 2 * HEAD_DIM
    pairs = own // pair
    assert pairs == 2
    out_y_came, out_x_came = swap(out_y_send, "var", 2), swap(out_x_send, "var", 1)
    first = attend_back(member_one, qkv, grad_heads, mixed_parts, lse_parts, 0, 512)
    first, out_y_came, out_x_came, in_y_send, in_x_send = fence(first, out_y_came, out_x_came, in_y_send, in_x_send)
    out_y, out_y_send, out_x, out_x_send = halve_both(out_y, out_y_came, out_x, out_x_came)
    first, out_y_send, out_x_send, qkv = fence(first, out_y_send, out_x_send, qkv)
    out_y_came, out_x_came = swap(out_y_send, "var", 1), swap(out_x_send, "var", 2)
    first_came = exchange(first)
    second = attend_back(member_one, qkv, grad_heads, mixed_parts, lse_parts, 1, 512)
    first_came, second, out_y_came, out_x_came, in_y_send, in_x_send = fence(
        first_came, second, out_y_came, out_x_came, in_y_send, in_x_send
    )
    second_came = exchange(second)
    in_y_came, in_x_came = swap(in_y_send, "var", 2), swap(in_x_send, "var", 1)
    out_keep, out_send = choose(high, out_y, out_y_came, out_x, out_x_came)
    weight_qkv = [
        jnp.dot(hidden_t, grads, preferred_element_type=f32).astype(bf16) for grads in (first, second)
    ]
    second_came, weight_qkv, out_send = fence(second_came, weight_qkv, out_send)
    out_halves = sum_over_chips(out_keep, out_send)
    grad_agg, grad_att, grad_gain_one, sample_sum = join(
        first_came, second_came, attn_qkv, resid_zero, gain_one[None], grad_resid_one, agg_out
    )

    def half_of(grad, which):
        half = grad.shape[1] // 2
        return lax.dynamic_slice_in_dim(grad, which * half, half, axis=1)

    last_send = jnp.concatenate(
        [
            jnp.where(core == 0, weight_qkv[1], weight_qkv[0]),
            jnp.dot(att_low, half_of(grad_agg, 1 - core), preferred_element_type=f32).astype(bf16),
        ],
        axis=1,
    )
    last_keep = jnp.concatenate(
        [
            jnp.where(core == 0, weight_qkv[0], weight_qkv[1]),
            jnp.dot(att_low, half_of(grad_agg, core), preferred_element_type=f32).astype(bf16),
        ],
        axis=1,
    )
    last_came = exchange(add(last_keep, swap(last_send, "patch", 1)).reshape(groups, own, -1))
    last_keep, last_send = gather_sources(high, last_came, 3 * pair)
    last_halves = sum_over_chips(last_keep, last_send)

    lead_pick = (lead_bucket[:, None] == jnp.arange(leads, dtype=jnp.int32)[None, :]).astype(f32)
    grad_lead = lead_pick.reshape(leads, 1) * sample_sum
    small = jnp.concatenate(
        [
            grad_bias.reshape(groups, -1),
            grad_gain_two.reshape(groups, own),
            grad_gain_one.reshape(groups, own),
            grad_lead.reshape(groups, -1),
        ],
        axis=1,
    )
    small_size = small.shape[1]
    free = 4
    small = jnp.pad(small, ((0, 0), (0, free * width - small_size))).reshape(groups, free, width)
    small = jnp.concatenate([lax.dynamic_index_in_dim(small, slots[k], 0, keepdims=False) for k in ORDER])

    field_own, tail, tail_send = aggregate_back(
        member_one, core_one, pixels, key_rows, values, grad_att, small, groups
    )
    tail_came = swap(tail_send, "patch", 1)
    field_slots = field_own.reshape(pixel_count, groups, channels, rows)
    field_parts = [swap(field_slots[:, k], "var", k) if k else field_slots[:, 0] for k in range(groups)]
    field_grad = place_field(member_one, field_parts).reshape(channels, pixel_count, samples, seq)

    tail = add(tail, tail_came)
    for bit in (1, 2):
        deep = tail.shape[0] // 2
        tail = add(tail[:deep], swap(tail[deep:], "var", bit))
    for bit in patch_bits():
        tail = add(tail, swap(tail, "patch", bit))
    half = width // 2
    other = swap(tail, "patch", 1)
    low, up = jnp.where(core == 0, tail, other), jnp.where(core == 0, other, tail)
    tail = jnp.concatenate([low[:, :half], up], axis=1)
    tails = from_all(tail, groups)
    stride = tail.shape[0]
    per_slot = (PIX + 1) * channels
    small_sum = tail[per_slot:, :width].astype(f32).reshape(-1)
    part_size = inner_width // groups
    sum_bias = small_sum[:part_size]
    sum_gain_two = small_sum[part_size : part_size + own]
    sum_gain_one = small_sum[part_size + own : part_size + 2 * own]
    sum_lead = small_sum[part_size + 2 * own : small_size].reshape(leads // groups, width)

    by_slot = stacked.reshape(PIX + 1, groups, channels, width).transpose(1, 0, 2, 3).reshape(groups, per_slot, width)
    by_slot = jnp.pad(by_slot, ((0, 0), (0, stride - per_slot), (0, 0))).reshape(groups * stride, width)
    own_ids = member * (vocab // groups) + jnp.arange(16, dtype=jnp.int32)
    own_pick = jnp.where(jnp.arange(16)[:, None] < vocab // groups, own_ids[:, None] == ids[None, :], False)
    own_pick = jnp.pad(
        own_pick.reshape(16, groups, channels), ((0, 0), (0, 0), (PIX * channels, stride - per_slot))
    ).reshape(16, groups * stride)
    sum_value, sum_key, sum_query, sum_rows = finish_tail(
        member_one,
        tails,
        by_slot,
        own_pick.astype(bf16),
        agg_value,
        query_keys,
        agg_key,
        agg_query.astype(f32)[None],
    )
    sum_query = sum_query.reshape(own)
    sum_patch = sum_rows[: PIX * channels].reshape(pixel_count, channels, width).transpose(1, 0, 2)
    sum_table = sum_rows[stride : stride + vocab // groups]

    in_y, in_y_send, in_x, in_x_send = halve_both(in_y, in_y_came, in_x, in_x_came)
    in_y_came, in_x_came = swap(in_y_send, "var", 1), swap(in_x_send, "var", 2)
    in_keep, in_send = choose(high, in_y, in_y_came, in_x, in_x_came)
    in_halves = sum_over_chips(in_keep, in_send)
    (sum_mlp_out,) = place(high, core_one, with_core(out_halves), [(0, 0, 0, half, half)], [width])
    half_in = inner_width // 2
    sum_mlp_in, sum_attn_out = place(
        high,
        core_one,
        with_core(in_halves),
        [(0, 0, 0, half_in, half_in), (1, half_in, 0, half, half)],
        [inner_width, width],
    )
    sum_qkv, sum_agg_out = place(
        high,
        core_one,
        with_core(last_halves),
        [(0, p * 3 * pair + t * pair, t * width + p * own, pair, pair) for p in range(groups) for t in range(3)]
        + [(1, groups * 3 * pair, 0, half, half)],
        [3 * width, width],
    )
    return (
        output,
        field_grad,
        sum_patch,
        sum_table,
        sum_query,
        sum_key,
        sum_value,
        sum_agg_out,
        sum_lead,
        sum_gain_one,
        sum_qkv,
        sum_attn_out,
        sum_gain_two,
        sum_mlp_in,
        sum_bias,
        sum_mlp_out,
    )


def solution(mesh):
    placed = (
        P("var", None, "patch", None),
        P(),
        P("patch"),
        P("var", None, None),
        P(),
        P(),
        P(),
        P(),
        P(),
        P(),
        P(),
        P(),
        P(),
        P(),
        P(),
        P(),
        P(),
        P("patch", "var", None),
    )
    return jax.shard_map(
        body,
        mesh=mesh,
        in_specs=placed,
        out_specs=(
            P("patch", "var", None),
            P("var", None, "patch", None),
            P("var", None, None),
            P("var", None),
            P("var"),
            P("var", None),
            P("var", None),
            P("var", None),
            P("var", None),
            P("var"),
            P("var", None),
            P("var", None),
            P("var"),
            P("var", None),
            P("var"),
            P("var", None),
        ),
        check_vma=False,
    )
```

```python
from functools import partial

import jax
import jax.numpy as jnp
from jax import lax
from jax.experimental import pallas as pl
from jax.experimental.pallas import tpu as pltpu
from jax.sharding import Mesh
from jax.sharding import PartitionSpec as P

HEADS = 16
PIX = 4
HEAD_DIM = 64
LEADS = 8
FREE = 4
ORDER = (0, 2, 1, 3)
BLOCKS = tuple((k, 0) for k in range(4)) + tuple((k, 1) for k in ORDER)

f32, bf16 = jnp.float32, jnp.bfloat16
highest = lax.Precision.HIGHEST
epsilon = 1e-05
NT = (((1,), (1,)), ((), ()))
LIGHT = pl.CostEstimate(flops=1, bytes_accessed=1, transcendentals=0)
TN = (((0,), (0,)), ((), ()))


def head_weights(pixels, key_ref, head):
    scores = key_ref[PIX, :, head : head + 1]
    for c in range(PIX):
        scores = scores + pixels[c] * key_ref[c, :, head : head + 1]
    soft = jnp.exp(scores - jnp.max(scores, axis=0, keepdims=True))
    return soft * (1.0 / jnp.sum(soft, axis=0, keepdims=True))


def slot_spans(member, own):
    return [pl.ds(pl.multiple_of((member[0] ^ k) * own, own), own) for k in ORDER]


def weighted_pixels(soft, pixels):
    return jnp.concatenate(
        [(soft * pixels[c]).astype(bf16) for c in range(PIX)] + [soft.astype(bf16)], axis=0
    )


def front_kernel(
    member,
    pixel_ref,
    key_ref,
    value_ref,
    out_ref,
    lead_ref,
    gain_ref,
    wq_ref,
    wk_ref,
    wv_ref,
    hidden_ref,
    qkv_ref,
    resid_ref,
    att_ref,
    att_scratch,
):
    pixels = [pixel_ref[c].astype(f32) for c in range(PIX)]
    for head in range(HEADS):
        soft = head_weights(pixels, key_ref, head)
        span = slice(head * HEAD_DIM, (head + 1) * HEAD_DIM)
        att_scratch[span, :] = jnp.dot(
            value_ref[span, :], weighted_pixels(soft, pixels), preferred_element_type=f32
        ).astype(bf16)
    att = att_scratch[...]
    resid = lax.dot_general(att, out_ref[...], TN, preferred_element_type=f32) + lead_ref[...]
    centered = resid - jnp.mean(resid, axis=1, keepdims=True)
    inverse = lax.rsqrt(jnp.mean(centered * centered, axis=1, keepdims=True) + epsilon)
    hidden = (centered * inverse * gain_ref[...]).astype(bf16)
    own = wq_ref.shape[1]
    hidden_ref[...] = hidden.T
    for t, weight in enumerate((wq_ref, wk_ref, wv_ref)):
        qkv_ref[:, t * own : (t + 1) * own] = jnp.dot(
            hidden, weight[...], preferred_element_type=f32
        ).astype(bf16)

    @pl.when(pl.program_id(0) == member[0])
    def _():
        resid_ref[...] = resid
        att_ref[...] = att


def front(member, pixels, key_rows, values_t, agg_out, lead_row, gain, attn_qkv, groups):
    width = agg_out.shape[0]
    own = width // groups
    channels, seq = pixels.shape[1:]
    rows = seq // groups
    spec = pltpu.PrefetchScalarGridSpec(
        num_scalar_prefetch=1,
        grid=(groups,),
        in_specs=[
            pl.BlockSpec((PIX, channels, rows), lambda i, m: (0, 0, i)),
            pl.BlockSpec(key_rows.shape, lambda i, m: (0, 0, 0)),
            pl.BlockSpec(values_t.shape, lambda i, m: (0, 0)),
            pl.BlockSpec(agg_out.shape, lambda i, m: (0, 0)),
            pl.BlockSpec((1, width), lambda i, m: (0, 0)),
            pl.BlockSpec((1, width), lambda i, m: (0, 0)),
            pl.BlockSpec((width, own), lambda i, m: (0, m[0])),
            pl.BlockSpec((width, own), lambda i, m: (0, groups + m[0])),
            pl.BlockSpec((width, own), lambda i, m: (0, 2 * groups + m[0])),
        ],
        out_specs=[
            pl.BlockSpec((width, rows), lambda i, m: (0, i)),
            pl.BlockSpec((rows, 3 * own), lambda i, m: (i, 0)),
            pl.BlockSpec((rows, width), lambda i, m: (0, 0)),
            pl.BlockSpec((width, rows), lambda i, m: (0, 0)),
        ],
        scratch_shapes=[pltpu.VMEM((width, rows), bf16)],
    )
    return pl.pallas_call(
        front_kernel,
        grid_spec=spec,
        out_shape=[
            jax.ShapeDtypeStruct((width, seq), bf16),
            jax.ShapeDtypeStruct((seq, 3 * own), bf16),
            jax.ShapeDtypeStruct((rows, width), f32),
            jax.ShapeDtypeStruct((width, rows), bf16),
        ],
        cost_estimate=LIGHT,
        name="front",
    )(member, pixels, key_rows, values_t, agg_out, lead_row, gain, attn_qkv, attn_qkv, attn_qkv)


def attend_kernel(member, q_ref, k_ref, v_ref, mixed_ref, lse_ref):
    rows = q_ref.shape[0]
    lane = lax.broadcasted_iota(jnp.int32, (1, 2 * HEAD_DIM), 1)
    queries = q_ref[...] * jnp.asarray(0.125, bf16)
    mixed = jnp.zeros((rows, 2 * HEAD_DIM), f32)
    for part in range(2):
        keep = (lane // HEAD_DIM) == part
        query = jnp.where(keep, queries, jnp.zeros_like(queries))
        scores = lax.dot_general(query, k_ref[...], NT, preferred_element_type=f32)
        top = jnp.max(scores, axis=1, keepdims=True)
        soft = jnp.exp(scores - top)
        total = jnp.sum(soft, axis=1, keepdims=True)
        out = jnp.dot(soft.astype(bf16), v_ref[...], preferred_element_type=f32)
        mixed = jnp.where(keep, out * (1.0 / total), mixed)
        lse = jnp.broadcast_to(top + jnp.log(total), (rows, 2 * HEAD_DIM))
        lse_ref[0, part : part + 1, :] = lse.T[0:1, :]
    mixed_ref[...] = mixed.astype(bf16)


def attend(member, qkv, slot, rows, block):
    seq = qkv.shape[0]
    pair = 2 * HEAD_DIM
    pairs = qkv.shape[1] // (3 * pair)
    steps = rows // block
    spec = pltpu.PrefetchScalarGridSpec(
        num_scalar_prefetch=1,
        grid=(pairs, steps),
        in_specs=[
            pl.BlockSpec((block, pair), lambda p, i, m: ((m[0] ^ slot) * steps + i, p)),
            pl.BlockSpec((seq, pair), lambda p, i, m: (0, pairs + p)),
            pl.BlockSpec((seq, pair), lambda p, i, m: (0, 2 * pairs + p)),
        ],
        out_specs=[
            pl.BlockSpec((block, pair), lambda p, i, m: (i, p)),
            pl.BlockSpec((1, 2, block), lambda p, i, m: (p, 0, i)),
        ],
    )
    return pl.pallas_call(
        attend_kernel,
        grid_spec=spec,
        out_shape=[
            jax.ShapeDtypeStruct((rows, pairs * pair), bf16),
            jax.ShapeDtypeStruct((pairs, 2, rows), f32),
        ],
        cost_estimate=LIGHT,
        name="attend",
    )(member, qkv, qkv, qkv)


def attend_back_kernel(member, q_ref, k_ref, v_ref, g_ref, *refs, chunk, groups):
    mixed_refs, lse_refs = refs[:groups], refs[groups : 2 * groups]
    out_ref, dk_acc, dv_acc, kt = refs[2 * groups :]
    i = pl.program_id(0)
    slot = i ^ member[0]
    mixed, lse_rows = mixed_refs[0][...], lse_refs[0][0]
    for k in range(1, groups):
        mixed = jnp.where(slot == k, mixed_refs[k][...], mixed)
        lse_rows = jnp.where(slot == k, lse_refs[k][0], lse_rows)
    block = q_ref.shape[0]
    seq = k_ref.shape[0]
    pair = 2 * HEAD_DIM
    lane = lax.broadcasted_iota(jnp.int32, (1, pair), 1)
    side = lax.broadcasted_iota(jnp.int32, (pair, 1), 0)

    @pl.when(i == 0)
    def _():
        dk_acc[...] = jnp.zeros_like(dk_acc)
        dv_acc[...] = jnp.zeros_like(dv_acc)
        kt[...] = k_ref[...].T

    queries = q_ref[...] * jnp.asarray(0.125, bf16)
    grads = g_ref[...]
    product = (grads.astype(f32) * mixed.astype(f32)).T
    grad_query = jnp.zeros((pair, block), f32)
    for part in range(2):
        keep = (lane // HEAD_DIM) == part
        query = jnp.where(keep, queries, jnp.zeros_like(queries))
        grad = jnp.where(keep, grads, jnp.zeros_like(grads))
        delta = jnp.sum(product[part * HEAD_DIM : (part + 1) * HEAD_DIM], axis=0, keepdims=True)
        lse = lse_rows[part : part + 1, :]
        total = jnp.zeros((pair, block), f32)
        for at in range(0, seq, chunk):
            span = pl.ds(at, chunk)
            scores = lax.dot_general(k_ref[span, :], query, NT, preferred_element_type=f32)
            soft = jnp.exp(scores - lse)
            through = lax.dot_general(v_ref[span, :], grad, NT, preferred_element_type=f32)
            grad_scores = (soft * (through - delta)).astype(bf16)
            dv_acc[span, :] += jnp.dot(soft.astype(bf16), grad, preferred_element_type=f32)
            dk_acc[span, :] += jnp.dot(grad_scores, query, preferred_element_type=f32)
            total += jnp.dot(kt[:, span], grad_scores, preferred_element_type=f32)
        grad_query = jnp.where((side // HEAD_DIM) == part, total, grad_query)
    out_ref[pl.ds(pl.multiple_of(i * block, block), block), 0:pair] = (grad_query.T * 0.125).astype(bf16)

    @pl.when(i == pl.num_programs(0) - 1)
    def _():
        out_ref[:, pair : 2 * pair] = dk_acc[...].astype(bf16)
        out_ref[:, 2 * pair : 3 * pair] = dv_acc[...].astype(bf16)


def attend_back(member, qkv, grads, mixed, lse, which, chunk):
    seq = qkv.shape[0]
    groups = len(mixed)
    rows = seq // groups
    pair = 2 * HEAD_DIM
    pairs = qkv.shape[1] // (3 * pair)
    spec = pltpu.PrefetchScalarGridSpec(
        num_scalar_prefetch=1,
        grid=(groups,),
        in_specs=[
            pl.BlockSpec((rows, pair), lambda i, m: (i, which)),
            pl.BlockSpec((seq, pair), lambda i, m: (0, pairs + which)),
            pl.BlockSpec((seq, pair), lambda i, m: (0, 2 * pairs + which)),
            pl.BlockSpec((rows, pair), lambda i, m: (i, which)),
        ]
        + [pl.BlockSpec((rows, pair), lambda i, m: (0, which))] * groups
        + [pl.BlockSpec((1, 2, rows), lambda i, m: (which, 0, 0))] * groups,
        out_specs=pl.BlockSpec((seq, 3 * pair), lambda i, m: (0, 0)),
        scratch_shapes=[pltpu.VMEM((seq, pair), f32), pltpu.VMEM((seq, pair), f32), pltpu.VMEM((pair, seq), bf16)],
    )
    return pl.pallas_call(
        partial(attend_back_kernel, chunk=min(chunk, seq), groups=groups),
        grid_spec=spec,
        out_shape=jax.ShapeDtypeStruct((seq, 3 * pair), bf16),
        cost_estimate=LIGHT,
        name="attend_back",
    )(member, qkv, qkv, qkv, grads, *mixed, *lse)


def put_tail(tail, values, span):
    groups = len(ORDER)
    channels = values.shape[0] // ((PIX + 1) * groups)
    stride = tail.shape[0] // groups
    for at, k in enumerate(ORDER):
        for c in range(PIX + 1):
            row, source = at * stride + c * channels, (c * groups + k) * channels
            tail[row : row + channels, span] = values[source : source + channels]


def aggregate_back_kernel(
    member, core, bucket, pixel_ref, key_ref, value_ref, grad_ref, bias_ref, gain2_ref, gain1_ref, sum_ref,
    field_ref, keep_ref, send_ref, tail
):
    count, rows = pixel_ref.shape[1:]
    pair = 2 * HEAD_DIM
    pixels = [pixel_ref[c].astype(f32) for c in range(PIX)]
    lane = lax.broadcasted_iota(jnp.int32, (1, pair), 1)
    side = lax.broadcasted_iota(jnp.int32, (pair, 1), 0)
    field = [jnp.zeros((count, rows), f32) for _ in range(PIX)]
    keys = [jnp.zeros((count, pair), f32) for _ in range(PIX + 1)]
    for which in range(HEADS // 2):
        span = slice(which * pair, (which + 1) * pair)
        values, grads = value_ref[:, span], grad_ref[span, :]
        total = jnp.zeros(((PIX + 1) * count, pair), f32)
        for part in range(2):
            head = which * 2 + part
            grad = jnp.where((side // HEAD_DIM) == part, grads, jnp.zeros_like(grads))
            through = jnp.dot(values, grad, preferred_element_type=f32)
            kinds = [through[c * count : (c + 1) * count] for c in range(PIX + 1)]
            soft = head_weights(pixels, key_ref, head)
            grad_soft = kinds[PIX]
            for c in range(PIX):
                grad_soft = grad_soft + pixels[c] * kinds[c]
            weighed = soft * grad_soft
            grad_scores = weighed - soft * jnp.sum(weighed, axis=0, keepdims=True)
            for c in range(PIX):
                field[c] = field[c] + soft * kinds[c] + grad_scores * key_ref[c, :, head : head + 1]
                keys[c] = jnp.where(lane == head, jnp.sum(grad_scores * pixels[c], axis=1, keepdims=True), keys[c])
            keys[PIX] = jnp.where(lane == head, jnp.sum(grad_scores, axis=1, keepdims=True), keys[PIX])
            total = total + lax.dot_general(weighted_pixels(soft, pixels), grad, NT, preferred_element_type=f32)
        put_tail(tail, total, span)
    for c in range(PIX):
        field_ref[c] = field[c].astype(bf16)
    width = value_ref.shape[1]
    put_tail(tail, jnp.concatenate(keys, axis=0), slice(width, width + pair))
    groups = len(ORDER)
    stride = tail.shape[0] // groups
    own, lines = width // groups, LEADS // groups
    for at, k in enumerate(ORDER):
        owner = member[0] ^ k
        start = (at + 1) * stride - FREE
        tail[start : start + FREE, :] = jnp.zeros((FREE, tail.shape[1]), f32)
        tail[start : start + 1, :width] = bias_ref[:, pl.ds(pl.multiple_of(owner * width, width), width)]
        chunk = pl.ds(pl.multiple_of(owner * own, own), own)
        tail[start + 1 : start + 2, :own] = gain2_ref[:, chunk]
        tail[start + 1 : start + 2, own : 2 * own] = gain1_ref[:, chunk]
        for line in range(lines):
            hit = bucket[0] == owner * lines + line
            tail[start + 2 + line : start + 3 + line, :width] = jnp.where(hit, sum_ref[...], 0.0)
    half = width // 2
    for ref, which in ((keep_ref, core[0]), (send_ref, 1 - core[0])):
        ref[:, :half] = tail[:, pl.ds(pl.multiple_of(which * half, half), half)].astype(bf16)
        ref[:, half:] = tail[:, width:].astype(bf16)


def aggregate_back(member, core, bucket, pixels, key_rows, values, grads, small, groups):
    count, seq = pixels.shape[1:]
    rows = seq // groups
    width = values.shape[1]
    deep = (PIX + 1) * count + FREE * groups
    wide = width // 2 + 2 * HEAD_DIM

    def whole(*shape):
        return pl.BlockSpec(shape, lambda i, *_: (0,) * len(shape))

    spec = pltpu.PrefetchScalarGridSpec(
        num_scalar_prefetch=3,
        grid=(1,),
        in_specs=[
            pl.BlockSpec((PIX, count, rows), lambda i, m, c, l: (0, 0, m[0])),
            whole(*key_rows.shape),
            whole(*values.shape),
            whole(*grads.shape),
            *[whole(*value.shape) for value in small],
        ],
        out_specs=[whole(PIX, count, rows), whole(deep, wide), whole(deep, wide)],
        scratch_shapes=[pltpu.VMEM((deep, width + 2 * HEAD_DIM), f32)],
    )
    return pl.pallas_call(
        aggregate_back_kernel,
        grid_spec=spec,
        out_shape=[
            jax.ShapeDtypeStruct((PIX, count, rows), bf16),
            jax.ShapeDtypeStruct((deep, wide), bf16),
            jax.ShapeDtypeStruct((deep, wide), bf16),
        ],
        cost_estimate=LIGHT,
        name="aggregate_back",
    )(member, core, bucket, pixels, key_rows, values, grads, *small)


def shape_of(*dims, kind=bf16):
    return jax.ShapeDtypeStruct(dims, kind)


def inner_kernel(
    member, core, mixed0, mixed1, mixed2, mixed3, wo_ref, resid_ref, gain_ref, w1_ref, b1_ref, ga_ref,
    act_ref, act_t_ref, send_ref, keep_ref, bias_ref, one_ref, hidden_ref, mixed_ref, hidden,
):
    j = pl.program_id(0)
    parts = (mixed0, mixed1, mixed2, mixed3)
    rows, own = mixed0.shape

    @pl.when(j == 0)
    def _():
        resid = resid_ref[...]
        for slot, part in enumerate(parts):
            owner = pl.ds(pl.multiple_of((member[0] ^ slot) * own, own), own)
            resid = resid + jnp.dot(part[...], wo_ref[owner, :], preferred_element_type=f32)
        one_ref[...] = resid
        centered = resid - jnp.mean(resid, axis=1, keepdims=True)
        scale = lax.rsqrt(jnp.mean(centered * centered, axis=1, keepdims=True) + epsilon)
        hidden[...] = (centered * scale * gain_ref[...]).astype(bf16)
        piece = own // 2
        for at, (slot, side) in enumerate(BLOCKS):
            start = pl.multiple_of((member[0] ^ slot) * own + side * piece, piece)
            hidden_ref[at * piece : (at + 1) * piece, :] = hidden[:, pl.ds(start, piece)].T
            mixed_ref[at * piece : (at + 1) * piece, :] = parts[slot][:, side * piece : (side + 1) * piece].T

    inner = jnp.dot(hidden[...], w1_ref[...], preferred_element_type=f32) + b1_ref[...]
    below = 0.5 + 0.5 * lax.erf(inner * 0.7071067811865476)
    act = (inner * below).astype(bf16)
    slope = below + inner * (jnp.exp(-0.5 * inner * inner) * 0.3989422804014327)
    gu = (slope * ga_ref[...].astype(f32)).astype(bf16)
    act_ref[...] = act
    act_t_ref[...] = act.T
    bias_ref[...] = jnp.sum(gu.astype(f32), axis=0, keepdims=True)

    @pl.when(j < len(parts))
    def _():
        send_ref[...] = gu

    @pl.when(j >= len(parts))
    def _():
        keep_ref[...] = gu


def inner_part(member, core, mixed, attn_out, resid, gain, mlp_in, bias, grad_act):
    rows, width = resid.shape
    inner = mlp_in.shape[1]
    groups = len(mixed)
    own = width // groups
    steps = 2 * groups
    block = inner // steps

    def natural(j, c):
        return ((j // groups) ^ (1 - c[0])) * groups + j % groups

    def spot(j, m, c):
        n = natural(j, c)
        slot = (n // 2) ^ m[0]
        return (jnp.where(n % 2 == 0, slot, 4 + (slot % 2) * 2 + slot // 2), 0)

    def whole(*shape):
        return pl.BlockSpec(shape, lambda j, m, c: (0,) * len(shape))

    def column(deep):
        return pl.BlockSpec((deep, block), lambda j, m, c: (0, natural(j, c)))

    spec = pltpu.PrefetchScalarGridSpec(
        num_scalar_prefetch=2,
        grid=(steps,),
        in_specs=[whole(rows, own)] * groups
        + [whole(width, width), whole(rows, width), whole(1, width)]
        + [column(width), column(1), column(rows)],
        out_specs=[
            column(rows),
            pl.BlockSpec((block, rows), spot),
            pl.BlockSpec((rows, block), lambda j, m, c: (0, jnp.minimum(j, groups - 1))),
            pl.BlockSpec((rows, block), lambda j, m, c: (0, jnp.maximum(j - groups, 0))),
            column(1),
            whole(rows, width),
            whole(width, rows),
            whole(width, rows),
        ],
        scratch_shapes=[pltpu.VMEM((rows, width), bf16)],
    )
    return pl.pallas_call(
        inner_kernel,
        grid_spec=spec,
        out_shape=[shape_of(rows, inner), shape_of(inner, rows)]
        + [shape_of(rows, inner // 2)] * 2
        + [shape_of(1, inner, kind=f32), shape_of(rows, width, kind=f32)]
        + [shape_of(width, rows)] * 2,
        cost_estimate=LIGHT,
        name="inner_part",
    )(member, core, *mixed, attn_out, resid, gain, mlp_in, bias, grad_act)


def outer_kernel(
    core, act_ref, send_ref, keep_ref, w1_ref, w2_ref, wo_ref, one_ref, gain_ref, g_ref,
    out_ref, gres_ref, gb_ref, gb_send_ref, gm_ref, ggain_ref, branch, grads,
):
    j = pl.program_id(0)
    groups, rows, own = gm_ref.shape
    half = send_ref.shape[1]
    branch[j] = jnp.dot(act_ref[...], w2_ref[...], preferred_element_type=f32)

    def columns(which):
        return w1_ref[:, pl.ds(pl.multiple_of(which * half, half), half)]

    grads[j] = lax.dot_general(
        send_ref[...], columns(1 - core[0]), NT, preferred_element_type=f32
    ) + lax.dot_general(keep_ref[...], columns(core[0]), NT, preferred_element_type=f32)

    @pl.when(j == pl.num_programs(0) - 1)
    def _():
        count = branch.shape[0]
        resid = one_ref[...]
        out_ref[...] = (resid + jnp.concatenate([branch[i] for i in range(count)], axis=1)).astype(bf16)
        centered = resid - jnp.mean(resid, axis=1, keepdims=True)
        scale = lax.rsqrt(jnp.mean(centered * centered, axis=1, keepdims=True) + epsilon)
        grad, plain = jnp.concatenate([grads[i] for i in range(count)], axis=1), centered * scale
        ggain_ref[...] = jnp.sum(grad * plain, axis=0, keepdims=True)
        grad = grad * gain_ref[...]
        first = jnp.mean(grad, axis=1, keepdims=True)
        second = jnp.mean(grad * plain, axis=1, keepdims=True)
        gres = g_ref[...].astype(f32) + scale * (grad - first - plain * second)
        gres_ref[...] = gres
        gb_ref[...] = gres.astype(bf16)
        width = gb_ref.shape[1]
        gb_send_ref[...] = gb_ref[:, pl.ds(pl.multiple_of((1 - core[0]) * (width // 2), width // 2), width // 2)]
        gb = gb_ref[...]
        for p in range(groups):
            gm_ref[p] = lax.dot_general(gb, wo_ref[p * own : (p + 1) * own, :], NT, preferred_element_type=f32).astype(
                bf16
            )


def outer_part(core, act, gu_send, gu_keep, mlp_in, mlp_out, attn_out, resid, gain, grad_out, groups):
    rows, width = resid.shape
    inner = mlp_in.shape[1]
    own = width // groups
    steps = 4
    block = width // steps

    def whole(*shape):
        return pl.BlockSpec(shape, lambda j, c: (0,) * len(shape))

    spec = pltpu.PrefetchScalarGridSpec(
        num_scalar_prefetch=1,
        grid=(steps,),
        in_specs=[
            whole(rows, inner),
            whole(rows, inner // 2),
            whole(rows, inner // 2),
            pl.BlockSpec((block, inner), lambda j, c: (j, 0)),
            pl.BlockSpec((inner, block), lambda j, c: (0, j)),
            whole(width, width),
            whole(rows, width),
            whole(1, width),
            whole(rows, width),
        ],
        out_specs=[
            whole(rows, width),
            whole(rows, width),
            whole(rows, width),
            whole(rows, width // 2),
            whole(groups, rows, own),
            whole(1, width),
        ],
        scratch_shapes=[pltpu.VMEM((steps, rows, block), f32), pltpu.VMEM((steps, rows, block), f32)],
    )
    return pl.pallas_call(
        outer_kernel,
        grid_spec=spec,
        out_shape=[
            shape_of(rows, width),
            shape_of(rows, width, kind=f32),
            shape_of(rows, width),
            shape_of(rows, width // 2),
            shape_of(groups, rows, own),
            shape_of(1, width, kind=f32),
        ],
        cost_estimate=LIGHT,
        name="outer_part",
    )(core, act, gu_send, gu_keep, mlp_in, mlp_out, attn_out, resid, gain, grad_out)


def both_dots(left, left_other, right, right_other):
    return jnp.dot(left[...], right[...], preferred_element_type=f32) + jnp.dot(
        left_other[...], right_other[...], preferred_element_type=f32
    )


def out_grad_kernel(core, left, left_other, right, right_other, *outs):
    total = both_dots(left, left_other, right, right_other).astype(bf16)
    for q, out in enumerate(outs):

        @pl.when(pl.program_id(0) == q)
        def _():
            out[...] = total


def out_grad(core, left, left_other, right, right_other):
    rows, deep = left.shape
    half = right.shape[1] // 2
    block = rows // 4

    spec = pltpu.PrefetchScalarGridSpec(
        num_scalar_prefetch=1,
        grid=(4,),
        in_specs=[pl.BlockSpec((block, deep), lambda i, c: (i, 0))] * 2
        + [
            pl.BlockSpec((deep, half), lambda i, c: (0, c[0])),
            pl.BlockSpec((deep, half), lambda i, c: (0, 0)),
        ],
        out_specs=[pl.BlockSpec((block, half), lambda i, c: (0, 0)) for q in range(4)],
    )
    return pl.pallas_call(
        out_grad_kernel,
        grid_spec=spec,
        out_shape=[shape_of(rows // 4, half)] * 4,
        cost_estimate=LIGHT,
        name="out_grad",
    )(core, left, left_other, right, right_other)


def in_grad_kernel(core, high, h, h_other, u, u_other, m, m_other, b, b_other, keep, send):
    units = u.shape[1]

    def put(out):
        out[:, :units] = both_dots(h, h_other, u, u_other).astype(bf16)
        out[:, units:] = both_dots(m, m_other, b, b_other).astype(bf16)

    @pl.when(pl.program_id(0) == 0)
    def _():
        put(send)

    @pl.when(pl.program_id(0) == 1)
    def _():
        put(keep)


def in_grad(core, high, h, h_other, u, u_other, m, m_other, b, b_other):
    rows, deep = h.shape
    units, branch = u.shape[1] // 2, b_other.shape[1] // 2

    def whole(*shape):
        return pl.BlockSpec(shape, lambda i, c, z: (0,) * len(shape))

    def side(i, c, z):
        return (0, z[0] ^ (1 - i))

    def core_side(i, c, z):
        return (0, 2 * c[0] + (z[0] ^ (1 - i)))

    spec = pltpu.PrefetchScalarGridSpec(
        num_scalar_prefetch=2,
        grid=(2,),
        in_specs=[
            whole(rows, deep),
            whole(rows, deep),
            pl.BlockSpec((deep, units), side),
            pl.BlockSpec((deep, units), side),
            whole(rows, deep),
            whole(rows, deep),
            pl.BlockSpec((deep, branch), core_side),
            pl.BlockSpec((deep, branch), side),
        ],
        out_specs=[whole(rows, units + branch)] * 2,
    )
    return pl.pallas_call(
        in_grad_kernel,
        grid_spec=spec,
        out_shape=[shape_of(rows, units + branch)] * 2,
        cost_estimate=LIGHT,
        name="in_grad",
    )(core, high, h, h_other, u, u_other, m, m_other, b, b_other)


def qkv_grad_kernel(core, h, h_other, *refs):
    out = refs[-1]
    for which in range(2):

        @pl.when(core[0] == which)
        def _():
            out[...] = both_dots(h, h_other, refs[which], refs[2 + which]).astype(bf16)


def qkv_grad(core, h, h_other, grads, others):
    rows, deep = h.shape
    cols = grads[0].shape[1]
    block = rows // 2
    spec = pltpu.PrefetchScalarGridSpec(
        num_scalar_prefetch=1,
        grid=(2,),
        in_specs=[pl.BlockSpec((block, deep), lambda i, c: (i, 0))] * 2
        + [pl.BlockSpec((deep, cols), lambda i, c: (0, 0))] * 4,
        out_specs=pl.BlockSpec((block, cols), lambda i, c: (i, 0)),
    )
    return pl.pallas_call(
        qkv_grad_kernel,
        grid_spec=spec,
        out_shape=shape_of(rows, cols),
        cost_estimate=LIGHT,
        name="qkv_grad",
    )(core, h, h_other, *grads, *others)


def last_grad_kernel(core, qkv_ref, a, a_other, g, g_other, out):
    cols = qkv_ref.shape[1]
    out[0, :, :cols] = qkv_ref[...]
    out[0, :, cols:] = both_dots(a, a_other, g, g_other).astype(bf16)


def last_grad(core, weight_qkv, att, att_other, grad, grad_other, groups):
    rows, deep = att.shape
    half = grad_other.shape[1]
    cols = weight_qkv.shape[1]
    block = rows // groups
    spec = pltpu.PrefetchScalarGridSpec(
        num_scalar_prefetch=1,
        grid=(groups,),
        in_specs=[
            pl.BlockSpec((block, cols), lambda i, c: (i, 0)),
            pl.BlockSpec((block, deep), lambda i, c: (i, 0)),
            pl.BlockSpec((block, deep), lambda i, c: (i, 0)),
            pl.BlockSpec((deep, half), lambda i, c: (0, c[0])),
            pl.BlockSpec((deep, half), lambda i, c: (0, 0)),
        ],
        out_specs=pl.BlockSpec((1, block, cols + half), lambda i, c: (i, 0, 0)),
    )
    return pl.pallas_call(
        last_grad_kernel,
        grid_spec=spec,
        out_shape=shape_of(groups, block, cols + half),
        cost_estimate=LIGHT,
        name="last_grad",
    )(core, weight_qkv, att, att_other, grad, grad_other)


def join_kernel(core, first_ref, second_ref, wq, wk, wv, resid_ref, gain_ref, gres_ref, out_ref, *refs):
    ga_ref, ga_send_ref, gatt_ref, ggain_ref, sum_ref, total = refs
    i = pl.program_id(0)
    pair = 2 * HEAD_DIM

    @pl.when(i == 0)
    def _():
        total[...] = jnp.zeros_like(total)

    grad = total[...]
    for t, weight in enumerate((wq, wk, wv)):
        span = slice(t * pair, (t + 1) * pair)
        left = jnp.concatenate([first_ref[:, span], second_ref[:, span]], axis=1)
        grad = grad + lax.dot_general(left, weight[...], NT, preferred_element_type=f32)
    total[...] = grad

    @pl.when(i == pl.num_programs(0) - 1)
    def _():
        resid = resid_ref[...]
        centered = resid - jnp.mean(resid, axis=1, keepdims=True)
        scale = lax.rsqrt(jnp.mean(centered * centered, axis=1, keepdims=True) + epsilon)
        plain = centered * scale
        grad = total[...]
        ggain_ref[...] = jnp.sum(grad * plain, axis=0, keepdims=True)
        grad = grad * gain_ref[...]
        first = jnp.mean(grad, axis=1, keepdims=True)
        second = jnp.mean(grad * plain, axis=1, keepdims=True)
        gres = gres_ref[...] + scale * (grad - first - plain * second)
        sum_ref[...] = jnp.sum(gres, axis=0, keepdims=True)
        ga = gres.astype(bf16)
        ga_ref[...] = ga
        half = ga_send_ref.shape[1]
        ga_send_ref[...] = ga_ref[:, pl.ds(pl.multiple_of((1 - core[0]) * half, half), half)]
        gatt_ref[...] = lax.dot_general(out_ref[...], ga, NT, preferred_element_type=f32).astype(bf16)


def join(core, first, second, attn_qkv, resid, gain, gres, agg_out):
    rows, width = resid.shape
    groups = first.shape[0] // rows
    own = width // groups
    cols = first.shape[1]

    def whole(*shape):
        return pl.BlockSpec(shape, lambda i, c: (0,) * len(shape))

    spec = pltpu.PrefetchScalarGridSpec(
        num_scalar_prefetch=1,
        grid=(groups,),
        in_specs=[
            pl.BlockSpec((rows, cols), lambda i, c: (i, 0)),
            pl.BlockSpec((rows, cols), lambda i, c: (i, 0)),
            pl.BlockSpec((width, own), lambda i, c: (0, i)),
            pl.BlockSpec((width, own), lambda i, c: (0, groups + i)),
            pl.BlockSpec((width, own), lambda i, c: (0, 2 * groups + i)),
            whole(rows, width),
            whole(1, width),
            whole(rows, width),
            whole(width, width),
        ],
        out_specs=[
            whole(rows, width),
            whole(rows, width // 2),
            whole(width, rows),
            whole(1, width),
            whole(1, width),
        ],
        scratch_shapes=[pltpu.VMEM((rows, width), f32)],
    )
    return pl.pallas_call(
        join_kernel,
        grid_spec=spec,
        out_shape=[
            shape_of(rows, width),
            shape_of(rows, width // 2),
            shape_of(width, rows),
            shape_of(1, width, kind=f32),
            shape_of(1, width, kind=f32),
        ],
        cost_estimate=LIGHT,
        name="join",
    )(core, first, second, attn_qkv, attn_qkv, attn_qkv, resid, gain, gres, agg_out)


def add(a, b):
    return (a.astype(f32) + b.astype(f32)).astype(bf16)


def split_add(a, b, count):
    deep = a.shape[0] // count
    return [add(a[i * deep : (i + 1) * deep], b[i * deep : (i + 1) * deep]) for i in range(count)]


def pick_add(a, b, which, axis):
    half = a.shape[axis] // 2
    return add(
        lax.dynamic_slice_in_dim(a, which * half, half, axis), lax.dynamic_slice_in_dim(b, which * half, half, axis)
    )


def choose(high, a, b, c, d):
    first, second = high == 0, high != 0
    keep = add(jnp.where(first, a, c), jnp.where(first, b, d))
    send = add(jnp.where(second, a, c), jnp.where(second, b, d))
    return keep, send


def whole_blocks(shapes):
    return [pl.BlockSpec(shape, lambda i, *_, n=len(shape): (0,) * n) for shape in shapes]


def gather_sources_kernel(high, came_ref, keep, send, *, cols):
    groups, half = came_ref.shape[0], keep.shape[0]
    for out, which in ((keep, high[0]), (send, 1 - high[0])):
        span = pl.ds(pl.multiple_of(which * half, half), half)
        total = jnp.zeros((half, came_ref.shape[2] - cols), f32)
        for p in range(groups):
            out[:, p * cols : (p + 1) * cols] = came_ref[p, span, :cols]
            total = total + came_ref[p, span, cols:].astype(f32)
        out[:, groups * cols :] = total.astype(bf16)


def gather_sources(high, came, cols):
    groups, rows, wide = came.shape
    shape = (rows // 2, groups * cols + wide - cols)
    spec = pltpu.PrefetchScalarGridSpec(
        num_scalar_prefetch=1, grid=(1,), in_specs=whole_blocks([came.shape]), out_specs=whole_blocks([shape] * 2)
    )
    return pl.pallas_call(
        partial(gather_sources_kernel, cols=cols),
        grid_spec=spec,
        out_shape=[jax.ShapeDtypeStruct(shape, bf16)] * 2,
        cost_estimate=LIGHT,
        name="gather_sources",
    )(high, came)


def turned(i, levels):
    total = 0
    for k in range(levels):
        total = total + (((i >> k) & 1) << (levels - 1 - k))
    return total


def place_out_kernel(first, second, out):
    half = first.shape[2]
    out[:, :half] = first[0].astype(f32)
    out[:, half:] = second[0].astype(f32)


def place_out(pieces, levels):
    _, rows, cols = pieces.shape
    chips = 2**levels
    return pl.pallas_call(
        place_out_kernel,
        grid=(chips,),
        in_specs=[
            pl.BlockSpec((1, rows, cols), lambda i, c=c: (2 * turned(i, levels) + c, 0, 0)) for c in range(2)
        ],
        out_specs=pl.BlockSpec((rows, 2 * cols), lambda i: (i, 0)),
        out_shape=shape_of(chips * rows, 2 * cols, kind=f32),
        cost_estimate=LIGHT,
        name="place_out",
    )(pieces, pieces)


def place_in_kernel(*refs, units):
    pieces, inner, branch = refs[:4], refs[4], refs[5]
    size = pieces[0].shape[2] - units
    for number, piece in enumerate(pieces):
        inner[:, number * units : (number + 1) * units] = piece[0, :, :units].astype(f32)
        branch[:, number * size : (number + 1) * size] = piece[0, :, units:].astype(f32)


def place_in(pieces, levels, units):
    _, rows, cols = pieces.shape
    blocks = 2 ** (levels - 1)

    def at(i, c, b):
        return (2 * (2 * turned(i, levels - 1) + b) + c, 0, 0)

    return pl.pallas_call(
        partial(place_in_kernel, units=units),
        grid=(blocks,),
        in_specs=[
            pl.BlockSpec((1, rows, cols), lambda i, c=c, b=b: at(i, c, b)) for c in range(2) for b in range(2)
        ],
        out_specs=[
            pl.BlockSpec((rows, 4 * units), lambda i: (i, 0)),
            pl.BlockSpec((rows, 4 * (cols - units)), lambda i: (i, 0)),
        ],
        out_shape=[
            shape_of(blocks * rows, 4 * units, kind=f32),
            shape_of(blocks * rows, 4 * (cols - units), kind=f32),
        ],
        cost_estimate=LIGHT,
        name="place_in",
    )(pieces, pieces, pieces, pieces)


def place_last_kernel(first, second, qkv, agg, *, groups):
    pair = 2 * HEAD_DIM
    half = agg.shape[1] // 2
    for c, piece in enumerate((first, second)):
        for p in range(groups):
            for t in range(3):
                source, target = (3 * p + t) * pair, ((t * groups + p) * 2 + c) * pair
                qkv[:, target : target + pair] = piece[0, :, source : source + pair].astype(f32)
        agg[:, c * half : (c + 1) * half] = piece[0, :, 3 * groups * pair :].astype(f32)


def place_last(pieces, levels, groups):
    _, rows, cols = pieces.shape
    chips = 2**levels
    wide = 6 * groups * HEAD_DIM
    return pl.pallas_call(
        partial(place_last_kernel, groups=groups),
        grid=(chips,),
        in_specs=[
            pl.BlockSpec((1, rows, cols), lambda i, c=c: (2 * turned(i, levels) + c, 0, 0)) for c in range(2)
        ],
        out_specs=[
            pl.BlockSpec((rows, 2 * wide), lambda i: (i, 0)),
            pl.BlockSpec((rows, 2 * (cols - wide)), lambda i: (i, 0)),
        ],
        out_shape=[
            shape_of(chips * rows, 2 * wide, kind=f32),
            shape_of(chips * rows, 2 * (cols - wide), kind=f32),
        ],
        cost_estimate=LIGHT,
        name="place_last",
    )(pieces, pieces)


def field_kernel(member, *refs):
    pieces, out = refs[:-1], refs[-1]
    kinds, channels, rows = pieces[0].shape
    for k, piece in enumerate(pieces):
        at = pl.ds(pl.multiple_of((member[0] ^ k) * rows, rows), rows)
        for c in range(kinds):
            out[:, c, at] = piece[c].astype(f32)


def place_field(member, pieces):
    kinds, channels, rows = pieces[0].shape
    shape = (channels, kinds, rows * len(pieces))
    spec = pltpu.PrefetchScalarGridSpec(
        num_scalar_prefetch=1,
        grid=(1,),
        in_specs=whole_blocks([p.shape for p in pieces]),
        out_specs=whole_blocks([shape])[0],
    )
    return pl.pallas_call(
        field_kernel, grid_spec=spec, out_shape=jax.ShapeDtypeStruct(shape, f32), name="place_field"
    )(member, *pieces)


def tail_kernel(member, *refs, groups):
    tails = refs[:groups]
    stacked_ref, pick_ref, value_ref, qk_ref, key_ref, query_ref = refs[groups : groups + 6]
    gvalue_ref, gkey_ref, gquery_ref, rows_ref, gqk = refs[groups + 6 :]
    width = value_ref.shape[0]
    own = gvalue_ref.shape[0]
    at = pl.ds(pl.multiple_of(member[0] * own, own), own)
    tail = jnp.concatenate([t[...] for t in tails], axis=0)
    values, keys = tail[:, :width], tail[:, width:]
    gvalue_ref[...] = lax.dot_general(stacked_ref[:, at], values, TN, preferred_element_type=f32)
    gqk[...] = lax.dot_general(stacked_ref[...], keys, TN, preferred_element_type=f32)
    head = lax.broadcasted_iota(jnp.int32, (keys.shape[1], width), 0)
    column = lax.broadcasted_iota(jnp.int32, (keys.shape[1], width), 1) // HEAD_DIM
    spread = jnp.where(head == column, 1.0, 0.0)
    gkey_ref[...] = (
        jnp.dot(gqk[at, :], spread, precision=highest, preferred_element_type=f32) * (query_ref[...] * 0.125)
    )
    by_head = lax.dot_general(gqk[...], key_ref[...].astype(f32), TN, precision=highest, preferred_element_type=f32)
    head = lax.broadcasted_iota(jnp.int32, by_head.shape, 0)
    column = (lax.broadcasted_iota(jnp.int32, by_head.shape, 1) + member[0] * own) // HEAD_DIM
    gquery_ref[...] = jnp.sum(jnp.where(head == column, by_head, 0.0), axis=0, keepdims=True) * 0.125
    own_rows = tails[0].shape[0]
    table = jnp.dot(pick_ref[...], tail, preferred_element_type=f32).astype(bf16)
    rows = jnp.concatenate([tail[:own_rows], table], axis=0)
    rows_ref[...] = lax.dot_general(rows[:, :width], value_ref[...], NT, preferred_element_type=f32) + lax.dot_general(
        rows[:, width:].astype(f32), qk_ref[...], NT, precision=highest, preferred_element_type=f32
    )


def finish_tail(member, tails, stacked, pick, agg_value, query_keys, agg_key, agg_query):
    groups = len(tails)
    width = agg_value.shape[0]
    own = width // groups
    deep = tails[0].shape[0] + pick.shape[0]
    args = [*tails, stacked, pick, agg_value, query_keys]
    spec = pltpu.PrefetchScalarGridSpec(
        num_scalar_prefetch=1,
        grid=(1,),
        in_specs=whole_blocks([x.shape for x in args])
        + [pl.BlockSpec((width, own), lambda i, m: (0, m[0])), pl.BlockSpec((1, width), lambda i, m: (0, 0))],
        out_specs=whole_blocks([(own, width), (own, width), (1, own), (deep, width)]),
        scratch_shapes=[pltpu.VMEM((width, query_keys.shape[1]), f32)],
    )
    return pl.pallas_call(
        partial(tail_kernel, groups=groups),
        grid_spec=spec,
        out_shape=[
            jax.ShapeDtypeStruct((own, width), f32),
            jax.ShapeDtypeStruct((own, width), f32),
            jax.ShapeDtypeStruct((1, own), f32),
            jax.ShapeDtypeStruct((deep, width), f32),
        ],
        cost_estimate=LIGHT,
        name="finish_tail",
    )(member, *args, agg_key, agg_query)


def fence(*values):
    return lax.optimization_barrier(values)


def swap(value, axis, bits):
    size = lax.axis_size(axis)
    return lax.ppermute(value, axis, [(i, i ^ bits) for i in range(size)])


def from_all(own, groups):
    return [own] + [swap(own, "var", k) for k in range(1, groups)]


def exchange(value):
    return lax.all_to_all(value, "var", split_axis=0, concat_axis=0, tiled=True)


def chip_bits():
    bits, bit = [], 1
    while bit < lax.axis_size("chip"):
        bits.append(bit)
        bit *= 2
    return bits


def is_high(bit):
    return (lax.axis_index("chip") // bit) % 2


def by_core(mine, other, core):
    return jnp.where(core == 0, mine, other), jnp.where(core == 0, other, mine)


def body(
    field_patches,
    var_ids,
    lead_bucket,
    patch_weight,
    var_embed,
    agg_query,
    agg_key,
    agg_value,
    agg_out,
    lead_table,
    ln1_gain,
    attn_qkv,
    attn_out,
    ln2_gain,
    mlp_in,
    mlp_in_bias,
    mlp_out,
    cotangent,
):
    groups = lax.axis_size("var")
    member = lax.axis_index("var")
    core = lax.axis_index("core")
    channels, pixel_count, samples, seq = field_patches.shape
    width = agg_key.shape[0]
    inner_width = mlp_in.shape[1]
    leads = lead_table.shape[0]
    vocab = var_embed.shape[0]
    rows = seq // groups
    own = width // groups
    count = channels * groups
    slots = [member ^ k for k in range(groups)]
    member_one = member.reshape(1).astype(jnp.int32)
    core_one = core.reshape(1).astype(jnp.int32)
    bits = chip_bits()
    assert bits
    high = is_high(bits[0])
    high_one = high.reshape(1).astype(jnp.int32)
    half = width // 2
    gain_one = ln1_gain.astype(f32)
    gain_two = ln2_gain.astype(f32)

    mine = jnp.concatenate(
        [
            field_patches.reshape(channels, pixel_count, seq).transpose(1, 0, 2),
            patch_weight.transpose(1, 0, 2),
        ],
        axis=2,
    )
    grad_out = cotangent.reshape(rows, width)
    grad_act = lax.dot_general(grad_out, mlp_out, NT, preferred_element_type=f32).astype(bf16)
    ids = jnp.concatenate([lax.dynamic_slice_in_dim(var_ids, slot * channels, channels) for slot in slots])
    table_pick = (ids[:, None] == jnp.arange(vocab, dtype=jnp.int32)[None, :]).astype(bf16)
    embeds = jnp.dot(table_pick, var_embed, preferred_element_type=f32).astype(bf16)
    head_of = jnp.arange(width, dtype=jnp.int32) // HEAD_DIM
    spread = head_of[:, None] == jnp.arange(2 * HEAD_DIM, dtype=jnp.int32)[None, :]
    query_block = jnp.where(spread, agg_query[:, None], jnp.zeros((), bf16))
    query_keys = jnp.dot(agg_key, query_block, preferred_element_type=f32) * 0.125
    lead_row = lax.dynamic_slice_in_dim(lead_table, lead_bucket[0], 1).astype(f32)
    grad_out_other = swap(lax.dynamic_slice_in_dim(grad_out, (1 - core) * half, half, axis=1), "core", 1)
    arrived, grad_act, embeds, query_keys, lead_row, grad_out_other = fence(
        from_all(mine, groups), grad_act, embeds, query_keys, lead_row, grad_out_other
    )
    pixels = jnp.concatenate([value[:, :, :seq] for value in arrived], axis=1)
    stacked = jnp.concatenate([value[:, :, seq:] for value in arrived], axis=1)
    stacked = jnp.concatenate([stacked, embeds[None]], axis=0).reshape(-1, width)
    key_rows = jnp.dot(stacked.astype(f32), query_keys, precision=highest).reshape(PIX + 1, count, 2 * HEAD_DIM)
    values = jnp.dot(stacked, agg_value, preferred_element_type=f32).astype(bf16)
    values_t = values.T

    hidden_t, qkv, resid_zero, att_low = front(
        member_one, pixels, key_rows, values_t, agg_out, lead_row, gain_one[None], attn_qkv, groups
    )

    hidden_t, att_low, qkv = fence(hidden_t, att_low, qkv)
    hidden_other, att_other = swap(hidden_t, "core", 1), swap(att_low, "core", 1)

    block = min(256, rows)
    mixed_parts, lse_parts, received = [None] * groups, [None] * groups, [None] * groups
    for k in reversed(range(groups)):
        mixed_parts[k], lse_parts[k] = attend(member_one, qkv, k, rows, block)
        if k + 1 < groups:
            received[k + 1], mixed_parts[k], qkv = fence(received[k + 1], mixed_parts[k], qkv)
            if k + 2 == groups:
                hidden_other, att_other, qkv = fence(hidden_other, att_other, qkv)
        received[k] = swap(mixed_parts[k], "var", k) if k else mixed_parts[k]

    act, act_t, gu_send, gu_keep, grad_bias, resid_one, hidden_two_t, mixed_t = inner_part(
        member_one, core_one, received, attn_out, resid_zero, gain_two[None], mlp_in, mlp_in_bias.astype(f32)[None], grad_act
    )
    gu_send, act_t, act, hidden_two_t, mixed_t = fence(gu_send, act_t, act, hidden_two_t, mixed_t)
    act_other, gu_other, hidden_two_other, mixed_other = (
        swap(value, "core", 1) for value in (act_t, gu_send, hidden_two_t, mixed_t)
    )
    output, grad_resid_one, grad_branch, branch_send, grad_mixed, grad_gain_two = outer_part(
        core_one, act, gu_send, gu_keep, mlp_in, mlp_out, attn_out, resid_one, gain_two[None], grad_out, groups
    )
    act_other, gu_other, hidden_two_other, mixed_other, grad_mixed, branch_send, output = fence(
        act_other, gu_other, hidden_two_other, mixed_other, grad_mixed, branch_send, output
    )
    output = output.reshape(samples, rows, width)

    branch_other = swap(branch_send, "core", 1)
    grad_heads = exchange(grad_mixed).reshape(seq, own)
    out_y, out_y_send, out_x, out_x_send = out_grad(core_one, act_t, act_other, grad_out, grad_out_other)
    branch_other, out_y, out_y_send, out_x, out_x_send = fence(branch_other, out_y, out_y_send, out_x, out_x_send)
    out_y_came, out_x_came = swap(out_y_send, "var", 2), swap(out_x_send, "var", 1)
    in_part, in_part_send = in_grad(
        core_one,
        high_one,
        hidden_two_t,
        hidden_two_other,
        gu_keep,
        gu_other,
        mixed_t,
        mixed_other,
        grad_branch,
        branch_other,
    )
    grad_heads, in_part_send, in_part = fence(grad_heads, in_part_send, in_part)

    pair = 2 * HEAD_DIM
    pairs = own // pair
    assert pairs == 2
    in_part_came = swap(in_part_send, "chip", bits[0])
    first = attend_back(member_one, qkv, grad_heads, mixed_parts, lse_parts, 0, 512)
    first, qkv, out_y_came, out_x_came = fence(first, qkv, out_y_came, out_x_came)
    out_y, out_y_send = split_add(out_y, out_y_came, 2)
    out_x, out_x_send = split_add(out_x, out_x_came, 2)
    first, qkv, out_y_send, out_x_send = fence(first, qkv, out_y_send, out_x_send)
    first_came = exchange(first)
    first_other = swap(first, "core", 1)
    out_y_came, out_x_came = swap(out_y_send, "var", 1), swap(out_x_send, "var", 2)
    second = attend_back(member_one, qkv, grad_heads, mixed_parts, lse_parts, 1, 512)
    first, first_came, first_other, second, in_part_came, out_y_came, out_x_came = fence(
        first, first_came, first_other, second, in_part_came, out_y_came, out_x_came
    )
    second_came = exchange(second)
    second_other = swap(second, "core", 1)
    out_keep, out_send = choose(high, out_y, out_y_came, out_x, out_x_came)
    out_came = swap(out_send, "chip", bits[0])
    in_y, in_y_send, in_x, in_x_send = split_add(in_part, in_part_came, 4)
    second_other, in_y_send, in_x_send = fence(second_other, in_y_send, in_x_send)
    weight_qkv = qkv_grad(core_one, hidden_t, hidden_other, (first, second), (first_other, second_other))
    second_came, weight_qkv, in_y_send, in_x_send, grad_resid_one = fence(
        second_came, weight_qkv, in_y_send, in_x_send, grad_resid_one
    )
    in_y_came, in_x_came = swap(in_y_send, "var", 2), swap(in_x_send, "var", 1)
    grad_agg, grad_agg_send, grad_att, grad_gain_one, sample_sum = join(
        core_one, first_came, second_came, attn_qkv, resid_zero, gain_one[None], grad_resid_one, agg_out
    )
    grad_agg_send, grad_att, out_came = fence(grad_agg_send, grad_att, out_came)
    grad_agg_other = swap(grad_agg_send, "core", 1)
    rest = bits[1:]

    def scatter_step(keep, came, bit):
        halves = [pick_add(keep, came, which, 0) for which in (is_high(bit), 1 - is_high(bit))]
        return halves[0], swap(halves[1], "chip", bit)

    out_keep, out_came = scatter_step(out_keep, out_came, rest[0])
    for bit in rest[1:]:
        out_keep, out_came = scatter_step(out_keep, out_came, bit)

    field_own, tail, tail_send = aggregate_back(
        member_one,
        core_one,
        lead_bucket,
        pixels,
        key_rows,
        values,
        grad_att,
        (grad_bias, grad_gain_two, grad_gain_one, sample_sum),
        groups,
    )
    tail, tail_send, grad_agg_other, in_y_came, in_x_came, out_came = fence(
        tail, tail_send, grad_agg_other, in_y_came, in_x_came, out_came
    )
    everyone = ("chip", "core")
    tail_came = swap(tail_send, "core", 1)
    in_y, in_y_send = split_add(in_y, in_y_came, 2)
    in_x, in_x_send = split_add(in_x, in_x_came, 2)
    in_y_came, in_x_came = swap(in_y_send, "var", 1), swap(in_x_send, "var", 2)
    last_send = last_grad(core_one, weight_qkv, att_low, att_other, grad_agg, grad_agg_other, groups)
    out_all = lax.all_gather(add(out_keep, out_came), everyone)
    tail, tail_came, last_send, in_y_came, in_x_came = fence(tail, tail_came, last_send, in_y_came, in_x_came)
    tail = add(tail, tail_came)
    deep = tail.shape[0] // 2
    tail_came = swap(tail[deep:], "var", 1)
    in_own = jnp.concatenate([add(in_y, in_y_came), add(in_x, in_x_came)], axis=0)
    for bit in rest:
        in_rows = in_own.shape[0] // 2
        in_own, in_send = (
            lax.dynamic_slice_in_dim(in_own, which * in_rows, in_rows) for which in (is_high(bit), 1 - is_high(bit))
        )
        in_came = swap(in_send, "chip", bit)
        if bit != rest[-1]:
            in_own = add(in_own, in_came)
    tail, tail_came, last_send = fence(tail, tail_came, last_send)
    tail = add(tail[:deep], tail_came)
    deep //= 2
    tail_came = swap(tail[deep:], "var", 2)
    tail, tail_came, last_send = fence(tail, tail_came, last_send)
    last_came = exchange(last_send)
    tail = add(tail[:deep], tail_came)
    tail_came = swap(tail, "chip", bits[0])
    tail, tail_came, in_came, last_came = fence(tail, tail_came, in_came, last_came)
    in_all = lax.all_gather(add(in_own, in_came), everyone)
    last_keep, last_send = gather_sources(high_one, last_came, 3 * pair)
    last_came = swap(last_send, "chip", bits[0])
    tail = add(tail, tail_came)
    for bit in rest:
        tail_came = swap(tail, "chip", bit)
        if bit != rest[-1]:
            tail = add(tail, tail_came)
    tail, tail_came, last_came = fence(tail, tail_came, last_came)
    tail = add(tail, tail_came)
    for bit in rest:
        last_keep, last_came = scatter_step(last_keep, last_came, bit)
    tail_came = swap(tail, "core", 1)
    tail, tail_came, last_came = fence(tail, tail_came, last_came)
    last_all = lax.all_gather(add(last_keep, last_came), everyone)
    low, up = by_core(tail, tail_came, core)
    tail = jnp.concatenate([low[:, :half], up], axis=1)
    tails = from_all(tail, groups)
    field_slots = field_own.reshape(pixel_count, groups, channels, rows)
    field_parts = [swap(field_slots[:, k], "var", k) if k else field_slots[:, 0] for k in range(groups)]
    stride = tail.shape[0]
    per_slot = (PIX + 1) * channels
    small_sum = tail[per_slot:, :width].astype(f32)
    part_size = inner_width // groups
    sum_bias = small_sum[0]
    sum_gain_two = small_sum[1, :own]
    sum_gain_one = small_sum[1, own : 2 * own]
    sum_lead = small_sum[2 : 2 + leads // groups]

    by_slot = stacked.reshape(PIX + 1, groups, channels, width).transpose(1, 0, 2, 3).reshape(groups, per_slot, width)
    by_slot = jnp.pad(by_slot, ((0, 0), (0, stride - per_slot), (0, 0))).reshape(groups * stride, width)
    own_ids = member * (vocab // groups) + jnp.arange(16, dtype=jnp.int32)
    own_pick = jnp.where(jnp.arange(16)[:, None] < vocab // groups, own_ids[:, None] == ids[None, :], False)
    own_pick = jnp.pad(
        own_pick.reshape(16, groups, channels), ((0, 0), (0, 0), (PIX * channels, stride - per_slot))
    ).reshape(16, groups * stride)
    sum_value, sum_key, sum_query, sum_rows = finish_tail(
        member_one,
        tails,
        by_slot,
        own_pick.astype(bf16),
        agg_value,
        query_keys,
        agg_key,
        agg_query.astype(f32)[None],
    )
    sum_query = sum_query.reshape(own)
    sum_patch = sum_rows[: PIX * channels].reshape(pixel_count, channels, width).transpose(1, 0, 2)
    sum_table = sum_rows[stride : stride + vocab // groups]
    field_grad = place_field(member_one, field_parts).reshape(channels, pixel_count, samples, seq)

    levels = len(bits)
    sum_mlp_out = place_out(out_all, levels)
    sum_mlp_in, sum_attn_out = place_in(in_all, levels, inner_width // 4)
    sum_qkv, sum_agg_out = place_last(last_all, levels, groups)
    return (
        output,
        field_grad,
        sum_patch,
        sum_table,
        sum_query,
        sum_key,
        sum_value,
        sum_agg_out,
        sum_lead,
        sum_gain_one,
        sum_qkv,
        sum_attn_out,
        sum_gain_two,
        sum_mlp_in,
        sum_bias,
        sum_mlp_out,
    )


def solution(mesh):
    members, patches = mesh.shape["var"], mesh.shape["patch"]
    chips = Mesh(mesh.devices.reshape(members, patches // 2, 2), ("var", "chip", "core"))
    patch = ("chip", "core")
    placed = (
        P("var", None, patch, None),
        P(),
        P(patch),
        P("var", None, None),
        *[P()] * 13,
        P(patch, "var", None),
    )
    return jax.shard_map(
        body,
        mesh=chips,
        in_specs=placed,
        out_specs=(
            P(patch, "var", None),
            P("var", None, patch, None),
            P("var", None, None),
            P("var", None),
            P("var"),
            P("var", None),
            P("var", None),
            P("var", None),
            P("var", None),
            P("var"),
            P("var", None),
            P("var", None),
            P("var"),
            P("var", None),
            P("var"),
            P("var", None),
        ),
        check_vma=False,
    )
```

```python
from functools import partial

import jax
import jax.numpy as jnp
from jax import lax
from jax.experimental import pallas as pl
from jax.experimental.pallas import tpu as pltpu
from jax.sharding import Mesh
from jax.sharding import PartitionSpec as P

HEADS = 16
PIX = 4
HEAD_DIM = 64
LEADS = 8
FREE = 4
ORDER = (0, 2, 1, 3)
BLOCKS = tuple((k, 0) for k in range(4)) + tuple((k, 1) for k in ORDER)

f32, bf16 = jnp.float32, jnp.bfloat16
highest = lax.Precision.HIGHEST
epsilon = 1e-05
NT = (((1,), (1,)), ((), ()))
LIGHT = pl.CostEstimate(flops=1, bytes_accessed=1, transcendentals=0)
TN = (((0,), (0,)), ((), ()))


def head_weights(pixels, key_ref, head):
    scores = key_ref[PIX, :, head : head + 1]
    for c in range(PIX):
        scores = scores + pixels[c] * key_ref[c, :, head : head + 1]
    soft = jnp.exp(scores - jnp.max(scores, axis=0, keepdims=True))
    return soft * (1.0 / jnp.sum(soft, axis=0, keepdims=True))


def slot_spans(member, own):
    return [pl.ds(pl.multiple_of((member[0] ^ k) * own, own), own) for k in ORDER]


def weighted_pixels(soft, pixels):
    return jnp.concatenate(
        [(soft * pixels[c]).astype(bf16) for c in range(PIX)] + [soft.astype(bf16)], axis=0
    )


def prepare_kernel(*refs, groups):
    blocks = refs[:groups]
    embed_ref, query_ref, weight_ref, pixel_ref, key_ref, value_ref, value_t_ref, slot_ref, stacked, by_slot = refs[groups:]
    channels = blocks[0].shape[1]
    seq = pixel_ref.shape[2]
    count = channels * groups
    stride = by_slot.shape[0] // groups
    by_slot[...] = jnp.zeros_like(by_slot)
    for k, block in enumerate(blocks):
        for c in range(PIX + 1):
            if c < PIX:
                pixel_ref[c, k * channels : (k + 1) * channels, :] = block[c, :, :seq].astype(f32)
                rows = block[c, :, seq:].astype(f32)
            else:
                rows = embed_ref[k * channels : (k + 1) * channels, :]
            stacked[c * count + k * channels : c * count + (k + 1) * channels, :] = rows
            by_slot[k * stride + c * channels : k * stride + (c + 1) * channels, :] = rows
    slot_ref[...] = by_slot[...].astype(bf16)
    keys = jnp.dot(stacked[...], query_ref[...], precision=highest, preferred_element_type=f32)
    for c in range(PIX + 1):
        key_ref[c] = keys[c * count : (c + 1) * count]
    values = jnp.dot(stacked[...].astype(bf16), weight_ref[...], preferred_element_type=f32).astype(bf16)
    value_ref[...] = values
    value_t_ref[...] = values.T


def prepare(blocks, embeds, query_keys, agg_value, seq):
    groups = len(blocks)
    channels = blocks[0].shape[1]
    count = channels * groups
    width = agg_value.shape[0]
    rows = (PIX + 1) * count
    deep = rows + FREE * groups
    return pl.pallas_call(
        partial(prepare_kernel, groups=groups),
        out_shape=[
            jax.ShapeDtypeStruct((PIX, count, seq), f32),
            jax.ShapeDtypeStruct((PIX + 1, count, query_keys.shape[1]), f32),
            jax.ShapeDtypeStruct((rows, width), bf16),
            jax.ShapeDtypeStruct((width, rows), bf16),
            jax.ShapeDtypeStruct((deep, width), bf16),
        ],
        scratch_shapes=[pltpu.VMEM((rows, width), f32), pltpu.VMEM((deep, width), f32)],
        cost_estimate=LIGHT,
        name="prepare",
    )(*blocks, embeds, query_keys, agg_value)


def front_kernel(
    member,
    pixel_ref,
    key_ref,
    value_ref,
    out_ref,
    lead_ref,
    gain_ref,
    wq_ref,
    wk_ref,
    wv_ref,
    hidden_ref,
    qkv_ref,
    resid_ref,
    att_ref,
    att_scratch,
):
    pixels = [pixel_ref[c] for c in range(PIX)]
    for head in range(HEADS):
        soft = head_weights(pixels, key_ref, head)
        span = slice(head * HEAD_DIM, (head + 1) * HEAD_DIM)
        att_scratch[span, :] = jnp.dot(
            value_ref[span, :], weighted_pixels(soft, pixels), preferred_element_type=f32
        ).astype(bf16)
    att = att_scratch[...]
    resid = lax.dot_general(att, out_ref[...], TN, preferred_element_type=f32) + lead_ref[...]
    centered = resid - jnp.mean(resid, axis=1, keepdims=True)
    inverse = lax.rsqrt(jnp.mean(centered * centered, axis=1, keepdims=True) + epsilon)
    hidden = (centered * inverse * gain_ref[...]).astype(bf16)
    own = wq_ref.shape[1]
    hidden_ref[...] = hidden.T
    for t, weight in enumerate((wq_ref, wk_ref, wv_ref)):
        qkv_ref[:, t * own : (t + 1) * own] = jnp.dot(
            hidden, weight[...], preferred_element_type=f32
        ).astype(bf16)

    @pl.when(pl.program_id(0) == member[0])
    def _():
        resid_ref[...] = resid
        att_ref[...] = att


def front(member, pixels, key_rows, values_t, agg_out, lead_row, gain, attn_qkv, groups):
    width = agg_out.shape[0]
    own = width // groups
    channels, seq = pixels.shape[1:]
    rows = seq // groups
    spec = pltpu.PrefetchScalarGridSpec(
        num_scalar_prefetch=1,
        grid=(groups,),
        in_specs=[
            pl.BlockSpec((PIX, channels, rows), lambda i, m: (0, 0, i)),
            pl.BlockSpec(key_rows.shape, lambda i, m: (0, 0, 0)),
            pl.BlockSpec(values_t.shape, lambda i, m: (0, 0)),
            pl.BlockSpec(agg_out.shape, lambda i, m: (0, 0)),
            pl.BlockSpec((1, width), lambda i, m: (0, 0)),
            pl.BlockSpec((1, width), lambda i, m: (0, 0)),
            pl.BlockSpec((width, own), lambda i, m: (0, m[0])),
            pl.BlockSpec((width, own), lambda i, m: (0, groups + m[0])),
            pl.BlockSpec((width, own), lambda i, m: (0, 2 * groups + m[0])),
        ],
        out_specs=[
            pl.BlockSpec((width, rows), lambda i, m: (0, i)),
            pl.BlockSpec((rows, 3 * own), lambda i, m: (i, 0)),
            pl.BlockSpec((rows, width), lambda i, m: (0, 0)),
            pl.BlockSpec((width, rows), lambda i, m: (0, 0)),
        ],
        scratch_shapes=[pltpu.VMEM((width, rows), bf16)],
    )
    return pl.pallas_call(
        front_kernel,
        grid_spec=spec,
        out_shape=[
            jax.ShapeDtypeStruct((width, seq), bf16),
            jax.ShapeDtypeStruct((seq, 3 * own), bf16),
            jax.ShapeDtypeStruct((rows, width), f32),
            jax.ShapeDtypeStruct((width, rows), bf16),
        ],
        cost_estimate=LIGHT,
        name="front",
    )(member, pixels, key_rows, values_t, agg_out, lead_row, gain, attn_qkv, attn_qkv, attn_qkv)


def attend_kernel(member, q_ref, k_ref, v_ref, mixed_ref, lse_ref):
    rows = q_ref.shape[0]
    lane = lax.broadcasted_iota(jnp.int32, (1, 2 * HEAD_DIM), 1)
    queries = q_ref[...] * jnp.asarray(0.125, bf16)
    mixed = jnp.zeros((rows, 2 * HEAD_DIM), f32)
    for part in range(2):
        keep = (lane // HEAD_DIM) == part
        query = jnp.where(keep, queries, jnp.zeros_like(queries))
        scores = lax.dot_general(query, k_ref[...], NT, preferred_element_type=f32)
        top = jnp.max(scores, axis=1, keepdims=True)
        soft = jnp.exp(scores - top)
        total = jnp.sum(soft, axis=1, keepdims=True)
        out = jnp.dot(soft.astype(bf16), v_ref[...], preferred_element_type=f32)
        mixed = jnp.where(keep, out * (1.0 / total), mixed)
        lse = jnp.broadcast_to(top + jnp.log(total), (rows, 2 * HEAD_DIM))
        lse_ref[0, part : part + 1, :] = lse.T[0:1, :]
    mixed_ref[...] = mixed.astype(bf16)


def attend(member, qkv, slot, rows, block):
    seq = qkv.shape[0]
    pair = 2 * HEAD_DIM
    pairs = qkv.shape[1] // (3 * pair)
    steps = rows // block
    spec = pltpu.PrefetchScalarGridSpec(
        num_scalar_prefetch=1,
        grid=(pairs, steps),
        in_specs=[
            pl.BlockSpec((block, pair), lambda p, i, m: ((m[0] ^ slot) * steps + i, p)),
            pl.BlockSpec((seq, pair), lambda p, i, m: (0, pairs + p)),
            pl.BlockSpec((seq, pair), lambda p, i, m: (0, 2 * pairs + p)),
        ],
        out_specs=[
            pl.BlockSpec((block, pair), lambda p, i, m: (i, p)),
            pl.BlockSpec((1, 2, block), lambda p, i, m: (p, 0, i)),
        ],
    )
    return pl.pallas_call(
        attend_kernel,
        grid_spec=spec,
        out_shape=[
            jax.ShapeDtypeStruct((rows, pairs * pair), bf16),
            jax.ShapeDtypeStruct((pairs, 2, rows), f32),
        ],
        cost_estimate=LIGHT,
        name="attend",
    )(member, qkv, qkv, qkv)


def attend_back_kernel(member, q_ref, k_ref, v_ref, g_ref, *refs, chunk, groups):
    mixed_refs, lse_refs = refs[:groups], refs[groups : 2 * groups]
    out_ref, dk_acc, dv_acc, kt = refs[2 * groups :]
    i = pl.program_id(0)
    slot = i ^ member[0]
    mixed, lse_rows = mixed_refs[0][...], lse_refs[0][0]
    for k in range(1, groups):
        mixed = jnp.where(slot == k, mixed_refs[k][...], mixed)
        lse_rows = jnp.where(slot == k, lse_refs[k][0], lse_rows)
    block = q_ref.shape[0]
    seq = k_ref.shape[0]
    pair = 2 * HEAD_DIM
    lane = lax.broadcasted_iota(jnp.int32, (1, pair), 1)
    side = lax.broadcasted_iota(jnp.int32, (pair, 1), 0)

    @pl.when(i == 0)
    def _():
        dk_acc[...] = jnp.zeros_like(dk_acc)
        dv_acc[...] = jnp.zeros_like(dv_acc)
        kt[...] = k_ref[...].T

    queries = q_ref[...] * jnp.asarray(0.125, bf16)
    grads = g_ref[...]
    product = (grads.astype(f32) * mixed.astype(f32)).T
    grad_query = jnp.zeros((pair, block), f32)
    for part in range(2):
        keep = (lane // HEAD_DIM) == part
        query = jnp.where(keep, queries, jnp.zeros_like(queries))
        grad = jnp.where(keep, grads, jnp.zeros_like(grads))
        delta = jnp.sum(product[part * HEAD_DIM : (part + 1) * HEAD_DIM], axis=0, keepdims=True)
        lse = lse_rows[part : part + 1, :]
        total = jnp.zeros((pair, block), f32)
        for at in range(0, seq, chunk):
            span = pl.ds(at, chunk)
            scores = lax.dot_general(k_ref[span, :], query, NT, preferred_element_type=f32)
            soft = jnp.exp(scores - lse)
            through = lax.dot_general(v_ref[span, :], grad, NT, preferred_element_type=f32)
            grad_scores = (soft * (through - delta)).astype(bf16)
            dv_acc[span, :] += jnp.dot(soft.astype(bf16), grad, preferred_element_type=f32)
            dk_acc[span, :] += jnp.dot(grad_scores, query, preferred_element_type=f32)
            total += jnp.dot(kt[:, span], grad_scores, preferred_element_type=f32)
        grad_query = jnp.where((side // HEAD_DIM) == part, total, grad_query)
    out_ref[pl.ds(pl.multiple_of(i * block, block), block), 0:pair] = (grad_query.T * 0.125).astype(bf16)

    @pl.when(i == pl.num_programs(0) - 1)
    def _():
        out_ref[:, pair : 2 * pair] = dk_acc[...].astype(bf16)
        out_ref[:, 2 * pair : 3 * pair] = dv_acc[...].astype(bf16)


def attend_back(member, qkv, grads, mixed, lse, which, chunk):
    seq = qkv.shape[0]
    groups = len(mixed)
    rows = seq // groups
    pair = 2 * HEAD_DIM
    pairs = qkv.shape[1] // (3 * pair)
    spec = pltpu.PrefetchScalarGridSpec(
        num_scalar_prefetch=1,
        grid=(groups,),
        in_specs=[
            pl.BlockSpec((rows, pair), lambda i, m: (i, which)),
            pl.BlockSpec((seq, pair), lambda i, m: (0, pairs + which)),
            pl.BlockSpec((seq, pair), lambda i, m: (0, 2 * pairs + which)),
            pl.BlockSpec((rows, pair), lambda i, m: (i, which)),
        ]
        + [pl.BlockSpec((rows, pair), lambda i, m: (0, which))] * groups
        + [pl.BlockSpec((1, 2, rows), lambda i, m: (which, 0, 0))] * groups,
        out_specs=pl.BlockSpec((seq, 3 * pair), lambda i, m: (0, 0)),
        scratch_shapes=[pltpu.VMEM((seq, pair), f32), pltpu.VMEM((seq, pair), f32), pltpu.VMEM((pair, seq), bf16)],
    )
    return pl.pallas_call(
        partial(attend_back_kernel, chunk=min(chunk, seq), groups=groups),
        grid_spec=spec,
        out_shape=jax.ShapeDtypeStruct((seq, 3 * pair), bf16),
        cost_estimate=LIGHT,
        name="attend_back",
    )(member, qkv, qkv, qkv, grads, *mixed, *lse)


def put_tail(tail, values, span):
    groups = len(ORDER)
    channels = values.shape[0] // ((PIX + 1) * groups)
    stride = tail.shape[0] // groups
    for at, k in enumerate(ORDER):
        for c in range(PIX + 1):
            row, source = at * stride + c * channels, (c * groups + k) * channels
            tail[row : row + channels, span] = values[source : source + channels]


def aggregate_back_kernel(
    member, core, bucket, pixel_ref, key_ref, value_ref, grad_ref, bias_ref, gain2_ref, gain1_ref, sum_ref,
    field_ref, keep_ref, send_ref, tail
):
    count, rows = pixel_ref.shape[1:]
    pair = 2 * HEAD_DIM
    pixels = [pixel_ref[c] for c in range(PIX)]
    lane = lax.broadcasted_iota(jnp.int32, (1, pair), 1)
    side = lax.broadcasted_iota(jnp.int32, (pair, 1), 0)
    field = [jnp.zeros((count, rows), f32) for _ in range(PIX)]
    keys = [jnp.zeros((count, pair), f32) for _ in range(PIX + 1)]
    for which in range(HEADS // 2):
        span = slice(which * pair, (which + 1) * pair)
        values, grads = value_ref[:, span], grad_ref[span, :]
        total = jnp.zeros(((PIX + 1) * count, pair), f32)
        for part in range(2):
            head = which * 2 + part
            grad = jnp.where((side // HEAD_DIM) == part, grads, jnp.zeros_like(grads))
            through = jnp.dot(values, grad, preferred_element_type=f32)
            kinds = [through[c * count : (c + 1) * count] for c in range(PIX + 1)]
            soft = head_weights(pixels, key_ref, head)
            grad_soft = kinds[PIX]
            for c in range(PIX):
                grad_soft = grad_soft + pixels[c] * kinds[c]
            weighed = soft * grad_soft
            grad_scores = weighed - soft * jnp.sum(weighed, axis=0, keepdims=True)
            for c in range(PIX):
                field[c] = field[c] + soft * kinds[c] + grad_scores * key_ref[c, :, head : head + 1]
                keys[c] = jnp.where(lane == head, jnp.sum(grad_scores * pixels[c], axis=1, keepdims=True), keys[c])
            keys[PIX] = jnp.where(lane == head, jnp.sum(grad_scores, axis=1, keepdims=True), keys[PIX])
            total = total + lax.dot_general(weighted_pixels(soft, pixels), grad, NT, preferred_element_type=f32)
        put_tail(tail, total, span)
    for c in range(PIX):
        field_ref[c] = field[c].astype(bf16)
    width = value_ref.shape[1]
    put_tail(tail, jnp.concatenate(keys, axis=0), slice(width, width + pair))
    groups = len(ORDER)
    stride = tail.shape[0] // groups
    own, lines = width // groups, LEADS // groups
    for at, k in enumerate(ORDER):
        owner = member[0] ^ k
        start = (at + 1) * stride - FREE
        tail[start : start + FREE, :] = jnp.zeros((FREE, tail.shape[1]), f32)
        tail[start : start + 1, :width] = bias_ref[:, pl.ds(pl.multiple_of(owner * width, width), width)]
        chunk = pl.ds(pl.multiple_of(owner * own, own), own)
        tail[start + 1 : start + 2, :own] = gain2_ref[:, chunk]
        tail[start + 1 : start + 2, own : 2 * own] = gain1_ref[:, chunk]
        for line in range(lines):
            hit = bucket[0] == owner * lines + line
            tail[start + 2 + line : start + 3 + line, :width] = jnp.where(hit, sum_ref[...], 0.0)
    half = width // 2
    for ref, which in ((keep_ref, core[0]), (send_ref, 1 - core[0])):
        ref[:, :half] = tail[:, pl.ds(pl.multiple_of(which * half, half), half)].astype(bf16)
        ref[:, half:] = tail[:, width:].astype(bf16)


def aggregate_back(member, core, bucket, pixels, key_rows, values, grads, small, groups):
    count, seq = pixels.shape[1:]
    rows = seq // groups
    width = values.shape[1]
    deep = (PIX + 1) * count + FREE * groups
    wide = width // 2 + 2 * HEAD_DIM

    def whole(*shape):
        return pl.BlockSpec(shape, lambda i, *_: (0,) * len(shape))

    spec = pltpu.PrefetchScalarGridSpec(
        num_scalar_prefetch=3,
        grid=(1,),
        in_specs=[
            pl.BlockSpec((PIX, count, rows), lambda i, m, c, l: (0, 0, m[0])),
            whole(*key_rows.shape),
            whole(*values.shape),
            whole(*grads.shape),
            *[whole(*value.shape) for value in small],
        ],
        out_specs=[whole(PIX, count, rows), whole(deep, wide), whole(deep, wide)],
        scratch_shapes=[pltpu.VMEM((deep, width + 2 * HEAD_DIM), f32)],
    )
    return pl.pallas_call(
        aggregate_back_kernel,
        grid_spec=spec,
        out_shape=[
            jax.ShapeDtypeStruct((PIX, count, rows), bf16),
            jax.ShapeDtypeStruct((deep, wide), bf16),
            jax.ShapeDtypeStruct((deep, wide), bf16),
        ],
        cost_estimate=LIGHT,
        name="aggregate_back",
    )(member, core, bucket, pixels, key_rows, values, grads, *small)


def shape_of(*dims, kind=bf16):
    return jax.ShapeDtypeStruct(dims, kind)


def inner_kernel(
    member, core, mixed0, mixed1, mixed2, mixed3, wo_ref, resid_ref, gain_ref, w1_ref, b1_ref, ga_ref,
    act_ref, act_t_ref, send_ref, keep_ref, bias_ref, one_ref, hidden_ref, mixed_ref, hidden,
):
    j = pl.program_id(0)
    parts = (mixed0, mixed1, mixed2, mixed3)
    rows, own = mixed0.shape

    @pl.when(j == 0)
    def _():
        resid = resid_ref[...]
        for slot, part in enumerate(parts):
            owner = pl.ds(pl.multiple_of((member[0] ^ slot) * own, own), own)
            resid = resid + jnp.dot(part[...], wo_ref[owner, :], preferred_element_type=f32)
        one_ref[...] = resid
        centered = resid - jnp.mean(resid, axis=1, keepdims=True)
        scale = lax.rsqrt(jnp.mean(centered * centered, axis=1, keepdims=True) + epsilon)
        hidden[...] = (centered * scale * gain_ref[...]).astype(bf16)
        piece = own // 2
        for at, (slot, side) in enumerate(BLOCKS):
            start = pl.multiple_of((member[0] ^ slot) * own + side * piece, piece)
            hidden_ref[at * piece : (at + 1) * piece, :] = hidden[:, pl.ds(start, piece)].T
            mixed_ref[at * piece : (at + 1) * piece, :] = parts[slot][:, side * piece : (side + 1) * piece].T

    inner = jnp.dot(hidden[...], w1_ref[...], preferred_element_type=f32) + b1_ref[...]
    below = 0.5 + 0.5 * lax.erf(inner * 0.7071067811865476)
    act = (inner * below).astype(bf16)
    slope = below + inner * (jnp.exp(-0.5 * inner * inner) * 0.3989422804014327)
    gu = (slope * ga_ref[...].astype(f32)).astype(bf16)
    act_ref[...] = act
    act_t_ref[...] = act.T
    bias_ref[...] = jnp.sum(gu.astype(f32), axis=0, keepdims=True)

    @pl.when(j < len(parts))
    def _():
        send_ref[...] = gu

    @pl.when(j >= len(parts))
    def _():
        keep_ref[...] = gu


def inner_part(member, core, mixed, attn_out, resid, gain, mlp_in, bias, grad_act):
    rows, width = resid.shape
    inner = mlp_in.shape[1]
    groups = len(mixed)
    own = width // groups
    steps = 2 * groups
    block = inner // steps

    def natural(j, c):
        return ((j // groups) ^ (1 - c[0])) * groups + j % groups

    def spot(j, m, c):
        n = natural(j, c)
        slot = (n // 2) ^ m[0]
        return (jnp.where(n % 2 == 0, slot, 4 + (slot % 2) * 2 + slot // 2), 0)

    def whole(*shape):
        return pl.BlockSpec(shape, lambda j, m, c: (0,) * len(shape))

    def column(deep):
        return pl.BlockSpec((deep, block), lambda j, m, c: (0, natural(j, c)))

    spec = pltpu.PrefetchScalarGridSpec(
        num_scalar_prefetch=2,
        grid=(steps,),
        in_specs=[whole(rows, own)] * groups
        + [whole(width, width), whole(rows, width), whole(1, width)]
        + [column(width), column(1), column(rows)],
        out_specs=[
            column(rows),
            pl.BlockSpec((block, rows), spot),
            pl.BlockSpec((rows, block), lambda j, m, c: (0, jnp.minimum(j, groups - 1))),
            pl.BlockSpec((rows, block), lambda j, m, c: (0, jnp.maximum(j - groups, 0))),
            column(1),
            whole(rows, width),
            whole(width, rows),
            whole(width, rows),
        ],
        scratch_shapes=[pltpu.VMEM((rows, width), bf16)],
    )
    return pl.pallas_call(
        inner_kernel,
        grid_spec=spec,
        out_shape=[shape_of(rows, inner), shape_of(inner, rows)]
        + [shape_of(rows, inner // 2)] * 2
        + [shape_of(1, inner, kind=f32), shape_of(rows, width, kind=f32)]
        + [shape_of(width, rows)] * 2,
        cost_estimate=LIGHT,
        name="inner_part",
    )(member, core, *mixed, attn_out, resid, gain, mlp_in, bias, grad_act)


def outer_kernel(
    core, act_ref, send_ref, keep_ref, w1_ref, w2_ref, wo_ref, one_ref, gain_ref, g_ref,
    out_ref, gres_ref, gb_ref, gb_send_ref, gm_ref, ggain_ref, branch, grads,
):
    j = pl.program_id(0)
    groups, rows, own = gm_ref.shape
    half = send_ref.shape[1]
    branch[j] = jnp.dot(act_ref[...], w2_ref[...], preferred_element_type=f32)

    def columns(which):
        return w1_ref[:, pl.ds(pl.multiple_of(which * half, half), half)]

    grads[j] = lax.dot_general(
        send_ref[...], columns(1 - core[0]), NT, preferred_element_type=f32
    ) + lax.dot_general(keep_ref[...], columns(core[0]), NT, preferred_element_type=f32)

    @pl.when(j == pl.num_programs(0) - 1)
    def _():
        count = branch.shape[0]
        resid = one_ref[...]
        out_ref[...] = (resid + jnp.concatenate([branch[i] for i in range(count)], axis=1)).astype(bf16)
        centered = resid - jnp.mean(resid, axis=1, keepdims=True)
        scale = lax.rsqrt(jnp.mean(centered * centered, axis=1, keepdims=True) + epsilon)
        grad, plain = jnp.concatenate([grads[i] for i in range(count)], axis=1), centered * scale
        ggain_ref[...] = jnp.sum(grad * plain, axis=0, keepdims=True)
        grad = grad * gain_ref[...]
        first = jnp.mean(grad, axis=1, keepdims=True)
        second = jnp.mean(grad * plain, axis=1, keepdims=True)
        gres = g_ref[...].astype(f32) + scale * (grad - first - plain * second)
        gres_ref[...] = gres
        gb_ref[...] = gres.astype(bf16)
        width = gb_ref.shape[1]
        gb_send_ref[...] = gb_ref[:, pl.ds(pl.multiple_of((1 - core[0]) * (width // 2), width // 2), width // 2)]
        gb = gb_ref[...]
        for p in range(groups):
            gm_ref[p] = lax.dot_general(gb, wo_ref[p * own : (p + 1) * own, :], NT, preferred_element_type=f32).astype(
                bf16
            )


def outer_part(core, act, gu_send, gu_keep, mlp_in, mlp_out, attn_out, resid, gain, grad_out, groups):
    rows, width = resid.shape
    inner = mlp_in.shape[1]
    own = width // groups
    steps = 4
    block = width // steps

    def whole(*shape):
        return pl.BlockSpec(shape, lambda j, c: (0,) * len(shape))

    spec = pltpu.PrefetchScalarGridSpec(
        num_scalar_prefetch=1,
        grid=(steps,),
        in_specs=[
            whole(rows, inner),
            whole(rows, inner // 2),
            whole(rows, inner // 2),
            pl.BlockSpec((block, inner), lambda j, c: (j, 0)),
            pl.BlockSpec((inner, block), lambda j, c: (0, j)),
            whole(width, width),
            whole(rows, width),
            whole(1, width),
            whole(rows, width),
        ],
        out_specs=[
            whole(rows, width),
            whole(rows, width),
            whole(rows, width),
            whole(rows, width // 2),
            whole(groups, rows, own),
            whole(1, width),
        ],
        scratch_shapes=[pltpu.VMEM((steps, rows, block), f32), pltpu.VMEM((steps, rows, block), f32)],
    )
    return pl.pallas_call(
        outer_kernel,
        grid_spec=spec,
        out_shape=[
            shape_of(rows, width),
            shape_of(rows, width, kind=f32),
            shape_of(rows, width),
            shape_of(rows, width // 2),
            shape_of(groups, rows, own),
            shape_of(1, width, kind=f32),
        ],
        cost_estimate=LIGHT,
        name="outer_part",
    )(core, act, gu_send, gu_keep, mlp_in, mlp_out, attn_out, resid, gain, grad_out)


def both_dots(left, left_other, right, right_other):
    return jnp.dot(left[...], right[...], preferred_element_type=f32) + jnp.dot(
        left_other[...], right_other[...], preferred_element_type=f32
    )


def out_grad_kernel(core, left, left_other, right, right_other, *outs):
    total = both_dots(left, left_other, right, right_other).astype(bf16)
    for q, out in enumerate(outs):

        @pl.when(pl.program_id(0) == q)
        def _():
            out[...] = total


def out_grad(core, left, left_other, right, right_other):
    rows, deep = left.shape
    half = right.shape[1] // 2
    block = rows // 4

    spec = pltpu.PrefetchScalarGridSpec(
        num_scalar_prefetch=1,
        grid=(4,),
        in_specs=[pl.BlockSpec((block, deep), lambda i, c: (i, 0))] * 2
        + [
            pl.BlockSpec((deep, half), lambda i, c: (0, c[0])),
            pl.BlockSpec((deep, half), lambda i, c: (0, 0)),
        ],
        out_specs=[pl.BlockSpec((block, half), lambda i, c: (0, 0)) for q in range(4)],
    )
    return pl.pallas_call(
        out_grad_kernel,
        grid_spec=spec,
        out_shape=[shape_of(rows // 4, half)] * 4,
        cost_estimate=LIGHT,
        name="out_grad",
    )(core, left, left_other, right, right_other)


def in_grad_kernel(core, high, h, h_other, u, u_other, m, m_other, b, b_other, keep, send):
    units = u.shape[1]

    def put(out):
        out[:, :units] = both_dots(h, h_other, u, u_other).astype(bf16)
        out[:, units:] = both_dots(m, m_other, b, b_other).astype(bf16)

    @pl.when(pl.program_id(0) == 0)
    def _():
        put(send)

    @pl.when(pl.program_id(0) == 1)
    def _():
        put(keep)


def in_grad(core, high, h, h_other, u, u_other, m, m_other, b, b_other):
    rows, deep = h.shape
    units, branch = u.shape[1] // 2, b_other.shape[1] // 2

    def whole(*shape):
        return pl.BlockSpec(shape, lambda i, c, z: (0,) * len(shape))

    def side(i, c, z):
        return (0, z[0] ^ (1 - i))

    def core_side(i, c, z):
        return (0, 2 * c[0] + (z[0] ^ (1 - i)))

    spec = pltpu.PrefetchScalarGridSpec(
        num_scalar_prefetch=2,
        grid=(2,),
        in_specs=[
            whole(rows, deep),
            whole(rows, deep),
            pl.BlockSpec((deep, units), side),
            pl.BlockSpec((deep, units), side),
            whole(rows, deep),
            whole(rows, deep),
            pl.BlockSpec((deep, branch), core_side),
            pl.BlockSpec((deep, branch), side),
        ],
        out_specs=[whole(rows, units + branch)] * 2,
    )
    return pl.pallas_call(
        in_grad_kernel,
        grid_spec=spec,
        out_shape=[shape_of(rows, units + branch)] * 2,
        cost_estimate=LIGHT,
        name="in_grad",
    )(core, high, h, h_other, u, u_other, m, m_other, b, b_other)


def qkv_grad_kernel(core, h, h_other, *refs):
    out = refs[-1]
    for which in range(2):

        @pl.when(core[0] == which)
        def _():
            out[...] = both_dots(h, h_other, refs[which], refs[2 + which]).astype(bf16)


def qkv_grad(core, h, h_other, grads, others):
    rows, deep = h.shape
    cols = grads[0].shape[1]
    block = rows // 2
    spec = pltpu.PrefetchScalarGridSpec(
        num_scalar_prefetch=1,
        grid=(2,),
        in_specs=[pl.BlockSpec((block, deep), lambda i, c: (i, 0))] * 2
        + [pl.BlockSpec((deep, cols), lambda i, c: (0, 0))] * 4,
        out_specs=pl.BlockSpec((block, cols), lambda i, c: (i, 0)),
    )
    return pl.pallas_call(
        qkv_grad_kernel,
        grid_spec=spec,
        out_shape=shape_of(rows, cols),
        cost_estimate=LIGHT,
        name="qkv_grad",
    )(core, h, h_other, *grads, *others)


def last_grad_kernel(core, qkv_ref, a, a_other, g, g_other, out):
    cols = qkv_ref.shape[1]
    out[0, :, :cols] = qkv_ref[...]
    out[0, :, cols:] = both_dots(a, a_other, g, g_other).astype(bf16)


def last_grad(core, weight_qkv, att, att_other, grad, grad_other, groups):
    rows, deep = att.shape
    half = grad_other.shape[1]
    cols = weight_qkv.shape[1]
    block = rows // groups
    spec = pltpu.PrefetchScalarGridSpec(
        num_scalar_prefetch=1,
        grid=(groups,),
        in_specs=[
            pl.BlockSpec((block, cols), lambda i, c: (i, 0)),
            pl.BlockSpec((block, deep), lambda i, c: (i, 0)),
            pl.BlockSpec((block, deep), lambda i, c: (i, 0)),
            pl.BlockSpec((deep, half), lambda i, c: (0, c[0])),
            pl.BlockSpec((deep, half), lambda i, c: (0, 0)),
        ],
        out_specs=pl.BlockSpec((1, block, cols + half), lambda i, c: (i, 0, 0)),
    )
    return pl.pallas_call(
        last_grad_kernel,
        grid_spec=spec,
        out_shape=shape_of(groups, block, cols + half),
        cost_estimate=LIGHT,
        name="last_grad",
    )(core, weight_qkv, att, att_other, grad, grad_other)


def join_kernel(core, first_ref, second_ref, wq, wk, wv, resid_ref, gain_ref, gres_ref, out_ref, *refs):
    ga_ref, ga_send_ref, gatt_ref, ggain_ref, sum_ref, total = refs
    i = pl.program_id(0)
    pair = 2 * HEAD_DIM

    @pl.when(i == 0)
    def _():
        total[...] = jnp.zeros_like(total)

    grad = total[...]
    for t, weight in enumerate((wq, wk, wv)):
        span = slice(t * pair, (t + 1) * pair)
        left = jnp.concatenate([first_ref[:, span], second_ref[:, span]], axis=1)
        grad = grad + lax.dot_general(left, weight[...], NT, preferred_element_type=f32)
    total[...] = grad

    @pl.when(i == pl.num_programs(0) - 1)
    def _():
        resid = resid_ref[...]
        centered = resid - jnp.mean(resid, axis=1, keepdims=True)
        scale = lax.rsqrt(jnp.mean(centered * centered, axis=1, keepdims=True) + epsilon)
        plain = centered * scale
        grad = total[...]
        ggain_ref[...] = jnp.sum(grad * plain, axis=0, keepdims=True)
        grad = grad * gain_ref[...]
        first = jnp.mean(grad, axis=1, keepdims=True)
        second = jnp.mean(grad * plain, axis=1, keepdims=True)
        gres = gres_ref[...] + scale * (grad - first - plain * second)
        sum_ref[...] = jnp.sum(gres, axis=0, keepdims=True)
        ga = gres.astype(bf16)
        ga_ref[...] = ga
        half = ga_send_ref.shape[1]
        ga_send_ref[...] = ga_ref[:, pl.ds(pl.multiple_of((1 - core[0]) * half, half), half)]
        gatt_ref[...] = lax.dot_general(out_ref[...], ga, NT, preferred_element_type=f32).astype(bf16)


def join(core, first, second, attn_qkv, resid, gain, gres, agg_out):
    rows, width = resid.shape
    groups = first.shape[0] // rows
    own = width // groups
    cols = first.shape[1]

    def whole(*shape):
        return pl.BlockSpec(shape, lambda i, c: (0,) * len(shape))

    spec = pltpu.PrefetchScalarGridSpec(
        num_scalar_prefetch=1,
        grid=(groups,),
        in_specs=[
            pl.BlockSpec((rows, cols), lambda i, c: (i, 0)),
            pl.BlockSpec((rows, cols), lambda i, c: (i, 0)),
            pl.BlockSpec((width, own), lambda i, c: (0, i)),
            pl.BlockSpec((width, own), lambda i, c: (0, groups + i)),
            pl.BlockSpec((width, own), lambda i, c: (0, 2 * groups + i)),
            whole(rows, width),
            whole(1, width),
            whole(rows, width),
            whole(width, width),
        ],
        out_specs=[
            whole(rows, width),
            whole(rows, width // 2),
            whole(width, rows),
            whole(1, width),
            whole(1, width),
        ],
        scratch_shapes=[pltpu.VMEM((rows, width), f32)],
    )
    return pl.pallas_call(
        join_kernel,
        grid_spec=spec,
        out_shape=[
            shape_of(rows, width),
            shape_of(rows, width // 2),
            shape_of(width, rows),
            shape_of(1, width, kind=f32),
            shape_of(1, width, kind=f32),
        ],
        cost_estimate=LIGHT,
        name="join",
    )(core, first, second, attn_qkv, attn_qkv, attn_qkv, resid, gain, gres, agg_out)


def add(a, b):
    return (a.astype(f32) + b.astype(f32)).astype(bf16)


def split_add(a, b, count):
    deep = a.shape[0] // count
    return [add(a[i * deep : (i + 1) * deep], b[i * deep : (i + 1) * deep]) for i in range(count)]


def pick_add(a, b, which, axis):
    half = a.shape[axis] // 2
    return add(
        lax.dynamic_slice_in_dim(a, which * half, half, axis), lax.dynamic_slice_in_dim(b, which * half, half, axis)
    )


def choose(high, a, b, c, d):
    first, second = high == 0, high != 0
    keep = add(jnp.where(first, a, c), jnp.where(first, b, d))
    send = add(jnp.where(second, a, c), jnp.where(second, b, d))
    return keep, send


def whole_blocks(shapes):
    return [pl.BlockSpec(shape, lambda i, *_, n=len(shape): (0,) * n) for shape in shapes]


def gather_sources_kernel(high, came_ref, keep, send, *, cols):
    groups, half = came_ref.shape[0], keep.shape[0]
    for out, which in ((keep, high[0]), (send, 1 - high[0])):
        span = pl.ds(pl.multiple_of(which * half, half), half)
        total = jnp.zeros((half, came_ref.shape[2] - cols), f32)
        for p in range(groups):
            out[:, p * cols : (p + 1) * cols] = came_ref[p, span, :cols]
            total = total + came_ref[p, span, cols:].astype(f32)
        out[:, groups * cols :] = total.astype(bf16)


def gather_sources(high, came, cols):
    groups, rows, wide = came.shape
    shape = (rows // 2, groups * cols + wide - cols)
    spec = pltpu.PrefetchScalarGridSpec(
        num_scalar_prefetch=1, grid=(1,), in_specs=whole_blocks([came.shape]), out_specs=whole_blocks([shape] * 2)
    )
    return pl.pallas_call(
        partial(gather_sources_kernel, cols=cols),
        grid_spec=spec,
        out_shape=[jax.ShapeDtypeStruct(shape, bf16)] * 2,
        cost_estimate=LIGHT,
        name="gather_sources",
    )(high, came)


def turned(i, levels):
    total = 0
    for k in range(levels):
        total = total + (((i >> k) & 1) << (levels - 1 - k))
    return total


def place_out_kernel(first, second, out):
    half = first.shape[2]
    out[:, :half] = first[0].astype(f32)
    out[:, half:] = second[0].astype(f32)


def place_out(pieces, levels):
    _, rows, cols = pieces.shape
    chips = 2**levels
    return pl.pallas_call(
        place_out_kernel,
        grid=(chips,),
        in_specs=[
            pl.BlockSpec((1, rows, cols), lambda i, c=c: (2 * turned(i, levels) + c, 0, 0)) for c in range(2)
        ],
        out_specs=pl.BlockSpec((rows, 2 * cols), lambda i: (i, 0)),
        out_shape=shape_of(chips * rows, 2 * cols, kind=f32),
        cost_estimate=LIGHT,
        name="place_out",
    )(pieces, pieces)


def place_in_kernel(*refs, units):
    pieces, inner, branch = refs[:4], refs[4], refs[5]
    size = pieces[0].shape[2] - units
    for number, piece in enumerate(pieces):
        inner[:, number * units : (number + 1) * units] = piece[0, :, :units].astype(f32)
        branch[:, number * size : (number + 1) * size] = piece[0, :, units:].astype(f32)


def place_in(pieces, levels, units):
    _, rows, cols = pieces.shape
    blocks = 2 ** (levels - 1)

    def at(i, c, b):
        return (2 * (2 * turned(i, levels - 1) + b) + c, 0, 0)

    return pl.pallas_call(
        partial(place_in_kernel, units=units),
        grid=(blocks,),
        in_specs=[
            pl.BlockSpec((1, rows, cols), lambda i, c=c, b=b: at(i, c, b)) for c in range(2) for b in range(2)
        ],
        out_specs=[
            pl.BlockSpec((rows, 4 * units), lambda i: (i, 0)),
            pl.BlockSpec((rows, 4 * (cols - units)), lambda i: (i, 0)),
        ],
        out_shape=[
            shape_of(blocks * rows, 4 * units, kind=f32),
            shape_of(blocks * rows, 4 * (cols - units), kind=f32),
        ],
        cost_estimate=LIGHT,
        name="place_in",
    )(pieces, pieces, pieces, pieces)


def place_last_kernel(first, second, qkv, agg, *, groups):
    pair = 2 * HEAD_DIM
    half = agg.shape[1] // 2
    for c, piece in enumerate((first, second)):
        for p in range(groups):
            for t in range(3):
                source, target = (3 * p + t) * pair, ((t * groups + p) * 2 + c) * pair
                qkv[:, target : target + pair] = piece[0, :, source : source + pair].astype(f32)
        agg[:, c * half : (c + 1) * half] = piece[0, :, 3 * groups * pair :].astype(f32)


def place_last(pieces, levels, groups):
    _, rows, cols = pieces.shape
    chips = 2**levels
    wide = 6 * groups * HEAD_DIM
    return pl.pallas_call(
        partial(place_last_kernel, groups=groups),
        grid=(chips,),
        in_specs=[
            pl.BlockSpec((1, rows, cols), lambda i, c=c: (2 * turned(i, levels) + c, 0, 0)) for c in range(2)
        ],
        out_specs=[
            pl.BlockSpec((rows, 2 * wide), lambda i: (i, 0)),
            pl.BlockSpec((rows, 2 * (cols - wide)), lambda i: (i, 0)),
        ],
        out_shape=[
            shape_of(chips * rows, 2 * wide, kind=f32),
            shape_of(chips * rows, 2 * (cols - wide), kind=f32),
        ],
        cost_estimate=LIGHT,
        name="place_last",
    )(pieces, pieces)


def field_kernel(member, *refs):
    pieces, out = refs[:-1], refs[-1]
    kinds, channels, rows = pieces[0].shape
    for k, piece in enumerate(pieces):
        at = pl.ds(pl.multiple_of((member[0] ^ k) * rows, rows), rows)
        for c in range(kinds):
            out[:, c, at] = piece[c].astype(f32)


def place_field(member, pieces):
    kinds, channels, rows = pieces[0].shape
    shape = (channels, kinds, rows * len(pieces))
    spec = pltpu.PrefetchScalarGridSpec(
        num_scalar_prefetch=1,
        grid=(1,),
        in_specs=whole_blocks([p.shape for p in pieces]),
        out_specs=whole_blocks([shape])[0],
    )
    return pl.pallas_call(
        field_kernel, grid_spec=spec, out_shape=jax.ShapeDtypeStruct(shape, f32), name="place_field"
    )(member, *pieces)


def tail_kernel(member, *refs, groups):
    tails = refs[:groups]
    stacked_ref, pick_ref, value_ref, qk_ref, key_ref, query_ref = refs[groups : groups + 6]
    gvalue_ref, gkey_ref, gquery_ref, rows_ref, gqk = refs[groups + 6 :]
    width = value_ref.shape[0]
    own = gvalue_ref.shape[0]
    at = pl.ds(pl.multiple_of(member[0] * own, own), own)
    tail = jnp.concatenate([t[...] for t in tails], axis=0)
    values, keys = tail[:, :width], tail[:, width:]
    gvalue_ref[...] = lax.dot_general(stacked_ref[:, at], values, TN, preferred_element_type=f32)
    gqk[...] = lax.dot_general(stacked_ref[...], keys, TN, preferred_element_type=f32)
    head = lax.broadcasted_iota(jnp.int32, (keys.shape[1], width), 0)
    column = lax.broadcasted_iota(jnp.int32, (keys.shape[1], width), 1) // HEAD_DIM
    spread = jnp.where(head == column, 1.0, 0.0)
    gkey_ref[...] = (
        jnp.dot(gqk[at, :], spread, precision=highest, preferred_element_type=f32) * (query_ref[...] * 0.125)
    )
    by_head = lax.dot_general(gqk[...], key_ref[...].astype(f32), TN, precision=highest, preferred_element_type=f32)
    head = lax.broadcasted_iota(jnp.int32, by_head.shape, 0)
    column = (lax.broadcasted_iota(jnp.int32, by_head.shape, 1) + member[0] * own) // HEAD_DIM
    gquery_ref[...] = jnp.sum(jnp.where(head == column, by_head, 0.0), axis=0, keepdims=True) * 0.125
    own_rows = tails[0].shape[0]
    table = jnp.dot(pick_ref[...], tail, preferred_element_type=f32).astype(bf16)
    rows = jnp.concatenate([tail[:own_rows], table], axis=0)
    rows_ref[...] = lax.dot_general(rows[:, :width], value_ref[...], NT, preferred_element_type=f32) + lax.dot_general(
        rows[:, width:].astype(f32), qk_ref[...], NT, precision=highest, preferred_element_type=f32
    )


def finish_tail(member, tails, stacked, pick, agg_value, query_keys, agg_key, agg_query):
    groups = len(tails)
    width = agg_value.shape[0]
    own = width // groups
    deep = tails[0].shape[0] + pick.shape[0]
    args = [*tails, stacked, pick, agg_value, query_keys]
    spec = pltpu.PrefetchScalarGridSpec(
        num_scalar_prefetch=1,
        grid=(1,),
        in_specs=whole_blocks([x.shape for x in args])
        + [pl.BlockSpec((width, own), lambda i, m: (0, m[0])), pl.BlockSpec((1, width), lambda i, m: (0, 0))],
        out_specs=whole_blocks([(own, width), (own, width), (1, own), (deep, width)]),
        scratch_shapes=[pltpu.VMEM((width, query_keys.shape[1]), f32)],
    )
    return pl.pallas_call(
        partial(tail_kernel, groups=groups),
        grid_spec=spec,
        out_shape=[
            jax.ShapeDtypeStruct((own, width), f32),
            jax.ShapeDtypeStruct((own, width), f32),
            jax.ShapeDtypeStruct((1, own), f32),
            jax.ShapeDtypeStruct((deep, width), f32),
        ],
        cost_estimate=LIGHT,
        name="finish_tail",
    )(member, *args, agg_key, agg_query)


def fence(*values):
    return lax.optimization_barrier(values)


def swap(value, axis, bits):
    size = lax.axis_size(axis)
    return lax.ppermute(value, axis, [(i, i ^ bits) for i in range(size)])


def from_all(own, groups):
    return [own] + [swap(own, "var", k) for k in range(1, groups)]


def exchange(value):
    return lax.all_to_all(value, "var", split_axis=0, concat_axis=0, tiled=True)


def chip_bits():
    bits, bit = [], 1
    while bit < lax.axis_size("chip"):
        bits.append(bit)
        bit *= 2
    return bits


def is_high(bit):
    return (lax.axis_index("chip") // bit) % 2


def by_core(mine, other, core):
    return jnp.where(core == 0, mine, other), jnp.where(core == 0, other, mine)


def body(
    field_patches,
    var_ids,
    lead_bucket,
    patch_weight,
    var_embed,
    agg_query,
    agg_key,
    agg_value,
    agg_out,
    lead_table,
    ln1_gain,
    attn_qkv,
    attn_out,
    ln2_gain,
    mlp_in,
    mlp_in_bias,
    mlp_out,
    cotangent,
):
    groups = lax.axis_size("var")
    member = lax.axis_index("var")
    core = lax.axis_index("core")
    channels, pixel_count, samples, seq = field_patches.shape
    width = agg_key.shape[0]
    inner_width = mlp_in.shape[1]
    leads = lead_table.shape[0]
    vocab = var_embed.shape[0]
    rows = seq // groups
    own = width // groups
    count = channels * groups
    slots = [member ^ k for k in range(groups)]
    member_one = member.reshape(1).astype(jnp.int32)
    core_one = core.reshape(1).astype(jnp.int32)
    bits = chip_bits()
    assert bits
    high = is_high(bits[0])
    high_one = high.reshape(1).astype(jnp.int32)
    half = width // 2
    gain_one = ln1_gain.astype(f32)
    gain_two = ln2_gain.astype(f32)

    mine = jnp.concatenate(
        [
            field_patches.reshape(channels, pixel_count, seq).transpose(1, 0, 2),
            patch_weight.transpose(1, 0, 2),
        ],
        axis=2,
    )
    grad_out = cotangent.reshape(rows, width)
    grad_act = lax.dot_general(grad_out, mlp_out, NT, preferred_element_type=f32).astype(bf16)
    ids = jnp.concatenate([lax.dynamic_slice_in_dim(var_ids, slot * channels, channels) for slot in slots])
    table_pick = (ids[:, None] == jnp.arange(vocab, dtype=jnp.int32)[None, :]).astype(bf16)
    embeds = jnp.dot(table_pick, var_embed, preferred_element_type=f32)
    head_of = jnp.arange(width, dtype=jnp.int32) // HEAD_DIM
    spread = head_of[:, None] == jnp.arange(2 * HEAD_DIM, dtype=jnp.int32)[None, :]
    query_block = jnp.where(spread, agg_query[:, None], jnp.zeros((), bf16))
    query_keys = jnp.dot(agg_key, query_block, preferred_element_type=f32) * 0.125
    lead_row = lax.dynamic_slice_in_dim(lead_table, lead_bucket[0], 1).astype(f32)
    grad_out_other = swap(lax.dynamic_slice_in_dim(grad_out, (1 - core) * half, half, axis=1), "core", 1)
    arrived, grad_act, embeds, query_keys, lead_row, grad_out_other = fence(
        from_all(mine, groups), grad_act, embeds, query_keys, lead_row, grad_out_other
    )
    pixels, key_rows, values, values_t, by_slot = prepare(arrived, embeds, query_keys, agg_value, seq)

    hidden_t, qkv, resid_zero, att_low = front(
        member_one, pixels, key_rows, values_t, agg_out, lead_row, gain_one[None], attn_qkv, groups
    )

    hidden_t, att_low, qkv = fence(hidden_t, att_low, qkv)
    hidden_other, att_other = swap(hidden_t, "core", 1), swap(att_low, "core", 1)

    block = min(256, rows)
    mixed_parts, lse_parts, received = [None] * groups, [None] * groups, [None] * groups
    for k in reversed(range(groups)):
        mixed_parts[k], lse_parts[k] = attend(member_one, qkv, k, rows, block)
        if k + 1 < groups:
            received[k + 1], mixed_parts[k], qkv = fence(received[k + 1], mixed_parts[k], qkv)
            if k + 2 == groups:
                hidden_other, att_other, qkv = fence(hidden_other, att_other, qkv)
        received[k] = swap(mixed_parts[k], "var", k) if k else mixed_parts[k]

    act, act_t, gu_send, gu_keep, grad_bias, resid_one, hidden_two_t, mixed_t = inner_part(
        member_one, core_one, received, attn_out, resid_zero, gain_two[None], mlp_in, mlp_in_bias.astype(f32)[None], grad_act
    )
    gu_send, act_t, act, hidden_two_t, mixed_t = fence(gu_send, act_t, act, hidden_two_t, mixed_t)
    act_other, gu_other, hidden_two_other, mixed_other = (
        swap(value, "core", 1) for value in (act_t, gu_send, hidden_two_t, mixed_t)
    )
    output, grad_resid_one, grad_branch, branch_send, grad_mixed, grad_gain_two = outer_part(
        core_one, act, gu_send, gu_keep, mlp_in, mlp_out, attn_out, resid_one, gain_two[None], grad_out, groups
    )
    act_other, gu_other, hidden_two_other, mixed_other, grad_mixed, branch_send, output = fence(
        act_other, gu_other, hidden_two_other, mixed_other, grad_mixed, branch_send, output
    )
    output = output.reshape(samples, rows, width)

    branch_other = swap(branch_send, "core", 1)
    grad_heads = exchange(grad_mixed).reshape(seq, own)
    out_y, out_y_send, out_x, out_x_send = out_grad(core_one, act_t, act_other, grad_out, grad_out_other)
    grad_heads, branch_other, out_y, out_y_send, out_x, out_x_send = fence(
        grad_heads, branch_other, out_y, out_y_send, out_x, out_x_send
    )
    out_y_came, out_x_came = swap(out_y_send, "var", 2), swap(out_x_send, "var", 1)
    in_part, in_part_send = in_grad(
        core_one,
        high_one,
        hidden_two_t,
        hidden_two_other,
        gu_keep,
        gu_other,
        mixed_t,
        mixed_other,
        grad_branch,
        branch_other,
    )
    grad_heads, in_part_send, in_part = fence(grad_heads, in_part_send, in_part)

    pair = 2 * HEAD_DIM
    pairs = own // pair
    assert pairs == 2
    in_part_came = swap(in_part_send, "chip", bits[0])
    first = attend_back(member_one, qkv, grad_heads, mixed_parts, lse_parts, 0, 512)
    first, qkv, out_y_came, out_x_came = fence(first, qkv, out_y_came, out_x_came)
    out_y, out_y_send = split_add(out_y, out_y_came, 2)
    out_x, out_x_send = split_add(out_x, out_x_came, 2)
    first, qkv, out_y_send, out_x_send = fence(first, qkv, out_y_send, out_x_send)
    first_came = exchange(first)
    first_other = swap(first, "core", 1)
    out_y_came, out_x_came = swap(out_y_send, "var", 1), swap(out_x_send, "var", 2)
    second = attend_back(member_one, qkv, grad_heads, mixed_parts, lse_parts, 1, 512)
    second_came = exchange(second)
    first_came, first_other, second, in_part_came, out_y_came, out_x_came = fence(
        first_came, first_other, second, in_part_came, out_y_came, out_x_came
    )
    second_other = swap(second, "core", 1)
    out_keep, out_send = choose(high, out_y, out_y_came, out_x, out_x_came)
    out_came = swap(out_send, "chip", bits[0])
    in_y, in_y_send, in_x, in_x_send = split_add(in_part, in_part_came, 4)
    second_other, in_y_send, in_x_send = fence(second_other, in_y_send, in_x_send)
    weight_qkv = qkv_grad(core_one, hidden_t, hidden_other, (first, second), (first_other, second_other))
    second_came, weight_qkv, in_y_send, in_x_send, grad_resid_one, out_came = fence(
        second_came, weight_qkv, in_y_send, in_x_send, grad_resid_one, out_came
    )
    everyone = ("chip", "core")
    rest = bits[1:]

    def scatter_parts(keep, came, bit):
        return [pick_add(keep, came, which, 0) for which in (is_high(bit), 1 - is_high(bit))]

    def scatter_step(keep, came, bit):
        keep, send = scatter_parts(keep, came, bit)
        return keep, swap(send, "chip", bit)

    out_keep, out_send = scatter_parts(out_keep, out_came, rest[0])
    second_came, out_send, in_y_send, in_x_send = fence(second_came, out_send, in_y_send, in_x_send)
    out_came = swap(out_send, "chip", rest[0])
    in_y_came, in_x_came = swap(in_y_send, "var", 2), swap(in_x_send, "var", 1)
    grad_agg, grad_agg_send, grad_att, grad_gain_one, sample_sum = join(
        core_one, first_came, second_came, attn_qkv, resid_zero, gain_one[None], grad_resid_one, agg_out
    )
    grad_agg, grad_agg_send, grad_att, out_came, in_y_came, in_x_came = fence(
        grad_agg, grad_agg_send, grad_att, out_came, in_y_came, in_x_came
    )
    for bit in rest[1:]:
        out_keep, out_came = scatter_step(out_keep, out_came, bit)
    out_all = lax.all_gather(add(out_keep, out_came), everyone)
    in_y, in_y_send = split_add(in_y, in_y_came, 2)
    in_x, in_x_send = split_add(in_x, in_x_came, 2)
    grad_att, grad_agg_send, in_y_send, in_x_send = fence(grad_att, grad_agg_send, in_y_send, in_x_send)
    grad_agg_other = swap(grad_agg_send, "core", 1)
    in_y_came, in_x_came = swap(in_y_send, "var", 1), swap(in_x_send, "var", 2)

    field_own, tail, tail_send = aggregate_back(
        member_one,
        core_one,
        lead_bucket,
        pixels,
        key_rows,
        values,
        grad_att,
        (grad_bias, grad_gain_two, grad_gain_one, sample_sum),
        groups,
    )
    tail, tail_send, grad_agg_other, in_y_came, in_x_came = fence(
        tail, tail_send, grad_agg_other, in_y_came, in_x_came
    )
    tail_came = swap(tail_send, "core", 1)
    in_own = jnp.concatenate([add(in_y, in_y_came), add(in_x, in_x_came)], axis=0)
    for bit in rest:
        in_rows = in_own.shape[0] // 2
        in_own, in_send = (
            lax.dynamic_slice_in_dim(in_own, which * in_rows, in_rows) for which in (is_high(bit), 1 - is_high(bit))
        )
        if bit != rest[-1]:
            in_own = add(in_own, swap(in_send, "chip", bit))
    in_send, grad_agg_other, tail_came = fence(in_send, grad_agg_other, tail_came)
    in_came = swap(in_send, "chip", rest[-1])
    last_send = last_grad(core_one, weight_qkv, att_low, att_other, grad_agg, grad_agg_other, groups)
    tail = add(tail, tail_came)
    deep = tail.shape[0] // 2
    tail_came = swap(tail[deep:], "var", 1)
    tail, tail_came, last_send = fence(tail, tail_came, last_send)
    tail = add(tail[:deep], tail_came)
    deep //= 2
    tail_came = swap(tail[deep:], "var", 2)
    tail, tail_came, last_send = fence(tail, tail_came, last_send)
    last_came = exchange(last_send)
    tail = add(tail[:deep], tail_came)
    tail_came = swap(tail, "chip", bits[0])
    tail, tail_came = fence(tail, tail_came)
    tail = add(tail, tail_came)
    for bit in rest:
        tail_came = swap(tail, "chip", bit)
        if bit != rest[-1]:
            tail = add(tail, tail_came)
    tail, tail_came, in_came, last_came = fence(tail, tail_came, in_came, last_came)
    last_keep, last_send = gather_sources(high_one, last_came, 3 * pair)
    tail = add(tail, tail_came)
    in_own = add(in_own, in_came)
    tail, last_send, in_own = fence(tail, last_send, in_own)
    last_came = swap(last_send, "chip", bits[0])
    tail_came = swap(tail, "core", 1)
    in_all = lax.all_gather(in_own, everyone)
    sum_mlp_out = place_out(out_all, len(bits))
    tail, tail_came, last_came, sum_mlp_out = fence(tail, tail_came, last_came, sum_mlp_out)
    for bit in rest[:-1]:
        last_keep, last_came = scatter_step(last_keep, last_came, bit)
    last_keep, last_send = scatter_parts(last_keep, last_came, rest[-1])
    low, up = by_core(tail, tail_came, core)
    tail = jnp.concatenate([low[:, :half], up], axis=1)
    tail, last_send = fence(tail, last_send)
    last_came = swap(last_send, "chip", rest[-1])
    tails = from_all(tail, groups)
    tails, last_came = fence(tails, last_came)
    last_all = lax.all_gather(add(last_keep, last_came), everyone)
    field_slots = field_own.reshape(pixel_count, groups, channels, rows)
    field_parts = [swap(field_slots[:, k], "var", k) if k else field_slots[:, 0] for k in range(groups)]
    stride = tail.shape[0]
    per_slot = (PIX + 1) * channels
    small_sum = tail[per_slot:, :width].astype(f32)
    part_size = inner_width // groups
    sum_bias = small_sum[0]
    sum_gain_two = small_sum[1, :own]
    sum_gain_one = small_sum[1, own : 2 * own]
    sum_lead = small_sum[2 : 2 + leads // groups]

    own_ids = member * (vocab // groups) + jnp.arange(16, dtype=jnp.int32)
    own_pick = jnp.where(jnp.arange(16)[:, None] < vocab // groups, own_ids[:, None] == ids[None, :], False)
    own_pick = jnp.pad(
        own_pick.reshape(16, groups, channels), ((0, 0), (0, 0), (PIX * channels, stride - per_slot))
    ).reshape(16, groups * stride)
    sum_value, sum_key, sum_query, sum_rows = finish_tail(
        member_one,
        tails,
        by_slot,
        own_pick.astype(bf16),
        agg_value,
        query_keys,
        agg_key,
        agg_query.astype(f32)[None],
    )
    sum_query = sum_query.reshape(own)
    sum_patch = sum_rows[: PIX * channels].reshape(pixel_count, channels, width).transpose(1, 0, 2)
    sum_table = sum_rows[stride : stride + vocab // groups]
    field_grad = place_field(member_one, field_parts).reshape(channels, pixel_count, samples, seq)

    levels = len(bits)
    sum_mlp_in, sum_attn_out = place_in(in_all, levels, inner_width // 4)
    sum_qkv, sum_agg_out = place_last(last_all, levels, groups)
    return (
        output,
        field_grad,
        sum_patch,
        sum_table,
        sum_query,
        sum_key,
        sum_value,
        sum_agg_out,
        sum_lead,
        sum_gain_one,
        sum_qkv,
        sum_attn_out,
        sum_gain_two,
        sum_mlp_in,
        sum_bias,
        sum_mlp_out,
    )


def solution(mesh):
    members, patches = mesh.shape["var"], mesh.shape["patch"]
    chips = Mesh(mesh.devices.reshape(members, patches // 2, 2), ("var", "chip", "core"))
    patch = ("chip", "core")
    placed = (
        P("var", None, patch, None),
        P(),
        P(patch),
        P("var", None, None),
        *[P()] * 13,
        P(patch, "var", None),
    )
    return jax.shard_map(
        body,
        mesh=chips,
        in_specs=placed,
        out_specs=(
            P(patch, "var", None),
            P("var", None, patch, None),
            P("var", None, None),
            P("var", None),
            P("var"),
            P("var", None),
            P("var", None),
            P("var", None),
            P("var", None),
            P("var"),
            P("var", None),
            P("var", None),
            P("var"),
            P("var", None),
            P("var"),
            P("var", None),
        ),
        check_vma=False,
    )
```

```python
from functools import partial

import jax
import jax.numpy as jnp
from jax import lax
from jax.experimental import pallas as pl
from jax.experimental.pallas import tpu as pltpu
from jax.sharding import Mesh
from jax.sharding import PartitionSpec as P

HEADS = 16
PIX = 4
HEAD_DIM = 64
LEADS = 8
FREE = 4
ORDER = (0, 2, 1, 3)
BLOCKS = tuple((k, 0) for k in range(4)) + tuple((k, 1) for k in ORDER)

f32, bf16 = jnp.float32, jnp.bfloat16
highest = lax.Precision.HIGHEST
epsilon = 1e-05
NT = (((1,), (1,)), ((), ()))
LIGHT = pl.CostEstimate(flops=1, bytes_accessed=1, transcendentals=0)
TN = (((0,), (0,)), ((), ()))


def head_weights(pixels, key_ref, head):
    scores = key_ref[PIX, :, head : head + 1]
    for c in range(PIX):
        scores = scores + pixels[c] * key_ref[c, :, head : head + 1]
    soft = jnp.exp(scores - jnp.max(scores, axis=0, keepdims=True))
    return soft * (1.0 / jnp.sum(soft, axis=0, keepdims=True))


def slot_spans(member, own):
    return [pl.ds(pl.multiple_of((member[0] ^ k) * own, own), own) for k in ORDER]


def weighted_pixels(soft, pixels):
    return jnp.concatenate(
        [(soft * pixels[c]).astype(bf16) for c in range(PIX)] + [soft.astype(bf16)], axis=0
    )


def prepare_kernel(*refs, groups):
    blocks = refs[:groups]
    embed_ref, query_ref, weight_ref, pixel_ref, key_ref, value_ref, value_t_ref, slot_ref, stacked, by_slot = refs[groups:]
    channels = blocks[0].shape[1]
    seq = pixel_ref.shape[2]
    count = channels * groups
    stride = by_slot.shape[0] // groups
    by_slot[...] = jnp.zeros_like(by_slot)
    for k, block in enumerate(blocks):
        for c in range(PIX + 1):
            if c < PIX:
                pixel_ref[c, k * channels : (k + 1) * channels, :] = block[c, :, :seq].astype(f32)
                rows = block[c, :, seq:].astype(f32)
            else:
                rows = embed_ref[k * channels : (k + 1) * channels, :]
            stacked[c * count + k * channels : c * count + (k + 1) * channels, :] = rows
            by_slot[k * stride + c * channels : k * stride + (c + 1) * channels, :] = rows
    slot_ref[...] = by_slot[...].astype(bf16)
    keys = jnp.dot(stacked[...], query_ref[...], precision=highest, preferred_element_type=f32)
    for c in range(PIX + 1):
        key_ref[c] = keys[c * count : (c + 1) * count]
    values = jnp.dot(stacked[...].astype(bf16), weight_ref[...], preferred_element_type=f32).astype(bf16)
    value_ref[...] = values
    value_t_ref[...] = values.T


def prepare(blocks, embeds, query_keys, agg_value, seq):
    groups = len(blocks)
    channels = blocks[0].shape[1]
    count = channels * groups
    width = agg_value.shape[0]
    rows = (PIX + 1) * count
    deep = rows + FREE * groups
    return pl.pallas_call(
        partial(prepare_kernel, groups=groups),
        out_shape=[
            jax.ShapeDtypeStruct((PIX, count, seq), f32),
            jax.ShapeDtypeStruct((PIX + 1, count, query_keys.shape[1]), f32),
            jax.ShapeDtypeStruct((rows, width), bf16),
            jax.ShapeDtypeStruct((width, rows), bf16),
            jax.ShapeDtypeStruct((deep, width), bf16),
        ],
        scratch_shapes=[pltpu.VMEM((rows, width), f32), pltpu.VMEM((deep, width), f32)],
        cost_estimate=LIGHT,
        name="prepare",
    )(*blocks, embeds, query_keys, agg_value)


def front_kernel(
    member,
    pixel_ref,
    key_ref,
    value_ref,
    out_ref,
    lead_ref,
    gain_ref,
    wq_ref,
    wk_ref,
    wv_ref,
    hidden_ref,
    qkv_ref,
    resid_ref,
    att_ref,
    att_scratch,
):
    pixels = [pixel_ref[c] for c in range(PIX)]
    for head in range(HEADS):
        soft = head_weights(pixels, key_ref, head)
        span = slice(head * HEAD_DIM, (head + 1) * HEAD_DIM)
        att_scratch[span, :] = jnp.dot(
            value_ref[span, :], weighted_pixels(soft, pixels), preferred_element_type=f32
        ).astype(bf16)
    att = att_scratch[...]
    resid = lax.dot_general(att, out_ref[...], TN, preferred_element_type=f32) + lead_ref[...]
    centered = resid - jnp.mean(resid, axis=1, keepdims=True)
    inverse = lax.rsqrt(jnp.mean(centered * centered, axis=1, keepdims=True) + epsilon)
    hidden = (centered * inverse * gain_ref[...]).astype(bf16)
    own = wq_ref.shape[1]
    hidden_ref[...] = hidden.T
    for t, weight in enumerate((wq_ref, wk_ref, wv_ref)):
        qkv_ref[:, t * own : (t + 1) * own] = jnp.dot(
            hidden, weight[...], preferred_element_type=f32
        ).astype(bf16)

    @pl.when(pl.program_id(0) == member[0])
    def _():
        resid_ref[...] = resid
        att_ref[...] = att


def front(member, pixels, key_rows, values_t, agg_out, lead_row, gain, attn_qkv, groups):
    width = agg_out.shape[0]
    own = width // groups
    channels, seq = pixels.shape[1:]
    rows = seq // groups
    spec = pltpu.PrefetchScalarGridSpec(
        num_scalar_prefetch=1,
        grid=(groups,),
        in_specs=[
            pl.BlockSpec((PIX, channels, rows), lambda i, m: (0, 0, i)),
            pl.BlockSpec(key_rows.shape, lambda i, m: (0, 0, 0)),
            pl.BlockSpec(values_t.shape, lambda i, m: (0, 0)),
            pl.BlockSpec(agg_out.shape, lambda i, m: (0, 0)),
            pl.BlockSpec((1, width), lambda i, m: (0, 0)),
            pl.BlockSpec((1, width), lambda i, m: (0, 0)),
            pl.BlockSpec((width, own), lambda i, m: (0, m[0])),
            pl.BlockSpec((width, own), lambda i, m: (0, groups + m[0])),
            pl.BlockSpec((width, own), lambda i, m: (0, 2 * groups + m[0])),
        ],
        out_specs=[
            pl.BlockSpec((width, rows), lambda i, m: (0, i)),
            pl.BlockSpec((rows, 3 * own), lambda i, m: (i, 0)),
            pl.BlockSpec((rows, width), lambda i, m: (0, 0)),
            pl.BlockSpec((width, rows), lambda i, m: (0, 0)),
        ],
        scratch_shapes=[pltpu.VMEM((width, rows), bf16)],
    )
    return pl.pallas_call(
        front_kernel,
        grid_spec=spec,
        out_shape=[
            jax.ShapeDtypeStruct((width, seq), bf16),
            jax.ShapeDtypeStruct((seq, 3 * own), bf16),
            jax.ShapeDtypeStruct((rows, width), f32),
            jax.ShapeDtypeStruct((width, rows), bf16),
        ],
        cost_estimate=LIGHT,
        name="front",
    )(member, pixels, key_rows, values_t, agg_out, lead_row, gain, attn_qkv, attn_qkv, attn_qkv)


def attend_kernel(member, q_ref, k_ref, v_ref, mixed_ref, lse_ref):
    rows = q_ref.shape[0]
    lane = lax.broadcasted_iota(jnp.int32, (1, 2 * HEAD_DIM), 1)
    queries = q_ref[...] * jnp.asarray(0.125, bf16)
    mixed = jnp.zeros((rows, 2 * HEAD_DIM), f32)
    keeps = [(lane // HEAD_DIM) == part for part in range(2)]
    both = [
        lax.dot_general(jnp.where(keep, queries, jnp.zeros_like(queries)), k_ref[...], NT, preferred_element_type=f32)
        for keep in keeps
    ]
    for part, (keep, scores) in enumerate(zip(keeps, both)):
        top = jnp.max(scores, axis=1, keepdims=True)
        soft = jnp.exp(scores - top)
        total = jnp.sum(soft, axis=1, keepdims=True)
        out = jnp.dot(soft.astype(bf16), v_ref[...], preferred_element_type=f32)
        mixed = jnp.where(keep, out * (1.0 / total), mixed)
        lse = jnp.broadcast_to(top + jnp.log(total), (rows, 2 * HEAD_DIM))
        lse_ref[0, part : part + 1, :] = lse.T[0:1, :]
    mixed_ref[...] = mixed.astype(bf16)


def attend(member, qkv, slot, rows, block):
    seq = qkv.shape[0]
    pair = 2 * HEAD_DIM
    pairs = qkv.shape[1] // (3 * pair)
    steps = rows // block
    spec = pltpu.PrefetchScalarGridSpec(
        num_scalar_prefetch=1,
        grid=(pairs, steps),
        in_specs=[
            pl.BlockSpec((block, pair), lambda p, i, m: ((m[0] ^ slot) * steps + i, p)),
            pl.BlockSpec((seq, pair), lambda p, i, m: (0, pairs + p)),
            pl.BlockSpec((seq, pair), lambda p, i, m: (0, 2 * pairs + p)),
        ],
        out_specs=[
            pl.BlockSpec((block, pair), lambda p, i, m: (i, p)),
            pl.BlockSpec((1, 2, block), lambda p, i, m: (p, 0, i)),
        ],
    )
    return pl.pallas_call(
        attend_kernel,
        grid_spec=spec,
        out_shape=[
            jax.ShapeDtypeStruct((rows, pairs * pair), bf16),
            jax.ShapeDtypeStruct((pairs, 2, rows), f32),
        ],
        cost_estimate=LIGHT,
        name="attend",
    )(member, qkv, qkv, qkv)


def attend_back_kernel(member, q_ref, k_ref, v_ref, g_ref, *refs, chunk, groups):
    mixed_refs, lse_refs = refs[:groups], refs[groups : 2 * groups]
    out_ref, dk_acc, dv_acc, kt = refs[2 * groups :]
    i = pl.program_id(0)
    slot = i ^ member[0]
    mixed, lse_rows = mixed_refs[0][...], lse_refs[0][0]
    for k in range(1, groups):
        mixed = jnp.where(slot == k, mixed_refs[k][...], mixed)
        lse_rows = jnp.where(slot == k, lse_refs[k][0], lse_rows)
    block = q_ref.shape[0]
    seq = k_ref.shape[0]
    pair = 2 * HEAD_DIM
    lane = lax.broadcasted_iota(jnp.int32, (1, pair), 1)
    side = lax.broadcasted_iota(jnp.int32, (pair, 1), 0)

    @pl.when(i == 0)
    def _():
        dk_acc[...] = jnp.zeros_like(dk_acc)
        dv_acc[...] = jnp.zeros_like(dv_acc)
        kt[...] = k_ref[...].T

    queries = q_ref[...] * jnp.asarray(0.125, bf16)
    grads = g_ref[...]
    product = (grads.astype(f32) * mixed.astype(f32)).T
    grad_query = jnp.zeros((pair, block), f32)
    for part in range(2):
        keep = (lane // HEAD_DIM) == part
        query = jnp.where(keep, queries, jnp.zeros_like(queries))
        grad = jnp.where(keep, grads, jnp.zeros_like(grads))
        delta = jnp.sum(product[part * HEAD_DIM : (part + 1) * HEAD_DIM], axis=0, keepdims=True)
        lse = lse_rows[part : part + 1, :]
        total = jnp.zeros((pair, block), f32)
        for at in range(0, seq, chunk):
            span = pl.ds(at, chunk)
            scores = lax.dot_general(k_ref[span, :], query, NT, preferred_element_type=f32)
            soft = jnp.exp(scores - lse)
            through = lax.dot_general(v_ref[span, :], grad, NT, preferred_element_type=f32)
            grad_scores = (soft * (through - delta)).astype(bf16)
            dv_acc[span, :] += jnp.dot(soft.astype(bf16), grad, preferred_element_type=f32)
            dk_acc[span, :] += jnp.dot(grad_scores, query, preferred_element_type=f32)
            total += jnp.dot(kt[:, span], grad_scores, preferred_element_type=f32)
        grad_query = jnp.where((side // HEAD_DIM) == part, total, grad_query)
    out_ref[pl.ds(pl.multiple_of(i * block, block), block), 0:pair] = (grad_query.T * 0.125).astype(bf16)

    @pl.when(i == pl.num_programs(0) - 1)
    def _():
        out_ref[:, pair : 2 * pair] = dk_acc[...].astype(bf16)
        out_ref[:, 2 * pair : 3 * pair] = dv_acc[...].astype(bf16)


def attend_back(member, qkv, grads, mixed, lse, which, chunk):
    seq = qkv.shape[0]
    groups = len(mixed)
    rows = seq // groups
    pair = 2 * HEAD_DIM
    pairs = qkv.shape[1] // (3 * pair)
    spec = pltpu.PrefetchScalarGridSpec(
        num_scalar_prefetch=1,
        grid=(groups,),
        in_specs=[
            pl.BlockSpec((rows, pair), lambda i, m: (i, which)),
            pl.BlockSpec((seq, pair), lambda i, m: (0, pairs + which)),
            pl.BlockSpec((seq, pair), lambda i, m: (0, 2 * pairs + which)),
            pl.BlockSpec((rows, pair), lambda i, m: (i, which)),
        ]
        + [pl.BlockSpec((rows, pair), lambda i, m: (0, which))] * groups
        + [pl.BlockSpec((1, 2, rows), lambda i, m: (which, 0, 0))] * groups,
        out_specs=pl.BlockSpec((seq, 3 * pair), lambda i, m: (0, 0)),
        scratch_shapes=[pltpu.VMEM((seq, pair), f32), pltpu.VMEM((seq, pair), f32), pltpu.VMEM((pair, seq), bf16)],
    )
    return pl.pallas_call(
        partial(attend_back_kernel, chunk=min(chunk, seq), groups=groups),
        grid_spec=spec,
        out_shape=jax.ShapeDtypeStruct((seq, 3 * pair), bf16),
        cost_estimate=LIGHT,
        name="attend_back",
    )(member, qkv, qkv, qkv, grads, *mixed, *lse)


def put_tail(tail, values, span):
    groups = len(ORDER)
    channels = values.shape[0] // ((PIX + 1) * groups)
    stride = tail.shape[0] // groups
    for at, k in enumerate(ORDER):
        for c in range(PIX + 1):
            row, source = at * stride + c * channels, (c * groups + k) * channels
            tail[row : row + channels, span] = values[source : source + channels]


def aggregate_back_kernel(
    member, core, bucket, pixel_ref, key_ref, value_ref, grad_ref, bias_ref, gain2_ref, gain1_ref, sum_ref,
    field_ref, keep_ref, send_ref, tail
):
    count, rows = pixel_ref.shape[1:]
    pair = 2 * HEAD_DIM
    pixels = [pixel_ref[c] for c in range(PIX)]
    lane = lax.broadcasted_iota(jnp.int32, (1, pair), 1)
    side = lax.broadcasted_iota(jnp.int32, (pair, 1), 0)
    field = [jnp.zeros((count, rows), f32) for _ in range(PIX)]
    keys = [jnp.zeros((count, pair), f32) for _ in range(PIX + 1)]
    for which in range(HEADS // 2):
        span = slice(which * pair, (which + 1) * pair)
        values, grads = value_ref[:, span], grad_ref[span, :]
        total = jnp.zeros(((PIX + 1) * count, pair), f32)
        for part in range(2):
            head = which * 2 + part
            grad = jnp.where((side // HEAD_DIM) == part, grads, jnp.zeros_like(grads))
            through = jnp.dot(values, grad, preferred_element_type=f32)
            kinds = [through[c * count : (c + 1) * count] for c in range(PIX + 1)]
            soft = head_weights(pixels, key_ref, head)
            grad_soft = kinds[PIX]
            for c in range(PIX):
                grad_soft = grad_soft + pixels[c] * kinds[c]
            weighed = soft * grad_soft
            grad_scores = weighed - soft * jnp.sum(weighed, axis=0, keepdims=True)
            for c in range(PIX):
                field[c] = field[c] + soft * kinds[c] + grad_scores * key_ref[c, :, head : head + 1]
                keys[c] = jnp.where(lane == head, jnp.sum(grad_scores * pixels[c], axis=1, keepdims=True), keys[c])
            keys[PIX] = jnp.where(lane == head, jnp.sum(grad_scores, axis=1, keepdims=True), keys[PIX])
            total = total + lax.dot_general(weighted_pixels(soft, pixels), grad, NT, preferred_element_type=f32)
        put_tail(tail, total, span)
    for c in range(PIX):
        field_ref[c] = field[c].astype(bf16)
    width = value_ref.shape[1]
    put_tail(tail, jnp.concatenate(keys, axis=0), slice(width, width + pair))
    groups = len(ORDER)
    stride = tail.shape[0] // groups
    own, lines = width // groups, LEADS // groups
    for at, k in enumerate(ORDER):
        owner = member[0] ^ k
        start = (at + 1) * stride - FREE
        tail[start : start + FREE, :] = jnp.zeros((FREE, tail.shape[1]), f32)
        tail[start : start + 1, :width] = bias_ref[:, pl.ds(pl.multiple_of(owner * width, width), width)]
        chunk = pl.ds(pl.multiple_of(owner * own, own), own)
        tail[start + 1 : start + 2, :own] = gain2_ref[:, chunk]
        tail[start + 1 : start + 2, own : 2 * own] = gain1_ref[:, chunk]
        for line in range(lines):
            hit = bucket[0] == owner * lines + line
            tail[start + 2 + line : start + 3 + line, :width] = jnp.where(hit, sum_ref[...], 0.0)
    half = width // 2
    for ref, which in ((keep_ref, core[0]), (send_ref, 1 - core[0])):
        ref[:, :half] = tail[:, pl.ds(pl.multiple_of(which * half, half), half)].astype(bf16)
        ref[:, half:] = tail[:, width:].astype(bf16)


def aggregate_back(member, core, bucket, pixels, key_rows, values, grads, small, groups):
    count, seq = pixels.shape[1:]
    rows = seq // groups
    width = values.shape[1]
    deep = (PIX + 1) * count + FREE * groups
    wide = width // 2 + 2 * HEAD_DIM

    def whole(*shape):
        return pl.BlockSpec(shape, lambda i, *_: (0,) * len(shape))

    spec = pltpu.PrefetchScalarGridSpec(
        num_scalar_prefetch=3,
        grid=(1,),
        in_specs=[
            pl.BlockSpec((PIX, count, rows), lambda i, m, c, l: (0, 0, m[0])),
            whole(*key_rows.shape),
            whole(*values.shape),
            whole(*grads.shape),
            *[whole(*value.shape) for value in small],
        ],
        out_specs=[whole(PIX, count, rows), whole(deep, wide), whole(deep, wide)],
        scratch_shapes=[pltpu.VMEM((deep, width + 2 * HEAD_DIM), f32)],
    )
    return pl.pallas_call(
        aggregate_back_kernel,
        grid_spec=spec,
        out_shape=[
            jax.ShapeDtypeStruct((PIX, count, rows), bf16),
            jax.ShapeDtypeStruct((deep, wide), bf16),
            jax.ShapeDtypeStruct((deep, wide), bf16),
        ],
        cost_estimate=LIGHT,
        name="aggregate_back",
    )(member, core, bucket, pixels, key_rows, values, grads, *small)


def shape_of(*dims, kind=bf16):
    return jax.ShapeDtypeStruct(dims, kind)


def inner_kernel(
    member, core, mixed0, mixed1, mixed2, mixed3, wo_ref, resid_ref, gain_ref, w1_ref, b1_ref, ga_ref,
    act_ref, act_t_ref, send_ref, keep_ref, bias_ref, one_ref, hidden_ref, mixed_ref, hidden,
):
    j = pl.program_id(0)
    parts = (mixed0, mixed1, mixed2, mixed3)
    rows, own = mixed0.shape

    @pl.when(j == 0)
    def _():
        resid = resid_ref[...]
        for slot, part in enumerate(parts):
            owner = pl.ds(pl.multiple_of((member[0] ^ slot) * own, own), own)
            resid = resid + jnp.dot(part[...], wo_ref[owner, :], preferred_element_type=f32)
        one_ref[...] = resid
        centered = resid - jnp.mean(resid, axis=1, keepdims=True)
        scale = lax.rsqrt(jnp.mean(centered * centered, axis=1, keepdims=True) + epsilon)
        hidden[...] = (centered * scale * gain_ref[...]).astype(bf16)
        piece = own // 2
        for at, (slot, side) in enumerate(BLOCKS):
            start = pl.multiple_of((member[0] ^ slot) * own + side * piece, piece)
            hidden_ref[at * piece : (at + 1) * piece, :] = hidden[:, pl.ds(start, piece)].T
            mixed_ref[at * piece : (at + 1) * piece, :] = parts[slot][:, side * piece : (side + 1) * piece].T

    inner = jnp.dot(hidden[...], w1_ref[...], preferred_element_type=f32) + b1_ref[...]
    below = 0.5 + 0.5 * lax.erf(inner * 0.7071067811865476)
    act = (inner * below).astype(bf16)
    slope = below + inner * (jnp.exp(-0.5 * inner * inner) * 0.3989422804014327)
    gu = (slope * ga_ref[...].astype(f32)).astype(bf16)
    act_ref[...] = act
    act_t_ref[...] = act.T
    bias_ref[...] = jnp.sum(gu.astype(f32), axis=0, keepdims=True)

    @pl.when(j < len(parts))
    def _():
        send_ref[...] = gu

    @pl.when(j >= len(parts))
    def _():
        keep_ref[...] = gu


def inner_part(member, core, mixed, attn_out, resid, gain, mlp_in, bias, grad_act):
    rows, width = resid.shape
    inner = mlp_in.shape[1]
    groups = len(mixed)
    own = width // groups
    steps = 2 * groups
    block = inner // steps

    def natural(j, c):
        return ((j // groups) ^ (1 - c[0])) * groups + j % groups

    def spot(j, m, c):
        n = natural(j, c)
        slot = (n // 2) ^ m[0]
        return (jnp.where(n % 2 == 0, slot, 4 + (slot % 2) * 2 + slot // 2), 0)

    def whole(*shape):
        return pl.BlockSpec(shape, lambda j, m, c: (0,) * len(shape))

    def column(deep):
        return pl.BlockSpec((deep, block), lambda j, m, c: (0, natural(j, c)))

    spec = pltpu.PrefetchScalarGridSpec(
        num_scalar_prefetch=2,
        grid=(steps,),
        in_specs=[whole(rows, own)] * groups
        + [whole(width, width), whole(rows, width), whole(1, width)]
        + [column(width), column(1), column(rows)],
        out_specs=[
            column(rows),
            pl.BlockSpec((block, rows), spot),
            pl.BlockSpec((rows, block), lambda j, m, c: (0, jnp.minimum(j, groups - 1))),
            pl.BlockSpec((rows, block), lambda j, m, c: (0, jnp.maximum(j - groups, 0))),
            column(1),
            whole(rows, width),
            whole(width, rows),
            whole(width, rows),
        ],
        scratch_shapes=[pltpu.VMEM((rows, width), bf16)],
    )
    return pl.pallas_call(
        inner_kernel,
        grid_spec=spec,
        out_shape=[shape_of(rows, inner), shape_of(inner, rows)]
        + [shape_of(rows, inner // 2)] * 2
        + [shape_of(1, inner, kind=f32), shape_of(rows, width, kind=f32)]
        + [shape_of(width, rows)] * 2,
        cost_estimate=LIGHT,
        name="inner_part",
    )(member, core, *mixed, attn_out, resid, gain, mlp_in, bias, grad_act)


def outer_kernel(
    core, act_ref, send_ref, keep_ref, w1_ref, w2_ref, wo_ref, one_ref, gain_ref, g_ref,
    out_ref, gres_ref, gb_ref, gb_send_ref, gm_ref, ggain_ref, branch, grads,
):
    j = pl.program_id(0)
    groups, rows, own = gm_ref.shape
    half = send_ref.shape[1]
    branch[j] = jnp.dot(act_ref[...], w2_ref[...], preferred_element_type=f32)

    def columns(which):
        return w1_ref[:, pl.ds(pl.multiple_of(which * half, half), half)]

    grads[j] = lax.dot_general(
        send_ref[...], columns(1 - core[0]), NT, preferred_element_type=f32
    ) + lax.dot_general(keep_ref[...], columns(core[0]), NT, preferred_element_type=f32)

    @pl.when(j == pl.num_programs(0) - 1)
    def _():
        count = branch.shape[0]
        resid = one_ref[...]
        out_ref[...] = (resid + jnp.concatenate([branch[i] for i in range(count)], axis=1)).astype(bf16)
        centered = resid - jnp.mean(resid, axis=1, keepdims=True)
        scale = lax.rsqrt(jnp.mean(centered * centered, axis=1, keepdims=True) + epsilon)
        grad, plain = jnp.concatenate([grads[i] for i in range(count)], axis=1), centered * scale
        ggain_ref[...] = jnp.sum(grad * plain, axis=0, keepdims=True)
        grad = grad * gain_ref[...]
        first = jnp.mean(grad, axis=1, keepdims=True)
        second = jnp.mean(grad * plain, axis=1, keepdims=True)
        gres = g_ref[...].astype(f32) + scale * (grad - first - plain * second)
        gres_ref[...] = gres
        gb_ref[...] = gres.astype(bf16)
        width = gb_ref.shape[1]
        gb_send_ref[...] = gb_ref[:, pl.ds(pl.multiple_of((1 - core[0]) * (width // 2), width // 2), width // 2)]
        gb = gb_ref[...]
        for p in range(groups):
            gm_ref[p] = lax.dot_general(gb, wo_ref[p * own : (p + 1) * own, :], NT, preferred_element_type=f32).astype(
                bf16
            )


def outer_part(core, act, gu_send, gu_keep, mlp_in, mlp_out, attn_out, resid, gain, grad_out, groups):
    rows, width = resid.shape
    inner = mlp_in.shape[1]
    own = width // groups
    steps = 4
    block = width // steps

    def whole(*shape):
        return pl.BlockSpec(shape, lambda j, c: (0,) * len(shape))

    spec = pltpu.PrefetchScalarGridSpec(
        num_scalar_prefetch=1,
        grid=(steps,),
        in_specs=[
            whole(rows, inner),
            whole(rows, inner // 2),
            whole(rows, inner // 2),
            pl.BlockSpec((block, inner), lambda j, c: (j, 0)),
            pl.BlockSpec((inner, block), lambda j, c: (0, j)),
            whole(width, width),
            whole(rows, width),
            whole(1, width),
            whole(rows, width),
        ],
        out_specs=[
            whole(rows, width),
            whole(rows, width),
            whole(rows, width),
            whole(rows, width // 2),
            whole(groups, rows, own),
            whole(1, width),
        ],
        scratch_shapes=[pltpu.VMEM((steps, rows, block), f32), pltpu.VMEM((steps, rows, block), f32)],
    )
    return pl.pallas_call(
        outer_kernel,
        grid_spec=spec,
        out_shape=[
            shape_of(rows, width),
            shape_of(rows, width, kind=f32),
            shape_of(rows, width),
            shape_of(rows, width // 2),
            shape_of(groups, rows, own),
            shape_of(1, width, kind=f32),
        ],
        cost_estimate=LIGHT,
        name="outer_part",
    )(core, act, gu_send, gu_keep, mlp_in, mlp_out, attn_out, resid, gain, grad_out)


def both_dots(left, left_other, right, right_other):
    return jnp.dot(left[...], right[...], preferred_element_type=f32) + jnp.dot(
        left_other[...], right_other[...], preferred_element_type=f32
    )


def out_grad_kernel(core, left, left_other, right, right_other, *outs):
    total = both_dots(left, left_other, right, right_other).astype(bf16)
    for q, out in enumerate(outs):

        @pl.when(pl.program_id(0) == q)
        def _():
            out[...] = total


def out_grad(core, left, left_other, right, right_other):
    rows, deep = left.shape
    half = right.shape[1] // 2
    block = rows // 4

    spec = pltpu.PrefetchScalarGridSpec(
        num_scalar_prefetch=1,
        grid=(4,),
        in_specs=[pl.BlockSpec((block, deep), lambda i, c: (i, 0))] * 2
        + [
            pl.BlockSpec((deep, half), lambda i, c: (0, c[0])),
            pl.BlockSpec((deep, half), lambda i, c: (0, 0)),
        ],
        out_specs=[pl.BlockSpec((block, half), lambda i, c: (0, 0)) for q in range(4)],
    )
    return pl.pallas_call(
        out_grad_kernel,
        grid_spec=spec,
        out_shape=[shape_of(rows // 4, half)] * 4,
        cost_estimate=LIGHT,
        name="out_grad",
    )(core, left, left_other, right, right_other)


def in_grad_kernel(core, high, h, h_other, u, u_other, m, m_other, b, b_other, keep, send):
    units = u.shape[1]
    first = both_dots(h, h_other, u, u_other).astype(bf16)
    last = both_dots(m, m_other, b, b_other).astype(bf16)
    for number, out in enumerate((send, keep)):

        @pl.when(pl.program_id(0) == number)
        def _():
            out[:, :units] = first
            out[:, units:] = last


def in_grad(core, high, h, h_other, u, u_other, m, m_other, b, b_other):
    rows, deep = h.shape
    units, branch = u.shape[1] // 2, b_other.shape[1] // 2

    def whole(*shape):
        return pl.BlockSpec(shape, lambda i, c, z: (0,) * len(shape))

    def side(i, c, z):
        return (0, z[0] ^ (1 - i))

    def core_side(i, c, z):
        return (0, 2 * c[0] + (z[0] ^ (1 - i)))

    spec = pltpu.PrefetchScalarGridSpec(
        num_scalar_prefetch=2,
        grid=(2,),
        in_specs=[
            whole(rows, deep),
            whole(rows, deep),
            pl.BlockSpec((deep, units), side),
            pl.BlockSpec((deep, units), side),
            whole(rows, deep),
            whole(rows, deep),
            pl.BlockSpec((deep, branch), core_side),
            pl.BlockSpec((deep, branch), side),
        ],
        out_specs=[whole(rows, units + branch)] * 2,
    )
    return pl.pallas_call(
        in_grad_kernel,
        grid_spec=spec,
        out_shape=[shape_of(rows, units + branch)] * 2,
        cost_estimate=LIGHT,
        name="in_grad",
    )(core, high, h, h_other, u, u_other, m, m_other, b, b_other)


def qkv_grad_kernel(core, h, h_other, *refs):
    out = refs[-1]
    for which in range(2):

        @pl.when(core[0] == which)
        def _():
            out[...] = both_dots(h, h_other, refs[which], refs[2 + which]).astype(bf16)


def qkv_grad(core, h, h_other, grads, others):
    rows, deep = h.shape
    cols = grads[0].shape[1]
    block = rows // 2
    spec = pltpu.PrefetchScalarGridSpec(
        num_scalar_prefetch=1,
        grid=(2,),
        in_specs=[pl.BlockSpec((block, deep), lambda i, c: (i, 0))] * 2
        + [pl.BlockSpec((deep, cols), lambda i, c: (0, 0))] * 4,
        out_specs=pl.BlockSpec((block, cols), lambda i, c: (i, 0)),
    )
    return pl.pallas_call(
        qkv_grad_kernel,
        grid_spec=spec,
        out_shape=shape_of(rows, cols),
        cost_estimate=LIGHT,
        name="qkv_grad",
    )(core, h, h_other, *grads, *others)


def last_grad_kernel(core, qkv_ref, a, a_other, g, g_other, out):
    cols = qkv_ref.shape[1]
    out[0, :, :cols] = qkv_ref[...]
    out[0, :, cols:] = both_dots(a, a_other, g, g_other).astype(bf16)


def last_grad(core, weight_qkv, att, att_other, grad, grad_other, groups):
    rows, deep = att.shape
    half = grad_other.shape[1]
    cols = weight_qkv.shape[1]
    block = rows // groups
    spec = pltpu.PrefetchScalarGridSpec(
        num_scalar_prefetch=1,
        grid=(groups,),
        in_specs=[
            pl.BlockSpec((block, cols), lambda i, c: (i, 0)),
            pl.BlockSpec((block, deep), lambda i, c: (i, 0)),
            pl.BlockSpec((block, deep), lambda i, c: (i, 0)),
            pl.BlockSpec((deep, half), lambda i, c: (0, c[0])),
            pl.BlockSpec((deep, half), lambda i, c: (0, 0)),
        ],
        out_specs=pl.BlockSpec((1, block, cols + half), lambda i, c: (i, 0, 0)),
    )
    return pl.pallas_call(
        last_grad_kernel,
        grid_spec=spec,
        out_shape=shape_of(groups, block, cols + half),
        cost_estimate=LIGHT,
        name="last_grad",
    )(core, weight_qkv, att, att_other, grad, grad_other)


def join_kernel(core, first_ref, second_ref, wq, wk, wv, resid_ref, gain_ref, gres_ref, out_ref, *refs):
    ga_ref, ga_send_ref, gatt_ref, ggain_ref, sum_ref, total = refs
    i = pl.program_id(0)
    pair = 2 * HEAD_DIM

    @pl.when(i == 0)
    def _():
        total[...] = jnp.zeros_like(total)

    spans = [slice(t * pair, (t + 1) * pair) for t in range(3)]
    left = jnp.concatenate([ref[:, span] for span in spans for ref in (first_ref, second_ref)], axis=1)
    weights = jnp.concatenate([wq[...], wk[...], wv[...]], axis=1)
    total[...] += lax.dot_general(left, weights, NT, preferred_element_type=f32)

    @pl.when(i == pl.num_programs(0) - 1)
    def _():
        resid = resid_ref[...]
        centered = resid - jnp.mean(resid, axis=1, keepdims=True)
        scale = lax.rsqrt(jnp.mean(centered * centered, axis=1, keepdims=True) + epsilon)
        plain = centered * scale
        grad = total[...]
        ggain_ref[...] = jnp.sum(grad * plain, axis=0, keepdims=True)
        grad = grad * gain_ref[...]
        first = jnp.mean(grad, axis=1, keepdims=True)
        second = jnp.mean(grad * plain, axis=1, keepdims=True)
        gres = gres_ref[...] + scale * (grad - first - plain * second)
        sum_ref[...] = jnp.sum(gres, axis=0, keepdims=True)
        ga = gres.astype(bf16)
        ga_ref[...] = ga
        half = ga_send_ref.shape[1]
        ga_send_ref[...] = ga_ref[:, pl.ds(pl.multiple_of((1 - core[0]) * half, half), half)]
        gatt_ref[...] = lax.dot_general(out_ref[...], ga, NT, preferred_element_type=f32).astype(bf16)


def join(core, first, second, attn_qkv, resid, gain, gres, agg_out):
    rows, width = resid.shape
    groups = first.shape[0] // rows
    own = width // groups
    cols = first.shape[1]

    def whole(*shape):
        return pl.BlockSpec(shape, lambda i, c: (0,) * len(shape))

    spec = pltpu.PrefetchScalarGridSpec(
        num_scalar_prefetch=1,
        grid=(groups,),
        in_specs=[
            pl.BlockSpec((rows, cols), lambda i, c: (i, 0)),
            pl.BlockSpec((rows, cols), lambda i, c: (i, 0)),
            pl.BlockSpec((width, own), lambda i, c: (0, i)),
            pl.BlockSpec((width, own), lambda i, c: (0, groups + i)),
            pl.BlockSpec((width, own), lambda i, c: (0, 2 * groups + i)),
            whole(rows, width),
            whole(1, width),
            whole(rows, width),
            whole(width, width),
        ],
        out_specs=[
            whole(rows, width),
            whole(rows, width // 2),
            whole(width, rows),
            whole(1, width),
            whole(1, width),
        ],
        scratch_shapes=[pltpu.VMEM((rows, width), f32)],
    )
    return pl.pallas_call(
        join_kernel,
        grid_spec=spec,
        out_shape=[
            shape_of(rows, width),
            shape_of(rows, width // 2),
            shape_of(width, rows),
            shape_of(1, width, kind=f32),
            shape_of(1, width, kind=f32),
        ],
        cost_estimate=LIGHT,
        name="join",
    )(core, first, second, attn_qkv, attn_qkv, attn_qkv, resid, gain, gres, agg_out)


def add(a, b):
    return (a.astype(f32) + b.astype(f32)).astype(bf16)


def split_add(a, b, count):
    deep = a.shape[0] // count
    return [add(a[i * deep : (i + 1) * deep], b[i * deep : (i + 1) * deep]) for i in range(count)]


def pick_add(a, b, which, axis):
    half = a.shape[axis] // 2
    return add(
        lax.dynamic_slice_in_dim(a, which * half, half, axis), lax.dynamic_slice_in_dim(b, which * half, half, axis)
    )


def choose(high, a, b, c, d):
    first, second = high == 0, high != 0
    keep = add(jnp.where(first, a, c), jnp.where(first, b, d))
    send = add(jnp.where(second, a, c), jnp.where(second, b, d))
    return keep, send


def whole_blocks(shapes):
    return [pl.BlockSpec(shape, lambda i, *_, n=len(shape): (0,) * n) for shape in shapes]


def gather_sources_kernel(high, came_ref, keep, send, *, cols):
    groups, half = came_ref.shape[0], keep.shape[0]
    for out, which in ((keep, high[0]), (send, 1 - high[0])):
        span = pl.ds(pl.multiple_of(which * half, half), half)
        total = jnp.zeros((half, came_ref.shape[2] - cols), f32)
        for p in range(groups):
            out[:, p * cols : (p + 1) * cols] = came_ref[p, span, :cols]
            total = total + came_ref[p, span, cols:].astype(f32)
        out[:, groups * cols :] = total.astype(bf16)


def gather_sources(high, came, cols):
    groups, rows, wide = came.shape
    shape = (rows // 2, groups * cols + wide - cols)
    spec = pltpu.PrefetchScalarGridSpec(
        num_scalar_prefetch=1, grid=(1,), in_specs=whole_blocks([came.shape]), out_specs=whole_blocks([shape] * 2)
    )
    return pl.pallas_call(
        partial(gather_sources_kernel, cols=cols),
        grid_spec=spec,
        out_shape=[jax.ShapeDtypeStruct(shape, bf16)] * 2,
        cost_estimate=LIGHT,
        name="gather_sources",
    )(high, came)


def turned(i, levels):
    total = 0
    for k in range(levels):
        total = total + (((i >> k) & 1) << (levels - 1 - k))
    return total


def assemble_kernel(where, *refs, order, levels, spans, low_rows):
    pieces, outs = refs[:4], refs[4:]
    deep = pieces[0].shape[0] // len(order)
    for number, ref in enumerate(pieces):
        core = where[1] if number < 2 else 1 - where[1]
        for at, bits in enumerate(order):
            chip = where[0] ^ (bits ^ (number % 2))
            low = low_bit(chip, levels)
            row = turned(chip >> 1, levels - 1)
            if low_rows:
                row = row + (low << (levels - 1))
            to = pl.ds(pl.multiple_of(row * deep, deep), deep)
            for out, source, size, base, by_core, by_low in spans:
                column = pl.multiple_of(base + core * by_core + low * by_low, 128)
                outs[out][to, pl.ds(column, size)] = ref[at * deep : (at + 1) * deep, source : source + size].astype(f32)


def assemble(where, pieces, levels, spans, widths, low_rows=True):
    order = [0]
    for bit in range(levels - 1, 0, -1):
        order = order + [bits ^ (3 if mirrored(levels) else 1 << bit) for bits in order]
    rows = pieces[0].shape[0] * (2 if low_rows else 1)
    shapes = [(rows, wide) for wide in widths]
    spec = pltpu.PrefetchScalarGridSpec(
        num_scalar_prefetch=1,
        grid=(1,),
        in_specs=whole_blocks([p.shape for p in pieces]),
        out_specs=whole_blocks(shapes),
    )
    return pl.pallas_call(
        partial(assemble_kernel, order=tuple(order), levels=levels, spans=tuple(spans), low_rows=low_rows),
        grid_spec=spec,
        out_shape=[shape_of(*shape, kind=f32) for shape in shapes],
        cost_estimate=LIGHT,
        name="assemble",
    )(where, *pieces)


def field_kernel(member, *refs):
    pieces, out = refs[:-1], refs[-1]
    kinds, channels, rows = pieces[0].shape
    for k, piece in enumerate(pieces):
        at = pl.ds(pl.multiple_of((member[0] ^ k) * rows, rows), rows)
        for c in range(kinds):
            out[:, c, at] = piece[c].astype(f32)


def place_field(member, pieces):
    kinds, channels, rows = pieces[0].shape
    shape = (channels, kinds, rows * len(pieces))
    spec = pltpu.PrefetchScalarGridSpec(
        num_scalar_prefetch=1,
        grid=(1,),
        in_specs=whole_blocks([p.shape for p in pieces]),
        out_specs=whole_blocks([shape])[0],
    )
    return pl.pallas_call(
        field_kernel, grid_spec=spec, out_shape=jax.ShapeDtypeStruct(shape, f32), name="place_field"
    )(member, *pieces)


def tail_kernel(member, *refs, groups):
    tails = refs[:groups]
    stacked_ref, pick_ref, value_ref, qk_ref, key_ref, query_ref = refs[groups : groups + 6]
    gvalue_ref, gkey_ref, gquery_ref, patch_ref, table_ref, gqk = refs[groups + 6 :]
    width = value_ref.shape[0]
    own = gvalue_ref.shape[0]
    at = pl.ds(pl.multiple_of(member[0] * own, own), own)
    tail = jnp.concatenate([t[...] for t in tails], axis=0)
    values, keys = tail[:, :width], tail[:, width:]
    gvalue_ref[...] = lax.dot_general(stacked_ref[:, at], values, TN, preferred_element_type=f32)
    gqk[...] = lax.dot_general(stacked_ref[...], keys, TN, preferred_element_type=f32)
    head = lax.broadcasted_iota(jnp.int32, (keys.shape[1], width), 0)
    column = lax.broadcasted_iota(jnp.int32, (keys.shape[1], width), 1) // HEAD_DIM
    spread = jnp.where(head == column, 1.0, 0.0)
    gkey_ref[...] = (
        jnp.dot(gqk[at, :], spread, precision=highest, preferred_element_type=f32) * (query_ref[...] * 0.125)
    )
    by_head = lax.dot_general(gqk[...], key_ref[...].astype(f32), TN, precision=highest, preferred_element_type=f32)
    head = lax.broadcasted_iota(jnp.int32, by_head.shape, 0)
    column = (lax.broadcasted_iota(jnp.int32, by_head.shape, 1) + member[0] * own) // HEAD_DIM
    gquery_ref[...] = jnp.sum(jnp.where(head == column, by_head, 0.0), axis=0, keepdims=True) * 0.125
    own_rows = tails[0].shape[0]
    table = jnp.dot(pick_ref[...], tail, preferred_element_type=f32).astype(bf16)
    rows = jnp.concatenate([tail[:own_rows], table], axis=0)
    total = lax.dot_general(rows[:, :width], value_ref[...], NT, preferred_element_type=f32) + lax.dot_general(
        rows[:, width:].astype(f32), qk_ref[...], NT, precision=highest, preferred_element_type=f32
    )
    channels = patch_ref.shape[0]
    for c in range(PIX):
        patch_ref[:, c, :] = total[c * channels : (c + 1) * channels]
    table_ref[...] = total[own_rows : own_rows + table_ref.shape[0]]


def finish_tail(member, tails, stacked, pick, agg_value, query_keys, agg_key, agg_query, channels, lines):
    groups = len(tails)
    width = agg_value.shape[0]
    own = width // groups
    args = [*tails, stacked, pick, agg_value, query_keys]
    spec = pltpu.PrefetchScalarGridSpec(
        num_scalar_prefetch=1,
        grid=(1,),
        in_specs=whole_blocks([x.shape for x in args])
        + [pl.BlockSpec((width, own), lambda i, m: (0, m[0])), pl.BlockSpec((1, width), lambda i, m: (0, 0))],
        out_specs=whole_blocks([(own, width), (own, width), (1, own), (channels, PIX, width), (lines, width)]),
        scratch_shapes=[pltpu.VMEM((width, query_keys.shape[1]), f32)],
    )
    return pl.pallas_call(
        partial(tail_kernel, groups=groups),
        grid_spec=spec,
        out_shape=[
            jax.ShapeDtypeStruct((own, width), f32),
            jax.ShapeDtypeStruct((own, width), f32),
            jax.ShapeDtypeStruct((1, own), f32),
            jax.ShapeDtypeStruct((channels, PIX, width), f32),
            jax.ShapeDtypeStruct((lines, width), f32),
        ],
        cost_estimate=LIGHT,
        name="finish_tail",
    )(member, *args, agg_key, agg_query)


def fence(*values):
    return lax.optimization_barrier(values)


def swap(value, axis, bits):
    size = lax.axis_size(axis)
    return lax.ppermute(value, axis, [(i, i ^ bits) for i in range(size)])


def from_all(own, groups):
    return [own] + [swap(own, "var", k) for k in range(1, groups)]


def exchange(value):
    return lax.all_to_all(value, "var", split_axis=0, concat_axis=0, tiled=True)


def chip_bits():
    bits, bit = [], 1
    while bit < lax.axis_size("chip"):
        bits.append(bit)
        bit *= 2
    return bits


def mirrored(levels):
    return levels == 2


def partner(bit):
    levels = len(chip_bits())
    return 3 if mirrored(levels) and bit == 2 else bit


def low_bit(chip, levels):
    return (chip ^ (chip >> 1)) & 1 if mirrored(levels) else chip & 1


def is_high(bit):
    chip = lax.axis_index("chip")
    return low_bit(chip, len(chip_bits())) if bit == 1 else (chip // bit) % 2


def stack_other(value, bit):
    return jnp.concatenate([value, swap(value, "chip", partner(bit))], axis=0)


def with_core(halves):
    return [*halves, *(swap(value, "core", 1) for value in halves)]


def by_core(mine, other, core):
    return jnp.where(core == 0, mine, other), jnp.where(core == 0, other, mine)


def body(
    field_patches,
    var_ids,
    lead_bucket,
    patch_weight,
    var_embed,
    agg_query,
    agg_key,
    agg_value,
    agg_out,
    lead_table,
    ln1_gain,
    attn_qkv,
    attn_out,
    ln2_gain,
    mlp_in,
    mlp_in_bias,
    mlp_out,
    cotangent,
):
    groups = lax.axis_size("var")
    member = lax.axis_index("var")
    core = lax.axis_index("core")
    channels, pixel_count, samples, seq = field_patches.shape
    width = agg_key.shape[0]
    inner_width = mlp_in.shape[1]
    leads = lead_table.shape[0]
    vocab = var_embed.shape[0]
    rows = seq // groups
    own = width // groups
    count = channels * groups
    slots = [member ^ k for k in range(groups)]
    member_one = member.reshape(1).astype(jnp.int32)
    core_one = core.reshape(1).astype(jnp.int32)
    bits = chip_bits()
    assert bits
    high = is_high(bits[0])
    high_one = high.reshape(1).astype(jnp.int32)
    half = width // 2
    gain_one = ln1_gain.astype(f32)
    gain_two = ln2_gain.astype(f32)

    mine = jnp.concatenate(
        [
            field_patches.reshape(channels, pixel_count, seq).transpose(1, 0, 2),
            patch_weight.transpose(1, 0, 2),
        ],
        axis=2,
    )
    grad_out = cotangent.reshape(rows, width)
    grad_act = lax.dot_general(grad_out, mlp_out, NT, preferred_element_type=f32).astype(bf16)
    ids = jnp.concatenate([lax.dynamic_slice_in_dim(var_ids, slot * channels, channels) for slot in slots])
    table_pick = (ids[:, None] == jnp.arange(vocab, dtype=jnp.int32)[None, :]).astype(bf16)
    embeds = jnp.dot(table_pick, var_embed, preferred_element_type=f32)
    head_of = jnp.arange(width, dtype=jnp.int32) // HEAD_DIM
    spread = head_of[:, None] == jnp.arange(2 * HEAD_DIM, dtype=jnp.int32)[None, :]
    query_block = jnp.where(spread, agg_query[:, None], jnp.zeros((), bf16))
    query_keys = jnp.dot(agg_key, query_block, preferred_element_type=f32) * 0.125
    lead_row = lax.dynamic_slice_in_dim(lead_table, lead_bucket[0], 1).astype(f32)
    grad_out_other = swap(lax.dynamic_slice_in_dim(grad_out, (1 - core) * half, half, axis=1), "core", 1)
    arrived, grad_act, embeds, query_keys, lead_row, grad_out_other = fence(
        from_all(mine, groups), grad_act, embeds, query_keys, lead_row, grad_out_other
    )
    pixels, key_rows, values, values_t, by_slot = prepare(arrived, embeds, query_keys, agg_value, seq)

    hidden_t, qkv, resid_zero, att_low = front(
        member_one, pixels, key_rows, values_t, agg_out, lead_row, gain_one[None], attn_qkv, groups
    )

    hidden_t, att_low, qkv = fence(hidden_t, att_low, qkv)
    hidden_other, att_other = swap(hidden_t, "core", 1), swap(att_low, "core", 1)

    block = min(256, rows)
    mixed_parts, lse_parts, received = [None] * groups, [None] * groups, [None] * groups
    for k in reversed(range(groups)):
        mixed_parts[k], lse_parts[k] = attend(member_one, qkv, k, rows, block)
        if k + 1 < groups:
            received[k + 1], mixed_parts[k], qkv = fence(received[k + 1], mixed_parts[k], qkv)
            if k + 2 == groups:
                hidden_other, att_other, qkv = fence(hidden_other, att_other, qkv)
        received[k] = swap(mixed_parts[k], "var", k) if k else mixed_parts[k]

    act, act_t, gu_send, gu_keep, grad_bias, resid_one, hidden_two_t, mixed_t = inner_part(
        member_one, core_one, received, attn_out, resid_zero, gain_two[None], mlp_in, mlp_in_bias.astype(f32)[None], grad_act
    )
    gu_send, act_t, act, hidden_two_t, mixed_t = fence(gu_send, act_t, act, hidden_two_t, mixed_t)
    act_other, gu_other, hidden_two_other, mixed_other = (
        swap(value, "core", 1) for value in (act_t, gu_send, hidden_two_t, mixed_t)
    )
    output, grad_resid_one, grad_branch, branch_send, grad_mixed, grad_gain_two = outer_part(
        core_one, act, gu_send, gu_keep, mlp_in, mlp_out, attn_out, resid_one, gain_two[None], grad_out, groups
    )
    act_other, gu_other, hidden_two_other, mixed_other, grad_mixed, branch_send, output = fence(
        act_other, gu_other, hidden_two_other, mixed_other, grad_mixed, branch_send, output
    )
    output = output.reshape(samples, rows, width)

    branch_other = swap(branch_send, "core", 1)
    grad_heads = exchange(grad_mixed).reshape(seq, own)
    out_y, out_y_send, out_x, out_x_send = out_grad(core_one, act_t, act_other, grad_out, grad_out_other)
    grad_heads, branch_other, out_y, out_y_send, out_x, out_x_send = fence(
        grad_heads, branch_other, out_y, out_y_send, out_x, out_x_send
    )
    out_y_came, out_x_came = swap(out_y_send, "var", 2), swap(out_x_send, "var", 1)
    in_part, in_part_send = in_grad(
        core_one,
        high_one,
        hidden_two_t,
        hidden_two_other,
        gu_keep,
        gu_other,
        mixed_t,
        mixed_other,
        grad_branch,
        branch_other,
    )
    grad_heads, in_part_send, in_part = fence(grad_heads, in_part_send, in_part)

    pair = 2 * HEAD_DIM
    pairs = own // pair
    assert pairs == 2
    in_part_came = swap(in_part_send, "chip", bits[0])
    first = attend_back(member_one, qkv, grad_heads, mixed_parts, lse_parts, 0, 512)
    first, qkv, out_y_came, out_x_came = fence(first, qkv, out_y_came, out_x_came)
    out_y, out_y_send = split_add(out_y, out_y_came, 2)
    out_x, out_x_send = split_add(out_x, out_x_came, 2)
    first, qkv, out_y_send, out_x_send = fence(first, qkv, out_y_send, out_x_send)
    first_came = exchange(first)
    first_other = swap(first, "core", 1)
    out_y_came, out_x_came = swap(out_y_send, "var", 1), swap(out_x_send, "var", 2)
    second = attend_back(member_one, qkv, grad_heads, mixed_parts, lse_parts, 1, 512)
    second_came = exchange(second)
    first_came, first_other, second, in_part_came, out_y_came, out_x_came = fence(
        first_came, first_other, second, in_part_came, out_y_came, out_x_came
    )
    second_other = swap(second, "core", 1)
    out_keep, out_send = choose(high, out_y, out_y_came, out_x, out_x_came)
    out_came = swap(out_send, "chip", bits[0])
    in_y, in_y_send, in_x, in_x_send = split_add(in_part, in_part_came, 4)
    second_other, in_y_send, in_x_send = fence(second_other, in_y_send, in_x_send)
    weight_qkv = qkv_grad(core_one, hidden_t, hidden_other, (first, second), (first_other, second_other))
    second_came, weight_qkv, in_y_send, in_x_send, grad_resid_one, out_came = fence(
        second_came, weight_qkv, in_y_send, in_x_send, grad_resid_one, out_came
    )
    rest = bits[1:]

    def scatter_parts(keep, came, bit):
        return [pick_add(keep, came, which, 0) for which in (is_high(bit), 1 - is_high(bit))]

    def scatter_step(keep, came, bit):
        keep, send = scatter_parts(keep, came, bit)
        return keep, swap(send, "chip", partner(bit))

    out_keep, out_send = scatter_parts(out_keep, out_came, rest[0])
    second_came, out_send, in_y_send, in_x_send = fence(second_came, out_send, in_y_send, in_x_send)
    out_came = swap(out_send, "chip", partner(rest[0]))
    in_y_came, in_x_came = swap(in_y_send, "var", 2), swap(in_x_send, "var", 1)
    grad_agg, grad_agg_send, grad_att, grad_gain_one, sample_sum = join(
        core_one, first_came, second_came, attn_qkv, resid_zero, gain_one[None], grad_resid_one, agg_out
    )
    grad_agg, grad_agg_send, grad_att, out_came, in_y_came, in_x_came = fence(
        grad_agg, grad_agg_send, grad_att, out_came, in_y_came, in_x_came
    )
    for bit in rest[1:]:
        out_keep, out_came = scatter_step(out_keep, out_came, bit)
    out_rows = add(out_keep, out_came)
    in_y, in_y_send = split_add(in_y, in_y_came, 2)
    in_x, in_x_send = split_add(in_x, in_x_came, 2)
    out_rows, grad_att, grad_agg_send, in_y_send, in_x_send = fence(
        out_rows, grad_att, grad_agg_send, in_y_send, in_x_send
    )
    out_other = swap(out_rows, "chip", partner(rest[-1]))
    grad_agg_other = swap(grad_agg_send, "core", 1)
    in_y_came, in_x_came = swap(in_y_send, "var", 1), swap(in_x_send, "var", 2)

    field_own, tail, tail_send = aggregate_back(
        member_one,
        core_one,
        lead_bucket,
        pixels,
        key_rows,
        values,
        grad_att,
        (grad_bias, grad_gain_two, grad_gain_one, sample_sum),
        groups,
    )
    tail, tail_send, grad_agg_other, in_y_came, in_x_came = fence(
        tail, tail_send, grad_agg_other, in_y_came, in_x_came
    )
    tail_came = swap(tail_send, "core", 1)
    in_own = jnp.concatenate([add(in_y, in_y_came), add(in_x, in_x_came)], axis=0)
    for bit in rest:
        in_rows = in_own.shape[0] // 2
        in_own, in_send = (
            lax.dynamic_slice_in_dim(in_own, which * in_rows, in_rows) for which in (is_high(bit), 1 - is_high(bit))
        )
        if bit != rest[-1]:
            in_own = add(in_own, swap(in_send, "chip", partner(bit)))
    in_send, grad_agg_other, tail_came = fence(in_send, grad_agg_other, tail_came)
    in_came = swap(in_send, "chip", partner(rest[-1]))
    tail = add(tail, tail_came)
    deep = tail.shape[0] // 2
    tail, grad_agg_other = fence(tail, grad_agg_other)
    tail_came = swap(tail[deep:], "var", 1)
    last_send = last_grad(core_one, weight_qkv, att_low, att_other, grad_agg, grad_agg_other, groups)
    tail, tail_came, last_send, out_other = fence(tail, tail_came, last_send, out_other)
    tail = add(tail[:deep], tail_came)
    deep //= 2
    tail_came = swap(tail[deep:], "var", 2)
    out_rows = jnp.concatenate([out_rows, out_other], axis=0)
    for bit in reversed(rest[:-1]):
        out_rows = stack_other(out_rows, bit)
    tail, tail_came, last_send, out_rows = fence(tail, tail_came, last_send, out_rows)
    last_came = exchange(last_send)
    tail = add(tail[:deep], tail_came)
    tail_came = swap(tail, "chip", bits[0])
    out_other = swap(out_rows, "chip", bits[0])
    last_came, in_came, tail, out_rows = fence(last_came, in_came, tail, out_rows)
    last_keep, last_send = gather_sources(high_one, last_came, 3 * pair)
    in_rows = add(in_own, in_came)
    last_send, in_rows, tail, tail_came = fence(last_send, in_rows, tail, tail_came)
    last_came = swap(last_send, "chip", bits[0])
    in_other = swap(in_rows, "chip", partner(rest[-1]))
    tail = add(tail, tail_came)
    for bit in rest:
        tail_came = swap(tail, "chip", partner(bit))
        if bit != rest[-1]:
            tail = add(tail, tail_came)
    tail, tail_came, out_rows, out_other = fence(tail, tail_came, out_rows, out_other)
    tail = add(tail, tail_came)
    tail_came = swap(tail, "core", 1)
    out_pieces = with_core([out_rows, out_other])
    tail, tail_came, out_pieces = fence(tail, tail_came, out_pieces)
    levels = len(bits)
    where = jnp.stack([lax.axis_index("chip"), core]).astype(jnp.int32)
    (sum_mlp_out,) = assemble(where, out_pieces, levels, [(0, 0, half, 0, half, 0)], [width])
    low, up = by_core(tail, tail_came, core)
    tail = jnp.concatenate([low[:, :half], up], axis=1)
    tail, sum_mlp_out, last_came, in_other = fence(tail, sum_mlp_out, last_came, in_other)
    for bit in rest[:-1]:
        last_keep, last_came = scatter_step(last_keep, last_came, bit)
    last_keep, last_send = scatter_parts(last_keep, last_came, rest[-1])
    in_rows = jnp.concatenate([in_rows, in_other], axis=0)
    for bit in reversed(rest[:-1]):
        in_rows = stack_other(in_rows, bit)
    tail, last_send, in_rows = fence(tail, last_send, in_rows)
    last_came = swap(last_send, "chip", partner(rest[-1]))
    tails = from_all(tail, groups)
    in_other = swap(in_rows, "chip", bits[0])
    tails = fence(*tails)
    stride = tail.shape[0]
    per_slot = (PIX + 1) * channels
    small_sum = tail[per_slot:, :width].astype(f32)
    part_size = inner_width // groups
    sum_bias = small_sum[0]
    sum_gain_two = small_sum[1, :own]
    sum_gain_one = small_sum[1, own : 2 * own]
    sum_lead = small_sum[2 : 2 + leads // groups]

    own_ids = member * (vocab // groups) + jnp.arange(16, dtype=jnp.int32)
    own_pick = jnp.where(jnp.arange(16)[:, None] < vocab // groups, own_ids[:, None] == ids[None, :], False)
    own_pick = jnp.pad(
        own_pick.reshape(16, groups, channels), ((0, 0), (0, 0), (PIX * channels, stride - per_slot))
    ).reshape(16, groups * stride)
    sum_value, sum_key, sum_query, sum_patch, sum_table = finish_tail(
        member_one,
        tails,
        by_slot,
        own_pick.astype(bf16),
        agg_value,
        query_keys,
        agg_key,
        agg_query.astype(f32)[None],
        channels,
        vocab // groups,
    )
    sum_query = sum_query.reshape(own)
    sum_value, last_came, in_rows = fence(sum_value, last_came, in_rows)
    last_rows = add(last_keep, last_came)
    last_other = swap(last_rows, "chip", partner(rest[-1]))
    field_slots = field_own.reshape(pixel_count, groups, channels, rows)
    field_parts = [swap(field_slots[:, k], "var", k) if k else field_slots[:, 0] for k in range(groups)]
    field_parts = fence(*field_parts)
    field_grad = place_field(member_one, field_parts).reshape(channels, pixel_count, samples, seq)
    field_grad, last_other, in_rows, in_other = fence(field_grad, last_other, in_rows, in_other)
    last_rows = jnp.concatenate([last_rows, last_other], axis=0)
    for bit in reversed(rest[:-1]):
        last_rows = stack_other(last_rows, bit)
    last_rows, in_rows, in_other = fence(last_rows, in_rows, in_other)
    last_other = swap(last_rows, "chip", bits[0])
    in_pieces = fence(*with_core([in_rows, in_other]))

    half_in = inner_width // 2
    units = half_in // 2
    sum_mlp_in, sum_attn_out = assemble(
        where,
        in_pieces,
        levels,
        [(0, 0, units, 0, half_in, units), (1, units, half // 2, 0, half, half // 2)],
        [inner_width, width],
        low_rows=False,
    )
    sum_mlp_in, last_rows, last_other, sum_patch, sum_table, field_grad = fence(
        sum_mlp_in, last_rows, last_other, sum_patch, sum_table, field_grad
    )
    sum_qkv, sum_agg_out = assemble(
        where,
        with_core([last_rows, last_other]),
        levels,
        [
            (0, (3 * p + t) * pair, pair, t * width + p * own, pair, 0)
            for p in range(groups)
            for t in range(3)
        ]
        + [(1, groups * 3 * pair, half, 0, half, 0)],
        [3 * width, width],
    )
    return (
        output,
        field_grad,
        sum_patch,
        sum_table,
        sum_query,
        sum_key,
        sum_value,
        sum_agg_out,
        sum_lead,
        sum_gain_one,
        sum_qkv,
        sum_attn_out,
        sum_gain_two,
        sum_mlp_in,
        sum_bias,
        sum_mlp_out,
    )


def solution(mesh):
    members, patches = mesh.shape["var"], mesh.shape["patch"]
    chips = Mesh(mesh.devices.reshape(members, patches // 2, 2), ("var", "chip", "core"))
    patch = ("chip", "core")
    placed = (
        P("var", None, patch, None),
        P(),
        P(patch),
        P("var", None, None),
        *[P()] * 13,
        P(patch, "var", None),
    )
    return jax.shard_map(
        body,
        mesh=chips,
        in_specs=placed,
        out_specs=(
            P(patch, "var", None),
            P("var", None, patch, None),
            P("var", None, None),
            P("var", None),
            P("var"),
            P("var", None),
            P("var", None),
            P("var", None),
            P("var", None),
            P("var"),
            P("var", None),
            P("var", None),
            P("var"),
            P("var", None),
            P("var"),
            P("var", None),
        ),
        check_vma=False,
    )
```

```python
from functools import partial

import jax
import jax.numpy as jnp
from jax import lax
from jax.experimental import pallas as pl
from jax.experimental.pallas import tpu as pltpu
from jax.sharding import Mesh
from jax.sharding import PartitionSpec as P

HEADS = 16
PIX = 4
HEAD_DIM = 64
LEADS = 8
FREE = 4
ORDER = (0, 2, 1, 3)
BLOCKS = tuple((k, 0) for k in range(4)) + tuple((k, 1) for k in ORDER)

f32, bf16 = jnp.float32, jnp.bfloat16
highest = lax.Precision.HIGHEST
epsilon = 1e-05
NT = (((1,), (1,)), ((), ()))
LIGHT = pl.CostEstimate(flops=1, bytes_accessed=1, transcendentals=0)
TN = (((0,), (0,)), ((), ()))


def head_weights(pixels, key_ref, head):
    scores = key_ref[PIX, :, head : head + 1]
    for c in range(PIX):
        scores = scores + pixels[c] * key_ref[c, :, head : head + 1]
    soft = jnp.exp(scores - jnp.max(scores, axis=0, keepdims=True))
    return soft * (1.0 / jnp.sum(soft, axis=0, keepdims=True))


def slot_spans(member, own):
    return [pl.ds(pl.multiple_of((member[0] ^ k) * own, own), own) for k in ORDER]


def weighted_pixels(soft, pixels):
    return jnp.concatenate(
        [(soft * pixels[c]).astype(bf16) for c in range(PIX)] + [soft.astype(bf16)], axis=0
    )


def prepare_kernel(*refs, groups):
    blocks = refs[:groups]
    pick_ref, embed_ref, query_ref, weight_ref, pixel_ref, key_ref, value_ref, value_t_ref, slot_ref, stacked, by_slot = refs[groups:]
    channels = blocks[0].shape[1]
    seq = pixel_ref.shape[2]
    count = channels * groups
    stride = by_slot.shape[0] // groups
    by_slot[...] = jnp.zeros_like(by_slot)
    embeds = jnp.dot(pick_ref[...], embed_ref[...], preferred_element_type=f32)
    for k, block in enumerate(blocks):
        for c in range(PIX + 1):
            if c < PIX:
                pixel_ref[c, k * channels : (k + 1) * channels, :] = block[c, :, :seq].astype(f32)
                rows = block[c, :, seq:].astype(f32)
            else:
                rows = embeds[k * channels : (k + 1) * channels, :]
            stacked[c * count + k * channels : c * count + (k + 1) * channels, :] = rows
            by_slot[k * stride + c * channels : k * stride + (c + 1) * channels, :] = rows
    slot_ref[...] = by_slot[...].astype(bf16)
    keys = jnp.dot(stacked[...], query_ref[...], precision=highest, preferred_element_type=f32)
    for c in range(PIX + 1):
        key_ref[c] = keys[c * count : (c + 1) * count]
    values = jnp.dot(stacked[...].astype(bf16), weight_ref[...], preferred_element_type=f32).astype(bf16)
    value_ref[...] = values
    value_t_ref[...] = values.T


def prepare(blocks, pick, var_embed, query_keys, agg_value, seq):
    groups = len(blocks)
    channels = blocks[0].shape[1]
    count = channels * groups
    width = agg_value.shape[0]
    rows = (PIX + 1) * count
    deep = rows + FREE * groups
    return pl.pallas_call(
        partial(prepare_kernel, groups=groups),
        out_shape=[
            jax.ShapeDtypeStruct((PIX, count, seq), f32),
            jax.ShapeDtypeStruct((PIX + 1, count, query_keys.shape[1]), f32),
            jax.ShapeDtypeStruct((rows, width), bf16),
            jax.ShapeDtypeStruct((width, rows), bf16),
            jax.ShapeDtypeStruct((deep, width), bf16),
        ],
        scratch_shapes=[pltpu.VMEM((rows, width), f32), pltpu.VMEM((deep, width), f32)],
        cost_estimate=LIGHT,
        name="prepare",
    )(*blocks, pick, var_embed, query_keys, agg_value)


def front_kernel(
    member,
    bucket,
    pixel_ref,
    key_ref,
    value_ref,
    out_ref,
    lead_ref,
    gain_ref,
    wq_ref,
    wk_ref,
    wv_ref,
    hidden_ref,
    qkv_ref,
    resid_ref,
    att_ref,
    att_scratch,
):
    pixels = [pixel_ref[c] for c in range(PIX)]
    for head in range(HEADS):
        soft = head_weights(pixels, key_ref, head)
        span = slice(head * HEAD_DIM, (head + 1) * HEAD_DIM)
        att_scratch[span, :] = jnp.dot(
            value_ref[span, :], weighted_pixels(soft, pixels), preferred_element_type=f32
        ).astype(bf16)
    att = att_scratch[...]
    line = lax.broadcasted_iota(jnp.int32, lead_ref.shape, 0)
    lead = jnp.sum(jnp.where(line == bucket[0], lead_ref[...].astype(f32), 0.0), axis=0, keepdims=True)
    resid = lax.dot_general(att, out_ref[...], TN, preferred_element_type=f32) + lead
    centered = resid - jnp.mean(resid, axis=1, keepdims=True)
    inverse = lax.rsqrt(jnp.mean(centered * centered, axis=1, keepdims=True) + epsilon)
    hidden = (centered * inverse * gain_ref[...]).astype(bf16)
    own = wq_ref.shape[1]
    hidden_ref[...] = hidden.T
    for t, weight in enumerate((wq_ref, wk_ref, wv_ref)):
        qkv_ref[:, t * own : (t + 1) * own] = jnp.dot(
            hidden, weight[...], preferred_element_type=f32
        ).astype(bf16)

    @pl.when(pl.program_id(0) == member[0])
    def _():
        resid_ref[...] = resid
        att_ref[...] = att


def front(member, bucket, pixels, key_rows, values_t, agg_out, lead_table, gain, attn_qkv, groups):
    width = agg_out.shape[0]
    own = width // groups
    channels, seq = pixels.shape[1:]
    rows = seq // groups
    spec = pltpu.PrefetchScalarGridSpec(
        num_scalar_prefetch=2,
        grid=(groups,),
        in_specs=[
            pl.BlockSpec((PIX, channels, rows), lambda i, m, l: (0, 0, i)),
            pl.BlockSpec(key_rows.shape, lambda i, m, l: (0, 0, 0)),
            pl.BlockSpec(values_t.shape, lambda i, m, l: (0, 0)),
            pl.BlockSpec(agg_out.shape, lambda i, m, l: (0, 0)),
            pl.BlockSpec(lead_table.shape, lambda i, m, l: (0, 0)),
            pl.BlockSpec((1, width), lambda i, m, l: (0, 0)),
            pl.BlockSpec((width, own), lambda i, m, l: (0, m[0])),
            pl.BlockSpec((width, own), lambda i, m, l: (0, groups + m[0])),
            pl.BlockSpec((width, own), lambda i, m, l: (0, 2 * groups + m[0])),
        ],
        out_specs=[
            pl.BlockSpec((width, rows), lambda i, m, l: (0, i)),
            pl.BlockSpec((rows, 3 * own), lambda i, m, l: (i, 0)),
            pl.BlockSpec((rows, width), lambda i, m, l: (0, 0)),
            pl.BlockSpec((width, rows), lambda i, m, l: (0, 0)),
        ],
        scratch_shapes=[pltpu.VMEM((width, rows), bf16)],
    )
    return pl.pallas_call(
        front_kernel,
        grid_spec=spec,
        out_shape=[
            jax.ShapeDtypeStruct((width, seq), bf16),
            jax.ShapeDtypeStruct((seq, 3 * own), bf16),
            jax.ShapeDtypeStruct((rows, width), f32),
            jax.ShapeDtypeStruct((width, rows), bf16),
        ],
        cost_estimate=LIGHT,
        name="front",
    )(member, bucket, pixels, key_rows, values_t, agg_out, lead_table, gain, attn_qkv, attn_qkv, attn_qkv)


def attend_kernel(member, q_ref, k_ref, v_ref, mixed_ref, lse_ref):
    rows = q_ref.shape[0]
    lane = lax.broadcasted_iota(jnp.int32, (1, 2 * HEAD_DIM), 1)
    queries = q_ref[...] * jnp.asarray(0.125, bf16)
    mixed = jnp.zeros((rows, 2 * HEAD_DIM), f32)
    seq = k_ref.shape[0]
    for part in range(2):
        keep = (lane // HEAD_DIM) == part
        query = jnp.where(keep, queries, jnp.zeros_like(queries))
        top = total = out = None
        for span in (slice(0, seq // 2), slice(seq // 2, seq)):
            scores = lax.dot_general(query, k_ref[span, :], NT, preferred_element_type=f32)
            peak = jnp.max(scores, axis=1, keepdims=True)
            if top is not None:
                peak = jnp.maximum(peak, top)
            soft = jnp.exp(scores - peak)
            weight = jnp.sum(soft, axis=1, keepdims=True)
            value = jnp.dot(soft.astype(bf16), v_ref[span, :], preferred_element_type=f32)
            if top is None:
                total, out = weight, value
            else:
                scale = jnp.exp(top - peak)
                total, out = total * scale + weight, out * scale + value
            top = peak
        mixed = jnp.where(keep, out * (1.0 / total), mixed)
        lse = jnp.broadcast_to(top + jnp.log(total), (rows, 2 * HEAD_DIM))
        lse_ref[0, part : part + 1, :] = lse.T[0:1, :]
    mixed_ref[...] = mixed.astype(bf16)


def attend(member, qkv, slot, rows, block):
    seq = qkv.shape[0]
    pair = 2 * HEAD_DIM
    pairs = qkv.shape[1] // (3 * pair)
    steps = rows // block
    spec = pltpu.PrefetchScalarGridSpec(
        num_scalar_prefetch=1,
        grid=(pairs, steps),
        in_specs=[
            pl.BlockSpec((block, pair), lambda p, i, m: ((m[0] ^ slot) * steps + i, p)),
            pl.BlockSpec((seq, pair), lambda p, i, m: (0, pairs + p)),
            pl.BlockSpec((seq, pair), lambda p, i, m: (0, 2 * pairs + p)),
        ],
        out_specs=[
            pl.BlockSpec((block, pair), lambda p, i, m: (i, p)),
            pl.BlockSpec((1, 2, block), lambda p, i, m: (p, 0, i)),
        ],
    )
    return pl.pallas_call(
        attend_kernel,
        grid_spec=spec,
        out_shape=[
            jax.ShapeDtypeStruct((rows, pairs * pair), bf16),
            jax.ShapeDtypeStruct((pairs, 2, rows), f32),
        ],
        cost_estimate=LIGHT,
        name="attend",
    )(member, qkv, qkv, qkv)


def attend_back_kernel(member, q_ref, k_ref, v_ref, g_ref, *refs, chunk, groups):
    mixed_refs, lse_refs = refs[:groups], refs[groups : 2 * groups]
    out_ref, dk_acc, dv_acc, kt = refs[2 * groups :]
    i = pl.program_id(0)
    slot = i ^ member[0]
    mixed, lse_rows = mixed_refs[0][...], lse_refs[0][0]
    for k in range(1, groups):
        mixed = jnp.where(slot == k, mixed_refs[k][...], mixed)
        lse_rows = jnp.where(slot == k, lse_refs[k][0], lse_rows)
    block = q_ref.shape[0]
    seq = k_ref.shape[0]
    pair = 2 * HEAD_DIM
    lane = lax.broadcasted_iota(jnp.int32, (1, pair), 1)
    side = lax.broadcasted_iota(jnp.int32, (pair, 1), 0)

    @pl.when(i == 0)
    def _():
        dk_acc[...] = jnp.zeros_like(dk_acc)
        dv_acc[...] = jnp.zeros_like(dv_acc)
        kt[...] = k_ref[...].T

    queries = q_ref[...] * jnp.asarray(0.125, bf16)
    grads = g_ref[...]
    product = (grads.astype(f32) * mixed.astype(f32)).T
    grad_query = jnp.zeros((pair, block), f32)
    for part in range(2):
        keep = (lane // HEAD_DIM) == part
        query = jnp.where(keep, queries, jnp.zeros_like(queries))
        grad = jnp.where(keep, grads, jnp.zeros_like(grads))
        delta = jnp.sum(product[part * HEAD_DIM : (part + 1) * HEAD_DIM], axis=0, keepdims=True)
        lse = lse_rows[part : part + 1, :]
        total = jnp.zeros((pair, block), f32)
        for at in range(0, seq, chunk):
            span = pl.ds(at, chunk)
            scores = lax.dot_general(k_ref[span, :], query, NT, preferred_element_type=f32)
            soft = jnp.exp(scores - lse)
            through = lax.dot_general(v_ref[span, :], grad, NT, preferred_element_type=f32)
            grad_scores = (soft * (through - delta)).astype(bf16)
            dv_acc[span, :] += jnp.dot(soft.astype(bf16), grad, preferred_element_type=f32)
            dk_acc[span, :] += jnp.dot(grad_scores, query, preferred_element_type=f32)
            total += jnp.dot(kt[:, span], grad_scores, preferred_element_type=f32)
        grad_query = jnp.where((side // HEAD_DIM) == part, total, grad_query)
    out_ref[pl.ds(pl.multiple_of(i * block, block), block), 0:pair] = (grad_query.T * 0.125).astype(bf16)

    @pl.when(i == pl.num_programs(0) - 1)
    def _():
        out_ref[:, pair : 2 * pair] = dk_acc[...].astype(bf16)
        out_ref[:, 2 * pair : 3 * pair] = dv_acc[...].astype(bf16)


def attend_back(member, qkv, grads, mixed, lse, which, chunk):
    seq = qkv.shape[0]
    groups = len(mixed)
    rows = seq // groups
    pair = 2 * HEAD_DIM
    pairs = qkv.shape[1] // (3 * pair)
    spec = pltpu.PrefetchScalarGridSpec(
        num_scalar_prefetch=1,
        grid=(groups,),
        in_specs=[
            pl.BlockSpec((rows, pair), lambda i, m: (i, which)),
            pl.BlockSpec((seq, pair), lambda i, m: (0, pairs + which)),
            pl.BlockSpec((seq, pair), lambda i, m: (0, 2 * pairs + which)),
            pl.BlockSpec((rows, pair), lambda i, m: (i, which)),
        ]
        + [pl.BlockSpec((rows, pair), lambda i, m: (0, which))] * groups
        + [pl.BlockSpec((1, 2, rows), lambda i, m: (which, 0, 0))] * groups,
        out_specs=pl.BlockSpec((seq, 3 * pair), lambda i, m: (0, 0)),
        scratch_shapes=[pltpu.VMEM((seq, pair), f32), pltpu.VMEM((seq, pair), f32), pltpu.VMEM((pair, seq), bf16)],
    )
    return pl.pallas_call(
        partial(attend_back_kernel, chunk=min(chunk, seq), groups=groups),
        grid_spec=spec,
        out_shape=jax.ShapeDtypeStruct((seq, 3 * pair), bf16),
        cost_estimate=LIGHT,
        name="attend_back",
    )(member, qkv, qkv, qkv, grads, *mixed, *lse)


def put_tail(tail, values, span):
    groups = len(ORDER)
    channels = values.shape[0] // ((PIX + 1) * groups)
    stride = tail.shape[0] // groups
    for at, k in enumerate(ORDER):
        for c in range(PIX + 1):
            row, source = at * stride + c * channels, (c * groups + k) * channels
            tail[row : row + channels, span] = values[source : source + channels]


def aggregate_back_kernel(
    member, core, bucket, pixel_ref, key_ref, value_ref, grad_ref, bias_ref, gain2_ref, gain1_ref, sum_ref,
    field_ref, keep_ref, send_ref, tail
):
    count, rows = pixel_ref.shape[1:]
    pair = 2 * HEAD_DIM
    pixels = [pixel_ref[c] for c in range(PIX)]
    lane = lax.broadcasted_iota(jnp.int32, (1, pair), 1)
    side = lax.broadcasted_iota(jnp.int32, (pair, 1), 0)
    field = [jnp.zeros((count, rows), f32) for _ in range(PIX)]
    keys = [jnp.zeros((count, pair), f32) for _ in range(PIX + 1)]
    for which in range(HEADS // 2):
        span = slice(which * pair, (which + 1) * pair)
        values, grads = value_ref[:, span], grad_ref[span, :]
        total = jnp.zeros(((PIX + 1) * count, pair), f32)
        for part in range(2):
            head = which * 2 + part
            grad = jnp.where((side // HEAD_DIM) == part, grads, jnp.zeros_like(grads))
            through = jnp.dot(values, grad, preferred_element_type=f32)
            kinds = [through[c * count : (c + 1) * count] for c in range(PIX + 1)]
            soft = head_weights(pixels, key_ref, head)
            grad_soft = kinds[PIX]
            for c in range(PIX):
                grad_soft = grad_soft + pixels[c] * kinds[c]
            weighed = soft * grad_soft
            grad_scores = weighed - soft * jnp.sum(weighed, axis=0, keepdims=True)
            for c in range(PIX):
                field[c] = field[c] + soft * kinds[c] + grad_scores * key_ref[c, :, head : head + 1]
                keys[c] = jnp.where(lane == head, jnp.sum(grad_scores * pixels[c], axis=1, keepdims=True), keys[c])
            keys[PIX] = jnp.where(lane == head, jnp.sum(grad_scores, axis=1, keepdims=True), keys[PIX])
            total = total + lax.dot_general(weighted_pixels(soft, pixels), grad, NT, preferred_element_type=f32)
        put_tail(tail, total, span)
    for c in range(PIX):
        field_ref[c] = field[c].astype(bf16)
    width = value_ref.shape[1]
    put_tail(tail, jnp.concatenate(keys, axis=0), slice(width, width + pair))
    groups = len(ORDER)
    stride = tail.shape[0] // groups
    own, lines = width // groups, LEADS // groups
    for at, k in enumerate(ORDER):
        owner = member[0] ^ k
        start = (at + 1) * stride - FREE
        tail[start : start + FREE, :] = jnp.zeros((FREE, tail.shape[1]), f32)
        tail[start : start + 1, :width] = bias_ref[:, pl.ds(pl.multiple_of(owner * width, width), width)]
        chunk = pl.ds(pl.multiple_of(owner * own, own), own)
        tail[start + 1 : start + 2, :own] = gain2_ref[:, chunk]
        tail[start + 1 : start + 2, own : 2 * own] = gain1_ref[:, chunk]
        for line in range(lines):
            hit = bucket[0] == owner * lines + line
            tail[start + 2 + line : start + 3 + line, :width] = jnp.where(hit, sum_ref[...], 0.0)
    half = width // 2
    for ref, which in ((keep_ref, core[0]), (send_ref, 1 - core[0])):
        ref[:, :half] = tail[:, pl.ds(pl.multiple_of(which * half, half), half)].astype(bf16)
        ref[:, half:] = tail[:, width:].astype(bf16)


def aggregate_back(member, core, bucket, pixels, key_rows, values, grads, small, groups):
    count, seq = pixels.shape[1:]
    rows = seq // groups
    width = values.shape[1]
    deep = (PIX + 1) * count + FREE * groups
    wide = width // 2 + 2 * HEAD_DIM

    def whole(*shape):
        return pl.BlockSpec(shape, lambda i, *_: (0,) * len(shape))

    spec = pltpu.PrefetchScalarGridSpec(
        num_scalar_prefetch=3,
        grid=(1,),
        in_specs=[
            pl.BlockSpec((PIX, count, rows), lambda i, m, c, l: (0, 0, m[0])),
            whole(*key_rows.shape),
            whole(*values.shape),
            whole(*grads.shape),
            *[whole(*value.shape) for value in small],
        ],
        out_specs=[whole(PIX, count, rows), whole(deep, wide), whole(deep, wide)],
        scratch_shapes=[pltpu.VMEM((deep, width + 2 * HEAD_DIM), f32)],
    )
    return pl.pallas_call(
        aggregate_back_kernel,
        grid_spec=spec,
        out_shape=[
            jax.ShapeDtypeStruct((PIX, count, rows), bf16),
            jax.ShapeDtypeStruct((deep, wide), bf16),
            jax.ShapeDtypeStruct((deep, wide), bf16),
        ],
        cost_estimate=LIGHT,
        name="aggregate_back",
    )(member, core, bucket, pixels, key_rows, values, grads, *small)


def shape_of(*dims, kind=bf16):
    return jax.ShapeDtypeStruct(dims, kind)


def inner_kernel(
    member, core, mixed0, mixed1, mixed2, mixed3, wo_ref, resid_ref, gain_ref, w1_ref, b1_ref, ga_ref,
    act_ref, act_t_ref, send_ref, keep_ref, bias_ref, one_ref, hidden_ref, mixed_ref, hidden,
):
    j = pl.program_id(0)
    parts = (mixed0, mixed1, mixed2, mixed3)
    rows, own = mixed0.shape

    @pl.when(j == 0)
    def _():
        resid = resid_ref[...]
        for slot, part in enumerate(parts):
            owner = pl.ds(pl.multiple_of((member[0] ^ slot) * own, own), own)
            resid = resid + jnp.dot(part[...], wo_ref[owner, :], preferred_element_type=f32)
        one_ref[...] = resid
        centered = resid - jnp.mean(resid, axis=1, keepdims=True)
        scale = lax.rsqrt(jnp.mean(centered * centered, axis=1, keepdims=True) + epsilon)
        hidden[...] = (centered * scale * gain_ref[...]).astype(bf16)
        piece = own // 2
        for at, (slot, side) in enumerate(BLOCKS):
            start = pl.multiple_of((member[0] ^ slot) * own + side * piece, piece)
            hidden_ref[at * piece : (at + 1) * piece, :] = hidden[:, pl.ds(start, piece)].T
            mixed_ref[at * piece : (at + 1) * piece, :] = parts[slot][:, side * piece : (side + 1) * piece].T

    inner = jnp.dot(hidden[...], w1_ref[...], preferred_element_type=f32) + b1_ref[...]
    below = 0.5 + 0.5 * lax.erf(inner * 0.7071067811865476)
    act = (inner * below).astype(bf16)
    slope = below + inner * (jnp.exp(-0.5 * inner * inner) * 0.3989422804014327)
    gu = (slope * ga_ref[...].astype(f32)).astype(bf16)
    act_ref[...] = act
    act_t_ref[...] = act.T
    bias_ref[...] = jnp.sum(gu.astype(f32), axis=0, keepdims=True)

    @pl.when(j < len(parts))
    def _():
        send_ref[...] = gu

    @pl.when(j >= len(parts))
    def _():
        keep_ref[...] = gu


def inner_part(member, core, mixed, attn_out, resid, gain, mlp_in, bias, grad_act):
    rows, width = resid.shape
    inner = mlp_in.shape[1]
    groups = len(mixed)
    own = width // groups
    steps = 2 * groups
    block = inner // steps

    def natural(j, c):
        return ((j // groups) ^ (1 - c[0])) * groups + j % groups

    def spot(j, m, c):
        n = natural(j, c)
        slot = (n // 2) ^ m[0]
        return (jnp.where(n % 2 == 0, slot, 4 + (slot % 2) * 2 + slot // 2), 0)

    def whole(*shape):
        return pl.BlockSpec(shape, lambda j, m, c: (0,) * len(shape))

    def column(deep):
        return pl.BlockSpec((deep, block), lambda j, m, c: (0, natural(j, c)))

    spec = pltpu.PrefetchScalarGridSpec(
        num_scalar_prefetch=2,
        grid=(steps,),
        in_specs=[whole(rows, own)] * groups
        + [whole(width, width), whole(rows, width), whole(1, width)]
        + [column(width), column(1), column(rows)],
        out_specs=[
            column(rows),
            pl.BlockSpec((block, rows), spot),
            pl.BlockSpec((rows, block), lambda j, m, c: (0, jnp.minimum(j, groups - 1))),
            pl.BlockSpec((rows, block), lambda j, m, c: (0, jnp.maximum(j - groups, 0))),
            column(1),
            whole(rows, width),
            whole(width, rows),
            whole(width, rows),
        ],
        scratch_shapes=[pltpu.VMEM((rows, width), bf16)],
    )
    return pl.pallas_call(
        inner_kernel,
        grid_spec=spec,
        out_shape=[shape_of(rows, inner), shape_of(inner, rows)]
        + [shape_of(rows, inner // 2)] * 2
        + [shape_of(1, inner, kind=f32), shape_of(rows, width, kind=f32)]
        + [shape_of(width, rows)] * 2,
        cost_estimate=LIGHT,
        name="inner_part",
    )(member, core, *mixed, attn_out, resid, gain, mlp_in, bias, grad_act)


def outer_kernel(
    core, act_ref, send_ref, keep_ref, w1_ref, w2_ref, wo_ref, one_ref, gain_ref, g_ref,
    out_ref, gres_ref, gb_ref, gb_send_ref, gm_ref, ggain_ref, branch, grads,
):
    j = pl.program_id(0)
    groups, rows, own = gm_ref.shape
    half = send_ref.shape[1]
    branch[j] = jnp.dot(act_ref[...], w2_ref[...], preferred_element_type=f32)

    def columns(which):
        return w1_ref[:, pl.ds(pl.multiple_of(which * half, half), half)]

    grads[j] = lax.dot_general(
        send_ref[...], columns(1 - core[0]), NT, preferred_element_type=f32
    ) + lax.dot_general(keep_ref[...], columns(core[0]), NT, preferred_element_type=f32)

    @pl.when(j == pl.num_programs(0) - 1)
    def _():
        count = branch.shape[0]
        resid = one_ref[...]
        out_ref[...] = (resid + jnp.concatenate([branch[i] for i in range(count)], axis=1)).astype(bf16)
        centered = resid - jnp.mean(resid, axis=1, keepdims=True)
        scale = lax.rsqrt(jnp.mean(centered * centered, axis=1, keepdims=True) + epsilon)
        grad, plain = jnp.concatenate([grads[i] for i in range(count)], axis=1), centered * scale
        ggain_ref[...] = jnp.sum(grad * plain, axis=0, keepdims=True)
        grad = grad * gain_ref[...]
        first = jnp.mean(grad, axis=1, keepdims=True)
        second = jnp.mean(grad * plain, axis=1, keepdims=True)
        gres = g_ref[...].astype(f32) + scale * (grad - first - plain * second)
        gres_ref[...] = gres
        gb_ref[...] = gres.astype(bf16)
        width = gb_ref.shape[1]
        gb_send_ref[...] = gb_ref[:, pl.ds(pl.multiple_of((1 - core[0]) * (width // 2), width // 2), width // 2)]
        gb = gb_ref[...]
        for p in range(groups):
            gm_ref[p] = lax.dot_general(gb, wo_ref[p * own : (p + 1) * own, :], NT, preferred_element_type=f32).astype(
                bf16
            )


def outer_part(core, act, gu_send, gu_keep, mlp_in, mlp_out, attn_out, resid, gain, grad_out, groups):
    rows, width = resid.shape
    inner = mlp_in.shape[1]
    own = width // groups
    steps = 4
    block = width // steps

    def whole(*shape):
        return pl.BlockSpec(shape, lambda j, c: (0,) * len(shape))

    spec = pltpu.PrefetchScalarGridSpec(
        num_scalar_prefetch=1,
        grid=(steps,),
        in_specs=[
            whole(rows, inner),
            whole(rows, inner // 2),
            whole(rows, inner // 2),
            pl.BlockSpec((block, inner), lambda j, c: (j, 0)),
            pl.BlockSpec((inner, block), lambda j, c: (0, j)),
            whole(width, width),
            whole(rows, width),
            whole(1, width),
            whole(rows, width),
        ],
        out_specs=[
            whole(rows, width),
            whole(rows, width),
            whole(rows, width),
            whole(rows, width // 2),
            whole(groups, rows, own),
            whole(1, width),
        ],
        scratch_shapes=[pltpu.VMEM((steps, rows, block), f32), pltpu.VMEM((steps, rows, block), f32)],
    )
    return pl.pallas_call(
        outer_kernel,
        grid_spec=spec,
        out_shape=[
            shape_of(rows, width),
            shape_of(rows, width, kind=f32),
            shape_of(rows, width),
            shape_of(rows, width // 2),
            shape_of(groups, rows, own),
            shape_of(1, width, kind=f32),
        ],
        cost_estimate=LIGHT,
        name="outer_part",
    )(core, act, gu_send, gu_keep, mlp_in, mlp_out, attn_out, resid, gain, grad_out)


def both_dots(left, left_other, right, right_other):
    return jnp.dot(left[...], right[...], preferred_element_type=f32) + jnp.dot(
        left_other[...], right_other[...], preferred_element_type=f32
    )


def out_grad_kernel(core, left, left_other, right, right_other, *outs):
    total = both_dots(left, left_other, right, right_other).astype(bf16)
    for q, out in enumerate(outs):

        @pl.when(pl.program_id(0) == q)
        def _():
            out[...] = total


def out_grad(core, left, left_other, right, right_other):
    rows, deep = left.shape
    half = right.shape[1] // 2
    block = rows // 4

    spec = pltpu.PrefetchScalarGridSpec(
        num_scalar_prefetch=1,
        grid=(4,),
        in_specs=[pl.BlockSpec((block, deep), lambda i, c: (i, 0))] * 2
        + [
            pl.BlockSpec((deep, half), lambda i, c: (0, c[0])),
            pl.BlockSpec((deep, half), lambda i, c: (0, 0)),
        ],
        out_specs=[pl.BlockSpec((block, half), lambda i, c: (0, 0)) for q in range(4)],
    )
    return pl.pallas_call(
        out_grad_kernel,
        grid_spec=spec,
        out_shape=[shape_of(rows // 4, half)] * 4,
        cost_estimate=LIGHT,
        name="out_grad",
    )(core, left, left_other, right, right_other)


def in_grad_kernel(core, high, h, h_other, u, u_other, m, m_other, b, b_other, keep, send):
    units = u.shape[1]
    first = both_dots(h, h_other, u, u_other).astype(bf16)
    last = both_dots(m, m_other, b, b_other).astype(bf16)
    for number, out in enumerate((send, keep)):

        @pl.when(pl.program_id(0) == number)
        def _():
            out[:, :units] = first
            out[:, units:] = last


def in_grad(core, high, h, h_other, u, u_other, m, m_other, b, b_other):
    rows, deep = h.shape
    units, branch = u.shape[1] // 2, b_other.shape[1] // 2

    def whole(*shape):
        return pl.BlockSpec(shape, lambda i, c, z: (0,) * len(shape))

    def side(i, c, z):
        return (0, z[0] ^ (1 - i))

    def core_side(i, c, z):
        return (0, 2 * c[0] + (z[0] ^ (1 - i)))

    spec = pltpu.PrefetchScalarGridSpec(
        num_scalar_prefetch=2,
        grid=(2,),
        in_specs=[
            whole(rows, deep),
            whole(rows, deep),
            pl.BlockSpec((deep, units), side),
            pl.BlockSpec((deep, units), side),
            whole(rows, deep),
            whole(rows, deep),
            pl.BlockSpec((deep, branch), core_side),
            pl.BlockSpec((deep, branch), side),
        ],
        out_specs=[whole(rows, units + branch)] * 2,
    )
    return pl.pallas_call(
        in_grad_kernel,
        grid_spec=spec,
        out_shape=[shape_of(rows, units + branch)] * 2,
        cost_estimate=LIGHT,
        name="in_grad",
    )(core, high, h, h_other, u, u_other, m, m_other, b, b_other)


def qkv_grad_kernel(core, h, h_other, *refs):
    out = refs[-1]
    for which in range(2):

        @pl.when(core[0] == which)
        def _():
            out[...] = both_dots(h, h_other, refs[which], refs[2 + which]).astype(bf16)


def qkv_grad(core, h, h_other, grads, others):
    rows, deep = h.shape
    cols = grads[0].shape[1]
    block = rows // 2
    spec = pltpu.PrefetchScalarGridSpec(
        num_scalar_prefetch=1,
        grid=(2,),
        in_specs=[pl.BlockSpec((block, deep), lambda i, c: (i, 0))] * 2
        + [pl.BlockSpec((deep, cols), lambda i, c: (0, 0))] * 4,
        out_specs=pl.BlockSpec((block, cols), lambda i, c: (i, 0)),
    )
    return pl.pallas_call(
        qkv_grad_kernel,
        grid_spec=spec,
        out_shape=shape_of(rows, cols),
        cost_estimate=LIGHT,
        name="qkv_grad",
    )(core, h, h_other, *grads, *others)


def last_grad_kernel(core, qkv_ref, a, a_other, g, g_other, out):
    cols = qkv_ref.shape[1]
    out[0, :, :cols] = qkv_ref[...]
    out[0, :, cols:] = both_dots(a, a_other, g, g_other).astype(bf16)


def last_grad(core, weight_qkv, att, att_other, grad, grad_other, groups):
    rows, deep = att.shape
    half = grad_other.shape[1]
    cols = weight_qkv.shape[1]
    block = rows // groups
    spec = pltpu.PrefetchScalarGridSpec(
        num_scalar_prefetch=1,
        grid=(groups,),
        in_specs=[
            pl.BlockSpec((block, cols), lambda i, c: (i, 0)),
            pl.BlockSpec((block, deep), lambda i, c: (i, 0)),
            pl.BlockSpec((block, deep), lambda i, c: (i, 0)),
            pl.BlockSpec((deep, half), lambda i, c: (0, c[0])),
            pl.BlockSpec((deep, half), lambda i, c: (0, 0)),
        ],
        out_specs=pl.BlockSpec((1, block, cols + half), lambda i, c: (i, 0, 0)),
    )
    return pl.pallas_call(
        last_grad_kernel,
        grid_spec=spec,
        out_shape=shape_of(groups, block, cols + half),
        cost_estimate=LIGHT,
        name="last_grad",
    )(core, weight_qkv, att, att_other, grad, grad_other)


def join_kernel(core, first_ref, second_ref, wq, wk, wv, resid_ref, gain_ref, gres_ref, out_ref, *refs):
    ga_ref, ga_send_ref, gatt_ref, ggain_ref, sum_ref, total = refs
    i = pl.program_id(0)
    pair = 2 * HEAD_DIM

    @pl.when(i == 0)
    def _():
        total[...] = jnp.zeros_like(total)

    spans = [slice(t * pair, (t + 1) * pair) for t in range(3)]
    left = jnp.concatenate([ref[:, span] for span in spans for ref in (first_ref, second_ref)], axis=1)
    weights = jnp.concatenate([wq[...], wk[...], wv[...]], axis=1)
    total[...] += lax.dot_general(left, weights, NT, preferred_element_type=f32)

    @pl.when(i == pl.num_programs(0) - 1)
    def _():
        resid = resid_ref[...]
        centered = resid - jnp.mean(resid, axis=1, keepdims=True)
        scale = lax.rsqrt(jnp.mean(centered * centered, axis=1, keepdims=True) + epsilon)
        plain = centered * scale
        grad = total[...]
        ggain_ref[...] = jnp.sum(grad * plain, axis=0, keepdims=True)
        grad = grad * gain_ref[...]
        first = jnp.mean(grad, axis=1, keepdims=True)
        second = jnp.mean(grad * plain, axis=1, keepdims=True)
        gres = gres_ref[...] + scale * (grad - first - plain * second)
        sum_ref[...] = jnp.sum(gres, axis=0, keepdims=True)
        ga = gres.astype(bf16)
        ga_ref[...] = ga
        half = ga_send_ref.shape[1]
        ga_send_ref[...] = ga_ref[:, pl.ds(pl.multiple_of((1 - core[0]) * half, half), half)]
        gatt_ref[...] = lax.dot_general(out_ref[...], ga, NT, preferred_element_type=f32).astype(bf16)


def join(core, first, second, attn_qkv, resid, gain, gres, agg_out):
    rows, width = resid.shape
    groups = first.shape[0] // rows
    own = width // groups
    cols = first.shape[1]

    def whole(*shape):
        return pl.BlockSpec(shape, lambda i, c: (0,) * len(shape))

    spec = pltpu.PrefetchScalarGridSpec(
        num_scalar_prefetch=1,
        grid=(groups,),
        in_specs=[
            pl.BlockSpec((rows, cols), lambda i, c: (i, 0)),
            pl.BlockSpec((rows, cols), lambda i, c: (i, 0)),
            pl.BlockSpec((width, own), lambda i, c: (0, i)),
            pl.BlockSpec((width, own), lambda i, c: (0, groups + i)),
            pl.BlockSpec((width, own), lambda i, c: (0, 2 * groups + i)),
            whole(rows, width),
            whole(1, width),
            whole(rows, width),
            whole(width, width),
        ],
        out_specs=[
            whole(rows, width),
            whole(rows, width // 2),
            whole(width, rows),
            whole(1, width),
            whole(1, width),
        ],
        scratch_shapes=[pltpu.VMEM((rows, width), f32)],
    )
    return pl.pallas_call(
        join_kernel,
        grid_spec=spec,
        out_shape=[
            shape_of(rows, width),
            shape_of(rows, width // 2),
            shape_of(width, rows),
            shape_of(1, width, kind=f32),
            shape_of(1, width, kind=f32),
        ],
        cost_estimate=LIGHT,
        name="join",
    )(core, first, second, attn_qkv, attn_qkv, attn_qkv, resid, gain, gres, agg_out)


def add(a, b):
    return (a.astype(f32) + b.astype(f32)).astype(bf16)


def split_add(a, b, count):
    deep = a.shape[0] // count
    return [add(a[i * deep : (i + 1) * deep], b[i * deep : (i + 1) * deep]) for i in range(count)]


def pick_add(a, b, which, axis):
    half = a.shape[axis] // 2
    return add(
        lax.dynamic_slice_in_dim(a, which * half, half, axis), lax.dynamic_slice_in_dim(b, which * half, half, axis)
    )


def whole_blocks(shapes):
    return [pl.BlockSpec(shape, lambda i, *_, n=len(shape): (0,) * n) for shape in shapes]


def choose_kernel(high, a, b, c, d, keep, send):
    for value, (first, second) in enumerate(((keep, send), (send, keep))):

        @pl.when(high[0] == value)
        def _():
            first[...] = add(a[...], b[...])
            second[...] = add(c[...], d[...])


def choose(high, a, b, c, d):
    rows, cols = a.shape
    block = pl.BlockSpec((rows // 2, cols), lambda i, z: (i, 0))
    return pl.pallas_call(
        choose_kernel,
        grid_spec=pltpu.PrefetchScalarGridSpec(
            num_scalar_prefetch=1, grid=(2,), in_specs=[block] * 4, out_specs=[block] * 2
        ),
        out_shape=[jax.ShapeDtypeStruct(a.shape, bf16)] * 2,
        cost_estimate=LIGHT,
        name="choose",
    )(high, a, b, c, d)


def gather_sources_kernel(high, came_ref, keep, send, *, cols):
    groups, half = came_ref.shape[0], keep.shape[0]
    for out, which in ((keep, high[0]), (send, 1 - high[0])):
        span = pl.ds(pl.multiple_of(which * half, half), half)
        total = jnp.zeros((half, came_ref.shape[2] - cols), f32)
        for p in range(groups):
            out[:, p * cols : (p + 1) * cols] = came_ref[p, span, :cols]
            total = total + came_ref[p, span, cols:].astype(f32)
        out[:, groups * cols :] = total.astype(bf16)


def gather_sources(high, came, cols):
    groups, rows, wide = came.shape
    shape = (rows // 2, groups * cols + wide - cols)
    spec = pltpu.PrefetchScalarGridSpec(
        num_scalar_prefetch=1, grid=(1,), in_specs=whole_blocks([came.shape]), out_specs=whole_blocks([shape] * 2)
    )
    return pl.pallas_call(
        partial(gather_sources_kernel, cols=cols),
        grid_spec=spec,
        out_shape=[jax.ShapeDtypeStruct(shape, bf16)] * 2,
        cost_estimate=LIGHT,
        name="gather_sources",
    )(high, came)


def turned(i, levels):
    total = 0
    for k in range(levels):
        total = total + (((i >> k) & 1) << (levels - 1 - k))
    return total


def assemble_kernel(where, *refs, order, levels, spans, low_rows):
    pieces, outs = refs[:4], refs[4:]
    deep = pieces[0].shape[0] // len(order)
    for number, ref in enumerate(pieces):
        core = where[1] if number < 2 else 1 - where[1]
        for at, bits in enumerate(order):
            chip = where[0] ^ (bits ^ (number % 2))
            low = low_bit(chip, levels)
            row = turned(chip >> 1, levels - 1)
            if low_rows:
                row = row + (low << (levels - 1))
            to = pl.ds(pl.multiple_of(row * deep, deep), deep)
            for out, source, size, base, by_core, by_low in spans:
                column = pl.multiple_of(base + core * by_core + low * by_low, 128)
                outs[out][to, pl.ds(column, size)] = ref[at * deep : (at + 1) * deep, source : source + size].astype(f32)


def assemble(where, pieces, levels, spans, widths, low_rows=True):
    order = [0]
    for bit in range(levels - 1, 0, -1):
        order = order + [bits ^ (3 if mirrored(levels) else 1 << bit) for bits in order]
    rows = pieces[0].shape[0] * (2 if low_rows else 1)
    shapes = [(rows, wide) for wide in widths]
    spec = pltpu.PrefetchScalarGridSpec(
        num_scalar_prefetch=1,
        grid=(1,),
        in_specs=whole_blocks([p.shape for p in pieces]),
        out_specs=whole_blocks(shapes),
    )
    return pl.pallas_call(
        partial(assemble_kernel, order=tuple(order), levels=levels, spans=tuple(spans), low_rows=low_rows),
        grid_spec=spec,
        out_shape=[shape_of(*shape, kind=f32) for shape in shapes],
        cost_estimate=LIGHT,
        name="assemble",
    )(where, *pieces)


def field_kernel(member, *refs):
    pieces, out = refs[:-1], refs[-1]
    kinds, channels, rows = pieces[0].shape
    for k, piece in enumerate(pieces):
        at = pl.ds(pl.multiple_of((member[0] ^ k) * rows, rows), rows)
        for c in range(kinds):
            out[:, c, at] = piece[c].astype(f32)


def place_field(member, pieces):
    kinds, channels, rows = pieces[0].shape
    shape = (channels, kinds, rows * len(pieces))
    spec = pltpu.PrefetchScalarGridSpec(
        num_scalar_prefetch=1,
        grid=(1,),
        in_specs=whole_blocks([p.shape for p in pieces]),
        out_specs=whole_blocks([shape])[0],
    )
    return pl.pallas_call(
        field_kernel, grid_spec=spec, out_shape=jax.ShapeDtypeStruct(shape, f32), name="place_field"
    )(member, *pieces)


def tail_kernel(member, *refs, groups):
    tails = refs[:groups]
    stacked_ref, pick_ref, value_ref, qk_ref, key_ref, query_ref = refs[groups : groups + 6]
    gvalue_ref, gkey_ref, gquery_ref, patch_ref, table_ref, gqk = refs[groups + 6 :]
    width = value_ref.shape[0]
    own = gvalue_ref.shape[0]
    at = pl.ds(pl.multiple_of(member[0] * own, own), own)
    tail = jnp.concatenate([t[...] for t in tails], axis=0)
    values, keys = tail[:, :width], tail[:, width:]
    gvalue_ref[...] = lax.dot_general(stacked_ref[:, at], values, TN, preferred_element_type=f32)
    gqk[...] = lax.dot_general(stacked_ref[...], keys, TN, preferred_element_type=f32)
    head = lax.broadcasted_iota(jnp.int32, (keys.shape[1], width), 0)
    column = lax.broadcasted_iota(jnp.int32, (keys.shape[1], width), 1) // HEAD_DIM
    spread = jnp.where(head == column, 1.0, 0.0)
    gkey_ref[...] = (
        jnp.dot(gqk[at, :], spread, precision=highest, preferred_element_type=f32) * (query_ref[...] * 0.125)
    )
    by_head = lax.dot_general(gqk[...], key_ref[...].astype(f32), TN, precision=highest, preferred_element_type=f32)
    head = lax.broadcasted_iota(jnp.int32, by_head.shape, 0)
    column = (lax.broadcasted_iota(jnp.int32, by_head.shape, 1) + member[0] * own) // HEAD_DIM
    gquery_ref[...] = jnp.sum(jnp.where(head == column, by_head, 0.0), axis=0, keepdims=True) * 0.125
    own_rows = tails[0].shape[0]
    table = jnp.dot(pick_ref[...], tail, preferred_element_type=f32).astype(bf16)
    rows = jnp.concatenate([tail[:own_rows], table], axis=0)
    total = lax.dot_general(rows[:, :width], value_ref[...], NT, preferred_element_type=f32) + lax.dot_general(
        rows[:, width:].astype(f32), qk_ref[...], NT, precision=highest, preferred_element_type=f32
    )
    channels = patch_ref.shape[0]
    for c in range(PIX):
        patch_ref[:, c, :] = total[c * channels : (c + 1) * channels]
    table_ref[...] = total[own_rows : own_rows + table_ref.shape[0]]


def finish_tail(member, tails, stacked, pick, agg_value, query_keys, agg_key, agg_query, channels, lines):
    groups = len(tails)
    width = agg_value.shape[0]
    own = width // groups
    args = [*tails, stacked, pick, agg_value, query_keys]
    spec = pltpu.PrefetchScalarGridSpec(
        num_scalar_prefetch=1,
        grid=(1,),
        in_specs=whole_blocks([x.shape for x in args])
        + [pl.BlockSpec((width, own), lambda i, m: (0, m[0])), pl.BlockSpec((1, width), lambda i, m: (0, 0))],
        out_specs=whole_blocks([(own, width), (own, width), (1, own), (channels, PIX, width), (lines, width)]),
        scratch_shapes=[pltpu.VMEM((width, query_keys.shape[1]), f32)],
    )
    return pl.pallas_call(
        partial(tail_kernel, groups=groups),
        grid_spec=spec,
        out_shape=[
            jax.ShapeDtypeStruct((own, width), f32),
            jax.ShapeDtypeStruct((own, width), f32),
            jax.ShapeDtypeStruct((1, own), f32),
            jax.ShapeDtypeStruct((channels, PIX, width), f32),
            jax.ShapeDtypeStruct((lines, width), f32),
        ],
        cost_estimate=LIGHT,
        name="finish_tail",
    )(member, *args, agg_key, agg_query)


def fence(*values):
    return lax.optimization_barrier(values)


def swap(value, axis, bits):
    size = lax.axis_size(axis)
    return lax.ppermute(value, axis, [(i, i ^ bits) for i in range(size)])


def from_all(own, groups):
    return [own] + [swap(own, "var", k) for k in range(1, groups)]


def exchange(value):
    return lax.all_to_all(value, "var", split_axis=0, concat_axis=0, tiled=True)


def chip_bits():
    bits, bit = [], 1
    while bit < lax.axis_size("chip"):
        bits.append(bit)
        bit *= 2
    return bits


def mirrored(levels):
    return levels == 2


def partner(bit):
    levels = len(chip_bits())
    return 3 if mirrored(levels) and bit == 2 else bit


def low_bit(chip, levels):
    return (chip ^ (chip >> 1)) & 1 if mirrored(levels) else chip & 1


def is_high(bit):
    chip = lax.axis_index("chip")
    return low_bit(chip, len(chip_bits())) if bit == 1 else (chip // bit) % 2


def stack_other(value, bit):
    return jnp.concatenate([value, swap(value, "chip", partner(bit))], axis=0)


def with_core(halves):
    return [*halves, *(swap(value, "core", 1) for value in halves)]


def by_core(mine, other, core):
    return jnp.where(core == 0, mine, other), jnp.where(core == 0, other, mine)


def body(
    field_patches,
    var_ids,
    lead_bucket,
    patch_weight,
    var_embed,
    agg_query,
    agg_key,
    agg_value,
    agg_out,
    lead_table,
    ln1_gain,
    attn_qkv,
    attn_out,
    ln2_gain,
    mlp_in,
    mlp_in_bias,
    mlp_out,
    cotangent,
):
    groups = lax.axis_size("var")
    member = lax.axis_index("var")
    core = lax.axis_index("core")
    channels, pixel_count, samples, seq = field_patches.shape
    width = agg_key.shape[0]
    inner_width = mlp_in.shape[1]
    leads = lead_table.shape[0]
    vocab = var_embed.shape[0]
    rows = seq // groups
    own = width // groups
    count = channels * groups
    slots = [member ^ k for k in range(groups)]
    member_one = member.reshape(1).astype(jnp.int32)
    core_one = core.reshape(1).astype(jnp.int32)
    bits = chip_bits()
    assert bits
    high = is_high(bits[0])
    high_one = high.reshape(1).astype(jnp.int32)
    half = width // 2
    gain_one = ln1_gain.astype(f32)
    gain_two = ln2_gain.astype(f32)

    mine = jnp.concatenate(
        [
            field_patches.reshape(channels, pixel_count, seq).transpose(1, 0, 2),
            patch_weight.transpose(1, 0, 2),
        ],
        axis=2,
    )
    grad_out = cotangent.reshape(rows, width)
    grad_act = lax.dot_general(grad_out, mlp_out, NT, preferred_element_type=f32).astype(bf16)
    ids = jnp.concatenate([lax.dynamic_slice_in_dim(var_ids, slot * channels, channels) for slot in slots])
    table_pick = (ids[:, None] == jnp.arange(vocab, dtype=jnp.int32)[None, :]).astype(bf16)
    head_of = jnp.arange(width, dtype=jnp.int32) // HEAD_DIM
    spread = head_of[:, None] == jnp.arange(2 * HEAD_DIM, dtype=jnp.int32)[None, :]
    query_block = jnp.where(spread, agg_query[:, None], jnp.zeros((), bf16))
    query_keys = jnp.dot(agg_key, query_block, preferred_element_type=f32) * 0.125
    grad_out_other = swap(lax.dynamic_slice_in_dim(grad_out, (1 - core) * half, half, axis=1), "core", 1)
    arrived, grad_act, table_pick, query_keys, grad_out_other = fence(
        from_all(mine, groups), grad_act, table_pick, query_keys, grad_out_other
    )
    pixels, key_rows, values, values_t, by_slot = prepare(
        arrived, table_pick, var_embed, query_keys, agg_value, seq
    )

    hidden_t, qkv, resid_zero, att_low = front(
        member_one, lead_bucket, pixels, key_rows, values_t, agg_out, lead_table, gain_one[None], attn_qkv, groups
    )

    hidden_t, att_low, qkv = fence(hidden_t, att_low, qkv)
    hidden_other, att_other = swap(hidden_t, "core", 1), swap(att_low, "core", 1)

    block = min(512, rows)
    mixed_parts, lse_parts, received = [None] * groups, [None] * groups, [None] * groups
    for k in reversed(range(groups)):
        mixed_parts[k], lse_parts[k] = attend(member_one, qkv, k, rows, block)
        if k + 1 < groups:
            received[k + 1], mixed_parts[k], qkv = fence(received[k + 1], mixed_parts[k], qkv)
            if k + 2 == groups:
                hidden_other, att_other, qkv = fence(hidden_other, att_other, qkv)
        received[k] = swap(mixed_parts[k], "var", k) if k else mixed_parts[k]

    act, act_t, gu_send, gu_keep, grad_bias, resid_one, hidden_two_t, mixed_t = inner_part(
        member_one, core_one, received, attn_out, resid_zero, gain_two[None], mlp_in, mlp_in_bias.astype(f32)[None], grad_act
    )
    gu_send, act_t, act, hidden_two_t, mixed_t = fence(gu_send, act_t, act, hidden_two_t, mixed_t)
    act_other, gu_other, hidden_two_other, mixed_other = (
        swap(value, "core", 1) for value in (act_t, gu_send, hidden_two_t, mixed_t)
    )
    output, grad_resid_one, grad_branch, branch_send, grad_mixed, grad_gain_two = outer_part(
        core_one, act, gu_send, gu_keep, mlp_in, mlp_out, attn_out, resid_one, gain_two[None], grad_out, groups
    )
    act_other, gu_other, hidden_two_other, mixed_other, grad_mixed, branch_send, output = fence(
        act_other, gu_other, hidden_two_other, mixed_other, grad_mixed, branch_send, output
    )
    output = output.reshape(samples, rows, width)

    branch_other = swap(branch_send, "core", 1)
    grad_heads = exchange(grad_mixed).reshape(seq, own)
    branch_other, act_t, act_other = fence(branch_other, act_t, act_other)
    out_y, out_y_send, out_x, out_x_send = out_grad(core_one, act_t, act_other, grad_out, grad_out_other)
    branch_other, out_y, out_y_send, out_x, out_x_send = fence(branch_other, out_y, out_y_send, out_x, out_x_send)
    in_part, in_part_send = in_grad(
        core_one,
        high_one,
        hidden_two_t,
        hidden_two_other,
        gu_keep,
        gu_other,
        mixed_t,
        mixed_other,
        grad_branch,
        branch_other,
    )
    out_y_came, out_x_came = swap(out_y_send, "var", 2), swap(out_x_send, "var", 1)
    grad_heads, in_part_send, in_part = fence(grad_heads, in_part_send, in_part)

    pair = 2 * HEAD_DIM
    pairs = own // pair
    assert pairs == 2
    in_part_came = swap(in_part_send, "chip", bits[0])
    first = attend_back(member_one, qkv, grad_heads, mixed_parts, lse_parts, 0, 512)
    first, qkv, out_y_came, out_x_came = fence(first, qkv, out_y_came, out_x_came)
    out_y, out_y_send = split_add(out_y, out_y_came, 2)
    out_x, out_x_send = split_add(out_x, out_x_came, 2)
    first, qkv, out_y_send, out_x_send = fence(first, qkv, out_y_send, out_x_send)
    first_came = exchange(first)
    first_other = swap(first, "core", 1)
    out_y_came, out_x_came = swap(out_y_send, "var", 1), swap(out_x_send, "var", 2)
    second = attend_back(member_one, qkv, grad_heads, mixed_parts, lse_parts, 1, 512)
    second_came = exchange(second)
    first_came, first_other, second, in_part_came, out_y_came, out_x_came = fence(
        first_came, first_other, second, in_part_came, out_y_came, out_x_came
    )
    second_other = swap(second, "core", 1)
    out_keep, out_send = choose(high_one, out_y, out_y_came, out_x, out_x_came)
    out_came = swap(out_send, "chip", bits[0])
    in_y, in_y_send, in_x, in_x_send = split_add(in_part, in_part_came, 4)
    second_other, in_y_send, in_x_send = fence(second_other, in_y_send, in_x_send)
    weight_qkv = qkv_grad(core_one, hidden_t, hidden_other, (first, second), (first_other, second_other))
    second_came, weight_qkv, in_y_send, in_x_send, grad_resid_one, out_came = fence(
        second_came, weight_qkv, in_y_send, in_x_send, grad_resid_one, out_came
    )
    rest = bits[1:]

    def scatter_parts(keep, came, bit):
        return [pick_add(keep, came, which, 0) for which in (is_high(bit), 1 - is_high(bit))]

    def scatter_step(keep, came, bit):
        keep, send = scatter_parts(keep, came, bit)
        return keep, swap(send, "chip", partner(bit))

    out_keep, out_send = scatter_parts(out_keep, out_came, rest[0])
    second_came, out_send, in_y_send, in_x_send = fence(second_came, out_send, in_y_send, in_x_send)
    out_came = swap(out_send, "chip", partner(rest[0]))
    in_y_came, in_x_came = swap(in_y_send, "var", 2), swap(in_x_send, "var", 1)
    grad_agg, grad_agg_send, grad_att, grad_gain_one, sample_sum = join(
        core_one, first_came, second_came, attn_qkv, resid_zero, gain_one[None], grad_resid_one, agg_out
    )
    grad_agg, grad_agg_send, grad_att, out_came, in_y_came, in_x_came = fence(
        grad_agg, grad_agg_send, grad_att, out_came, in_y_came, in_x_came
    )
    for bit in rest[1:]:
        out_keep, out_came = scatter_step(out_keep, out_came, bit)
    out_rows = add(out_keep, out_came)
    in_y, in_y_send = split_add(in_y, in_y_came, 2)
    in_x, in_x_send = split_add(in_x, in_x_came, 2)
    out_rows, grad_att, grad_agg_send, in_y_send, in_x_send = fence(
        out_rows, grad_att, grad_agg_send, in_y_send, in_x_send
    )
    out_other = swap(out_rows, "chip", partner(rest[-1]))
    grad_agg_other = swap(grad_agg_send, "core", 1)
    in_y_came, in_x_came = swap(in_y_send, "var", 1), swap(in_x_send, "var", 2)

    field_own, tail, tail_send = aggregate_back(
        member_one,
        core_one,
        lead_bucket,
        pixels,
        key_rows,
        values,
        grad_att,
        (grad_bias, grad_gain_two, grad_gain_one, sample_sum),
        groups,
    )
    tail, tail_send, grad_agg_other, in_y_came, in_x_came = fence(
        tail, tail_send, grad_agg_other, in_y_came, in_x_came
    )
    tail_came = swap(tail_send, "core", 1)
    in_own = jnp.concatenate([add(in_y, in_y_came), add(in_x, in_x_came)], axis=0)
    for bit in rest:
        in_rows = in_own.shape[0] // 2
        in_own, in_send = (
            lax.dynamic_slice_in_dim(in_own, which * in_rows, in_rows) for which in (is_high(bit), 1 - is_high(bit))
        )
        if bit != rest[-1]:
            in_own = add(in_own, swap(in_send, "chip", partner(bit)))
    in_send, grad_agg_other, tail_came = fence(in_send, grad_agg_other, tail_came)
    in_came = swap(in_send, "chip", partner(rest[-1]))
    tail = add(tail, tail_came)
    deep = tail.shape[0] // 2
    tail, grad_agg_other = fence(tail, grad_agg_other)
    tail_came = swap(tail[deep:], "var", 1)
    last_send = last_grad(core_one, weight_qkv, att_low, att_other, grad_agg, grad_agg_other, groups)
    tail, tail_came, last_send, out_other = fence(tail, tail_came, last_send, out_other)
    tail = add(tail[:deep], tail_came)
    deep //= 2
    tail_came = swap(tail[deep:], "var", 2)
    out_rows = jnp.concatenate([out_rows, out_other], axis=0)
    for bit in reversed(rest[:-1]):
        out_rows = stack_other(out_rows, bit)
    tail, tail_came, last_send, out_rows, in_came = fence(tail, tail_came, last_send, out_rows, in_came)
    last_came = exchange(last_send)
    in_rows = add(in_own, in_came)
    tail = add(tail[:deep], tail_came)
    in_rows, tail, out_rows = fence(in_rows, tail, out_rows)
    in_other = swap(in_rows, "chip", partner(rest[-1]))
    tail_came = swap(tail, "chip", bits[0])
    out_other = swap(out_rows, "chip", bits[0])
    last_came, tail, out_rows = fence(last_came, tail, out_rows)
    last_keep, last_send = gather_sources(high_one, last_came, 3 * pair)
    last_send, tail, tail_came, in_other = fence(last_send, tail, tail_came, in_other)
    last_came = swap(last_send, "chip", bits[0])
    tail = add(tail, tail_came)
    for bit in rest:
        tail_came = swap(tail, "chip", partner(bit))
        if bit != rest[-1]:
            tail = add(tail, tail_came)
    tail, tail_came, out_rows, out_other = fence(tail, tail_came, out_rows, out_other)
    tail = add(tail, tail_came)
    tail_came = swap(tail, "core", 1)
    out_pieces = with_core([out_rows, out_other])
    tail, tail_came, out_pieces = fence(tail, tail_came, out_pieces)
    levels = len(bits)
    where = jnp.stack([lax.axis_index("chip"), core]).astype(jnp.int32)
    (sum_mlp_out,) = assemble(where, out_pieces, levels, [(0, 0, half, 0, half, 0)], [width])
    low, up = by_core(tail, tail_came, core)
    tail = jnp.concatenate([low[:, :half], up], axis=1)
    tail, sum_mlp_out, last_came, in_other = fence(tail, sum_mlp_out, last_came, in_other)
    for bit in rest[:-1]:
        last_keep, last_came = scatter_step(last_keep, last_came, bit)
    last_keep, last_send = scatter_parts(last_keep, last_came, rest[-1])
    in_rows = jnp.concatenate([in_rows, in_other], axis=0)
    for bit in reversed(rest[:-1]):
        in_rows = stack_other(in_rows, bit)
    tail, last_send, in_rows = fence(tail, last_send, in_rows)
    last_came = swap(last_send, "chip", partner(rest[-1]))
    tails = from_all(tail, groups)
    in_other = swap(in_rows, "chip", bits[0])
    tails = fence(*tails)
    stride = tail.shape[0]
    per_slot = (PIX + 1) * channels
    small_sum = tail[per_slot:, :width].astype(f32)
    part_size = inner_width // groups
    sum_bias = small_sum[0]
    sum_gain_two = small_sum[1, :own]
    sum_gain_one = small_sum[1, own : 2 * own]
    sum_lead = small_sum[2 : 2 + leads // groups]

    own_ids = member * (vocab // groups) + jnp.arange(16, dtype=jnp.int32)
    own_pick = jnp.where(jnp.arange(16)[:, None] < vocab // groups, own_ids[:, None] == ids[None, :], False)
    own_pick = jnp.pad(
        own_pick.reshape(16, groups, channels), ((0, 0), (0, 0), (PIX * channels, stride - per_slot))
    ).reshape(16, groups * stride)
    sum_value, sum_key, sum_query, sum_patch, sum_table = finish_tail(
        member_one,
        tails,
        by_slot,
        own_pick.astype(bf16),
        agg_value,
        query_keys,
        agg_key,
        agg_query.astype(f32)[None],
        channels,
        vocab // groups,
    )
    sum_query = sum_query.reshape(own)
    sum_value, last_came, in_rows = fence(sum_value, last_came, in_rows)
    last_rows = add(last_keep, last_came)
    last_other = swap(last_rows, "chip", partner(rest[-1]))
    field_slots = field_own.reshape(pixel_count, groups, channels, rows)
    field_parts = [swap(field_slots[:, k], "var", k) if k else field_slots[:, 0] for k in range(groups)]
    field_parts = fence(*field_parts)
    field_grad = place_field(member_one, field_parts).reshape(channels, pixel_count, samples, seq)
    field_grad, last_other, in_rows, in_other = fence(field_grad, last_other, in_rows, in_other)
    last_rows = jnp.concatenate([last_rows, last_other], axis=0)
    for bit in reversed(rest[:-1]):
        last_rows = stack_other(last_rows, bit)
    last_rows, in_rows, in_other = fence(last_rows, in_rows, in_other)
    last_other = swap(last_rows, "chip", bits[0])
    in_pieces = fence(*with_core([in_rows, in_other]))

    half_in = inner_width // 2
    units = half_in // 2
    sum_mlp_in, sum_attn_out = assemble(
        where,
        in_pieces,
        levels,
        [(0, 0, units, 0, half_in, units), (1, units, half // 2, 0, half, half // 2)],
        [inner_width, width],
        low_rows=False,
    )
    sum_mlp_in, last_rows, last_other, sum_patch, sum_table, field_grad = fence(
        sum_mlp_in, last_rows, last_other, sum_patch, sum_table, field_grad
    )
    sum_qkv, sum_agg_out = assemble(
        where,
        with_core([last_rows, last_other]),
        levels,
        [
            (0, (3 * p + t) * pair, pair, t * width + p * own, pair, 0)
            for p in range(groups)
            for t in range(3)
        ]
        + [(1, groups * 3 * pair, half, 0, half, 0)],
        [3 * width, width],
    )
    return (
        output,
        field_grad,
        sum_patch,
        sum_table,
        sum_query,
        sum_key,
        sum_value,
        sum_agg_out,
        sum_lead,
        sum_gain_one,
        sum_qkv,
        sum_attn_out,
        sum_gain_two,
        sum_mlp_in,
        sum_bias,
        sum_mlp_out,
    )


def solution(mesh):
    members, patches = mesh.shape["var"], mesh.shape["patch"]
    chips = Mesh(mesh.devices.reshape(members, patches // 2, 2), ("var", "chip", "core"))
    patch = ("chip", "core")
    placed = (
        P("var", None, patch, None),
        P(),
        P(patch),
        P("var", None, None),
        *[P()] * 13,
        P(patch, "var", None),
    )
    return jax.shard_map(
        body,
        mesh=chips,
        in_specs=placed,
        out_specs=(
            P(patch, "var", None),
            P("var", None, patch, None),
            P("var", None, None),
            P("var", None),
            P("var"),
            P("var", None),
            P("var", None),
            P("var", None),
            P("var", None),
            P("var"),
            P("var", None),
            P("var", None),
            P("var"),
            P("var", None),
            P("var"),
            P("var", None),
        ),
        check_vma=False,
    )
```

```python
from functools import partial

import jax
import jax.numpy as jnp
from jax import lax
from jax.experimental import pallas as pl
from jax.experimental.pallas import tpu as pltpu
from jax.sharding import Mesh
from jax.sharding import PartitionSpec as P

HEADS = 16
PIX = 4
HEAD_DIM = 64
LEADS = 8
FREE = 4
ORDER = (0, 2, 1, 3)
BLOCKS = tuple((k, 0) for k in range(4)) + tuple((k, 1) for k in ORDER)

f32, bf16 = jnp.float32, jnp.bfloat16
highest = lax.Precision.HIGHEST
epsilon = 1e-05
NT = (((1,), (1,)), ((), ()))
LIGHT = pl.CostEstimate(flops=1, bytes_accessed=1, transcendentals=0)
TN = (((0,), (0,)), ((), ()))


def head_weights(pixels, key_ref, head):
    scores = key_ref[PIX, :, head : head + 1]
    for c in range(PIX):
        scores = scores + pixels[c] * key_ref[c, :, head : head + 1]
    soft = jnp.exp(scores - jnp.max(scores, axis=0, keepdims=True))
    return soft * (1.0 / jnp.sum(soft, axis=0, keepdims=True))


def slot_spans(member, own):
    return [pl.ds(pl.multiple_of((member[0] ^ k) * own, own), own) for k in ORDER]


def weighted_pixels(soft, pixels):
    return jnp.concatenate(
        [(soft * pixels[c]).astype(bf16) for c in range(PIX)] + [soft.astype(bf16)], axis=0
    )


def prepare_kernel(*refs, groups):
    blocks = refs[:groups]
    pick_ref, embed_ref, query_ref, weight_ref, pixel_ref, key_ref, value_ref, value_t_ref, slot_ref, stacked, by_slot = refs[groups:]
    channels = blocks[0].shape[0]
    seq = pixel_ref.shape[2]
    count = channels * groups
    stride = by_slot.shape[0] // groups
    by_slot[...] = jnp.zeros_like(by_slot)
    embeds = jnp.dot(pick_ref[...], embed_ref[...], preferred_element_type=f32)
    for k, block in enumerate(blocks):
        for c in range(PIX + 1):
            if c < PIX:
                pixel_ref[c, k * channels : (k + 1) * channels, :] = block[:, c, :seq].astype(f32)
                rows = block[:, c, seq:].astype(f32)
            else:
                rows = embeds[k * channels : (k + 1) * channels, :]
            stacked[c * count + k * channels : c * count + (k + 1) * channels, :] = rows
            by_slot[k * stride + c * channels : k * stride + (c + 1) * channels, :] = rows
    slot_ref[...] = by_slot[...].astype(bf16)
    keys = jnp.dot(stacked[...], query_ref[...], precision=highest, preferred_element_type=f32)
    for c in range(PIX + 1):
        key_ref[c] = keys[c * count : (c + 1) * count]
    values = jnp.dot(stacked[...].astype(bf16), weight_ref[...], preferred_element_type=f32).astype(bf16)
    value_ref[...] = values
    value_t_ref[...] = values.T


def prepare(blocks, pick, var_embed, query_keys, agg_value, seq):
    groups = len(blocks)
    channels = blocks[0].shape[0]
    count = channels * groups
    width = agg_value.shape[0]
    rows = (PIX + 1) * count
    deep = rows + FREE * groups
    return pl.pallas_call(
        partial(prepare_kernel, groups=groups),
        out_shape=[
            jax.ShapeDtypeStruct((PIX, count, seq), f32),
            jax.ShapeDtypeStruct((PIX + 1, count, query_keys.shape[1]), f32),
            jax.ShapeDtypeStruct((rows, width), bf16),
            jax.ShapeDtypeStruct((width, rows), bf16),
            jax.ShapeDtypeStruct((deep, width), bf16),
        ],
        scratch_shapes=[pltpu.VMEM((rows, width), f32), pltpu.VMEM((deep, width), f32)],
        cost_estimate=LIGHT,
        name="prepare",
    )(*blocks, pick, var_embed, query_keys, agg_value)


def front_kernel(
    member,
    bucket,
    pixel_ref,
    key_ref,
    value_ref,
    out_ref,
    lead_ref,
    gain_ref,
    wq_ref,
    wk_ref,
    wv_ref,
    hidden_ref,
    qkv_ref,
    resid_ref,
    att_ref,
    att_scratch,
):
    pixels = [pixel_ref[c] for c in range(PIX)]
    for head in range(HEADS):
        soft = head_weights(pixels, key_ref, head)
        span = slice(head * HEAD_DIM, (head + 1) * HEAD_DIM)
        att_scratch[span, :] = jnp.dot(
            value_ref[span, :], weighted_pixels(soft, pixels), preferred_element_type=f32
        ).astype(bf16)
    att = att_scratch[...]
    line = lax.broadcasted_iota(jnp.int32, lead_ref.shape, 0)
    lead = jnp.sum(jnp.where(line == bucket[0], lead_ref[...].astype(f32), 0.0), axis=0, keepdims=True)
    resid = lax.dot_general(att, out_ref[...], TN, preferred_element_type=f32) + lead
    centered = resid - jnp.mean(resid, axis=1, keepdims=True)
    inverse = lax.rsqrt(jnp.mean(centered * centered, axis=1, keepdims=True) + epsilon)
    hidden = (centered * inverse * gain_ref[...]).astype(bf16)
    own = wq_ref.shape[1]
    hidden_ref[...] = hidden.T
    for t, weight in enumerate((wq_ref, wk_ref, wv_ref)):
        qkv_ref[:, t * own : (t + 1) * own] = jnp.dot(
            hidden, weight[...], preferred_element_type=f32
        ).astype(bf16)

    @pl.when(pl.program_id(0) == member[0])
    def _():
        resid_ref[...] = resid
        att_ref[...] = att


def front(member, bucket, pixels, key_rows, values_t, agg_out, lead_table, gain, attn_qkv, groups):
    width = agg_out.shape[0]
    own = width // groups
    channels, seq = pixels.shape[1:]
    rows = seq // groups
    spec = pltpu.PrefetchScalarGridSpec(
        num_scalar_prefetch=2,
        grid=(groups,),
        in_specs=[
            pl.BlockSpec((PIX, channels, rows), lambda i, m, l: (0, 0, i)),
            pl.BlockSpec(key_rows.shape, lambda i, m, l: (0, 0, 0)),
            pl.BlockSpec(values_t.shape, lambda i, m, l: (0, 0)),
            pl.BlockSpec(agg_out.shape, lambda i, m, l: (0, 0)),
            pl.BlockSpec(lead_table.shape, lambda i, m, l: (0, 0)),
            pl.BlockSpec((1, width), lambda i, m, l: (0, 0)),
            pl.BlockSpec((width, own), lambda i, m, l: (0, m[0])),
            pl.BlockSpec((width, own), lambda i, m, l: (0, groups + m[0])),
            pl.BlockSpec((width, own), lambda i, m, l: (0, 2 * groups + m[0])),
        ],
        out_specs=[
            pl.BlockSpec((width, rows), lambda i, m, l: (0, i)),
            pl.BlockSpec((rows, 3 * own), lambda i, m, l: (i, 0)),
            pl.BlockSpec((rows, width), lambda i, m, l: (0, 0)),
            pl.BlockSpec((width, rows), lambda i, m, l: (0, 0)),
        ],
        scratch_shapes=[pltpu.VMEM((width, rows), bf16)],
    )
    return pl.pallas_call(
        front_kernel,
        grid_spec=spec,
        out_shape=[
            jax.ShapeDtypeStruct((width, seq), bf16),
            jax.ShapeDtypeStruct((seq, 3 * own), bf16),
            jax.ShapeDtypeStruct((rows, width), f32),
            jax.ShapeDtypeStruct((width, rows), bf16),
        ],
        cost_estimate=LIGHT,
        name="front",
    )(member, bucket, pixels, key_rows, values_t, agg_out, lead_table, gain, attn_qkv, attn_qkv, attn_qkv)


def attend_kernel(member, q_ref, k_ref, v_ref, mixed_ref, lse_ref):
    rows = q_ref.shape[0]
    lane = lax.broadcasted_iota(jnp.int32, (1, 2 * HEAD_DIM), 1)
    queries = q_ref[...] * jnp.asarray(0.125, bf16)
    mixed = jnp.zeros((rows, 2 * HEAD_DIM), f32)
    seq = k_ref.shape[0]
    for part in range(2):
        keep = (lane // HEAD_DIM) == part
        query = jnp.where(keep, queries, jnp.zeros_like(queries))
        top = total = out = None
        for span in (slice(0, seq // 2), slice(seq // 2, seq)):
            scores = lax.dot_general(query, k_ref[span, :], NT, preferred_element_type=f32)
            peak = jnp.max(scores, axis=1, keepdims=True)
            if top is not None:
                peak = jnp.maximum(peak, top)
            soft = jnp.exp(scores - peak)
            weight = jnp.sum(soft, axis=1, keepdims=True)
            value = jnp.dot(soft.astype(bf16), v_ref[span, :], preferred_element_type=f32)
            if top is None:
                total, out = weight, value
            else:
                scale = jnp.exp(top - peak)
                total, out = total * scale + weight, out * scale + value
            top = peak
        mixed = jnp.where(keep, out * (1.0 / total), mixed)
        lse = jnp.broadcast_to(top + jnp.log(total), (rows, 2 * HEAD_DIM))
        lse_ref[0, part : part + 1, :] = lse.T[0:1, :]
    mixed_ref[...] = mixed.astype(bf16)


def attend(member, qkv, slot, rows, block):
    seq = qkv.shape[0]
    pair = 2 * HEAD_DIM
    pairs = qkv.shape[1] // (3 * pair)
    steps = rows // block
    spec = pltpu.PrefetchScalarGridSpec(
        num_scalar_prefetch=1,
        grid=(pairs, steps),
        in_specs=[
            pl.BlockSpec((block, pair), lambda p, i, m: ((m[0] ^ slot) * steps + i, p)),
            pl.BlockSpec((seq, pair), lambda p, i, m: (0, pairs + p)),
            pl.BlockSpec((seq, pair), lambda p, i, m: (0, 2 * pairs + p)),
        ],
        out_specs=[
            pl.BlockSpec((block, pair), lambda p, i, m: (i, p)),
            pl.BlockSpec((1, 2, block), lambda p, i, m: (p, 0, i)),
        ],
    )
    return pl.pallas_call(
        attend_kernel,
        grid_spec=spec,
        out_shape=[
            jax.ShapeDtypeStruct((rows, pairs * pair), bf16),
            jax.ShapeDtypeStruct((pairs, 2, rows), f32),
        ],
        cost_estimate=LIGHT,
        name="attend",
    )(member, qkv, qkv, qkv)


def attend_back_kernel(member, q_ref, k_ref, v_ref, g_ref, *refs, chunk, groups):
    mixed_refs, lse_refs = refs[:groups], refs[groups : 2 * groups]
    out_ref, dk_acc, dv_acc, kt = refs[2 * groups :]
    i = pl.program_id(0)
    slot = i ^ member[0]
    mixed, lse_rows = mixed_refs[0][...], lse_refs[0][0]
    for k in range(1, groups):
        mixed = jnp.where(slot == k, mixed_refs[k][...], mixed)
        lse_rows = jnp.where(slot == k, lse_refs[k][0], lse_rows)
    block = q_ref.shape[0]
    seq = k_ref.shape[0]
    pair = 2 * HEAD_DIM
    lane = lax.broadcasted_iota(jnp.int32, (1, pair), 1)
    side = lax.broadcasted_iota(jnp.int32, (pair, 1), 0)

    @pl.when(i == 0)
    def _():
        dk_acc[...] = jnp.zeros_like(dk_acc)
        dv_acc[...] = jnp.zeros_like(dv_acc)
        kt[...] = k_ref[...].T

    queries = q_ref[...] * jnp.asarray(0.125, bf16)
    grads = g_ref[...]
    product = (grads.astype(f32) * mixed.astype(f32)).T
    grad_query = jnp.zeros((pair, block), f32)
    for part in range(2):
        keep = (lane // HEAD_DIM) == part
        query = jnp.where(keep, queries, jnp.zeros_like(queries))
        grad = jnp.where(keep, grads, jnp.zeros_like(grads))
        delta = jnp.sum(product[part * HEAD_DIM : (part + 1) * HEAD_DIM], axis=0, keepdims=True)
        lse = lse_rows[part : part + 1, :]
        total = jnp.zeros((pair, block), f32)
        for at in range(0, seq, chunk):
            span = pl.ds(at, chunk)
            scores = lax.dot_general(k_ref[span, :], query, NT, preferred_element_type=f32)
            soft = jnp.exp(scores - lse)
            through = lax.dot_general(v_ref[span, :], grad, NT, preferred_element_type=f32)
            grad_scores = (soft * (through - delta)).astype(bf16)
            dv_acc[span, :] += jnp.dot(soft.astype(bf16), grad, preferred_element_type=f32)
            dk_acc[span, :] += jnp.dot(grad_scores, query, preferred_element_type=f32)
            total += jnp.dot(kt[:, span], grad_scores, preferred_element_type=f32)
        grad_query = jnp.where((side // HEAD_DIM) == part, total, grad_query)
    out_ref[pl.ds(pl.multiple_of(i * block, block), block), 0:pair] = (grad_query.T * 0.125).astype(bf16)

    @pl.when(i == pl.num_programs(0) - 1)
    def _():
        out_ref[:, pair : 2 * pair] = dk_acc[...].astype(bf16)
        out_ref[:, 2 * pair : 3 * pair] = dv_acc[...].astype(bf16)


def attend_back(member, qkv, grads, mixed, lse, which, chunk):
    seq = qkv.shape[0]
    groups = len(mixed)
    rows = seq // groups
    pair = 2 * HEAD_DIM
    pairs = qkv.shape[1] // (3 * pair)
    spec = pltpu.PrefetchScalarGridSpec(
        num_scalar_prefetch=1,
        grid=(groups,),
        in_specs=[
            pl.BlockSpec((rows, pair), lambda i, m: (i, which)),
            pl.BlockSpec((seq, pair), lambda i, m: (0, pairs + which)),
            pl.BlockSpec((seq, pair), lambda i, m: (0, 2 * pairs + which)),
            pl.BlockSpec((rows, pair), lambda i, m: (i, which)),
        ]
        + [pl.BlockSpec((rows, pair), lambda i, m: (0, which))] * groups
        + [pl.BlockSpec((1, 2, rows), lambda i, m: (which, 0, 0))] * groups,
        out_specs=pl.BlockSpec((seq, 3 * pair), lambda i, m: (0, 0)),
        scratch_shapes=[pltpu.VMEM((seq, pair), f32), pltpu.VMEM((seq, pair), f32), pltpu.VMEM((pair, seq), bf16)],
    )
    return pl.pallas_call(
        partial(attend_back_kernel, chunk=min(chunk, seq), groups=groups),
        grid_spec=spec,
        out_shape=jax.ShapeDtypeStruct((seq, 3 * pair), bf16),
        cost_estimate=LIGHT,
        name="attend_back",
    )(member, qkv, qkv, qkv, grads, *mixed, *lse)


def put_tail(tail, values, span):
    groups = len(ORDER)
    channels = values.shape[0] // ((PIX + 1) * groups)
    stride = tail.shape[0] // groups
    for at, k in enumerate(ORDER):
        for c in range(PIX + 1):
            row, source = at * stride + c * channels, (c * groups + k) * channels
            tail[row : row + channels, span] = values[source : source + channels]


def aggregate_back_kernel(
    member, core, bucket, pixel_ref, key_ref, value_ref, grad_ref, bias_ref, gain2_ref, gain1_ref, sum_ref,
    field_ref, keep_ref, send_ref, tail
):
    count, rows = pixel_ref.shape[1:]
    pair = 2 * HEAD_DIM
    pixels = [pixel_ref[c] for c in range(PIX)]
    lane = lax.broadcasted_iota(jnp.int32, (1, pair), 1)
    side = lax.broadcasted_iota(jnp.int32, (pair, 1), 0)
    field = [jnp.zeros((count, rows), f32) for _ in range(PIX)]
    keys = [jnp.zeros((count, pair), f32) for _ in range(PIX + 1)]
    for which in range(HEADS // 2):
        span = slice(which * pair, (which + 1) * pair)
        values, grads = value_ref[:, span], grad_ref[span, :]
        total = jnp.zeros(((PIX + 1) * count, pair), f32)
        for part in range(2):
            head = which * 2 + part
            grad = jnp.where((side // HEAD_DIM) == part, grads, jnp.zeros_like(grads))
            through = jnp.dot(values, grad, preferred_element_type=f32)
            kinds = [through[c * count : (c + 1) * count] for c in range(PIX + 1)]
            soft = head_weights(pixels, key_ref, head)
            grad_soft = kinds[PIX]
            for c in range(PIX):
                grad_soft = grad_soft + pixels[c] * kinds[c]
            weighed = soft * grad_soft
            grad_scores = weighed - soft * jnp.sum(weighed, axis=0, keepdims=True)
            for c in range(PIX):
                field[c] = field[c] + soft * kinds[c] + grad_scores * key_ref[c, :, head : head + 1]
                keys[c] = jnp.where(lane == head, jnp.sum(grad_scores * pixels[c], axis=1, keepdims=True), keys[c])
            keys[PIX] = jnp.where(lane == head, jnp.sum(grad_scores, axis=1, keepdims=True), keys[PIX])
            total = total + lax.dot_general(weighted_pixels(soft, pixels), grad, NT, preferred_element_type=f32)
        put_tail(tail, total, span)
    for c in range(PIX):
        field_ref[c] = field[c].astype(bf16)
    width = value_ref.shape[1]
    put_tail(tail, jnp.concatenate(keys, axis=0), slice(width, width + pair))
    groups = len(ORDER)
    stride = tail.shape[0] // groups
    own, lines = width // groups, LEADS // groups
    for at, k in enumerate(ORDER):
        owner = member[0] ^ k
        start = (at + 1) * stride - FREE
        tail[start : start + FREE, :] = jnp.zeros((FREE, tail.shape[1]), f32)
        tail[start : start + 1, :width] = bias_ref[:, pl.ds(pl.multiple_of(owner * width, width), width)]
        chunk = pl.ds(pl.multiple_of(owner * own, own), own)
        tail[start + 1 : start + 2, :own] = gain2_ref[:, chunk]
        tail[start + 1 : start + 2, own : 2 * own] = gain1_ref[:, chunk]
        for line in range(lines):
            hit = bucket[0] == owner * lines + line
            tail[start + 2 + line : start + 3 + line, :width] = jnp.where(hit, sum_ref[...], 0.0)
    half = width // 2
    for ref, which in ((keep_ref, core[0]), (send_ref, 1 - core[0])):
        ref[:, :half] = tail[:, pl.ds(pl.multiple_of(which * half, half), half)].astype(bf16)
        ref[:, half:] = tail[:, width:].astype(bf16)


def aggregate_back(member, core, bucket, pixels, key_rows, values, grads, small, groups):
    count, seq = pixels.shape[1:]
    rows = seq // groups
    width = values.shape[1]
    deep = (PIX + 1) * count + FREE * groups
    wide = width // 2 + 2 * HEAD_DIM

    def whole(*shape):
        return pl.BlockSpec(shape, lambda i, *_: (0,) * len(shape))

    spec = pltpu.PrefetchScalarGridSpec(
        num_scalar_prefetch=3,
        grid=(1,),
        in_specs=[
            pl.BlockSpec((PIX, count, rows), lambda i, m, c, l: (0, 0, m[0])),
            whole(*key_rows.shape),
            whole(*values.shape),
            whole(*grads.shape),
            *[whole(*value.shape) for value in small],
        ],
        out_specs=[whole(PIX, count, rows), whole(deep, wide), whole(deep, wide)],
        scratch_shapes=[pltpu.VMEM((deep, width + 2 * HEAD_DIM), f32)],
    )
    return pl.pallas_call(
        aggregate_back_kernel,
        grid_spec=spec,
        out_shape=[
            jax.ShapeDtypeStruct((PIX, count, rows), bf16),
            jax.ShapeDtypeStruct((deep, wide), bf16),
            jax.ShapeDtypeStruct((deep, wide), bf16),
        ],
        cost_estimate=LIGHT,
        name="aggregate_back",
    )(member, core, bucket, pixels, key_rows, values, grads, *small)


def shape_of(*dims, kind=bf16):
    return jax.ShapeDtypeStruct(dims, kind)


def inner_kernel(
    member, core, mixed0, mixed1, mixed2, mixed3, wo_ref, resid_ref, gain_ref, w1_ref, b1_ref, ga_ref,
    act_ref, act_t_ref, send_ref, keep_ref, bias_ref, one_ref, hidden_ref, mixed_ref, hidden,
):
    j = pl.program_id(0)
    parts = (mixed0, mixed1, mixed2, mixed3)
    rows, own = mixed0.shape

    @pl.when(j == 0)
    def _():
        resid = resid_ref[...]
        for slot, part in enumerate(parts):
            owner = pl.ds(pl.multiple_of((member[0] ^ slot) * own, own), own)
            resid = resid + jnp.dot(part[...], wo_ref[owner, :], preferred_element_type=f32)
        one_ref[...] = resid
        centered = resid - jnp.mean(resid, axis=1, keepdims=True)
        scale = lax.rsqrt(jnp.mean(centered * centered, axis=1, keepdims=True) + epsilon)
        hidden[...] = (centered * scale * gain_ref[...]).astype(bf16)
        piece = own // 2
        for at, (slot, side) in enumerate(BLOCKS):
            start = pl.multiple_of((member[0] ^ slot) * own + side * piece, piece)
            hidden_ref[at * piece : (at + 1) * piece, :] = hidden[:, pl.ds(start, piece)].T
            mixed_ref[at * piece : (at + 1) * piece, :] = parts[slot][:, side * piece : (side + 1) * piece].T

    inner = jnp.dot(hidden[...], w1_ref[...], preferred_element_type=f32) + b1_ref[...]
    below = 0.5 + 0.5 * lax.erf(inner * 0.7071067811865476)
    act = (inner * below).astype(bf16)
    slope = below + inner * (jnp.exp(-0.5 * inner * inner) * 0.3989422804014327)
    gu = (slope * ga_ref[...].astype(f32)).astype(bf16)
    act_ref[...] = act
    act_t_ref[...] = act.T
    bias_ref[...] = jnp.sum(gu.astype(f32), axis=0, keepdims=True)

    @pl.when(j < len(parts))
    def _():
        send_ref[...] = gu

    @pl.when(j >= len(parts))
    def _():
        keep_ref[...] = gu


def inner_part(member, core, mixed, attn_out, resid, gain, mlp_in, bias, grad_act):
    rows, width = resid.shape
    inner = mlp_in.shape[1]
    groups = len(mixed)
    own = width // groups
    steps = 2 * groups
    block = inner // steps

    def natural(j, c):
        return ((j // groups) ^ (1 - c[0])) * groups + j % groups

    def spot(j, m, c):
        n = natural(j, c)
        slot = (n // 2) ^ m[0]
        return (jnp.where(n % 2 == 0, slot, 4 + (slot % 2) * 2 + slot // 2), 0)

    def whole(*shape):
        return pl.BlockSpec(shape, lambda j, m, c: (0,) * len(shape))

    def column(deep):
        return pl.BlockSpec((deep, block), lambda j, m, c: (0, natural(j, c)))

    spec = pltpu.PrefetchScalarGridSpec(
        num_scalar_prefetch=2,
        grid=(steps,),
        in_specs=[whole(rows, own)] * groups
        + [whole(width, width), whole(rows, width), whole(1, width)]
        + [column(width), column(1), column(rows)],
        out_specs=[
            column(rows),
            pl.BlockSpec((block, rows), spot),
            pl.BlockSpec((rows, block), lambda j, m, c: (0, jnp.minimum(j, groups - 1))),
            pl.BlockSpec((rows, block), lambda j, m, c: (0, jnp.maximum(j - groups, 0))),
            column(1),
            whole(rows, width),
            whole(width, rows),
            whole(width, rows),
        ],
        scratch_shapes=[pltpu.VMEM((rows, width), bf16)],
    )
    return pl.pallas_call(
        inner_kernel,
        grid_spec=spec,
        out_shape=[shape_of(rows, inner), shape_of(inner, rows)]
        + [shape_of(rows, inner // 2)] * 2
        + [shape_of(1, inner, kind=f32), shape_of(rows, width, kind=f32)]
        + [shape_of(width, rows)] * 2,
        cost_estimate=LIGHT,
        name="inner_part",
    )(member, core, *mixed, attn_out, resid, gain, mlp_in, bias, grad_act)


def outer_kernel(
    core, act_ref, send_ref, keep_ref, w1_ref, w2_ref, wo_ref, one_ref, gain_ref, g_ref,
    out_ref, gres_ref, gb_ref, gb_send_ref, gm_ref, ggain_ref, branch, grads,
):
    j = pl.program_id(0)
    groups, rows, own = gm_ref.shape
    half = send_ref.shape[1]
    branch[j] = jnp.dot(act_ref[...], w2_ref[...], preferred_element_type=f32)

    def columns(which):
        return w1_ref[:, pl.ds(pl.multiple_of(which * half, half), half)]

    grads[j] = lax.dot_general(
        send_ref[...], columns(1 - core[0]), NT, preferred_element_type=f32
    ) + lax.dot_general(keep_ref[...], columns(core[0]), NT, preferred_element_type=f32)

    @pl.when(j == pl.num_programs(0) - 1)
    def _():
        count = branch.shape[0]
        resid = one_ref[...]
        out_ref[...] = (resid + jnp.concatenate([branch[i] for i in range(count)], axis=1)).astype(bf16)
        centered = resid - jnp.mean(resid, axis=1, keepdims=True)
        scale = lax.rsqrt(jnp.mean(centered * centered, axis=1, keepdims=True) + epsilon)
        grad, plain = jnp.concatenate([grads[i] for i in range(count)], axis=1), centered * scale
        ggain_ref[...] = jnp.sum(grad * plain, axis=0, keepdims=True)
        grad = grad * gain_ref[...]
        first = jnp.mean(grad, axis=1, keepdims=True)
        second = jnp.mean(grad * plain, axis=1, keepdims=True)
        gres = g_ref[...].astype(f32) + scale * (grad - first - plain * second)
        gres_ref[...] = gres
        gb_ref[...] = gres.astype(bf16)
        width = gb_ref.shape[1]
        gb_send_ref[...] = gb_ref[:, pl.ds(pl.multiple_of((1 - core[0]) * (width // 2), width // 2), width // 2)]
        gb = gb_ref[...]
        for p in range(groups):
            gm_ref[p] = lax.dot_general(gb, wo_ref[p * own : (p + 1) * own, :], NT, preferred_element_type=f32).astype(
                bf16
            )


def outer_part(core, act, gu_send, gu_keep, mlp_in, mlp_out, attn_out, resid, gain, grad_out, groups):
    rows, width = resid.shape
    inner = mlp_in.shape[1]
    own = width // groups
    steps = 4
    block = width // steps

    def whole(*shape):
        return pl.BlockSpec(shape, lambda j, c: (0,) * len(shape))

    spec = pltpu.PrefetchScalarGridSpec(
        num_scalar_prefetch=1,
        grid=(steps,),
        in_specs=[
            whole(rows, inner),
            whole(rows, inner // 2),
            whole(rows, inner // 2),
            pl.BlockSpec((block, inner), lambda j, c: (j, 0)),
            pl.BlockSpec((inner, block), lambda j, c: (0, j)),
            whole(width, width),
            whole(rows, width),
            whole(1, width),
            whole(rows, width),
        ],
        out_specs=[
            whole(rows, width),
            whole(rows, width),
            whole(rows, width),
            whole(rows, width // 2),
            whole(groups, rows, own),
            whole(1, width),
        ],
        scratch_shapes=[pltpu.VMEM((steps, rows, block), f32), pltpu.VMEM((steps, rows, block), f32)],
    )
    return pl.pallas_call(
        outer_kernel,
        grid_spec=spec,
        out_shape=[
            shape_of(rows, width),
            shape_of(rows, width, kind=f32),
            shape_of(rows, width),
            shape_of(rows, width // 2),
            shape_of(groups, rows, own),
            shape_of(1, width, kind=f32),
        ],
        cost_estimate=LIGHT,
        name="outer_part",
    )(core, act, gu_send, gu_keep, mlp_in, mlp_out, attn_out, resid, gain, grad_out)


def both_dots(left, left_other, right, right_other):
    return jnp.dot(left[...], right[...], preferred_element_type=f32) + jnp.dot(
        left_other[...], right_other[...], preferred_element_type=f32
    )


def out_grad_kernel(core, left, left_other, right, right_other, *outs):
    total = both_dots(left, left_other, right, right_other).astype(bf16)
    for q, out in enumerate(outs):

        @pl.when(pl.program_id(0) == q)
        def _():
            out[...] = total


def out_grad(core, left, left_other, right, right_other):
    rows, deep = left.shape
    half = right.shape[1] // 2
    block = rows // 4

    spec = pltpu.PrefetchScalarGridSpec(
        num_scalar_prefetch=1,
        grid=(4,),
        in_specs=[pl.BlockSpec((block, deep), lambda i, c: (i, 0))] * 2
        + [
            pl.BlockSpec((deep, half), lambda i, c: (0, c[0])),
            pl.BlockSpec((deep, half), lambda i, c: (0, 0)),
        ],
        out_specs=[pl.BlockSpec((block, half), lambda i, c: (0, 0)) for q in range(4)],
    )
    return pl.pallas_call(
        out_grad_kernel,
        grid_spec=spec,
        out_shape=[shape_of(rows // 4, half)] * 4,
        cost_estimate=LIGHT,
        name="out_grad",
    )(core, left, left_other, right, right_other)


def in_grad_kernel(core, high, h, h_other, u, u_other, m, m_other, b, b_other, keep, send):
    units = u.shape[1]

    def put(out):
        out[:, :units] = both_dots(h, h_other, u, u_other).astype(bf16)
        out[:, units:] = both_dots(m, m_other, b, b_other).astype(bf16)

    @pl.when(pl.program_id(0) == 0)
    def _():
        put(send)

    @pl.when(pl.program_id(0) == 1)
    def _():
        put(keep)


def in_grad(core, high, h, h_other, u, u_other, m, m_other, b, b_other):
    rows, deep = h.shape
    units, branch = u.shape[1] // 2, b_other.shape[1] // 2

    def whole(*shape):
        return pl.BlockSpec(shape, lambda i, c, z: (0,) * len(shape))

    def side(i, c, z):
        return (0, z[0] ^ (1 - i))

    def core_side(i, c, z):
        return (0, 2 * c[0] + (z[0] ^ (1 - i)))

    spec = pltpu.PrefetchScalarGridSpec(
        num_scalar_prefetch=2,
        grid=(2,),
        in_specs=[
            whole(rows, deep),
            whole(rows, deep),
            pl.BlockSpec((deep, units), side),
            pl.BlockSpec((deep, units), side),
            whole(rows, deep),
            whole(rows, deep),
            pl.BlockSpec((deep, branch), core_side),
            pl.BlockSpec((deep, branch), side),
        ],
        out_specs=[whole(rows, units + branch)] * 2,
    )
    return pl.pallas_call(
        in_grad_kernel,
        grid_spec=spec,
        out_shape=[shape_of(rows, units + branch)] * 2,
        cost_estimate=LIGHT,
        name="in_grad",
    )(core, high, h, h_other, u, u_other, m, m_other, b, b_other)


def qkv_grad_kernel(core, h, h_other, *refs):
    out = refs[-1]
    for which in range(2):

        @pl.when(core[0] == which)
        def _():
            out[...] = both_dots(h, h_other, refs[which], refs[2 + which]).astype(bf16)


def qkv_grad(core, h, h_other, grads, others):
    rows, deep = h.shape
    cols = grads[0].shape[1]
    block = rows // 2
    spec = pltpu.PrefetchScalarGridSpec(
        num_scalar_prefetch=1,
        grid=(2,),
        in_specs=[pl.BlockSpec((block, deep), lambda i, c: (i, 0))] * 2
        + [pl.BlockSpec((deep, cols), lambda i, c: (0, 0))] * 4,
        out_specs=pl.BlockSpec((block, cols), lambda i, c: (i, 0)),
    )
    return pl.pallas_call(
        qkv_grad_kernel,
        grid_spec=spec,
        out_shape=shape_of(rows, cols),
        cost_estimate=LIGHT,
        name="qkv_grad",
    )(core, h, h_other, *grads, *others)


def last_grad_kernel(core, qkv_ref, a, a_other, g, g_other, out):
    cols = qkv_ref.shape[1]
    out[0, :, :cols] = qkv_ref[...]
    out[0, :, cols:] = both_dots(a, a_other, g, g_other).astype(bf16)


def last_grad(core, weight_qkv, att, att_other, grad, grad_other, groups):
    rows, deep = att.shape
    half = grad_other.shape[1]
    cols = weight_qkv.shape[1]
    block = rows // groups
    spec = pltpu.PrefetchScalarGridSpec(
        num_scalar_prefetch=1,
        grid=(groups,),
        in_specs=[
            pl.BlockSpec((block, cols), lambda i, c: (i, 0)),
            pl.BlockSpec((block, deep), lambda i, c: (i, 0)),
            pl.BlockSpec((block, deep), lambda i, c: (i, 0)),
            pl.BlockSpec((deep, half), lambda i, c: (0, c[0])),
            pl.BlockSpec((deep, half), lambda i, c: (0, 0)),
        ],
        out_specs=pl.BlockSpec((1, block, cols + half), lambda i, c: (i, 0, 0)),
    )
    return pl.pallas_call(
        last_grad_kernel,
        grid_spec=spec,
        out_shape=shape_of(groups, block, cols + half),
        cost_estimate=LIGHT,
        name="last_grad",
    )(core, weight_qkv, att, att_other, grad, grad_other)


def join_kernel(core, first_ref, second_ref, wq, wk, wv, resid_ref, gain_ref, gres_ref, out_ref, *refs):
    ga_ref, ga_send_ref, gatt_ref, ggain_ref, sum_ref, total = refs
    i = pl.program_id(0)
    pair = 2 * HEAD_DIM

    @pl.when(i == 0)
    def _():
        total[...] = jnp.zeros_like(total)

    spans = [slice(t * pair, (t + 1) * pair) for t in range(3)]
    left = jnp.concatenate([ref[:, span] for span in spans for ref in (first_ref, second_ref)], axis=1)
    weights = jnp.concatenate([wq[...], wk[...], wv[...]], axis=1)
    total[...] += lax.dot_general(left, weights, NT, preferred_element_type=f32)

    @pl.when(i == pl.num_programs(0) - 1)
    def _():
        resid = resid_ref[...]
        centered = resid - jnp.mean(resid, axis=1, keepdims=True)
        scale = lax.rsqrt(jnp.mean(centered * centered, axis=1, keepdims=True) + epsilon)
        plain = centered * scale
        grad = total[...]
        ggain_ref[...] = jnp.sum(grad * plain, axis=0, keepdims=True)
        grad = grad * gain_ref[...]
        first = jnp.mean(grad, axis=1, keepdims=True)
        second = jnp.mean(grad * plain, axis=1, keepdims=True)
        gres = gres_ref[...] + scale * (grad - first - plain * second)
        sum_ref[...] = jnp.sum(gres, axis=0, keepdims=True)
        ga = gres.astype(bf16)
        ga_ref[...] = ga
        half = ga_send_ref.shape[1]
        ga_send_ref[...] = ga_ref[:, pl.ds(pl.multiple_of((1 - core[0]) * half, half), half)]
        gatt_ref[...] = lax.dot_general(out_ref[...], ga, NT, preferred_element_type=f32).astype(bf16)


def join(core, first, second, attn_qkv, resid, gain, gres, agg_out):
    rows, width = resid.shape
    groups = first.shape[0] // rows
    own = width // groups
    cols = first.shape[1]

    def whole(*shape):
        return pl.BlockSpec(shape, lambda i, c: (0,) * len(shape))

    spec = pltpu.PrefetchScalarGridSpec(
        num_scalar_prefetch=1,
        grid=(groups,),
        in_specs=[
            pl.BlockSpec((rows, cols), lambda i, c: (i, 0)),
            pl.BlockSpec((rows, cols), lambda i, c: (i, 0)),
            pl.BlockSpec((width, own), lambda i, c: (0, i)),
            pl.BlockSpec((width, own), lambda i, c: (0, groups + i)),
            pl.BlockSpec((width, own), lambda i, c: (0, 2 * groups + i)),
            whole(rows, width),
            whole(1, width),
            whole(rows, width),
            whole(width, width),
        ],
        out_specs=[
            whole(rows, width),
            whole(rows, width // 2),
            whole(width, rows),
            whole(1, width),
            whole(1, width),
        ],
        scratch_shapes=[pltpu.VMEM((rows, width), f32)],
    )
    return pl.pallas_call(
        join_kernel,
        grid_spec=spec,
        out_shape=[
            shape_of(rows, width),
            shape_of(rows, width // 2),
            shape_of(width, rows),
            shape_of(1, width, kind=f32),
            shape_of(1, width, kind=f32),
        ],
        cost_estimate=LIGHT,
        name="join",
    )(core, first, second, attn_qkv, attn_qkv, attn_qkv, resid, gain, gres, agg_out)


def add(a, b):
    return (a.astype(f32) + b.astype(f32)).astype(bf16)


def split_add(a, b, count):
    deep = a.shape[0] // count
    return [add(a[i * deep : (i + 1) * deep], b[i * deep : (i + 1) * deep]) for i in range(count)]


def pick_add(a, b, which, axis):
    half = a.shape[axis] // 2
    return add(
        lax.dynamic_slice_in_dim(a, which * half, half, axis), lax.dynamic_slice_in_dim(b, which * half, half, axis)
    )


def whole_blocks(shapes):
    return [pl.BlockSpec(shape, lambda i, *_, n=len(shape): (0,) * n) for shape in shapes]


def choose_kernel(high, a, b, c, d, keep, send):
    for value, (first, second) in enumerate(((keep, send), (send, keep))):

        @pl.when(high[0] == value)
        def _():
            first[...] = add(a[...], b[...])
            second[...] = add(c[...], d[...])


def choose(high, a, b, c, d):
    rows, cols = a.shape
    block = pl.BlockSpec((rows // 2, cols), lambda i, z: (i, 0))
    return pl.pallas_call(
        choose_kernel,
        grid_spec=pltpu.PrefetchScalarGridSpec(
            num_scalar_prefetch=1, grid=(2,), in_specs=[block] * 4, out_specs=[block] * 2
        ),
        out_shape=[jax.ShapeDtypeStruct(a.shape, bf16)] * 2,
        cost_estimate=LIGHT,
        name="choose",
    )(high, a, b, c, d)


def gather_sources_kernel(high, came_ref, keep, send, *, cols):
    groups, half = came_ref.shape[0], keep.shape[0]
    for out, which in ((keep, high[0]), (send, 1 - high[0])):
        span = pl.ds(pl.multiple_of(which * half, half), half)
        total = jnp.zeros((half, came_ref.shape[2] - cols), f32)
        for p in range(groups):
            out[:, p * cols : (p + 1) * cols] = came_ref[p, span, :cols]
            total = total + came_ref[p, span, cols:].astype(f32)
        out[:, groups * cols :] = total.astype(bf16)


def gather_sources(high, came, cols):
    groups, rows, wide = came.shape
    shape = (rows // 2, groups * cols + wide - cols)
    spec = pltpu.PrefetchScalarGridSpec(
        num_scalar_prefetch=1, grid=(1,), in_specs=whole_blocks([came.shape]), out_specs=whole_blocks([shape] * 2)
    )
    return pl.pallas_call(
        partial(gather_sources_kernel, cols=cols),
        grid_spec=spec,
        out_shape=[jax.ShapeDtypeStruct(shape, bf16)] * 2,
        cost_estimate=LIGHT,
        name="gather_sources",
    )(high, came)


def turned(i, levels):
    total = 0
    for k in range(levels):
        total = total + (((i >> k) & 1) << (levels - 1 - k))
    return total


def assemble_kernel(where, *refs, order, levels, spans, low_rows):
    pieces, outs = refs[:4], refs[4:]
    deep = pieces[0].shape[0] // len(order)
    for number, ref in enumerate(pieces):
        core = where[1] if number < 2 else 1 - where[1]
        for at, bits in enumerate(order):
            chip = where[0] ^ (bits ^ (number % 2))
            low = low_bit(chip, levels)
            row = turned(chip >> 1, levels - 1)
            if low_rows:
                row = row + (low << (levels - 1))
            to = pl.ds(pl.multiple_of(row * deep, deep), deep)
            for out, source, size, base, by_core, by_low in spans:
                column = pl.multiple_of(base + core * by_core + low * by_low, 128)
                outs[out][to, pl.ds(column, size)] = ref[at * deep : (at + 1) * deep, source : source + size].astype(f32)


def assemble(where, pieces, levels, spans, widths, low_rows=True):
    order = [0]
    for bit in range(levels - 1, 0, -1):
        order = order + [bits ^ (3 if mirrored(levels) else 1 << bit) for bits in order]
    rows = pieces[0].shape[0] * (2 if low_rows else 1)
    shapes = [(rows, wide) for wide in widths]
    spec = pltpu.PrefetchScalarGridSpec(
        num_scalar_prefetch=1,
        grid=(1,),
        in_specs=whole_blocks([p.shape for p in pieces]),
        out_specs=whole_blocks(shapes),
    )
    return pl.pallas_call(
        partial(assemble_kernel, order=tuple(order), levels=levels, spans=tuple(spans), low_rows=low_rows),
        grid_spec=spec,
        out_shape=[shape_of(*shape, kind=f32) for shape in shapes],
        cost_estimate=LIGHT,
        name="assemble",
    )(where, *pieces)


def field_kernel(member, *refs):
    pieces, out = refs[:-1], refs[-1]
    kinds, channels, rows = pieces[0].shape
    for k, piece in enumerate(pieces):
        at = pl.ds(pl.multiple_of((member[0] ^ k) * rows, rows), rows)
        for c in range(kinds):
            out[:, c, at] = piece[c].astype(f32)


def place_field(member, pieces):
    kinds, channels, rows = pieces[0].shape
    shape = (channels, kinds, rows * len(pieces))
    spec = pltpu.PrefetchScalarGridSpec(
        num_scalar_prefetch=1,
        grid=(1,),
        in_specs=whole_blocks([p.shape for p in pieces]),
        out_specs=whole_blocks([shape])[0],
    )
    return pl.pallas_call(
        field_kernel, grid_spec=spec, out_shape=jax.ShapeDtypeStruct(shape, f32), name="place_field"
    )(member, *pieces)


def tail_kernel(member, *refs, groups):
    tails = refs[:groups]
    stacked_ref, pick_ref, value_ref, qk_ref, key_ref, query_ref = refs[groups : groups + 6]
    gvalue_ref, gkey_ref, gquery_ref, patch_ref, table_ref, gqk = refs[groups + 6 :]
    width = value_ref.shape[0]
    own = gvalue_ref.shape[0]
    at = pl.ds(pl.multiple_of(member[0] * own, own), own)
    tail = jnp.concatenate([t[...] for t in tails], axis=0)
    values, keys = tail[:, :width], tail[:, width:]
    gvalue_ref[...] = lax.dot_general(stacked_ref[:, at], values, TN, preferred_element_type=f32)
    gqk[...] = lax.dot_general(stacked_ref[...], keys, TN, preferred_element_type=f32)
    head = lax.broadcasted_iota(jnp.int32, (keys.shape[1], width), 0)
    column = lax.broadcasted_iota(jnp.int32, (keys.shape[1], width), 1) // HEAD_DIM
    spread = jnp.where(head == column, 1.0, 0.0)
    gkey_ref[...] = (
        jnp.dot(gqk[at, :], spread, precision=highest, preferred_element_type=f32) * (query_ref[...] * 0.125)
    )
    by_head = lax.dot_general(gqk[...], key_ref[...].astype(f32), TN, precision=highest, preferred_element_type=f32)
    head = lax.broadcasted_iota(jnp.int32, by_head.shape, 0)
    column = (lax.broadcasted_iota(jnp.int32, by_head.shape, 1) + member[0] * own) // HEAD_DIM
    gquery_ref[...] = jnp.sum(jnp.where(head == column, by_head, 0.0), axis=0, keepdims=True) * 0.125
    own_rows = tails[0].shape[0]
    table = jnp.dot(pick_ref[...], tail, preferred_element_type=f32).astype(bf16)
    rows = jnp.concatenate([tail[:own_rows], table], axis=0)
    total = lax.dot_general(rows[:, :width], value_ref[...], NT, preferred_element_type=f32) + lax.dot_general(
        rows[:, width:].astype(f32), qk_ref[...], NT, precision=highest, preferred_element_type=f32
    )
    channels = patch_ref.shape[0]
    for c in range(PIX):
        patch_ref[:, c, :] = total[c * channels : (c + 1) * channels]
    table_ref[...] = total[own_rows : own_rows + table_ref.shape[0]]


def finish_tail(member, tails, stacked, pick, agg_value, query_keys, agg_key, agg_query, channels, lines):
    groups = len(tails)
    width = agg_value.shape[0]
    own = width // groups
    args = [*tails, stacked, pick, agg_value, query_keys]
    spec = pltpu.PrefetchScalarGridSpec(
        num_scalar_prefetch=1,
        grid=(1,),
        in_specs=whole_blocks([x.shape for x in args])
        + [pl.BlockSpec((width, own), lambda i, m: (0, m[0])), pl.BlockSpec((1, width), lambda i, m: (0, 0))],
        out_specs=whole_blocks([(own, width), (own, width), (1, own), (channels, PIX, width), (lines, width)]),
        scratch_shapes=[pltpu.VMEM((width, query_keys.shape[1]), f32)],
    )
    return pl.pallas_call(
        partial(tail_kernel, groups=groups),
        grid_spec=spec,
        out_shape=[
            jax.ShapeDtypeStruct((own, width), f32),
            jax.ShapeDtypeStruct((own, width), f32),
            jax.ShapeDtypeStruct((1, own), f32),
            jax.ShapeDtypeStruct((channels, PIX, width), f32),
            jax.ShapeDtypeStruct((lines, width), f32),
        ],
        cost_estimate=LIGHT,
        name="finish_tail",
    )(member, *args, agg_key, agg_query)


def fence(*values):
    return lax.optimization_barrier(values)


def swap(value, axis, bits):
    size = lax.axis_size(axis)
    return lax.ppermute(value, axis, [(i, i ^ bits) for i in range(size)])


def from_all(own, groups):
    return [own] + [swap(own, "var", k) for k in range(1, groups)]


def exchange(value):
    return lax.all_to_all(value, "var", split_axis=0, concat_axis=0, tiled=True)


def chip_bits():
    bits, bit = [], 1
    while bit < lax.axis_size("chip"):
        bits.append(bit)
        bit *= 2
    return bits


def mirrored(levels):
    return levels == 2


def partner(bit):
    levels = len(chip_bits())
    return 3 if mirrored(levels) and bit == 2 else bit


def low_bit(chip, levels):
    return (chip ^ (chip >> 1)) & 1 if mirrored(levels) else chip & 1


def is_high(bit):
    chip = lax.axis_index("chip")
    return low_bit(chip, len(chip_bits())) if bit == 1 else (chip // bit) % 2


def stack_other(value, bit):
    return jnp.concatenate([value, swap(value, "chip", partner(bit))], axis=0)


def with_core(halves):
    return [*halves, *(swap(value, "core", 1) for value in halves)]


def by_core(mine, other, core):
    return jnp.where(core == 0, mine, other), jnp.where(core == 0, other, mine)


def body(
    field_patches,
    var_ids,
    lead_bucket,
    patch_weight,
    var_embed,
    agg_query,
    agg_key,
    agg_value,
    agg_out,
    lead_table,
    ln1_gain,
    attn_qkv,
    attn_out,
    ln2_gain,
    mlp_in,
    mlp_in_bias,
    mlp_out,
    cotangent,
):
    groups = lax.axis_size("var")
    member = lax.axis_index("var")
    core = lax.axis_index("core")
    channels, pixel_count, samples, seq = field_patches.shape
    width = agg_key.shape[0]
    inner_width = mlp_in.shape[1]
    leads = lead_table.shape[0]
    vocab = var_embed.shape[0]
    rows = seq // groups
    own = width // groups
    count = channels * groups
    slots = [member ^ k for k in range(groups)]
    member_one = member.reshape(1).astype(jnp.int32)
    core_one = core.reshape(1).astype(jnp.int32)
    bits = chip_bits()
    assert bits
    high = is_high(bits[0])
    high_one = high.reshape(1).astype(jnp.int32)
    half = width // 2
    gain_one = ln1_gain.astype(f32)
    gain_two = ln2_gain.astype(f32)

    mine = jnp.concatenate(
        [
            field_patches.reshape(channels, pixel_count, seq),
            patch_weight,
        ],
        axis=2,
    )
    grad_out = cotangent.reshape(rows, width)
    grad_act = lax.dot_general(grad_out, mlp_out, NT, preferred_element_type=f32).astype(bf16)
    ids = jnp.concatenate([lax.dynamic_slice_in_dim(var_ids, slot * channels, channels) for slot in slots])
    table_pick = (ids[:, None] == jnp.arange(vocab, dtype=jnp.int32)[None, :]).astype(bf16)
    head_of = jnp.arange(width, dtype=jnp.int32) // HEAD_DIM
    spread = head_of[:, None] == jnp.arange(2 * HEAD_DIM, dtype=jnp.int32)[None, :]
    query_block = jnp.where(spread, agg_query[:, None], jnp.zeros((), bf16))
    query_keys = jnp.dot(agg_key, query_block, preferred_element_type=f32) * 0.125
    grad_out_other = swap(lax.dynamic_slice_in_dim(grad_out, (1 - core) * half, half, axis=1), "core", 1)
    arrived, grad_act, table_pick, query_keys, grad_out_other = fence(
        from_all(mine, groups), grad_act, table_pick, query_keys, grad_out_other
    )
    pixels, key_rows, values, values_t, by_slot = prepare(
        arrived, table_pick, var_embed, query_keys, agg_value, seq
    )

    hidden_t, qkv, resid_zero, att_low = front(
        member_one, lead_bucket, pixels, key_rows, values_t, agg_out, lead_table, gain_one[None], attn_qkv, groups
    )

    hidden_t, att_low, qkv = fence(hidden_t, att_low, qkv)
    hidden_other, att_other = swap(hidden_t, "core", 1), swap(att_low, "core", 1)

    block = min(512, rows)
    mixed_parts, lse_parts, received = [None] * groups, [None] * groups, [None] * groups
    for k in reversed(range(groups)):
        mixed_parts[k], lse_parts[k] = attend(member_one, qkv, k, rows, block)
        if k + 1 < groups:
            received[k + 1], mixed_parts[k], qkv = fence(received[k + 1], mixed_parts[k], qkv)
            if k + 2 == groups:
                hidden_other, att_other, qkv = fence(hidden_other, att_other, qkv)
        received[k] = swap(mixed_parts[k], "var", k) if k else mixed_parts[k]

    act, act_t, gu_send, gu_keep, grad_bias, resid_one, hidden_two_t, mixed_t = inner_part(
        member_one, core_one, received, attn_out, resid_zero, gain_two[None], mlp_in, mlp_in_bias.astype(f32)[None], grad_act
    )
    gu_send, act_t, act, hidden_two_t, mixed_t = fence(gu_send, act_t, act, hidden_two_t, mixed_t)
    act_other, gu_other, hidden_two_other, mixed_other = (
        swap(value, "core", 1) for value in (act_t, gu_send, hidden_two_t, mixed_t)
    )
    output, grad_resid_one, grad_branch, branch_send, grad_mixed, grad_gain_two = outer_part(
        core_one, act, gu_send, gu_keep, mlp_in, mlp_out, attn_out, resid_one, gain_two[None], grad_out, groups
    )
    act_other, gu_other, hidden_two_other, mixed_other, grad_mixed, branch_send, output = fence(
        act_other, gu_other, hidden_two_other, mixed_other, grad_mixed, branch_send, output
    )
    output = output.reshape(samples, rows, width)

    branch_other = swap(branch_send, "core", 1)
    grad_heads = exchange(grad_mixed).reshape(seq, own)
    branch_other, act_t, act_other = fence(branch_other, act_t, act_other)
    out_y, out_y_send, out_x, out_x_send = out_grad(core_one, act_t, act_other, grad_out, grad_out_other)
    branch_other, out_y, out_y_send, out_x, out_x_send = fence(branch_other, out_y, out_y_send, out_x, out_x_send)
    in_part, in_part_send = in_grad(
        core_one,
        high_one,
        hidden_two_t,
        hidden_two_other,
        gu_keep,
        gu_other,
        mixed_t,
        mixed_other,
        grad_branch,
        branch_other,
    )
    out_y_came, out_x_came = swap(out_y_send, "var", 2), swap(out_x_send, "var", 1)
    grad_heads, in_part_send, in_part = fence(grad_heads, in_part_send, in_part)

    pair = 2 * HEAD_DIM
    pairs = own // pair
    assert pairs == 2
    in_part_came = swap(in_part_send, "chip", bits[0])
    first = attend_back(member_one, qkv, grad_heads, mixed_parts, lse_parts, 0, 512)
    first, qkv, out_y_came, out_x_came = fence(first, qkv, out_y_came, out_x_came)
    out_y, out_y_send = split_add(out_y, out_y_came, 2)
    out_x, out_x_send = split_add(out_x, out_x_came, 2)
    first, qkv, out_y_send, out_x_send = fence(first, qkv, out_y_send, out_x_send)
    first_came = exchange(first)
    first_other = swap(first, "core", 1)
    out_y_came, out_x_came = swap(out_y_send, "var", 1), swap(out_x_send, "var", 2)
    second = attend_back(member_one, qkv, grad_heads, mixed_parts, lse_parts, 1, 512)
    second_came = exchange(second)
    first_came, first_other, second, in_part_came, out_y_came, out_x_came = fence(
        first_came, first_other, second, in_part_came, out_y_came, out_x_came
    )
    second_other = swap(second, "core", 1)
    out_keep, out_send = choose(high_one, out_y, out_y_came, out_x, out_x_came)
    out_came = swap(out_send, "chip", bits[0])
    in_y, in_y_send, in_x, in_x_send = split_add(in_part, in_part_came, 4)
    second_other, in_y_send, in_x_send = fence(second_other, in_y_send, in_x_send)
    weight_qkv = qkv_grad(core_one, hidden_t, hidden_other, (first, second), (first_other, second_other))
    second_came, weight_qkv, in_y_send, in_x_send, grad_resid_one, out_came = fence(
        second_came, weight_qkv, in_y_send, in_x_send, grad_resid_one, out_came
    )
    rest = bits[1:]

    def scatter_parts(keep, came, bit):
        return [pick_add(keep, came, which, 0) for which in (is_high(bit), 1 - is_high(bit))]

    def scatter_step(keep, came, bit):
        keep, send = scatter_parts(keep, came, bit)
        return keep, swap(send, "chip", partner(bit))

    out_keep, out_send = scatter_parts(out_keep, out_came, rest[0])
    second_came, out_send, in_y_send, in_x_send = fence(second_came, out_send, in_y_send, in_x_send)
    out_came = swap(out_send, "chip", partner(rest[0]))
    in_y_came, in_x_came = swap(in_y_send, "var", 2), swap(in_x_send, "var", 1)
    grad_agg, grad_agg_send, grad_att, grad_gain_one, sample_sum = join(
        core_one, first_came, second_came, attn_qkv, resid_zero, gain_one[None], grad_resid_one, agg_out
    )
    grad_agg, grad_agg_send, grad_att, out_came, in_y_came, in_x_came = fence(
        grad_agg, grad_agg_send, grad_att, out_came, in_y_came, in_x_came
    )
    for bit in rest[1:]:
        out_keep, out_came = scatter_step(out_keep, out_came, bit)
    out_rows = add(out_keep, out_came)
    in_y, in_y_send = split_add(in_y, in_y_came, 2)
    in_x, in_x_send = split_add(in_x, in_x_came, 2)
    out_rows, grad_att, grad_agg_send, in_y_send, in_x_send = fence(
        out_rows, grad_att, grad_agg_send, in_y_send, in_x_send
    )
    out_other = swap(out_rows, "chip", partner(rest[-1]))
    grad_agg_other = swap(grad_agg_send, "core", 1)
    in_y_came, in_x_came = swap(in_y_send, "var", 1), swap(in_x_send, "var", 2)

    field_own, tail, tail_send = aggregate_back(
        member_one,
        core_one,
        lead_bucket,
        pixels,
        key_rows,
        values,
        grad_att,
        (grad_bias, grad_gain_two, grad_gain_one, sample_sum),
        groups,
    )
    tail, tail_send, grad_agg_other, in_y_came, in_x_came = fence(
        tail, tail_send, grad_agg_other, in_y_came, in_x_came
    )
    tail_came = swap(tail_send, "core", 1)
    in_own = jnp.concatenate([add(in_y, in_y_came), add(in_x, in_x_came)], axis=0)
    for bit in rest:
        in_rows = in_own.shape[0] // 2
        in_own, in_send = (
            lax.dynamic_slice_in_dim(in_own, which * in_rows, in_rows) for which in (is_high(bit), 1 - is_high(bit))
        )
        if bit != rest[-1]:
            in_own = add(in_own, swap(in_send, "chip", partner(bit)))
    in_send, grad_agg_other, tail_came = fence(in_send, grad_agg_other, tail_came)
    in_came = swap(in_send, "chip", partner(rest[-1]))
    tail = add(tail, tail_came)
    deep = tail.shape[0] // 2
    tail, grad_agg_other = fence(tail, grad_agg_other)
    tail_came = swap(tail[deep:], "var", 1)
    last_send = last_grad(core_one, weight_qkv, att_low, att_other, grad_agg, grad_agg_other, groups)
    tail, tail_came, last_send, out_other = fence(tail, tail_came, last_send, out_other)
    tail = add(tail[:deep], tail_came)
    deep //= 2
    tail_came = swap(tail[deep:], "var", 2)
    out_rows = jnp.concatenate([out_rows, out_other], axis=0)
    for bit in reversed(rest[:-1]):
        out_rows = stack_other(out_rows, bit)
    tail, tail_came, last_send, out_rows, in_came = fence(tail, tail_came, last_send, out_rows, in_came)
    last_came = exchange(last_send)
    in_rows = add(in_own, in_came)
    tail = add(tail[:deep], tail_came)
    in_rows, tail, out_rows = fence(in_rows, tail, out_rows)
    in_other = swap(in_rows, "chip", partner(rest[-1]))
    tail_came = swap(tail, "chip", bits[0])
    out_other = swap(out_rows, "chip", bits[0])
    last_came, tail, out_rows = fence(last_came, tail, out_rows)
    last_keep, last_send = gather_sources(high_one, last_came, 3 * pair)
    last_send, tail, tail_came, in_other = fence(last_send, tail, tail_came, in_other)
    last_came = swap(last_send, "chip", bits[0])
    tail = add(tail, tail_came)
    for bit in rest:
        tail_came = swap(tail, "chip", partner(bit))
        if bit != rest[-1]:
            tail = add(tail, tail_came)
    tail, tail_came, out_rows, out_other = fence(tail, tail_came, out_rows, out_other)
    tail = add(tail, tail_came)
    tail_came = swap(tail, "core", 1)
    out_pieces = with_core([out_rows, out_other])
    tail, tail_came, out_pieces = fence(tail, tail_came, out_pieces)
    levels = len(bits)
    where = jnp.stack([lax.axis_index("chip"), core]).astype(jnp.int32)
    (sum_mlp_out,) = assemble(where, out_pieces, levels, [(0, 0, half, 0, half, 0)], [width])
    low, up = by_core(tail, tail_came, core)
    tail = jnp.concatenate([low[:, :half], up], axis=1)
    tail, sum_mlp_out, last_came, in_other = fence(tail, sum_mlp_out, last_came, in_other)
    for bit in rest[:-1]:
        last_keep, last_came = scatter_step(last_keep, last_came, bit)
    last_keep, last_send = scatter_parts(last_keep, last_came, rest[-1])
    in_rows = jnp.concatenate([in_rows, in_other], axis=0)
    for bit in reversed(rest[:-1]):
        in_rows = stack_other(in_rows, bit)
    tail, last_send, in_rows = fence(tail, last_send, in_rows)
    last_came = swap(last_send, "chip", partner(rest[-1]))
    tails = from_all(tail, groups)
    in_other = swap(in_rows, "chip", bits[0])
    tails = fence(*tails)
    stride = tail.shape[0]
    per_slot = (PIX + 1) * channels
    small_sum = tail[per_slot:, :width].astype(f32)
    part_size = inner_width // groups
    sum_bias = small_sum[0]
    sum_gain_two = small_sum[1, :own]
    sum_gain_one = small_sum[1, own : 2 * own]
    sum_lead = small_sum[2 : 2 + leads // groups]

    own_ids = member * (vocab // groups) + jnp.arange(16, dtype=jnp.int32)
    own_pick = jnp.where(jnp.arange(16)[:, None] < vocab // groups, own_ids[:, None] == ids[None, :], False)
    own_pick = jnp.pad(
        own_pick.reshape(16, groups, channels), ((0, 0), (0, 0), (PIX * channels, stride - per_slot))
    ).reshape(16, groups * stride)
    sum_value, sum_key, sum_query, sum_patch, sum_table = finish_tail(
        member_one,
        tails,
        by_slot,
        own_pick.astype(bf16),
        agg_value,
        query_keys,
        agg_key,
        agg_query.astype(f32)[None],
        channels,
        vocab // groups,
    )
    sum_query = sum_query.reshape(own)
    sum_value, last_came, in_rows = fence(sum_value, last_came, in_rows)
    last_rows = add(last_keep, last_came)
    last_other = swap(last_rows, "chip", partner(rest[-1]))
    field_slots = field_own.reshape(pixel_count, groups, channels, rows)
    field_parts = [swap(field_slots[:, k], "var", k) if k else field_slots[:, 0] for k in range(groups)]
    field_parts = fence(*field_parts)
    field_grad = place_field(member_one, field_parts).reshape(channels, pixel_count, samples, seq)
    field_grad, last_other, in_rows, in_other = fence(field_grad, last_other, in_rows, in_other)
    last_rows = jnp.concatenate([last_rows, last_other], axis=0)
    for bit in reversed(rest[:-1]):
        last_rows = stack_other(last_rows, bit)
    last_rows, in_rows, in_other = fence(last_rows, in_rows, in_other)
    last_other = swap(last_rows, "chip", bits[0])
    in_pieces = fence(*with_core([in_rows, in_other]))

    half_in = inner_width // 2
    units = half_in // 2
    sum_mlp_in, sum_attn_out = assemble(
        where,
        in_pieces,
        levels,
        [(0, 0, units, 0, half_in, units), (1, units, half // 2, 0, half, half // 2)],
        [inner_width, width],
        low_rows=False,
    )
    sum_mlp_in, last_rows, last_other, sum_patch, sum_table, field_grad = fence(
        sum_mlp_in, last_rows, last_other, sum_patch, sum_table, field_grad
    )
    sum_qkv, sum_agg_out = assemble(
        where,
        with_core([last_rows, last_other]),
        levels,
        [
            (0, (3 * p + t) * pair, pair, t * width + p * own, pair, 0)
            for p in range(groups)
            for t in range(3)
        ]
        + [(1, groups * 3 * pair, half, 0, half, 0)],
        [3 * width, width],
    )
    return (
        output,
        field_grad,
        sum_patch,
        sum_table,
        sum_query,
        sum_key,
        sum_value,
        sum_agg_out,
        sum_lead,
        sum_gain_one,
        sum_qkv,
        sum_attn_out,
        sum_gain_two,
        sum_mlp_in,
        sum_bias,
        sum_mlp_out,
    )


def solution(mesh):
    members, patches = mesh.shape["var"], mesh.shape["patch"]
    chips = Mesh(mesh.devices.reshape(members, patches // 2, 2), ("var", "chip", "core"))
    patch = ("chip", "core")
    placed = (
        P("var", None, patch, None),
        P(),
        P(patch),
        P("var", None, None),
        *[P()] * 13,
        P(patch, "var", None),
    )
    return jax.shard_map(
        body,
        mesh=chips,
        in_specs=placed,
        out_specs=(
            P(patch, "var", None),
            P("var", None, patch, None),
            P("var", None, None),
            P("var", None),
            P("var"),
            P("var", None),
            P("var", None),
            P("var", None),
            P("var", None),
            P("var"),
            P("var", None),
            P("var", None),
            P("var"),
            P("var", None),
            P("var"),
            P("var", None),
        ),
        check_vma=False,
    )
```

```python
from functools import partial

import jax
import jax.numpy as jnp
from jax import lax
from jax.experimental import pallas as pl
from jax.experimental.pallas import tpu as pltpu
from jax.sharding import Mesh
from jax.sharding import PartitionSpec as P

HEADS = 16
PIX = 4
HEAD_DIM = 64
LEADS = 8
FREE = 4
ORDER = (0, 2, 1, 3)
BLOCKS = tuple((k, 0) for k in range(4)) + tuple((k, 1) for k in ORDER)

f32, bf16 = jnp.float32, jnp.bfloat16
highest = lax.Precision.HIGHEST
epsilon = 1e-05
NT = (((1,), (1,)), ((), ()))
LIGHT = pl.CostEstimate(flops=1, bytes_accessed=1, transcendentals=0)
TN = (((0,), (0,)), ((), ()))


def head_weights(pixels, key_ref, head):
    scores = key_ref[PIX, :, head : head + 1]
    for c in range(PIX):
        scores = scores + pixels[c] * key_ref[c, :, head : head + 1]
    soft = jnp.exp(scores - jnp.max(scores, axis=0, keepdims=True))
    return soft * (1.0 / jnp.sum(soft, axis=0, keepdims=True))


def slot_spans(member, own):
    return [pl.ds(pl.multiple_of((member[0] ^ k) * own, own), own) for k in ORDER]


def weighted_pixels(soft, pixels):
    return jnp.concatenate(
        [(soft * pixels[c]).astype(bf16) for c in range(PIX)] + [soft.astype(bf16)], axis=0
    )


def prepare_kernel(*refs, groups):
    blocks = refs[:groups]
    pick_ref, embed_ref, query_ref, weight_ref, pixel_ref, key_ref, value_ref, value_t_ref, slot_ref, stacked, by_slot = refs[groups:]
    channels = blocks[0].shape[0]
    seq = pixel_ref.shape[2]
    count = channels * groups
    stride = by_slot.shape[0] // groups
    by_slot[...] = jnp.zeros_like(by_slot)
    embeds = jnp.dot(pick_ref[...], embed_ref[...], preferred_element_type=f32)
    for k, block in enumerate(blocks):
        for c in range(PIX + 1):
            if c < PIX:
                pixel_ref[c, k * channels : (k + 1) * channels, :] = block[:, c, :seq].astype(f32)
                rows = block[:, c, seq:].astype(f32)
            else:
                rows = embeds[k * channels : (k + 1) * channels, :]
            stacked[c * count + k * channels : c * count + (k + 1) * channels, :] = rows
            by_slot[k * stride + c * channels : k * stride + (c + 1) * channels, :] = rows
    slot_ref[...] = by_slot[...].astype(bf16)
    keys = jnp.dot(stacked[...], query_ref[...], precision=highest, preferred_element_type=f32)
    for c in range(PIX + 1):
        key_ref[c] = keys[c * count : (c + 1) * count]
    values = jnp.dot(stacked[...].astype(bf16), weight_ref[...], preferred_element_type=f32).astype(bf16)
    value_ref[...] = values
    value_t_ref[...] = values.T


def prepare(blocks, pick, var_embed, query_keys, agg_value, seq):
    groups = len(blocks)
    channels = blocks[0].shape[0]
    count = channels * groups
    width = agg_value.shape[0]
    rows = (PIX + 1) * count
    deep = rows + FREE * groups
    return pl.pallas_call(
        partial(prepare_kernel, groups=groups),
        out_shape=[
            jax.ShapeDtypeStruct((PIX, count, seq), f32),
            jax.ShapeDtypeStruct((PIX + 1, count, query_keys.shape[1]), f32),
            jax.ShapeDtypeStruct((rows, width), bf16),
            jax.ShapeDtypeStruct((width, rows), bf16),
            jax.ShapeDtypeStruct((deep, width), bf16),
        ],
        scratch_shapes=[pltpu.VMEM((rows, width), f32), pltpu.VMEM((deep, width), f32)],
        cost_estimate=LIGHT,
        name="prepare",
    )(*blocks, pick, var_embed, query_keys, agg_value)


def front_kernel(
    member,
    bucket,
    pixel_ref,
    key_ref,
    value_ref,
    out_ref,
    lead_ref,
    gain_ref,
    wq_ref,
    wk_ref,
    wv_ref,
    hidden_ref,
    qkv_ref,
    resid_ref,
    att_ref,
    att_scratch,
):
    pixels = [pixel_ref[c] for c in range(PIX)]
    for head in range(HEADS):
        soft = head_weights(pixels, key_ref, head)
        span = slice(head * HEAD_DIM, (head + 1) * HEAD_DIM)
        att_scratch[span, :] = jnp.dot(
            value_ref[span, :], weighted_pixels(soft, pixels), preferred_element_type=f32
        ).astype(bf16)
    att = att_scratch[...]
    line = lax.broadcasted_iota(jnp.int32, lead_ref.shape, 0)
    lead = jnp.sum(jnp.where(line == bucket[0], lead_ref[...].astype(f32), 0.0), axis=0, keepdims=True)
    resid = lax.dot_general(att, out_ref[...], TN, preferred_element_type=f32) + lead
    centered = resid - jnp.mean(resid, axis=1, keepdims=True)
    inverse = lax.rsqrt(jnp.mean(centered * centered, axis=1, keepdims=True) + epsilon)
    hidden = (centered * inverse * gain_ref[...]).astype(bf16)
    own = wq_ref.shape[1]
    hidden_ref[...] = hidden.T
    for t, weight in enumerate((wq_ref, wk_ref, wv_ref)):
        qkv_ref[:, t * own : (t + 1) * own] = jnp.dot(
            hidden, weight[...], preferred_element_type=f32
        ).astype(bf16)

    @pl.when(pl.program_id(0) == member[0])
    def _():
        resid_ref[...] = resid
        att_ref[...] = att


def front(member, bucket, pixels, key_rows, values_t, agg_out, lead_table, gain, attn_qkv, groups):
    width = agg_out.shape[0]
    own = width // groups
    channels, seq = pixels.shape[1:]
    rows = seq // groups
    spec = pltpu.PrefetchScalarGridSpec(
        num_scalar_prefetch=2,
        grid=(groups,),
        in_specs=[
            pl.BlockSpec((PIX, channels, rows), lambda i, m, l: (0, 0, i)),
            pl.BlockSpec(key_rows.shape, lambda i, m, l: (0, 0, 0)),
            pl.BlockSpec(values_t.shape, lambda i, m, l: (0, 0)),
            pl.BlockSpec(agg_out.shape, lambda i, m, l: (0, 0)),
            pl.BlockSpec(lead_table.shape, lambda i, m, l: (0, 0)),
            pl.BlockSpec((1, width), lambda i, m, l: (0, 0)),
            pl.BlockSpec((width, own), lambda i, m, l: (0, m[0])),
            pl.BlockSpec((width, own), lambda i, m, l: (0, groups + m[0])),
            pl.BlockSpec((width, own), lambda i, m, l: (0, 2 * groups + m[0])),
        ],
        out_specs=[
            pl.BlockSpec((width, rows), lambda i, m, l: (0, i)),
            pl.BlockSpec((rows, 3 * own), lambda i, m, l: (i, 0)),
            pl.BlockSpec((rows, width), lambda i, m, l: (0, 0)),
            pl.BlockSpec((width, rows), lambda i, m, l: (0, 0)),
        ],
        scratch_shapes=[pltpu.VMEM((width, rows), bf16)],
    )
    return pl.pallas_call(
        front_kernel,
        grid_spec=spec,
        out_shape=[
            jax.ShapeDtypeStruct((width, seq), bf16),
            jax.ShapeDtypeStruct((seq, 3 * own), bf16),
            jax.ShapeDtypeStruct((rows, width), f32),
            jax.ShapeDtypeStruct((width, rows), bf16),
        ],
        cost_estimate=LIGHT,
        name="front",
    )(member, bucket, pixels, key_rows, values_t, agg_out, lead_table, gain, attn_qkv, attn_qkv, attn_qkv)


def attend_kernel(member, q_ref, k_ref, v_ref, mixed_ref, lse_ref):
    rows = q_ref.shape[0]
    lane = lax.broadcasted_iota(jnp.int32, (1, 2 * HEAD_DIM), 1)
    queries = q_ref[...] * jnp.asarray(0.125, bf16)
    mixed = jnp.zeros((rows, 2 * HEAD_DIM), f32)
    seq = k_ref.shape[0]
    for part in range(2):
        keep = (lane // HEAD_DIM) == part
        query = jnp.where(keep, queries, jnp.zeros_like(queries))
        top = total = out = None
        for span in (slice(0, seq // 2), slice(seq // 2, seq)):
            scores = lax.dot_general(query, k_ref[span, :], NT, preferred_element_type=f32)
            peak = jnp.max(scores, axis=1, keepdims=True)
            if top is not None:
                peak = jnp.maximum(peak, top)
            soft = jnp.exp(scores - peak)
            weight = jnp.sum(soft, axis=1, keepdims=True)
            value = jnp.dot(soft.astype(bf16), v_ref[span, :], preferred_element_type=f32)
            if top is None:
                total, out = weight, value
            else:
                scale = jnp.exp(top - peak)
                total, out = total * scale + weight, out * scale + value
            top = peak
        mixed = jnp.where(keep, out * (1.0 / total), mixed)
        lse = jnp.broadcast_to(top + jnp.log(total), (rows, 2 * HEAD_DIM))
        lse_ref[0, part : part + 1, :] = lse.T[0:1, :]
    mixed_ref[...] = mixed.astype(bf16)


def attend(member, qkv, slot, rows, block):
    seq = qkv.shape[0]
    pair = 2 * HEAD_DIM
    pairs = qkv.shape[1] // (3 * pair)
    steps = rows // block
    spec = pltpu.PrefetchScalarGridSpec(
        num_scalar_prefetch=1,
        grid=(pairs, steps),
        in_specs=[
            pl.BlockSpec((block, pair), lambda p, i, m: ((m[0] ^ slot) * steps + i, p)),
            pl.BlockSpec((seq, pair), lambda p, i, m: (0, pairs + p)),
            pl.BlockSpec((seq, pair), lambda p, i, m: (0, 2 * pairs + p)),
        ],
        out_specs=[
            pl.BlockSpec((block, pair), lambda p, i, m: (i, p)),
            pl.BlockSpec((1, 2, block), lambda p, i, m: (p, 0, i)),
        ],
    )
    return pl.pallas_call(
        attend_kernel,
        grid_spec=spec,
        out_shape=[
            jax.ShapeDtypeStruct((rows, pairs * pair), bf16),
            jax.ShapeDtypeStruct((pairs, 2, rows), f32),
        ],
        cost_estimate=LIGHT,
        name="attend",
    )(member, qkv, qkv, qkv)


def attend_back_kernel(member, q_ref, k_ref, v_ref, g_ref, *refs, chunk, groups):
    mixed_refs, lse_refs = refs[:groups], refs[groups : 2 * groups]
    out_ref, dk_acc, dv_acc, kt = refs[2 * groups :]
    i = pl.program_id(0)
    slot = i ^ member[0]
    mixed, lse_rows = mixed_refs[0][...], lse_refs[0][0]
    for k in range(1, groups):
        mixed = jnp.where(slot == k, mixed_refs[k][...], mixed)
        lse_rows = jnp.where(slot == k, lse_refs[k][0], lse_rows)
    block = q_ref.shape[0]
    seq = k_ref.shape[0]
    pair = 2 * HEAD_DIM
    lane = lax.broadcasted_iota(jnp.int32, (1, pair), 1)
    side = lax.broadcasted_iota(jnp.int32, (pair, 1), 0)

    @pl.when(i == 0)
    def _():
        dk_acc[...] = jnp.zeros_like(dk_acc)
        dv_acc[...] = jnp.zeros_like(dv_acc)
        kt[...] = k_ref[...].T

    queries = q_ref[...] * jnp.asarray(0.125, bf16)
    grads = g_ref[...]
    product = (grads.astype(f32) * mixed.astype(f32)).T
    grad_query = jnp.zeros((pair, block), f32)
    for part in range(2):
        keep = (lane // HEAD_DIM) == part
        query = jnp.where(keep, queries, jnp.zeros_like(queries))
        grad = jnp.where(keep, grads, jnp.zeros_like(grads))
        delta = jnp.sum(product[part * HEAD_DIM : (part + 1) * HEAD_DIM], axis=0, keepdims=True)
        lse = lse_rows[part : part + 1, :]
        total = jnp.zeros((pair, block), f32)
        for at in range(0, seq, chunk):
            span = pl.ds(at, chunk)
            scores = lax.dot_general(k_ref[span, :], query, NT, preferred_element_type=f32)
            soft = jnp.exp(scores - lse)
            through = lax.dot_general(v_ref[span, :], grad, NT, preferred_element_type=f32)
            grad_scores = (soft * (through - delta)).astype(bf16)
            dv_acc[span, :] += jnp.dot(soft.astype(bf16), grad, preferred_element_type=f32)
            dk_acc[span, :] += jnp.dot(grad_scores, query, preferred_element_type=f32)
            total += jnp.dot(kt[:, span], grad_scores, preferred_element_type=f32)
        grad_query = jnp.where((side // HEAD_DIM) == part, total, grad_query)
    out_ref[pl.ds(pl.multiple_of(i * block, block), block), 0:pair] = (grad_query.T * 0.125).astype(bf16)

    @pl.when(i == pl.num_programs(0) - 1)
    def _():
        out_ref[:, pair : 2 * pair] = dk_acc[...].astype(bf16)
        out_ref[:, 2 * pair : 3 * pair] = dv_acc[...].astype(bf16)


def attend_back(member, qkv, grads, mixed, lse, which, chunk):
    seq = qkv.shape[0]
    groups = len(mixed)
    rows = seq // groups
    pair = 2 * HEAD_DIM
    pairs = qkv.shape[1] // (3 * pair)
    spec = pltpu.PrefetchScalarGridSpec(
        num_scalar_prefetch=1,
        grid=(groups,),
        in_specs=[
            pl.BlockSpec((rows, pair), lambda i, m: (i, which)),
            pl.BlockSpec((seq, pair), lambda i, m: (0, pairs + which)),
            pl.BlockSpec((seq, pair), lambda i, m: (0, 2 * pairs + which)),
            pl.BlockSpec((rows, pair), lambda i, m: (i, which)),
        ]
        + [pl.BlockSpec((rows, pair), lambda i, m: (0, which))] * groups
        + [pl.BlockSpec((1, 2, rows), lambda i, m: (which, 0, 0))] * groups,
        out_specs=pl.BlockSpec((seq, 3 * pair), lambda i, m: (0, 0)),
        scratch_shapes=[pltpu.VMEM((seq, pair), f32), pltpu.VMEM((seq, pair), f32), pltpu.VMEM((pair, seq), bf16)],
    )
    return pl.pallas_call(
        partial(attend_back_kernel, chunk=min(chunk, seq), groups=groups),
        grid_spec=spec,
        out_shape=jax.ShapeDtypeStruct((seq, 3 * pair), bf16),
        cost_estimate=LIGHT,
        name="attend_back",
    )(member, qkv, qkv, qkv, grads, *mixed, *lse)


def put_tail(tail, values, span):
    groups = len(ORDER)
    channels = values.shape[0] // ((PIX + 1) * groups)
    stride = tail.shape[0] // groups
    for at, k in enumerate(ORDER):
        for c in range(PIX + 1):
            row, source = at * stride + c * channels, (c * groups + k) * channels
            tail[row : row + channels, span] = values[source : source + channels]


def aggregate_back_kernel(
    member, core, bucket, pixel_ref, key_ref, value_ref, grad_ref, bias_ref, gain2_ref, gain1_ref, sum_ref,
    field_ref, keep_ref, send_ref, tail
):
    count, rows = pixel_ref.shape[1:]
    pair = 2 * HEAD_DIM
    pixels = [pixel_ref[c] for c in range(PIX)]
    lane = lax.broadcasted_iota(jnp.int32, (1, pair), 1)
    side = lax.broadcasted_iota(jnp.int32, (pair, 1), 0)
    field = [jnp.zeros((count, rows), f32) for _ in range(PIX)]
    keys = [jnp.zeros((count, pair), f32) for _ in range(PIX + 1)]
    for which in range(HEADS // 2):
        span = slice(which * pair, (which + 1) * pair)
        values, grads = value_ref[:, span], grad_ref[span, :]
        total = jnp.zeros(((PIX + 1) * count, pair), f32)
        for part in range(2):
            head = which * 2 + part
            grad = jnp.where((side // HEAD_DIM) == part, grads, jnp.zeros_like(grads))
            through = jnp.dot(values, grad, preferred_element_type=f32)
            kinds = [through[c * count : (c + 1) * count] for c in range(PIX + 1)]
            soft = head_weights(pixels, key_ref, head)
            grad_soft = kinds[PIX]
            for c in range(PIX):
                grad_soft = grad_soft + pixels[c] * kinds[c]
            weighed = soft * grad_soft
            grad_scores = weighed - soft * jnp.sum(weighed, axis=0, keepdims=True)
            for c in range(PIX):
                field[c] = field[c] + soft * kinds[c] + grad_scores * key_ref[c, :, head : head + 1]
                keys[c] = jnp.where(lane == head, jnp.sum(grad_scores * pixels[c], axis=1, keepdims=True), keys[c])
            keys[PIX] = jnp.where(lane == head, jnp.sum(grad_scores, axis=1, keepdims=True), keys[PIX])
            total = total + lax.dot_general(weighted_pixels(soft, pixels), grad, NT, preferred_element_type=f32)
        put_tail(tail, total, span)
    for c in range(PIX):
        field_ref[c] = field[c].astype(bf16)
    width = value_ref.shape[1]
    put_tail(tail, jnp.concatenate(keys, axis=0), slice(width, width + pair))
    groups = len(ORDER)
    stride = tail.shape[0] // groups
    own, lines = width // groups, LEADS // groups
    for at, k in enumerate(ORDER):
        owner = member[0] ^ k
        start = (at + 1) * stride - FREE
        tail[start : start + FREE, :] = jnp.zeros((FREE, tail.shape[1]), f32)
        tail[start : start + 1, :width] = bias_ref[:, pl.ds(pl.multiple_of(owner * width, width), width)]
        chunk = pl.ds(pl.multiple_of(owner * own, own), own)
        tail[start + 1 : start + 2, :own] = gain2_ref[:, chunk]
        tail[start + 1 : start + 2, own : 2 * own] = gain1_ref[:, chunk]
        for line in range(lines):
            hit = bucket[0] == owner * lines + line
            tail[start + 2 + line : start + 3 + line, :width] = jnp.where(hit, sum_ref[...], 0.0)
    half = width // 2
    for ref, which in ((keep_ref, core[0]), (send_ref, 1 - core[0])):
        ref[:, :half] = tail[:, pl.ds(pl.multiple_of(which * half, half), half)].astype(bf16)
        ref[:, half:] = tail[:, width:].astype(bf16)


def aggregate_back(member, core, bucket, pixels, key_rows, values, grads, small, groups):
    count, seq = pixels.shape[1:]
    rows = seq // groups
    width = values.shape[1]
    deep = (PIX + 1) * count + FREE * groups
    wide = width // 2 + 2 * HEAD_DIM

    def whole(*shape):
        return pl.BlockSpec(shape, lambda i, *_: (0,) * len(shape))

    spec = pltpu.PrefetchScalarGridSpec(
        num_scalar_prefetch=3,
        grid=(1,),
        in_specs=[
            pl.BlockSpec((PIX, count, rows), lambda i, m, c, l: (0, 0, m[0])),
            whole(*key_rows.shape),
            whole(*values.shape),
            whole(*grads.shape),
            *[whole(*value.shape) for value in small],
        ],
        out_specs=[whole(PIX, count, rows), whole(deep, wide), whole(deep, wide)],
        scratch_shapes=[pltpu.VMEM((deep, width + 2 * HEAD_DIM), f32)],
    )
    return pl.pallas_call(
        aggregate_back_kernel,
        grid_spec=spec,
        out_shape=[
            jax.ShapeDtypeStruct((PIX, count, rows), bf16),
            jax.ShapeDtypeStruct((deep, wide), bf16),
            jax.ShapeDtypeStruct((deep, wide), bf16),
        ],
        cost_estimate=LIGHT,
        name="aggregate_back",
    )(member, core, bucket, pixels, key_rows, values, grads, *small)


def shape_of(*dims, kind=bf16):
    return jax.ShapeDtypeStruct(dims, kind)


def inner_kernel(
    member, core, mixed0, mixed1, mixed2, mixed3, wo_ref, resid_ref, gain_ref, w1_ref, b1_ref, ga_ref,
    act_ref, act_t_ref, send_ref, keep_ref, bias_ref, one_ref, hidden_ref, mixed_ref, hidden,
):
    j = pl.program_id(0)
    parts = (mixed0, mixed1, mixed2, mixed3)
    rows, own = mixed0.shape

    @pl.when(j == 0)
    def _():
        resid = resid_ref[...]
        for slot, part in enumerate(parts):
            owner = pl.ds(pl.multiple_of((member[0] ^ slot) * own, own), own)
            resid = resid + jnp.dot(part[...], wo_ref[owner, :], preferred_element_type=f32)
        one_ref[...] = resid
        centered = resid - jnp.mean(resid, axis=1, keepdims=True)
        scale = lax.rsqrt(jnp.mean(centered * centered, axis=1, keepdims=True) + epsilon)
        hidden[...] = (centered * scale * gain_ref[...]).astype(bf16)
        piece = own // 2
        for at, (slot, side) in enumerate(BLOCKS):
            start = pl.multiple_of((member[0] ^ slot) * own + side * piece, piece)
            hidden_ref[at * piece : (at + 1) * piece, :] = hidden[:, pl.ds(start, piece)].T
            mixed_ref[at * piece : (at + 1) * piece, :] = parts[slot][:, side * piece : (side + 1) * piece].T

    inner = jnp.dot(hidden[...], w1_ref[...], preferred_element_type=f32) + b1_ref[...]
    below = 0.5 + 0.5 * lax.erf(inner * 0.7071067811865476)
    act = (inner * below).astype(bf16)
    slope = below + inner * (jnp.exp(-0.5 * inner * inner) * 0.3989422804014327)
    gu = (slope * ga_ref[...].astype(f32)).astype(bf16)
    act_ref[...] = act
    act_t_ref[...] = act.T
    bias_ref[...] = jnp.sum(gu.astype(f32), axis=0, keepdims=True)

    @pl.when(j < len(parts))
    def _():
        send_ref[...] = gu

    @pl.when(j >= len(parts))
    def _():
        keep_ref[...] = gu


def inner_part(member, core, mixed, attn_out, resid, gain, mlp_in, bias, grad_act):
    rows, width = resid.shape
    inner = mlp_in.shape[1]
    groups = len(mixed)
    own = width // groups
    steps = 2 * groups
    block = inner // steps

    def natural(j, c):
        return ((j // groups) ^ (1 - c[0])) * groups + j % groups

    def spot(j, m, c):
        n = natural(j, c)
        slot = (n // 2) ^ m[0]
        return (jnp.where(n % 2 == 0, slot, 4 + (slot % 2) * 2 + slot // 2), 0)

    def whole(*shape):
        return pl.BlockSpec(shape, lambda j, m, c: (0,) * len(shape))

    def column(deep):
        return pl.BlockSpec((deep, block), lambda j, m, c: (0, natural(j, c)))

    spec = pltpu.PrefetchScalarGridSpec(
        num_scalar_prefetch=2,
        grid=(steps,),
        in_specs=[whole(rows, own)] * groups
        + [whole(width, width), whole(rows, width), whole(1, width)]
        + [column(width), column(1), column(rows)],
        out_specs=[
            column(rows),
            pl.BlockSpec((block, rows), spot),
            pl.BlockSpec((rows, block), lambda j, m, c: (0, jnp.minimum(j, groups - 1))),
            pl.BlockSpec((rows, block), lambda j, m, c: (0, jnp.maximum(j - groups, 0))),
            column(1),
            whole(rows, width),
            whole(width, rows),
            whole(width, rows),
        ],
        scratch_shapes=[pltpu.VMEM((rows, width), bf16)],
    )
    return pl.pallas_call(
        inner_kernel,
        grid_spec=spec,
        out_shape=[shape_of(rows, inner), shape_of(inner, rows)]
        + [shape_of(rows, inner // 2)] * 2
        + [shape_of(1, inner, kind=f32), shape_of(rows, width, kind=f32)]
        + [shape_of(width, rows)] * 2,
        cost_estimate=LIGHT,
        name="inner_part",
    )(member, core, *mixed, attn_out, resid, gain, mlp_in, bias, grad_act)


def outer_kernel(
    core, act_ref, send_ref, keep_ref, w1_ref, w2_ref, wo_ref, one_ref, gain_ref, g_ref,
    out_ref, gres_ref, gb_ref, gb_send_ref, gm_ref, ggain_ref, branch, grads,
):
    j = pl.program_id(0)
    groups, rows, own = gm_ref.shape
    half = send_ref.shape[1]
    branch[j] = jnp.dot(act_ref[...], w2_ref[...], preferred_element_type=f32)

    def columns(which):
        return w1_ref[:, pl.ds(pl.multiple_of(which * half, half), half)]

    grads[j] = lax.dot_general(
        send_ref[...], columns(1 - core[0]), NT, preferred_element_type=f32
    ) + lax.dot_general(keep_ref[...], columns(core[0]), NT, preferred_element_type=f32)

    @pl.when(j == pl.num_programs(0) - 1)
    def _():
        count = branch.shape[0]
        resid = one_ref[...]
        out_ref[...] = (resid + jnp.concatenate([branch[i] for i in range(count)], axis=1)).astype(bf16)
        centered = resid - jnp.mean(resid, axis=1, keepdims=True)
        scale = lax.rsqrt(jnp.mean(centered * centered, axis=1, keepdims=True) + epsilon)
        grad, plain = jnp.concatenate([grads[i] for i in range(count)], axis=1), centered * scale
        ggain_ref[...] = jnp.sum(grad * plain, axis=0, keepdims=True)
        grad = grad * gain_ref[...]
        first = jnp.mean(grad, axis=1, keepdims=True)
        second = jnp.mean(grad * plain, axis=1, keepdims=True)
        gres = g_ref[...].astype(f32) + scale * (grad - first - plain * second)
        gres_ref[...] = gres
        gb_ref[...] = gres.astype(bf16)
        width = gb_ref.shape[1]
        gb_send_ref[...] = gb_ref[:, pl.ds(pl.multiple_of((1 - core[0]) * (width // 2), width // 2), width // 2)]
        gb = gb_ref[...]
        for p in range(groups):
            gm_ref[p] = lax.dot_general(gb, wo_ref[p * own : (p + 1) * own, :], NT, preferred_element_type=f32).astype(
                bf16
            )


def outer_part(core, act, gu_send, gu_keep, mlp_in, mlp_out, attn_out, resid, gain, grad_out, groups):
    rows, width = resid.shape
    inner = mlp_in.shape[1]
    own = width // groups
    steps = 4
    block = width // steps

    def whole(*shape):
        return pl.BlockSpec(shape, lambda j, c: (0,) * len(shape))

    spec = pltpu.PrefetchScalarGridSpec(
        num_scalar_prefetch=1,
        grid=(steps,),
        in_specs=[
            whole(rows, inner),
            whole(rows, inner // 2),
            whole(rows, inner // 2),
            pl.BlockSpec((block, inner), lambda j, c: (j, 0)),
            pl.BlockSpec((inner, block), lambda j, c: (0, j)),
            whole(width, width),
            whole(rows, width),
            whole(1, width),
            whole(rows, width),
        ],
        out_specs=[
            whole(rows, width),
            whole(rows, width),
            whole(rows, width),
            whole(rows, width // 2),
            whole(groups, rows, own),
            whole(1, width),
        ],
        scratch_shapes=[pltpu.VMEM((steps, rows, block), f32), pltpu.VMEM((steps, rows, block), f32)],
    )
    return pl.pallas_call(
        outer_kernel,
        grid_spec=spec,
        out_shape=[
            shape_of(rows, width),
            shape_of(rows, width, kind=f32),
            shape_of(rows, width),
            shape_of(rows, width // 2),
            shape_of(groups, rows, own),
            shape_of(1, width, kind=f32),
        ],
        cost_estimate=LIGHT,
        name="outer_part",
    )(core, act, gu_send, gu_keep, mlp_in, mlp_out, attn_out, resid, gain, grad_out)


def both_dots(left, left_other, right, right_other):
    return jnp.dot(left[...], right[...], preferred_element_type=f32) + jnp.dot(
        left_other[...], right_other[...], preferred_element_type=f32
    )


def out_grad_kernel(core, left, left_other, right, right_other, *outs):
    total = both_dots(left, left_other, right, right_other).astype(bf16)
    for q, out in enumerate(outs):

        @pl.when(pl.program_id(0) == q)
        def _():
            out[...] = total


def out_grad(core, left, left_other, right, right_other):
    rows, deep = left.shape
    half = right.shape[1] // 2
    block = rows // 4

    spec = pltpu.PrefetchScalarGridSpec(
        num_scalar_prefetch=1,
        grid=(4,),
        in_specs=[pl.BlockSpec((block, deep), lambda i, c: (i, 0))] * 2
        + [
            pl.BlockSpec((deep, half), lambda i, c: (0, c[0])),
            pl.BlockSpec((deep, half), lambda i, c: (0, 0)),
        ],
        out_specs=[pl.BlockSpec((block, half), lambda i, c: (0, 0)) for q in range(4)],
    )
    return pl.pallas_call(
        out_grad_kernel,
        grid_spec=spec,
        out_shape=[shape_of(rows // 4, half)] * 4,
        cost_estimate=LIGHT,
        name="out_grad",
    )(core, left, left_other, right, right_other)


def in_grad_kernel(core, high, h, h_other, u, u_other, m, m_other, b, b_other, keep, send):
    units = u.shape[1]

    def put(out):
        out[:, :units] = both_dots(h, h_other, u, u_other).astype(bf16)
        out[:, units:] = both_dots(m, m_other, b, b_other).astype(bf16)

    @pl.when(pl.program_id(0) == 0)
    def _():
        put(send)

    @pl.when(pl.program_id(0) == 1)
    def _():
        put(keep)


def in_grad(core, high, h, h_other, u, u_other, m, m_other, b, b_other):
    rows, deep = h.shape
    units, branch = u.shape[1] // 2, b_other.shape[1] // 2

    def whole(*shape):
        return pl.BlockSpec(shape, lambda i, c, z: (0,) * len(shape))

    def side(i, c, z):
        return (0, z[0] ^ (1 - i))

    def core_side(i, c, z):
        return (0, 2 * c[0] + (z[0] ^ (1 - i)))

    spec = pltpu.PrefetchScalarGridSpec(
        num_scalar_prefetch=2,
        grid=(2,),
        in_specs=[
            whole(rows, deep),
            whole(rows, deep),
            pl.BlockSpec((deep, units), side),
            pl.BlockSpec((deep, units), side),
            whole(rows, deep),
            whole(rows, deep),
            pl.BlockSpec((deep, branch), core_side),
            pl.BlockSpec((deep, branch), side),
        ],
        out_specs=[whole(rows, units + branch)] * 2,
    )
    return pl.pallas_call(
        in_grad_kernel,
        grid_spec=spec,
        out_shape=[shape_of(rows, units + branch)] * 2,
        cost_estimate=LIGHT,
        name="in_grad",
    )(core, high, h, h_other, u, u_other, m, m_other, b, b_other)


def qkv_grad_kernel(core, h, h_other, *refs):
    out = refs[-1]
    for which in range(2):

        @pl.when(core[0] == which)
        def _():
            out[...] = both_dots(h, h_other, refs[which], refs[2 + which]).astype(bf16)


def qkv_grad(core, h, h_other, grads, others):
    rows, deep = h.shape
    cols = grads[0].shape[1]
    block = rows // 2
    spec = pltpu.PrefetchScalarGridSpec(
        num_scalar_prefetch=1,
        grid=(2,),
        in_specs=[pl.BlockSpec((block, deep), lambda i, c: (i, 0))] * 2
        + [pl.BlockSpec((deep, cols), lambda i, c: (0, 0))] * 4,
        out_specs=pl.BlockSpec((block, cols), lambda i, c: (i, 0)),
    )
    return pl.pallas_call(
        qkv_grad_kernel,
        grid_spec=spec,
        out_shape=shape_of(rows, cols),
        cost_estimate=LIGHT,
        name="qkv_grad",
    )(core, h, h_other, *grads, *others)


def last_grad_kernel(core, qkv_ref, a, a_other, g, g_other, out):
    cols = qkv_ref.shape[1]
    out[0, :, :cols] = qkv_ref[...]
    out[0, :, cols:] = both_dots(a, a_other, g, g_other).astype(bf16)


def last_grad(core, weight_qkv, att, att_other, grad, grad_other, groups):
    rows, deep = att.shape
    half = grad_other.shape[1]
    cols = weight_qkv.shape[1]
    block = rows // groups
    spec = pltpu.PrefetchScalarGridSpec(
        num_scalar_prefetch=1,
        grid=(groups,),
        in_specs=[
            pl.BlockSpec((block, cols), lambda i, c: (i, 0)),
            pl.BlockSpec((block, deep), lambda i, c: (i, 0)),
            pl.BlockSpec((block, deep), lambda i, c: (i, 0)),
            pl.BlockSpec((deep, half), lambda i, c: (0, c[0])),
            pl.BlockSpec((deep, half), lambda i, c: (0, 0)),
        ],
        out_specs=pl.BlockSpec((1, block, cols + half), lambda i, c: (i, 0, 0)),
    )
    return pl.pallas_call(
        last_grad_kernel,
        grid_spec=spec,
        out_shape=shape_of(groups, block, cols + half),
        cost_estimate=LIGHT,
        name="last_grad",
    )(core, weight_qkv, att, att_other, grad, grad_other)


def join_kernel(core, first_ref, second_ref, wq, wk, wv, resid_ref, gain_ref, gres_ref, out_ref, *refs):
    ga_ref, ga_send_ref, gatt_ref, ggain_ref, sum_ref, total, resid_rows, gres_rows = refs
    i = pl.program_id(0)
    pair = 2 * HEAD_DIM

    @pl.when(i == 0)
    def _():
        total[...] = jnp.zeros_like(total)

    deep = resid_ref.shape[0]
    here = pl.ds(pl.multiple_of(i * deep, deep), deep)
    resid_rows[here, :] = resid_ref[...]
    gres_rows[here, :] = gres_ref[...]
    spans = [slice(t * pair, (t + 1) * pair) for t in range(3)]
    left = jnp.concatenate([ref[:, span] for span in spans for ref in (first_ref, second_ref)], axis=1)
    weights = jnp.concatenate([wq[...], wk[...], wv[...]], axis=1)
    total[...] += lax.dot_general(left, weights, NT, preferred_element_type=f32)

    @pl.when(i == pl.num_programs(0) - 1)
    def _():
        resid = resid_rows[...]
        centered = resid - jnp.mean(resid, axis=1, keepdims=True)
        scale = lax.rsqrt(jnp.mean(centered * centered, axis=1, keepdims=True) + epsilon)
        plain = centered * scale
        grad = total[...]
        ggain_ref[...] = jnp.sum(grad * plain, axis=0, keepdims=True)
        grad = grad * gain_ref[...]
        first = jnp.mean(grad, axis=1, keepdims=True)
        second = jnp.mean(grad * plain, axis=1, keepdims=True)
        gres = gres_rows[...] + scale * (grad - first - plain * second)
        sum_ref[...] = jnp.sum(gres, axis=0, keepdims=True)
        ga = gres.astype(bf16)
        ga_ref[...] = ga
        half = ga_send_ref.shape[1]
        ga_send_ref[...] = ga_ref[:, pl.ds(pl.multiple_of((1 - core[0]) * half, half), half)]
        gatt_ref[...] = lax.dot_general(out_ref[...], ga, NT, preferred_element_type=f32).astype(bf16)


def join(core, first, second, attn_qkv, resid, gain, gres, agg_out):
    rows, width = resid.shape
    groups = first.shape[0] // rows
    own = width // groups
    cols = first.shape[1]

    def whole(*shape):
        return pl.BlockSpec(shape, lambda i, c: (0,) * len(shape))

    spec = pltpu.PrefetchScalarGridSpec(
        num_scalar_prefetch=1,
        grid=(groups,),
        in_specs=[
            pl.BlockSpec((rows, cols), lambda i, c: (i, 0)),
            pl.BlockSpec((rows, cols), lambda i, c: (i, 0)),
            pl.BlockSpec((width, own), lambda i, c: (0, i)),
            pl.BlockSpec((width, own), lambda i, c: (0, groups + i)),
            pl.BlockSpec((width, own), lambda i, c: (0, 2 * groups + i)),
            pl.BlockSpec((rows // groups, width), lambda i, c: (i, 0)),
            whole(1, width),
            pl.BlockSpec((rows // groups, width), lambda i, c: (i, 0)),
            whole(width, width),
        ],
        out_specs=[
            whole(rows, width),
            whole(rows, width // 2),
            whole(width, rows),
            whole(1, width),
            whole(1, width),
        ],
        scratch_shapes=[pltpu.VMEM((rows, width), f32)] * 3,
    )
    return pl.pallas_call(
        join_kernel,
        grid_spec=spec,
        out_shape=[
            shape_of(rows, width),
            shape_of(rows, width // 2),
            shape_of(width, rows),
            shape_of(1, width, kind=f32),
            shape_of(1, width, kind=f32),
        ],
        cost_estimate=LIGHT,
        name="join",
    )(core, first, second, attn_qkv, attn_qkv, attn_qkv, resid, gain, gres, agg_out)


def add(a, b):
    return (a.astype(f32) + b.astype(f32)).astype(bf16)


def split_add(a, b, count):
    deep = a.shape[0] // count
    return [add(a[i * deep : (i + 1) * deep], b[i * deep : (i + 1) * deep]) for i in range(count)]


def pick_add(a, b, which, axis):
    half = a.shape[axis] // 2
    return add(
        lax.dynamic_slice_in_dim(a, which * half, half, axis), lax.dynamic_slice_in_dim(b, which * half, half, axis)
    )


def whole_blocks(shapes):
    return [pl.BlockSpec(shape, lambda i, *_, n=len(shape): (0,) * n) for shape in shapes]


def choose_kernel(high, a, b, c, d, keep, send):
    for value, (first, second) in enumerate(((keep, send), (send, keep))):

        @pl.when(high[0] == value)
        def _():
            first[...] = add(a[...], b[...])
            second[...] = add(c[...], d[...])


def choose(high, a, b, c, d):
    rows, cols = a.shape
    block = pl.BlockSpec((rows // 2, cols), lambda i, z: (i, 0))
    return pl.pallas_call(
        choose_kernel,
        grid_spec=pltpu.PrefetchScalarGridSpec(
            num_scalar_prefetch=1, grid=(2,), in_specs=[block] * 4, out_specs=[block] * 2
        ),
        out_shape=[jax.ShapeDtypeStruct(a.shape, bf16)] * 2,
        cost_estimate=LIGHT,
        name="choose",
    )(high, a, b, c, d)


def gather_sources_kernel(high, came_ref, keep, send, *, cols):
    groups, half = came_ref.shape[0], keep.shape[0]
    for out, which in ((keep, high[0]), (send, 1 - high[0])):
        span = pl.ds(pl.multiple_of(which * half, half), half)
        total = jnp.zeros((half, came_ref.shape[2] - cols), f32)
        for p in range(groups):
            out[:, p * cols : (p + 1) * cols] = came_ref[p, span, :cols]
            total = total + came_ref[p, span, cols:].astype(f32)
        out[:, groups * cols :] = total.astype(bf16)


def gather_sources(high, came, cols):
    groups, rows, wide = came.shape
    shape = (rows // 2, groups * cols + wide - cols)
    spec = pltpu.PrefetchScalarGridSpec(
        num_scalar_prefetch=1, grid=(1,), in_specs=whole_blocks([came.shape]), out_specs=whole_blocks([shape] * 2)
    )
    return pl.pallas_call(
        partial(gather_sources_kernel, cols=cols),
        grid_spec=spec,
        out_shape=[jax.ShapeDtypeStruct(shape, bf16)] * 2,
        cost_estimate=LIGHT,
        name="gather_sources",
    )(high, came)


def turned(i, levels):
    total = 0
    for k in range(levels):
        total = total + (((i >> k) & 1) << (levels - 1 - k))
    return total


def assemble_kernel(where, *refs, order, levels, spans, low_rows):
    pieces, outs = refs[:4], refs[4:]
    deep = pieces[0].shape[0] // len(order)
    for number, ref in enumerate(pieces):
        core = where[1] if number < 2 else 1 - where[1]
        for at, bits in enumerate(order):
            chip = where[0] ^ (bits ^ (number % 2))
            low = low_bit(chip, levels)
            row = turned(chip >> 1, levels - 1)
            if low_rows:
                row = row + (low << (levels - 1))
            to = pl.ds(pl.multiple_of(row * deep, deep), deep)
            for out, source, size, base, by_core, by_low in spans:
                column = pl.multiple_of(base + core * by_core + low * by_low, 128)
                outs[out][to, pl.ds(column, size)] = ref[at * deep : (at + 1) * deep, source : source + size].astype(f32)


def assemble(where, pieces, levels, spans, widths, low_rows=True):
    order = [0]
    for bit in range(levels - 1, 0, -1):
        order = order + [bits ^ (3 if mirrored(levels) else 1 << bit) for bits in order]
    rows = pieces[0].shape[0] * (2 if low_rows else 1)
    shapes = [(rows, wide) for wide in widths]
    spec = pltpu.PrefetchScalarGridSpec(
        num_scalar_prefetch=1,
        grid=(1,),
        in_specs=whole_blocks([p.shape for p in pieces]),
        out_specs=whole_blocks(shapes),
    )
    return pl.pallas_call(
        partial(assemble_kernel, order=tuple(order), levels=levels, spans=tuple(spans), low_rows=low_rows),
        grid_spec=spec,
        out_shape=[shape_of(*shape, kind=f32) for shape in shapes],
        cost_estimate=LIGHT,
        name="assemble",
    )(where, *pieces)


def field_kernel(member, *refs):
    pieces, out = refs[:-1], refs[-1]
    kinds, channels, rows = pieces[0].shape
    for k, piece in enumerate(pieces):
        at = pl.ds(pl.multiple_of((member[0] ^ k) * rows, rows), rows)
        for c in range(kinds):
            out[:, c, at] = piece[c].astype(f32)


def place_field(member, pieces):
    kinds, channels, rows = pieces[0].shape
    shape = (channels, kinds, rows * len(pieces))
    spec = pltpu.PrefetchScalarGridSpec(
        num_scalar_prefetch=1,
        grid=(1,),
        in_specs=whole_blocks([p.shape for p in pieces]),
        out_specs=whole_blocks([shape])[0],
    )
    return pl.pallas_call(
        field_kernel, grid_spec=spec, out_shape=jax.ShapeDtypeStruct(shape, f32), name="place_field"
    )(member, *pieces)


def tail_kernel(member, *refs, groups):
    tails = refs[:groups]
    stacked_ref, pick_ref, value_ref, qk_ref, key_ref, query_ref = refs[groups : groups + 6]
    gvalue_ref, gkey_ref, gquery_ref, patch_ref, table_ref, gqk = refs[groups + 6 :]
    width = value_ref.shape[0]
    own = gvalue_ref.shape[0]
    at = pl.ds(pl.multiple_of(member[0] * own, own), own)
    tail = jnp.concatenate([t[...] for t in tails], axis=0)
    values, keys = tail[:, :width], tail[:, width:]
    gvalue_ref[...] = lax.dot_general(stacked_ref[:, at], values, TN, preferred_element_type=f32)
    gqk[...] = lax.dot_general(stacked_ref[...], keys, TN, preferred_element_type=f32)
    head = lax.broadcasted_iota(jnp.int32, (keys.shape[1], width), 0)
    column = lax.broadcasted_iota(jnp.int32, (keys.shape[1], width), 1) // HEAD_DIM
    spread = jnp.where(head == column, 1.0, 0.0)
    gkey_ref[...] = (
        jnp.dot(gqk[at, :], spread, precision=highest, preferred_element_type=f32) * (query_ref[...] * 0.125)
    )
    by_head = lax.dot_general(gqk[...], key_ref[...].astype(f32), TN, precision=highest, preferred_element_type=f32)
    head = lax.broadcasted_iota(jnp.int32, by_head.shape, 0)
    column = (lax.broadcasted_iota(jnp.int32, by_head.shape, 1) + member[0] * own) // HEAD_DIM
    gquery_ref[...] = jnp.sum(jnp.where(head == column, by_head, 0.0), axis=0, keepdims=True) * 0.125
    own_rows = tails[0].shape[0]
    table = jnp.dot(pick_ref[...], tail, preferred_element_type=f32).astype(bf16)
    rows = jnp.concatenate([tail[:own_rows], table], axis=0)
    total = lax.dot_general(rows[:, :width], value_ref[...], NT, preferred_element_type=f32) + lax.dot_general(
        rows[:, width:].astype(f32), qk_ref[...], NT, precision=highest, preferred_element_type=f32
    )
    channels = patch_ref.shape[0]
    for c in range(PIX):
        patch_ref[:, c, :] = total[c * channels : (c + 1) * channels]
    table_ref[...] = total[own_rows : own_rows + table_ref.shape[0]]


def finish_tail(member, tails, stacked, pick, agg_value, query_keys, agg_key, agg_query, channels, lines):
    groups = len(tails)
    width = agg_value.shape[0]
    own = width // groups
    args = [*tails, stacked, pick, agg_value, query_keys]
    spec = pltpu.PrefetchScalarGridSpec(
        num_scalar_prefetch=1,
        grid=(1,),
        in_specs=whole_blocks([x.shape for x in args])
        + [pl.BlockSpec((width, own), lambda i, m: (0, m[0])), pl.BlockSpec((1, width), lambda i, m: (0, 0))],
        out_specs=whole_blocks([(own, width), (own, width), (1, own), (channels, PIX, width), (lines, width)]),
        scratch_shapes=[pltpu.VMEM((width, query_keys.shape[1]), f32)],
    )
    return pl.pallas_call(
        partial(tail_kernel, groups=groups),
        grid_spec=spec,
        out_shape=[
            jax.ShapeDtypeStruct((own, width), f32),
            jax.ShapeDtypeStruct((own, width), f32),
            jax.ShapeDtypeStruct((1, own), f32),
            jax.ShapeDtypeStruct((channels, PIX, width), f32),
            jax.ShapeDtypeStruct((lines, width), f32),
        ],
        cost_estimate=LIGHT,
        name="finish_tail",
    )(member, *args, agg_key, agg_query)


def fence(*values):
    return lax.optimization_barrier(values)


def swap(value, axis, bits):
    size = lax.axis_size(axis)
    return lax.ppermute(value, axis, [(i, i ^ bits) for i in range(size)])


def from_all(own, groups):
    return [own] + [swap(own, "var", k) for k in range(1, groups)]


def exchange(value):
    return lax.all_to_all(value, "var", split_axis=0, concat_axis=0, tiled=True)


def chip_bits():
    bits, bit = [], 1
    while bit < lax.axis_size("chip"):
        bits.append(bit)
        bit *= 2
    return bits


def mirrored(levels):
    return levels == 2


def partner(bit):
    levels = len(chip_bits())
    return 3 if mirrored(levels) and bit == 2 else bit


def low_bit(chip, levels):
    return (chip ^ (chip >> 1)) & 1 if mirrored(levels) else chip & 1


def is_high(bit):
    chip = lax.axis_index("chip")
    return low_bit(chip, len(chip_bits())) if bit == 1 else (chip // bit) % 2


def stack_other(value, bit):
    return jnp.concatenate([value, swap(value, "chip", partner(bit))], axis=0)


def with_core(halves):
    return [*halves, *(swap(value, "core", 1) for value in halves)]


def by_core(mine, other, core):
    return jnp.where(core == 0, mine, other), jnp.where(core == 0, other, mine)


def body(
    field_patches,
    var_ids,
    lead_bucket,
    patch_weight,
    var_embed,
    agg_query,
    agg_key,
    agg_value,
    agg_out,
    lead_table,
    ln1_gain,
    attn_qkv,
    attn_out,
    ln2_gain,
    mlp_in,
    mlp_in_bias,
    mlp_out,
    cotangent,
):
    groups = lax.axis_size("var")
    member = lax.axis_index("var")
    core = lax.axis_index("core")
    channels, pixel_count, samples, seq = field_patches.shape
    width = agg_key.shape[0]
    inner_width = mlp_in.shape[1]
    leads = lead_table.shape[0]
    vocab = var_embed.shape[0]
    rows = seq // groups
    own = width // groups
    count = channels * groups
    slots = [member ^ k for k in range(groups)]
    member_one = member.reshape(1).astype(jnp.int32)
    core_one = core.reshape(1).astype(jnp.int32)
    bits = chip_bits()
    assert bits
    high = is_high(bits[0])
    high_one = high.reshape(1).astype(jnp.int32)
    half = width // 2
    gain_one = ln1_gain.astype(f32)
    gain_two = ln2_gain.astype(f32)

    mine = jnp.concatenate(
        [
            field_patches.reshape(channels, pixel_count, seq),
            patch_weight,
        ],
        axis=2,
    )
    grad_out = cotangent.reshape(rows, width)
    grad_act = lax.dot_general(grad_out, mlp_out, NT, preferred_element_type=f32).astype(bf16)
    ids = jnp.concatenate([lax.dynamic_slice_in_dim(var_ids, slot * channels, channels) for slot in slots])
    table_pick = (ids[:, None] == jnp.arange(vocab, dtype=jnp.int32)[None, :]).astype(bf16)
    head_of = jnp.arange(width, dtype=jnp.int32) // HEAD_DIM
    spread = head_of[:, None] == jnp.arange(2 * HEAD_DIM, dtype=jnp.int32)[None, :]
    query_block = jnp.where(spread, agg_query[:, None], jnp.zeros((), bf16))
    query_keys = jnp.dot(agg_key, query_block, preferred_element_type=f32) * 0.125
    grad_out_other = swap(lax.dynamic_slice_in_dim(grad_out, (1 - core) * half, half, axis=1), "core", 1)
    arrived, grad_act, table_pick, query_keys, grad_out_other = fence(
        from_all(mine, groups), grad_act, table_pick, query_keys, grad_out_other
    )
    pixels, key_rows, values, values_t, by_slot = prepare(
        arrived, table_pick, var_embed, query_keys, agg_value, seq
    )

    hidden_t, qkv, resid_zero, att_low = front(
        member_one, lead_bucket, pixels, key_rows, values_t, agg_out, lead_table, gain_one[None], attn_qkv, groups
    )

    hidden_t, att_low, qkv = fence(hidden_t, att_low, qkv)
    hidden_other, att_other = swap(hidden_t, "core", 1), swap(att_low, "core", 1)

    block = min(512, rows)
    mixed_parts, lse_parts, received = [None] * groups, [None] * groups, [None] * groups
    for k in reversed(range(groups)):
        mixed_parts[k], lse_parts[k] = attend(member_one, qkv, k, rows, block)
        if k + 1 < groups:
            received[k + 1], mixed_parts[k], qkv = fence(received[k + 1], mixed_parts[k], qkv)
            if k + 2 == groups:
                hidden_other, att_other, qkv = fence(hidden_other, att_other, qkv)
        received[k] = swap(mixed_parts[k], "var", k) if k else mixed_parts[k]

    act, act_t, gu_send, gu_keep, grad_bias, resid_one, hidden_two_t, mixed_t = inner_part(
        member_one, core_one, received, attn_out, resid_zero, gain_two[None], mlp_in, mlp_in_bias.astype(f32)[None], grad_act
    )
    gu_send, act_t, act, hidden_two_t, mixed_t = fence(gu_send, act_t, act, hidden_two_t, mixed_t)
    act_other, gu_other, hidden_two_other, mixed_other = (
        swap(value, "core", 1) for value in (act_t, gu_send, hidden_two_t, mixed_t)
    )
    output, grad_resid_one, grad_branch, branch_send, grad_mixed, grad_gain_two = outer_part(
        core_one, act, gu_send, gu_keep, mlp_in, mlp_out, attn_out, resid_one, gain_two[None], grad_out, groups
    )
    act_other, gu_other, hidden_two_other, mixed_other, grad_mixed, branch_send, output = fence(
        act_other, gu_other, hidden_two_other, mixed_other, grad_mixed, branch_send, output
    )
    output = output.reshape(samples, rows, width)

    branch_other = swap(branch_send, "core", 1)
    grad_heads = exchange(grad_mixed).reshape(seq, own)
    branch_other, act_t, act_other = fence(branch_other, act_t, act_other)
    out_y, out_y_send, out_x, out_x_send = out_grad(core_one, act_t, act_other, grad_out, grad_out_other)
    branch_other, out_y, out_y_send, out_x, out_x_send = fence(branch_other, out_y, out_y_send, out_x, out_x_send)
    in_part, in_part_send = in_grad(
        core_one,
        high_one,
        hidden_two_t,
        hidden_two_other,
        gu_keep,
        gu_other,
        mixed_t,
        mixed_other,
        grad_branch,
        branch_other,
    )
    out_y_came, out_x_came = swap(out_y_send, "var", 2), swap(out_x_send, "var", 1)
    grad_heads, in_part_send, in_part = fence(grad_heads, in_part_send, in_part)

    pair = 2 * HEAD_DIM
    pairs = own // pair
    assert pairs == 2
    in_part_came = swap(in_part_send, "chip", bits[0])
    first = attend_back(member_one, qkv, grad_heads, mixed_parts, lse_parts, 0, 512)
    first, qkv, out_y_came, out_x_came = fence(first, qkv, out_y_came, out_x_came)
    out_y, out_y_send = split_add(out_y, out_y_came, 2)
    out_x, out_x_send = split_add(out_x, out_x_came, 2)
    first, qkv, out_y_send, out_x_send = fence(first, qkv, out_y_send, out_x_send)
    first_came = exchange(first)
    first_other = swap(first, "core", 1)
    out_y_came, out_x_came = swap(out_y_send, "var", 1), swap(out_x_send, "var", 2)
    second = attend_back(member_one, qkv, grad_heads, mixed_parts, lse_parts, 1, 512)
    second_came = exchange(second)
    first_came, first_other, second, in_part_came, out_y_came, out_x_came = fence(
        first_came, first_other, second, in_part_came, out_y_came, out_x_came
    )
    second_other = swap(second, "core", 1)
    out_keep, out_send = choose(high_one, out_y, out_y_came, out_x, out_x_came)
    out_came = swap(out_send, "chip", bits[0])
    in_y, in_y_send, in_x, in_x_send = split_add(in_part, in_part_came, 4)
    second_other, in_y_send, in_x_send = fence(second_other, in_y_send, in_x_send)
    weight_qkv = qkv_grad(core_one, hidden_t, hidden_other, (first, second), (first_other, second_other))
    second_came, weight_qkv, in_y_send, in_x_send, grad_resid_one, out_came = fence(
        second_came, weight_qkv, in_y_send, in_x_send, grad_resid_one, out_came
    )
    rest = bits[1:]

    def scatter_parts(keep, came, bit):
        return [pick_add(keep, came, which, 0) for which in (is_high(bit), 1 - is_high(bit))]

    def scatter_step(keep, came, bit):
        keep, send = scatter_parts(keep, came, bit)
        return keep, swap(send, "chip", partner(bit))

    out_keep, out_send = scatter_parts(out_keep, out_came, rest[0])
    second_came, out_send, in_y_send, in_x_send = fence(second_came, out_send, in_y_send, in_x_send)
    out_came = swap(out_send, "chip", partner(rest[0]))
    in_y_came, in_x_came = swap(in_y_send, "var", 2), swap(in_x_send, "var", 1)
    grad_agg, grad_agg_send, grad_att, grad_gain_one, sample_sum = join(
        core_one, first_came, second_came, attn_qkv, resid_zero, gain_one[None], grad_resid_one, agg_out
    )
    grad_agg, grad_agg_send, grad_att, out_came, in_y_came, in_x_came = fence(
        grad_agg, grad_agg_send, grad_att, out_came, in_y_came, in_x_came
    )
    for bit in rest[1:]:
        out_keep, out_came = scatter_step(out_keep, out_came, bit)
    out_rows = add(out_keep, out_came)
    in_y, in_y_send = split_add(in_y, in_y_came, 2)
    in_x, in_x_send = split_add(in_x, in_x_came, 2)
    out_rows, grad_att, grad_agg_send, in_y_send, in_x_send = fence(
        out_rows, grad_att, grad_agg_send, in_y_send, in_x_send
    )
    out_other = swap(out_rows, "chip", partner(rest[-1]))
    grad_agg_other = swap(grad_agg_send, "core", 1)
    in_y_came, in_x_came = swap(in_y_send, "var", 1), swap(in_x_send, "var", 2)

    field_own, tail, tail_send = aggregate_back(
        member_one,
        core_one,
        lead_bucket,
        pixels,
        key_rows,
        values,
        grad_att,
        (grad_bias, grad_gain_two, grad_gain_one, sample_sum),
        groups,
    )
    tail, tail_send, grad_agg_other, in_y_came, in_x_came = fence(
        tail, tail_send, grad_agg_other, in_y_came, in_x_came
    )
    tail_came = swap(tail_send, "core", 1)
    in_own = jnp.concatenate([add(in_y, in_y_came), add(in_x, in_x_came)], axis=0)
    for bit in rest:
        in_rows = in_own.shape[0] // 2
        in_own, in_send = (
            lax.dynamic_slice_in_dim(in_own, which * in_rows, in_rows) for which in (is_high(bit), 1 - is_high(bit))
        )
        if bit != rest[-1]:
            in_own = add(in_own, swap(in_send, "chip", partner(bit)))
    in_send, grad_agg_other, tail_came = fence(in_send, grad_agg_other, tail_came)
    in_came = swap(in_send, "chip", partner(rest[-1]))
    tail = add(tail, tail_came)
    deep = tail.shape[0] // 2
    tail, grad_agg_other = fence(tail, grad_agg_other)
    tail_came = swap(tail[deep:], "var", 1)
    last_send = last_grad(core_one, weight_qkv, att_low, att_other, grad_agg, grad_agg_other, groups)
    tail, tail_came, last_send, out_other = fence(tail, tail_came, last_send, out_other)
    tail = add(tail[:deep], tail_came)
    deep //= 2
    tail_came = swap(tail[deep:], "var", 2)
    out_rows = jnp.concatenate([out_rows, out_other], axis=0)
    for bit in reversed(rest[:-1]):
        out_rows = stack_other(out_rows, bit)
    tail, tail_came, last_send, out_rows, in_came = fence(tail, tail_came, last_send, out_rows, in_came)
    last_came = exchange(last_send)
    in_rows = add(in_own, in_came)
    tail = add(tail[:deep], tail_came)
    in_rows, tail, out_rows = fence(in_rows, tail, out_rows)
    in_other = swap(in_rows, "chip", partner(rest[-1]))
    tail_came = swap(tail, "chip", bits[0])
    out_other = swap(out_rows, "chip", bits[0])
    last_came, tail, out_rows = fence(last_came, tail, out_rows)
    last_keep, last_send = gather_sources(high_one, last_came, 3 * pair)
    last_send, tail, tail_came, in_other = fence(last_send, tail, tail_came, in_other)
    last_came = swap(last_send, "chip", bits[0])
    tail = add(tail, tail_came)
    for bit in rest:
        tail_came = swap(tail, "chip", partner(bit))
        if bit != rest[-1]:
            tail = add(tail, tail_came)
    tail, tail_came, out_rows, out_other = fence(tail, tail_came, out_rows, out_other)
    tail = add(tail, tail_came)
    tail_came = swap(tail, "core", 1)
    out_pieces = with_core([out_rows, out_other])
    tail, tail_came, out_pieces = fence(tail, tail_came, out_pieces)
    levels = len(bits)
    where = jnp.stack([lax.axis_index("chip"), core]).astype(jnp.int32)
    (sum_mlp_out,) = assemble(where, out_pieces, levels, [(0, 0, half, 0, half, 0)], [width])
    low, up = by_core(tail, tail_came, core)
    tail = jnp.concatenate([low[:, :half], up], axis=1)
    tail, sum_mlp_out, last_came, in_other = fence(tail, sum_mlp_out, last_came, in_other)
    for bit in rest[:-1]:
        last_keep, last_came = scatter_step(last_keep, last_came, bit)
    last_keep, last_send = scatter_parts(last_keep, last_came, rest[-1])
    in_rows = jnp.concatenate([in_rows, in_other], axis=0)
    for bit in reversed(rest[:-1]):
        in_rows = stack_other(in_rows, bit)
    tail, last_send, in_rows = fence(tail, last_send, in_rows)
    last_came = swap(last_send, "chip", partner(rest[-1]))
    tails = from_all(tail, groups)
    in_other = swap(in_rows, "chip", bits[0])
    tails = fence(*tails)
    stride = tail.shape[0]
    per_slot = (PIX + 1) * channels
    small_sum = tail[per_slot:, :width].astype(f32)
    part_size = inner_width // groups
    sum_bias = small_sum[0]
    sum_gain_two = small_sum[1, :own]
    sum_gain_one = small_sum[1, own : 2 * own]
    sum_lead = small_sum[2 : 2 + leads // groups]

    own_ids = member * (vocab // groups) + jnp.arange(16, dtype=jnp.int32)
    own_pick = jnp.where(jnp.arange(16)[:, None] < vocab // groups, own_ids[:, None] == ids[None, :], False)
    own_pick = jnp.pad(
        own_pick.reshape(16, groups, channels), ((0, 0), (0, 0), (PIX * channels, stride - per_slot))
    ).reshape(16, groups * stride)
    sum_value, sum_key, sum_query, sum_patch, sum_table = finish_tail(
        member_one,
        tails,
        by_slot,
        own_pick.astype(bf16),
        agg_value,
        query_keys,
        agg_key,
        agg_query.astype(f32)[None],
        channels,
        vocab // groups,
    )
    sum_query = sum_query.reshape(own)
    sum_value, last_came, in_rows = fence(sum_value, last_came, in_rows)
    last_rows = add(last_keep, last_came)
    last_other = swap(last_rows, "chip", partner(rest[-1]))
    field_slots = field_own.reshape(pixel_count, groups, channels, rows)
    field_parts = [swap(field_slots[:, k], "var", k) if k else field_slots[:, 0] for k in range(groups)]
    field_parts = fence(*field_parts)
    field_grad = place_field(member_one, field_parts).reshape(channels, pixel_count, samples, seq)
    field_grad, last_other, in_rows, in_other = fence(field_grad, last_other, in_rows, in_other)
    last_rows = jnp.concatenate([last_rows, last_other], axis=0)
    for bit in reversed(rest[:-1]):
        last_rows = stack_other(last_rows, bit)
    last_rows, in_rows, in_other = fence(last_rows, in_rows, in_other)
    last_other = swap(last_rows, "chip", bits[0])
    in_pieces = fence(*with_core([in_rows, in_other]))

    half_in = inner_width // 2
    units = half_in // 2
    sum_mlp_in, sum_attn_out = assemble(
        where,
        in_pieces,
        levels,
        [(0, 0, units, 0, half_in, units), (1, units, half // 2, 0, half, half // 2)],
        [inner_width, width],
        low_rows=False,
    )
    sum_mlp_in, last_rows, last_other, sum_patch, sum_table, field_grad = fence(
        sum_mlp_in, last_rows, last_other, sum_patch, sum_table, field_grad
    )
    sum_qkv, sum_agg_out = assemble(
        where,
        with_core([last_rows, last_other]),
        levels,
        [
            (0, (3 * p + t) * pair, pair, t * width + p * own, pair, 0)
            for p in range(groups)
            for t in range(3)
        ]
        + [(1, groups * 3 * pair, half, 0, half, 0)],
        [3 * width, width],
    )
    return (
        output,
        field_grad,
        sum_patch,
        sum_table,
        sum_query,
        sum_key,
        sum_value,
        sum_agg_out,
        sum_lead,
        sum_gain_one,
        sum_qkv,
        sum_attn_out,
        sum_gain_two,
        sum_mlp_in,
        sum_bias,
        sum_mlp_out,
    )


def solution(mesh):
    members, patches = mesh.shape["var"], mesh.shape["patch"]
    chips = Mesh(mesh.devices.reshape(members, patches // 2, 2), ("var", "chip", "core"))
    patch = ("chip", "core")
    placed = (
        P("var", None, patch, None),
        P(),
        P(patch),
        P("var", None, None),
        *[P()] * 13,
        P(patch, "var", None),
    )
    return jax.shard_map(
        body,
        mesh=chips,
        in_specs=placed,
        out_specs=(
            P(patch, "var", None),
            P("var", None, patch, None),
            P("var", None, None),
            P("var", None),
            P("var"),
            P("var", None),
            P("var", None),
            P("var", None),
            P("var", None),
            P("var"),
            P("var", None),
            P("var", None),
            P("var"),
            P("var", None),
            P("var"),
            P("var", None),
        ),
        check_vma=False,
    )
```
